32 devices in a mesh: tower: 2 (over x), dp: 16 (over z, y, core).
Axes of the slice: x: 2, y: 2, z: 4, core: 2. Of those that a mesh axis runs over, the one named last changes fastest.
Arguments:
- tokens: bfloat16 [2, 256, 64, 768], P('tower', 'dp'), may hold values from -6 to 6
- segments: int32 [256, 64], P('dp'), may hold values from 0 to 3, never falling along the last dimension, each value on 1 to 32 neighbouring positions
- caption_image: int32 [256, 4], P('dp'), may hold values from 0 to 255
- logit_scale: float32 [1], replicated, may hold values from 30 to 80
- first_gain: bfloat16 [2, 768], P('tower'), may hold values from 0.5 to 1.5
- first_bias: bfloat16 [2, 768], P('tower'), may hold values from -1.1953125 to 1.1953125
- triple_weight: bfloat16 [2, 768, 2304], P('tower'), may hold values from -0.21875 to 0.21875
- query_bias: bfloat16 [2, 768], P('tower'), may hold values from -1.1953125 to 1.1953125
- value_bias: bfloat16 [2, 768], P('tower'), may hold values from -1.1953125 to 1.1953125
- output_weight: bfloat16 [2, 768, 768], P('tower'), may hold values from -0.875 to 0.875
- output_bias: bfloat16 [2, 768], P('tower'), may hold values from -1.1953125 to 1.1953125
- second_gain: bfloat16 [2, 768], P('tower'), may hold values from 0.5 to 1.5
- second_bias: bfloat16 [2, 768], P('tower'), may hold values from -1.1953125 to 1.1953125
- expand_weight: bfloat16 [2, 768, 3072], P('tower'), may hold values from -0.21875 to 0.21875
- expand_bias: bfloat16 [2, 3072], P('tower'), may hold values from -1.1953125 to 1.1953125
- shrink_weight: bfloat16 [2, 3072, 768], P('tower'), may hold values from -0.109375 to 0.109375
- shrink_bias: bfloat16 [2, 768], P('tower'), may hold values from -1.1953125 to 1.1953125
Outputs:
- loss: float32 [1], replicated
- scale_grad: float32 [1], replicated
- input_grad: float32 [2, 256, 64, 768], P('tower', 'dp')
- first_gain_grad: float32 [768], P(('tower', 'dp'))
- first_bias_grad: float32 [768], P(('tower', 'dp'))
- triple_weight_grad: float32 [768, 2304], P(('tower', 'dp'))
- query_bias_grad: float32 [768], P(('tower', 'dp'))
- value_bias_grad: float32 [768], P(('tower', 'dp'))
- output_weight_grad: float32 [768, 768], P(('tower', 'dp'))
- output_bias_grad: float32 [768], P(('tower', 'dp'))
- second_gain_grad: float32 [768], P(('tower', 'dp'))
- second_bias_grad: float32 [768], P(('tower', 'dp'))
- expand_weight_grad: float32 [768, 3072], P(('tower', 'dp'))
- expand_bias_grad: float32 [3072], P(('tower', 'dp'))
- shrink_weight_grad: float32 [3072, 768], P(('tower', 'dp'))
- shrink_bias_grad: float32 [768], P(('tower', 'dp'))
The draws below stay inside these ranges and needn't reach their ends.
Inputs may be any that keep to these rules, and one draw needn't show every extreme that they name: `segments`: every text row holds captions 0 to 3 in order, each at 1 to 32 positions.
All inputs are finite; a program needn't handle non-finite values.
Results may differ from the reference program's by a relative error of at most 0.012.
The reference program's roundings to bfloat16 on the way count: a program that leaves them out, or rounds other values in their place, can miss the bound.
Values may be sent and summed in bfloat16 or wider, within the bound.
A program may use at most 256 MiB of HBM per device.

```python
import math
import jax
import jax.numpy as jnp
import numpy as np
from jax import lax

D = 768
HEADS = 12
HD = 64
FF = 3072
SEQ = 64
IMG_TOK = 50
CAPS = 4
ROWS_DEV = 16
CAP_MOST = 32
ROWS = 256
IMAGES = 256
CAPTIONS = 1024
N_TOWER = 2
N_DP = 16


def touch_ends(drawn, stream_key, smallest, high):
    longest = drawn.shape.index(max(drawn.shape))
    spots = []
    for shift in (0, 1):
        where = [jax.random.randint(jax.random.fold_in(stream_key, axis), (), 0, length) for axis, length in enumerate(drawn.shape)]
        where[longest] = (where[longest] + shift) % drawn.shape[longest]
        spots.append(tuple(where))
    return drawn.at[spots[0]].set(smallest).at[spots[1]].set(high)


def block_levels(own_key, dims, shards, least, largest):
    factor_of, own = 1.0, jax.random.fold_in(own_key, 6)
    for dim, shards_of in shards:
        heights = jnp.exp(jax.random.uniform(jax.random.fold_in(own, dim), (shards_of,), jnp.float32, least / len(shards), largest / len(shards)))
        factor_of = factor_of * jnp.repeat(heights, dims[dim] // shards_of).reshape([-1 if axis == dim else 1 for axis in range(len(dims))])
    return factor_of


def length_profile(amount, total, limit, slope):
    portions = [(1 << 20) // math.isqrt(rank ** slope) + 1 for rank in range(2, amount + 1)]
    rest, holding = total - limit - (amount - 1), [1] * (amount - 1)
    while rest > 0:
        free = [i for i in range(amount - 1) if holding[i] < limit]
        whole, budget = sum([portions[i] for i in free]), rest
        for i in free:
            more = min(limit - holding[i], max(1, budget * portions[i] // whole), rest)
            holding[i] = holding[i] + more
            rest = rest - more
    return np.array([limit] + holding)


def uneven_parts(own_key, count, total, bound, skew):
    if count == 2:
        one = jax.random.randint(own_key, (), max(1, total - bound), min(bound, total - 1) + 1)
        return jnp.stack([one, total - one])
    tallies = jnp.asarray(length_profile(count, total, bound, skew), jnp.int32)
    couples = (count - 1) // 2
    giver, sink = tallies[1:1 + 2 * couples:2], tallies[2:2 + 2 * couples:2]
    slack = jnp.minimum(giver - 1, bound - sink)
    shifted = jax.random.randint(jax.random.fold_in(own_key, 1), (couples,), 0, 1 << 20) % (slack + 1)
    tallies = tallies.at[1:1 + 2 * couples:2].set(giver - shifted).at[2:2 + 2 * couples:2].set(sink + shifted)
    return tallies[jax.random.permutation(jax.random.fold_in(own_key, 2), count)]


def scatter_about(own_key, dims, width, reach, cuts=(), held_as=jnp.bfloat16):
    level = block_levels(own_key, dims, cuts, -0.22, 0.18) if cuts else 1.0
    drawn = jax.random.normal(own_key, dims, jnp.float32) * width * level
    return jnp.minimum(jnp.maximum(drawn, -reach), reach).astype(held_as)


def setup_inputs(seed: int = 0) -> dict:
    key_of = jax.random.split(jax.random.key(seed), 18)
    return {
        "tokens": scatter_about(key_of[0], (N_TOWER, ROWS, SEQ, D), 1.0, 6.0, ((0, 2), (1, 16))),
        "segments": jax.vmap(lambda own: jnp.searchsorted(jnp.cumsum(uneven_parts(own, CAPS, SEQ, CAP_MOST, 2)), jnp.arange(SEQ), side="right"))(jax.random.split(key_of[1], ROWS)).reshape((ROWS, SEQ)).astype(jnp.int32),
        "caption_image": touch_ends(jax.random.randint(key_of[2], (ROWS, CAPS), 0, IMAGES), jax.random.fold_in(key_of[2], 1), 0, IMAGES - 1).astype(jnp.int32),
        "logit_scale": jnp.clip(jax.random.uniform(key_of[3], (1,), jnp.float32, 30.0, 80.0), 30.0, 80.0),
        "first_gain": jnp.clip(1.0 + 0.1 * jax.random.normal(key_of[4], (N_TOWER, D), jnp.float32), 0.5, 1.5).astype(jnp.bfloat16),
        "first_bias": scatter_about(key_of[5], (N_TOWER, D), 0.2, 1.1953125, ((0, 2),)),
        "triple_weight": scatter_about(key_of[6], (N_TOWER, D, 3 * D), D ** -0.5, 0.21875, ((0, 2),)),
        "query_bias": scatter_about(key_of[7], (N_TOWER, D), 0.2, 1.1953125, ((0, 2),)),
        "value_bias": scatter_about(key_of[8], (N_TOWER, D), 0.2, 1.1953125, ((0, 2),)),
        "output_weight": scatter_about(key_of[9], (N_TOWER, D, D), (D // 16) ** -0.5, 0.875, ((0, 2),)),
        "output_bias": scatter_about(key_of[10], (N_TOWER, D), 0.2, 1.1953125, ((0, 2),)),
        "second_gain": jnp.clip(1.0 + 0.1 * jax.random.normal(key_of[11], (N_TOWER, D), jnp.float32), 0.5, 1.5).astype(jnp.bfloat16),
        "second_bias": scatter_about(key_of[12], (N_TOWER, D), 0.2, 1.1953125, ((0, 2),)),
        "expand_weight": scatter_about(key_of[13], (N_TOWER, D, FF), D ** -0.5, 0.21875, ((0, 2),)),
        "expand_bias": scatter_about(key_of[14], (N_TOWER, FF), 0.2, 1.1953125, ((0, 2),)),
        "shrink_weight": scatter_about(key_of[15], (N_TOWER, FF, D), FF ** -0.5, 0.109375, ((0, 2),)),
        "shrink_bias": scatter_about(key_of[16], (N_TOWER, D), 0.2, 1.1953125, ((0, 2),)),
    }


HIGH = lax.Precision.HIGHEST

@jax.custom_vjp
def low(v):
    return lax.optimization_barrier(v.astype(jnp.bfloat16)).astype(jnp.float32)

@jax.custom_vjp
def low_back(v):
    return v

def low_keep(v):
    return (low(v), None)

def low_pass(kept, grad):
    return (grad,)

def back_keep(v):
    return (v, None)

def back_low(kept, grad):
    return (low(grad),)
low.defvjp(low_keep, low_pass)
low_back.defvjp(back_keep, back_low)

def layer_norm(values, gain, shift):
    center = values - lax.optimization_barrier(jnp.mean(values, axis=-1, keepdims=True))
    spread = lax.rsqrt(lax.optimization_barrier(jnp.mean(center * center, axis=-1, keepdims=True)) + 1e-05)
    return center * spread * gain + shift

def project(values, weight):
    return jnp.einsum('rtd,de->rte', values, weight, precision=HIGH)

def block(params, inputs, seg_ids):
    gain_one, shift_one, triple_w, query_shift, value_shift, output_w, output_shift, gain_two, shift_two, expand_w, expand_shift, shrink_w, shrink_shift = params
    rows_here = inputs.shape[0]
    normed_one = low(layer_norm(inputs, gain_one, shift_one))
    triple = low_back(project(normed_one, triple_w))
    queries = low(triple[..., :D] + query_shift).reshape(rows_here, SEQ, HEADS, HD)
    key_heads = low(triple[..., D:2 * D]).reshape(rows_here, SEQ, HEADS, HD)
    value_heads = low(triple[..., 2 * D:] + value_shift).reshape(rows_here, SEQ, HEADS, HD)
    scores = low_back(jnp.einsum('rqhc,rkhc->rhqk', queries, key_heads, precision=HIGH) * 0.125)
    same_seg = (seg_ids[:, :, None] == seg_ids[:, None, :])[:, None, :, :]
    scores = jnp.where(same_seg, scores, -1e+30)
    attn_probs = low(jax.nn.softmax(scores, axis=-1))
    mixed_heads = jnp.einsum('rhqk,rkhc->rqhc', attn_probs, value_heads, precision=HIGH).reshape(rows_here, SEQ, D)
    mixed_low = low(low_back(mixed_heads))
    hidden = inputs + low_back(project(mixed_low, output_w)) + output_shift
    normed_two = low(layer_norm(hidden, gain_two, shift_two))
    expanded = low_back(project(normed_two, expand_w)) + expand_shift
    activated = low(jax.nn.gelu(expanded))
    return hidden + low_back(project(activated, shrink_w)) + shrink_shift

def pool(block_out, seg_ids):
    slot_ids = jnp.arange(CAPS, dtype=jnp.int32)
    member = (seg_ids[:, None, :] == slot_ids[None, :, None]).astype(jnp.float32)
    counts = jnp.maximum(lax.optimization_barrier(jnp.sum(member, axis=2)), 1.0)
    pooled = jnp.einsum('rst,rtd->rsd', member, block_out, precision=HIGH) / counts[:, :, None]
    return pooled * lax.rsqrt(lax.optimization_barrier(jnp.sum(pooled * pooled, axis=2, keepdims=True)) + 1e-06)

def embed(params, inputs, seg_ids):

    def one_block(pieces):
        return pool(block(params, pieces[0], pieces[1]), pieces[1])
    blocks_in = (inputs.reshape(N_DP, ROWS_DEV, SEQ, D), seg_ids.reshape(N_DP, ROWS_DEV, SEQ))
    result = lax.map(jax.checkpoint(one_block), blocks_in)
    return result.reshape(N_DP * ROWS_DEV, CAPS, D)

def reference(tokens, segments, caption_image, logit_scale, first_gain, first_bias, triple_weight, query_bias, value_bias, output_weight, output_bias, second_gain, second_bias, expand_weight, expand_bias, shrink_weight, shrink_bias):
    stacked = (first_gain, first_bias, triple_weight, query_bias, value_bias, output_weight, output_bias, second_gain, second_bias, expand_weight, expand_bias, shrink_weight, shrink_bias)
    image_params = tuple((weight[0].astype(jnp.float32) for weight in stacked))
    text_params = tuple((weight[1].astype(jnp.float32) for weight in stacked))
    position = jnp.arange(SEQ, dtype=jnp.int32)
    image_segs = jnp.broadcast_to((position >= IMG_TOK).astype(jnp.int32)[None, :], (ROWS, SEQ))
    image_emb = low(embed(image_params, tokens[0].astype(jnp.float32), image_segs)[:, 0, :])
    targets = caption_image.reshape(-1).astype(jnp.int32)

    def text_loss(text_in, params, factor):
        text_emb = low(embed(params, text_in, segments)).reshape(CAPTIONS, D)
        similar = low_back(jnp.dot(text_emb, image_emb.T, precision=HIGH))
        logits = factor[0] * similar
        row_peak = lax.optimization_barrier(jnp.max(logits, axis=1, keepdims=True))
        log_total = row_peak[:, 0] + jnp.log(lax.optimization_barrier(jnp.sum(jnp.exp(logits - row_peak), axis=1)))
        picked = jnp.take_along_axis(logits, targets[:, None], axis=1)[:, 0]
        return jnp.sum(log_total - picked)
    total, pullback = jax.vjp(text_loss, tokens[1].astype(jnp.float32), text_params, logit_scale)
    text_grad, param_grads, factor_grad = pullback(jnp.ones((), jnp.float32))
    input_grad = jnp.stack([jnp.zeros_like(text_grad), text_grad])
    loss = (total / CAPTIONS).reshape(1)
    return (loss, factor_grad, input_grad, param_grads[0], param_grads[1], param_grads[2], param_grads[3], param_grads[4], param_grads[5], param_grads[6], param_grads[7], param_grads[8], param_grads[9], param_grads[10], param_grads[11], param_grads[12])
```

```python
import functools

import jax
import jax.numpy as jnp
from jax import lax
from jax.experimental import pallas as pl
from jax.experimental.pallas import tpu as pltpu
from jax.sharding import PartitionSpec as P

HEADS = 12
IMG_TOK = 50
CAPS = 4

f32, bf16 = jnp.float32, jnp.bfloat16
GELU_C = 0.7978845608028654
GELU_A = 0.044715
STEP_ROWS = 4


def mm(a, b):
    return jnp.dot(a, b, preferred_element_type=f32)


def mm_nt(a, b):
    return lax.dot_general(a, b, (((1,), (1,)), ((), ())), preferred_element_type=f32)


def mm_tn(a, b):
    return lax.dot_general(a, b, (((0,), (0,)), ((), ())), preferred_element_type=f32)


def stats(x):
    center = x - jnp.mean(x, axis=-1, keepdims=True)
    spread = lax.rsqrt(jnp.mean(center * center, axis=-1, keepdims=True) + 1e-05)
    return center * spread, spread


def low_pair(x):
    high = x.astype(bf16)
    return high, (x - high.astype(f32)).astype(bf16)


def fwd_kernel(tok, seg, g1, b1, qb, vb, ob, g2, b2, eb, sb, w3h, woh, weh, wsh,
               qkv, probs, mixed, hidden, act, slope, member_out, pooled_out, count_out,
               w3, wo, we, ws, pool_acc, count_acc, sems):
    i = pl.program_id(0)
    steps = pl.num_programs(0)
    rows_here, length = seg.shape
    slots = rows_here * CAPS
    feat = tok.shape[1]
    block = tok.shape[0]
    is_text = lax.axis_index("tower") == 1
    copies = [pltpu.make_async_copy(src, dst, sems.at[n])
              for n, (src, dst) in enumerate(((w3h, w3), (woh, wo), (weh, we), (wsh, ws)))]

    @pl.when(i == 0)
    def _():
        for c in copies:
            c.start()
        pool_acc[...] = jnp.zeros_like(pool_acc)
        count_acc[...] = jnp.zeros_like(count_acc)

    def arrive(n):
        @pl.when(i == 0)
        def _():
            copies[n].wait()

    x = tok[...].astype(f32)
    norm, _ = stats(x)
    n1 = (norm * g1[...].astype(f32) + b1[...].astype(f32)).astype(bf16)
    arrive(0)
    qkv[:, :feat] = (mm(n1, w3[:, :feat]) + qb[...].astype(f32)).astype(bf16)
    qkv[:, feat:2 * feat] = mm(n1, w3[:, feat:2 * feat]).astype(bf16)
    qkv[:, 2 * feat:] = (mm(n1, w3[:, 2 * feat:]) + vb[...].astype(f32)).astype(bf16)

    image_seg = (lax.broadcasted_iota(jnp.int32, (1, length), 1) >= IMG_TOK).astype(jnp.int32)
    row_segs = []
    for r in range(STEP_ROWS):
        s = seg[pl.ds(STEP_ROWS * i + r, 1), :]
        row_segs.append(jnp.where(is_text, s, image_seg))
    lane = lax.broadcasted_iota(jnp.int32, (128, 128), 1)
    first_half = lane < 64
    slot_lanes = []
    for pair in range(STEP_ROWS // 2):
        base = STEP_ROWS * i + 2 * pair
        keyed = jnp.concatenate(
            [row_segs[2 * pair] * rows_here + base, row_segs[2 * pair + 1] * rows_here + (base + 1)], axis=1)
        slot_lanes.append(keyed)
        across = jnp.broadcast_to(keyed.astype(f32), (128, 128))
        bias = jnp.where(across == across.T, 0.0, -1e30)
        bias = jnp.concatenate([bias, bias], axis=0)
        t0 = pair * 128
        for hp in range(HEADS // 2):
            c0 = hp * 128
            q = qkv[t0:t0 + 128, c0:c0 + 128] * jnp.asarray(0.125, bf16)
            k = qkv[t0:t0 + 128, feat + c0:feat + c0 + 128]
            v = qkv[t0:t0 + 128, 2 * feat + c0:2 * feat + c0 + 128]
            zero = jnp.zeros_like(q)
            q2 = jnp.concatenate([jnp.where(first_half, q, zero), jnp.where(first_half, zero, q)], axis=0)
            s = mm_nt(q2, k) + bias
            e = jnp.exp(s - jnp.max(s, axis=-1, keepdims=True))
            p = (e * (1.0 / jnp.sum(e, axis=-1, keepdims=True))).astype(bf16)
            probs[256 * pair:256 * (pair + 1), c0:c0 + 128] = p
            o = mm(p, v)
            mixed[t0:t0 + 128, c0:c0 + 128] = jnp.where(first_half, o[:128], o[128:]).astype(bf16)

    arrive(1)
    hid = x + mm(mixed[...], wo[...]) + ob[...].astype(f32)
    hidden[...] = hid
    norm2, _ = stats(hid)
    n2 = (norm2 * g2[...].astype(f32) + b2[...].astype(f32)).astype(bf16)
    arrive(2)
    arrive(3)
    out = hid + sb[...].astype(f32)
    tile = 768
    for f in range(0, we.shape[1], tile):
        v = mm(n2, we[:, f:f + tile]) + eb[:, f:f + tile].astype(f32)
        v2 = v * v
        cv = v * GELU_C
        t = jnp.tanh(cv * (1.0 + GELU_A * v2))
        h = 0.5 + 0.5 * t
        a = (v * h).astype(bf16)
        act[:, f:f + tile] = a
        slope[:, f:f + tile] = (h + h * (1.0 - h) * ((2.0 * cv) * (1.0 + (3.0 * GELU_A) * v2))).astype(bf16)
        out = out + mm(a, ws[f:f + tile, :])
    slot_row = jnp.concatenate(slot_lanes, axis=1)
    hot = (lax.broadcasted_iota(jnp.int32, (slots, block), 0) == slot_row)
    member = hot.astype(f32).astype(bf16)
    member_out[...] = member
    out_hi, out_lo = low_pair(out)
    pool_acc[...] += mm(member, out_hi) + mm(member, out_lo)
    count_acc[...] += jnp.broadcast_to(jnp.sum(hot.astype(f32), axis=1, keepdims=True), count_acc.shape)

    @pl.when(i == steps - 1)
    def _():
        counts = jnp.maximum(count_acc[...], 1.0)
        count_out[...] = counts
        pooled_out[...] = pool_acc[...] / counts[:, :1]


def forward(tokens, segments, g1, b1, w3, qb, vb, wo, ob, g2, b2, we, eb, ws, sb):
    count, feat = tokens.shape
    rows_here, length = segments.shape
    slots = rows_here * CAPS
    ff = we.shape[1]
    block = STEP_ROWS * length
    steps = count // block
    pairs = STEP_ROWS // 2
    whole = lambda a: pl.BlockSpec(a.shape, lambda i: (0,) * a.ndim)
    rows = lambda width: pl.BlockSpec((block, width), lambda i: (i, 0))
    anyw = pl.BlockSpec(memory_space=pl.ANY)
    smalls = (g1, b1, qb, vb, ob, g2, b2, eb, sb)
    return pl.pallas_call(
        fwd_kernel,
        grid=(steps,),
        in_specs=[rows(feat), whole(segments)] + [whole(a) for a in smalls] + [anyw] * 4,
        out_specs=[rows(3 * feat),
                   pl.BlockSpec((256 * pairs, feat), lambda i: (i, 0)),
                   rows(feat), rows(feat), rows(ff), rows(ff),
                   pl.BlockSpec((slots, block), lambda i: (0, i)),
                   pl.BlockSpec((slots, feat), lambda i: (0, 0)),
                   pl.BlockSpec((slots, 128), lambda i: (0, 0))],
        out_shape=[jax.ShapeDtypeStruct((count, 3 * feat), bf16),
                   jax.ShapeDtypeStruct((steps * pairs * 256, feat), bf16),
                   jax.ShapeDtypeStruct((count, feat), bf16),
                   jax.ShapeDtypeStruct((count, feat), f32),
                   jax.ShapeDtypeStruct((count, ff), bf16),
                   jax.ShapeDtypeStruct((count, ff), bf16),
                   jax.ShapeDtypeStruct((slots, count), bf16),
                   jax.ShapeDtypeStruct((slots, feat), f32),
                   jax.ShapeDtypeStruct((slots, 128), f32)],
        scratch_shapes=[pltpu.VMEM(w3.shape, bf16), pltpu.VMEM(wo.shape, bf16), pltpu.VMEM(we.shape, bf16),
                        pltpu.VMEM(ws.shape, bf16), pltpu.VMEM((slots, feat), f32), pltpu.VMEM((slots, 128), f32),
                        pltpu.SemaphoreType.DMA((4,))],
        compiler_params=pltpu.CompilerParams(vmem_limit_bytes=56 << 20, dimension_semantics=("arbitrary",)),
        name="fwd",
    )(tokens, segments, *smalls, w3, wo, we, ws)


MESH = pl.DeviceIdType.MESH
PLANE = 8
BLK = 256
CH = 768
HALF = CH // 2
ROWS = HALF // PLANE
N_CH = 12


def fold(x):
    return jnp.sum(x.reshape(x.shape[0] // 8, 8, x.shape[1]), axis=0)


def bwd_kernel(member, pooled, count, caption, scale, g1, b1, g2, b2,
               qkv_h, probs_h, mixed_h, hidden_h, act_h, slope_h, tok_h, w3_h, wo_h, we_h, ws_h,
               tw_out, ow_out, ew_out, sw_out, in_out, vec_out,
               cs, snd, prv, own, prcv, swrcv, fin, swfin,
               gol, gn2, hid, spread2, n2b, n1b, tok, act, slope, ws, we, ge, qkv, w3, wo, inbuf,
               imgs, elow, ebsum, attn_sum, vec, vecrcv, vecall,
               ld, psend, precv, xsend, xrecv, plsend, plrecv, swsend, swrecv, fsend, frecv, fout,
               gsend, grecv, esend, erecv, vsend, vrecv, outsem):
    t = lax.axis_index("tower")
    d = lax.axis_index("dp")
    p = d // 2
    c = lax.rem(d, 2)
    is_text = t == 1
    count_t = gol.shape[0]
    blocks = count_t // BLK
    feat = CH
    rows_here = caption.shape[0]
    other = 1 - c

    def peer(k):
        return lax.rem(p + k, PLANE)

    def at_core(tt, pp):
        return (tt, pp * 2 + c)

    partner = (t, p * 2 + other)

    def remote(src, dst, ssem, rsem, dev):
        return pltpu.make_async_remote_copy(src_ref=src, dst_ref=dst, send_sem=ssem, recv_sem=rsem,
                                            device_id=dev, device_id_type=MESH)

    barrier = pltpu.get_barrier_semaphore()
    pl.semaphore_signal(barrier, inc=1, device_id=partner, device_id_type=MESH)
    pl.semaphore_signal(barrier, inc=1, device_id=at_core(1 - t, p), device_id_type=MESH)
    for k in range(1, PLANE):
        pl.semaphore_signal(barrier, inc=1, device_id=at_core(t, peer(k)), device_id_type=MESH)
        pl.semaphore_signal(barrier, inc=1, device_id=at_core(1 - t, peer(k)), device_id_type=MESH)

    pooled_v = pooled[...]
    inverse = lax.rsqrt(jnp.sum(pooled_v * pooled_v, axis=1, keepdims=True) + 1e-06)
    emb = pooled_v * inverse
    emb_low = emb.astype(bf16)

    def lane(q):
        return jnp.where(q < 8, q // 2, q - 4)

    def pair_copy(q):
        return remote(snd.at[lax.rem(q, 2)], prv.at[q], psend.at[q], precv.at[q], partner)

    def x_copy(q):
        return remote(cs.at[q, 0:HALF], cs.at[q, 0:HALF], xsend.at[q], xrecv.at[q], at_core(1 - t, p))

    def plane_copy(q, k):
        row = pl.multiple_of(HALF * t + ROWS * peer(k), 16)
        return remote(cs.at[q, pl.ds(row, ROWS)], prcv.at[lane(q), k], plsend.at[q, k], plrecv.at[q, k],
                      at_core(t, peer(k)))

    def sw_copy(q, zz, y):
        to = 2 * zz + y
        k = lax.rem(to - p + PLANE, PLANE)
        row = pl.multiple_of(HALF * t + 4 * ROWS * y, 16)
        return remote(cs.at[q, pl.ds(row, 4 * ROWS)], swrcv.at[k], swsend.at[zz, y], swrecv.at[k], at_core(t, to))

    def plane_send(q):
        for k in range(1, PLANE):
            plane_copy(q, k).start()

    def sw_send(q, zz):
        for y in range(2):
            @pl.when(p != 2 * zz + y)
            def _():
                sw_copy(q, zz, y).start()

    def sw_sent(q, zz):
        for y in range(2):
            @pl.when(p != 2 * zz + y)
            def _():
                sw_copy(q, zz, y).wait_send()

    def chip_sum(q):
        pair_copy(q).wait_recv()
        slot = lax.rem(q, 2)
        for r in range(0, CH, 128):
            cs[q, r:r + 128, :] = (own[slot, r:r + 128, :] + prv[q, r:r + 128, :].astype(f32)).astype(bf16)
        x_copy(q).start()

    def chunk(q, left, right_of):
        slot = lax.rem(q, 2)

        @pl.when(q >= 2)
        def _():
            pair_copy(q - 2).wait_send()
        for mine in (False, True):
            right = right_of(c if mine else other)
            for r in range(0, CH, 256):
                part = mm_tn(left[:, r:r + 256], right)
                if mine:
                    own[slot, r:r + 256, :] = part
                else:
                    snd[slot, r:r + 256, :] = part.astype(bf16)
            if not mine:
                pair_copy(q).start()

    def gather_copy(k):
        return remote(elow, imgs.at[c, p], gsend.at[k], grecv.at[k], at_core(1 - t, peer(k)))

    def share_copy():
        return remote(imgs.at[c], imgs.at[c], esend, erecv, partner)

    def load(n, src, dst):
        return pltpu.make_async_copy(src, dst, ld.at[n])

    def tile_loads(i):
        s = lax.rem(i, 2)
        out = []
        ff = act_h.shape[1]
        for h in range(2):
            col = pl.multiple_of((ff // 2) * h + HALF * i, 128)
            here = pl.ds(HALF * h, HALF)
            out.append(load(8 * s + 4 * h, act_h.at[:, pl.ds(col, HALF)], act.at[s, :, here]))
            out.append(load(8 * s + 4 * h + 1, slope_h.at[:, pl.ds(col, HALF)], slope.at[s, :, here]))
            out.append(load(8 * s + 4 * h + 2, ws_h.at[pl.ds(col, HALF)], ws.at[s, here]))
            out.append(load(8 * s + 4 * h + 3, we_h.at[:, pl.ds(col, HALF)], we.at[s, :, here]))
        return out

    hid_load = load(16, hidden_h, hid)
    tok_load = load(17, tok_h, tok)
    qkv_load = load(18, qkv_h, qkv)
    w3_load = load(19, w3_h, w3)
    wo_load = load(20, wo_h, wo)
    mixed_load = load(21, mixed_h, slope.at[0])
    probs_loads = [load(22 + h, probs_h.at[pl.ds(count_t * h, count_t)], act.at[h]) for h in range(2)]

    @pl.when(t == 0)
    def _():
        elow[...] = emb_low[:rows_here]
        pl.semaphore_wait(barrier, 2 * PLANE)
        for k in range(PLANE):
            gather_copy(k).start()
        inbuf[0] = jnp.zeros_like(inbuf[0])
        for m in range(blocks):
            pltpu.make_async_copy(inbuf.at[0], in_out.at[pl.ds(BLK * m, BLK)], outsem.at[m]).start()

        @pl.loop(0, 4)
        def _(i):
            x_copy(2 * i).wait_recv()
            sw_send(2 * i, i)
            x_copy(2 * i + 1).wait_recv()
            plane_send(2 * i + 1)

        @pl.loop(8, N_CH)
        def _(q):
            x_copy(q).wait_recv()
            plane_send(q)
        for k in range(PLANE):
            gather_copy(k).wait_send()
        for m in range(blocks):
            pltpu.make_async_copy(inbuf.at[0], in_out.at[pl.ds(BLK * m, BLK)], outsem.at[m]).wait()

    @pl.when(is_text)
    def _():
        hid_load.start()
        tok_load.start()
        for cp in tile_loads(0):
            cp.start()
        for cp in tile_loads(1):
            cp.start()
        qkv_load.start()
        w3_load.start()
        wo_load.start()
        gain2, shift2 = g2[...].astype(f32), b2[...].astype(f32)
        gain1, shift1 = g1[...].astype(f32), b1[...].astype(f32)
        hid_load.wait()

        @pl.loop(0, blocks)
        def _(m):
            here = pl.ds(pl.multiple_of(m * BLK, BLK), BLK)
            norm, spread = stats(hid[here, :])
            n2b[here, :] = (norm * gain2 + shift2).astype(bf16)
            hid[here, :] = norm
            spread2[here, :] = spread
        tok_load.wait()

        @pl.loop(0, blocks)
        def _(m):
            here = pl.ds(pl.multiple_of(m * BLK, BLK), BLK)
            norm, _s = stats(tok[here, :].astype(f32))
            n1b[here, :] = (norm * gain1 + shift1).astype(bf16)
        gn2[...] = jnp.zeros_like(gn2)
        attn_sum[...] = jnp.zeros_like(attn_sum)
        vec[...] = jnp.zeros_like(vec)
        pl.semaphore_wait(barrier, 2 * PLANE)
        for k in range(PLANE):
            gather_copy(k).wait_recv()
        share_copy().start()
        share_copy().wait_send()
        remote(imgs.at[other], imgs.at[other], esend, erecv, partner).wait_recv()

        table = imgs[...].reshape(2 * PLANE * rows_here, feat)
        dots = mm_nt(emb_low, table)
        factor = scale[0]
        logits = factor * dots
        peak = jnp.max(logits, axis=1, keepdims=True)
        weight = jnp.exp(logits - peak)
        total = jnp.sum(weight, axis=1, keepdims=True)
        wanted = jnp.concatenate([caption[:, s:s + 1] for s in range(CAPS)], axis=0)
        span = 2 * rows_here
        inside = lax.rem(wanted, span)
        wanted = (inside // rows_here) * (PLANE * rows_here) + (wanted // span) * rows_here + lax.rem(inside, rows_here)
        hot = (lax.broadcasted_iota(jnp.int32, dots.shape, 1) == wanted).astype(f32)
        picked = jnp.sum(logits * hot, axis=1, keepdims=True)
        loss_here = jnp.sum(peak + jnp.log(total) - picked, axis=0, keepdims=True)
        grad_logits = weight / total - hot
        factor_here = jnp.sum(jnp.sum(grad_logits * dots, axis=1, keepdims=True), axis=0, keepdims=True)
        grad_emb = mm((factor * grad_logits).astype(bf16), table)
        counts = count[:, :1]
        grad_pool = inverse * (grad_emb - emb * jnp.sum(emb * grad_emb, axis=1, keepdims=True))
        vec[7:8, :] = jnp.sum(grad_pool, axis=0, keepdims=True)
        column = lax.broadcasted_iota(jnp.int32, (1, feat), 1)
        vec[12:13, :] = jnp.where(column == 0, loss_here, jnp.where(column == 1, factor_here, 0.0))
        gp_hi, gp_lo = low_pair(grad_pool / counts)
        for m in range(blocks):
            gol[BLK * m:BLK * (m + 1), :] = mm_tn(member[:, BLK * m:BLK * (m + 1)], gp_hi).astype(bf16)

        @pl.loop(0, 4)
        def _(i):
            s = lax.rem(i, 2)
            for cp in tile_loads(i):
                cp.wait()
            chunk(2 * i, act.at[s], lambda h: gol[:, pl.ds(pl.multiple_of(HALF * h, 128), HALF)])

            @pl.when(i > 0)
            def _():
                chip_sum(2 * i - 1)
                plane_send(2 * i - 1)
            sums = jnp.zeros((8, feat), f32)
            for m in range(blocks):
                here = slice(BLK * m, BLK * (m + 1))
                grad = mm_nt(gol[here, :], ws[s]) * slope[s, here, :].astype(f32)
                sums = sums + fold(grad)
                ge[here, :] = grad.astype(bf16)
            sums = jnp.sum(sums, axis=0, keepdims=True)
            for h in range(2):
                ebsum[:, pl.ds(pl.multiple_of(4 * HALF * h + HALF * i, 128), HALF)] = sums[:, HALF * h:HALF * (h + 1)]
            chunk(2 * i + 1, n2b, lambda h: ge[:, pl.ds(pl.multiple_of(HALF * h, 128), HALF)])
            chip_sum(2 * i)
            sw_send(2 * i, i)
            for m in range(blocks):
                here = slice(BLK * m, BLK * (m + 1))
                gn2[here, :] += mm_nt(ge[here, :], we[s])

            @pl.when(i < 2)
            def _():
                for cp in tile_loads(i + 2):
                    cp.start()

            @pl.when(i == 2)
            def _():
                mixed_load.start()
                probs_loads[0].start()
        probs_loads[1].start()
        chip_sum(7)
        plane_send(7)

        zeros8 = jnp.zeros((8, feat), f32)

        def norm2_back(m, sums):
            here = pl.ds(pl.multiple_of(m * BLK, BLK), BLK)
            norm, g_in = hid[here, :], gn2[here, :]
            hot_m = member[:, here]
            grad_out = mm_tn(hot_m, gp_hi) + mm_tn(hot_m, gp_lo)
            g = g_in * gain2
            back = spread2[here, :] * (g - jnp.mean(g, axis=1, keepdims=True)
                                       - norm * jnp.mean(g * norm, axis=1, keepdims=True))
            gh = grad_out + back
            gn2[here, :] = gh
            gol[here, :] = gh.astype(bf16)
            return (sums[0] + fold(g_in * norm), sums[1] + fold(g_in), sums[2] + fold(gh))
        sums = lax.fori_loop(0, blocks, norm2_back, (zeros8, zeros8, zeros8))
        for row, x in ((5, sums[0]), (6, sums[1]), (4, sums[2])):
            vec[row:row + 1, :] = jnp.sum(x, axis=0, keepdims=True)
        for n in range(4):
            vec[8 + n:9 + n, :] = ebsum[:, feat * n:feat * (n + 1)]

        mixed_load.wait()
        chunk(8, slope.at[0], lambda h: gol[:, pl.ds(pl.multiple_of(HALF * h, 128), HALF)])
        wo_load.wait()
        for m in range(blocks):
            here = slice(BLK * m, BLK * (m + 1))
            ge[here, :] = mm_nt(gol[here, :], wo[...]).astype(bf16)
        chip_sum(8)
        plane_send(8)

        qkv_load.wait()
        for cp in probs_loads:
            cp.wait()
        first_half = lax.broadcasted_iota(jnp.int32, (128, 128), 1) < 64

        def split(x):
            zero = jnp.zeros_like(x)
            return jnp.concatenate([jnp.where(first_half, x, zero), jnp.where(first_half, zero, x)], axis=0)

        @pl.loop(0, count_t // 128)
        def _(rp):
            here = pl.ds(pl.multiple_of(rp * 128, 128), 128)
            half = rp // (count_t // 256)
            prow = pl.ds(pl.multiple_of(lax.rem(rp, count_t // 256) * 256, 256), 256)
            for hp in range(HEADS // 2):
                c0 = hp * 128
                q, k, v = (qkv[here, feat * n + c0:feat * n + c0 + 128] for n in range(3))
                gm2 = split(ge[here, c0:c0 + 128])
                probs = act[half, prow, c0:c0 + 128]
                probs_f = probs.astype(f32)
                gp = mm_nt(gm2, v)
                weighted = probs_f * gp
                gs = (weighted - probs_f * jnp.sum(weighted, axis=1, keepdims=True)).astype(bf16)
                gv = mm_tn(probs, gm2)
                gk = mm_tn(gs, split(q)) * 0.125
                gq2 = mm(gs, k)
                gq = jnp.where(first_half, gq2[:128], gq2[128:]) * 0.125
                for n, x in ((0, gq), (1, gk), (2, gv)):
                    qkv[here, feat * n + c0:feat * n + c0 + 128] = x.astype(bf16)
                    if n != 1:
                        at = slice((feat if n else 0) + c0, (feat if n else 0) + c0 + 128)
                        attn_sum[:, at] += fold(x)
        vec[2:3, :] = jnp.sum(attn_sum[:, :feat], axis=0, keepdims=True)
        vec[3:4, :] = jnp.sum(attn_sum[:, feat:], axis=0, keepdims=True)

        @pl.loop(0, 3)
        def _(j):
            chunk(9 + j, n1b, lambda h: qkv[:, pl.ds(pl.multiple_of(CH * j + HALF * h, 128), HALF)])

            @pl.when(j > 0)
            def _():
                chip_sum(8 + j)
                plane_send(8 + j)
        w3_load.wait()

        def norm1_back(m, sums):
            here = pl.ds(pl.multiple_of(m * BLK, BLK), BLK)
            slot = lax.rem(m, 2)

            def out_copy(mm_):
                return pltpu.make_async_copy(inbuf.at[lax.rem(mm_, 2)],
                                             in_out.at[pl.ds(pl.multiple_of(mm_ * BLK, BLK), BLK)], outsem.at[mm_])

            g_in = mm_nt(qkv[here, :], w3[...])

            @pl.when(m == 0)
            def _():
                chip_sum(11)
                plane_send(11)

            @pl.when(m >= 2)
            def _():
                out_copy(m - 2).wait()
            norm, spread = stats(tok[here, :].astype(f32))
            g = g_in * gain1
            back = spread * (g - jnp.mean(g, axis=1, keepdims=True)
                             - norm * jnp.mean(g * norm, axis=1, keepdims=True))
            inbuf[slot] = gn2[here, :] + back
            out_copy(m).start()
            return (sums[0] + fold(g_in * norm), sums[1] + fold(g_in))
        sums = lax.fori_loop(0, blocks, norm1_back, (zeros8, zeros8))
        for row, x in ((0, sums[0]), (1, sums[1])):
            vec[row:row + 1, :] = jnp.sum(x, axis=0, keepdims=True)
        for m in (blocks - 2, blocks - 1):
            pltpu.make_async_copy(inbuf.at[m % 2], in_out.at[pl.ds(BLK * m, BLK)], outsem.at[m]).wait()

    mine8 = pl.ds(pl.multiple_of(8 * c, 8), 8)
    their8 = pl.ds(pl.multiple_of(8 * other, 8), 8)

    def v_pair():
        return remote(vec.at[their8], vecrcv.at[0], vsend.at[0], vrecv.at[0], partner)

    def v_plane(k):
        return remote(vec.at[mine8], vecrcv.at[k], vsend.at[k], vrecv.at[k], at_core(t, peer(k)))

    def v_share(half):
        return remote(vecall.at[half], vecall.at[half], vsend.at[8], vrecv.at[8], partner)

    def v_across():
        return remote(vecall, vecall, vsend.at[9], vrecv.at[9], at_core(1 - t, p))

    @pl.when(is_text)
    def _():
        v_pair().start()
        v_pair().wait_recv()
        vec[mine8, :] += vecrcv[0]
        for k in range(1, PLANE):
            v_plane(k).start()

    def total_of(block, get):
        out = block
        for k in range(1, PLANE):
            out = out + get(k).astype(f32)
        return out

    def finish(q, out, col, base):
        for k in range(1, PLANE):
            plane_copy(q, k).wait_recv()
        row = pl.multiple_of(HALF * t + ROWS * p, 16)
        fin[lane(q)] = total_of(cs[q, pl.ds(row, ROWS), :].astype(f32), lambda k: prcv[lane(q), k])
        keep_copy(q, out, col).start()
        give_copy(q, out, col).start()

    def keep_copy(q, out, col):
        n = ROWS // 2
        return pltpu.make_async_copy(fin.at[lane(q), pl.ds(pl.multiple_of(n * c, 8), n)], out.at[:, pl.ds(col, HALF)],
                                     fout.at[q])

    def give_copy(q, out, col):
        n = ROWS // 2
        return remote(fin.at[lane(q), pl.ds(pl.multiple_of(n * other, 8), n)], out.at[:, pl.ds(col, HALF)],
                      fsend.at[q], frecv.at[q], partner)

    def sw_keep():
        n = 2 * ROWS
        return pltpu.make_async_copy(swfin.at[pl.ds(pl.multiple_of(n * c, 8), n)],
                                     sw_out.at[:, pl.ds(pl.multiple_of(HALF * c, 128), HALF)], fout.at[0])

    def sw_give():
        n = 2 * ROWS
        return remote(swfin.at[pl.ds(pl.multiple_of(n * other, 8), n)],
                      sw_out.at[:, pl.ds(pl.multiple_of(HALF * c, 128), HALF)], fsend.at[0], frecv.at[0], partner)

    def wait_frecv(q, out, col_other):
        n = ROWS // 2
        remote(fin.at[lane(q), pl.ds(pl.multiple_of(n * other, 8), n)], out.at[:, pl.ds(col_other, HALF)],
               fsend.at[q], frecv.at[q], partner).wait_recv()

    for k in range(1, PLANE):
        remote(cs.at[0, 0:4 * ROWS], swrcv.at[k], swsend.at[0, 0], swrecv.at[k], partner).wait_recv()
    sw_q = 2 * (p // 2)
    sw_row = pl.multiple_of(HALF * t + 4 * ROWS * lax.rem(p, 2), 16)
    swfin[...] = total_of(cs[sw_q, pl.ds(sw_row, 4 * ROWS), :].astype(f32), lambda k: swrcv[k])
    sw_keep().start()
    sw_give().start()

    def ew_col(i, h):
        return pl.multiple_of(4 * HALF * h + HALF * i, 128)

    def tw_col(j, h):
        return pl.multiple_of(CH * j + HALF * h, 128)

    def ow_col(h):
        return pl.multiple_of(HALF * h, 128)

    @pl.loop(0, 4)
    def _(i):
        finish(2 * i + 1, ew_out, ew_col(i, c), None)
    finish(8, ow_out, ow_col(c), None)

    @pl.loop(0, 3)
    def _(j):
        finish(9 + j, tw_out, tw_col(j, c), None)

    @pl.when(is_text)
    def _():
        for k in range(1, PLANE):
            v_plane(k).wait_recv()
        vecall[c] = total_of(vec[mine8, :], lambda k: vecrcv[k])
        v_share(c).start()
        v_share(other).wait_recv()
        v_across().start()
        v_across().wait_send()
        v_share(c).wait_send()
        v_pair().wait_send()
        for k in range(1, PLANE):
            v_plane(k).wait_send()
        for q in (N_CH - 2, N_CH - 1):
            pair_copy(q).wait_send()

        @pl.loop(0, N_CH)
        def _(q):
            x_copy(q).wait_send()

    @pl.when(t == 0)
    def _():
        v_across().wait_recv()
    vec_out[...] = vecall[...]

    @pl.loop(0, 4)
    def _(i):
        sw_sent(2 * i, i)
        for k in range(1, PLANE):
            plane_copy(2 * i + 1, k).wait_send()
        keep_copy(2 * i + 1, ew_out, ew_col(i, c)).wait()
        give_copy(2 * i + 1, ew_out, ew_col(i, c)).wait_send()
        wait_frecv(2 * i + 1, ew_out, ew_col(i, other))

    @pl.loop(8, N_CH)
    def _(q):
        for k in range(1, PLANE):
            plane_copy(q, k).wait_send()
    keep_copy(8, ow_out, ow_col(c)).wait()
    give_copy(8, ow_out, ow_col(c)).wait_send()
    wait_frecv(8, ow_out, ow_col(other))

    @pl.loop(0, 3)
    def _(j):
        keep_copy(9 + j, tw_out, tw_col(j, c)).wait()
        give_copy(9 + j, tw_out, tw_col(j, c)).wait_send()
        wait_frecv(9 + j, tw_out, tw_col(j, other))
    sw_keep().wait()
    sw_give().wait_send()
    remote(swfin.at[pl.ds(0, 2 * ROWS)], sw_out.at[:, pl.ds(pl.multiple_of(HALF * other, 128), HALF)],
           fsend.at[0], frecv.at[0], partner).wait_recv()

    @pl.when(is_text)
    def _():
        pass


def backward(member, pooled, count, caption, scale, g1, b1, g2, b2,
             qkv, probs, mixed, hidden, act, slope, tokens, w3, wo, we, ws):
    n_tok, feat = tokens.shape
    rows_here = caption.shape[0]
    ff = we.shape[1]
    dma = pltpu.SemaphoreType.DMA
    vm = pltpu.VMEM
    vspec = pl.BlockSpec(memory_space=pltpu.VMEM)
    sspec = pl.BlockSpec(memory_space=pltpu.SMEM)
    anyw = pl.BlockSpec(memory_space=pl.ANY)
    shape = jax.ShapeDtypeStruct
    scratch = [
        vm((N_CH, CH, HALF), bf16), vm((2, CH, HALF), bf16), vm((N_CH, CH, HALF), bf16), vm((2, CH, HALF), f32),
        vm((N_CH - 4, PLANE, ROWS, HALF), bf16), vm((PLANE, 4 * ROWS, HALF), bf16),
        vm((N_CH - 4, ROWS, HALF), f32), vm((4 * ROWS, HALF), f32),
        vm((n_tok, feat), bf16), vm((n_tok, feat), f32), vm((n_tok, feat), f32), vm((n_tok, 1), f32),
        vm((n_tok, feat), bf16), vm((n_tok, feat), bf16), vm((n_tok, feat), bf16),
        vm((2, n_tok, CH), bf16), vm((2, n_tok, CH), bf16), vm((2, CH, feat), bf16), vm((2, feat, CH), bf16),
        vm((n_tok, feat), bf16), vm((n_tok, 3 * feat), bf16), vm(w3.shape, bf16), vm(wo.shape, bf16),
        vm((2, BLK, feat), f32),
        vm((2, PLANE, rows_here, feat), bf16), vm((rows_here, feat), bf16), vm((1, ff), f32), vm((8, 2 * feat), f32),
        vm((16, feat), f32), vm((PLANE, 8, feat), f32), vm((2, 8, feat), f32),
        dma((24,)), dma((N_CH,)), dma((N_CH,)), dma((N_CH,)), dma((N_CH,)), dma((N_CH, PLANE)), dma((N_CH, PLANE)),
        dma((4, 2)), dma((PLANE,)), dma((N_CH,)), dma((N_CH,)), dma((N_CH,)),
        dma((PLANE,)), dma((PLANE,)), dma, dma, dma((10,)), dma((10,)), dma((n_tok // BLK,)),
    ]
    return pl.pallas_call(
        bwd_kernel,
        in_specs=[vspec] * 4 + [sspec] + [vspec] * 4 + [anyw] * 11,
        out_specs=[anyw] * 5 + [vspec],
        out_shape=[shape((ROWS // 2, 3 * feat), f32), shape((ROWS // 2, feat), f32), shape((ROWS // 2, ff), f32),
                   shape((2 * ROWS, feat), f32), shape((n_tok, feat), f32), shape((2, 8, feat), f32)],
        scratch_shapes=scratch,
        compiler_params=pltpu.CompilerParams(vmem_limit_bytes=61 << 20, collective_id=0, has_side_effects=True),
        name="bwd",
    )(member, pooled, count, caption, scale, g1, b1, g2, b2,
      qkv, probs, mixed, hidden, act, slope, tokens, w3, wo, we, ws)


def hand_out_kernel(scale_by, vec, tw, ow, ew, sw, inp, loss, factor, *rest):
    smalls, bigs, sems = rest[:9], rest[9:14], rest[14]
    moves = [pltpu.make_async_copy(src, dst, sems.at[n]) for n, (src, dst) in enumerate(zip((tw, ow, ew, sw, inp), bigs))]
    for move in moves:
        move.start()
    feat = vec.shape[2]
    width = smalls[0].shape[1]
    wide = smalls[8].shape[1]
    g = lax.axis_index("tower") * lax.axis_size("dp") + lax.axis_index("dp")
    turned = pltpu.roll(vec[0], lax.rem(feat - width * g, feat), axis=1)
    for n in range(8):
        smalls[n][...] = turned[n:n + 1, :width]
    per_row = feat // wide
    row = vec[1, pl.ds(g // per_row, 1), :]
    rows = jnp.broadcast_to(row, (8, feat))
    smalls[8][...] = pltpu.roll(rows, lax.rem(feat - wide * lax.rem(g, per_row), feat), axis=1)[:1, :wide]
    loss[...] = vec[1, 4:5, 0:1] * scale_by
    factor[...] = vec[1, 4:5, 1:2]
    for move in moves:
        move.wait()


def hand_out(vec, tw, ow, ew, sw, inp, captions):
    devices = lax.axis_size("tower") * lax.axis_size("dp")
    feat = vec.shape[2]
    shape = jax.ShapeDtypeStruct
    bigs = (tw, ow, ew, sw, inp)
    vspec = pl.BlockSpec(memory_space=pltpu.VMEM)
    anyw = pl.BlockSpec(memory_space=pl.ANY)
    return pl.pallas_call(
        functools.partial(hand_out_kernel, 1.0 / captions),
        in_specs=[vspec] + [anyw] * 5,
        out_specs=[vspec] * 11 + [anyw] * 5,
        out_shape=[shape((1, 1), f32)] * 2 + [shape((1, feat // devices), f32)] * 8
        + [shape((1, ew.shape[1] // devices), f32)] + [shape(a.shape, f32) for a in bigs],
        scratch_shapes=[pltpu.SemaphoreType.DMA((5,))],
        name="hand_out",
    )(vec, *bigs)


def local_fast(tokens, segments, caption_image, logit_scale, first_gain, first_bias, triple_weight, query_bias,
               value_bias, output_weight, output_bias, second_gain, second_bias, expand_weight, expand_bias,
               shrink_weight, shrink_bias):
    rows_here, length, feat = tokens.shape[1:]
    flat = tokens[0].reshape(rows_here * length, feat)
    w3, wo, we, ws = triple_weight[0], output_weight[0], expand_weight[0], shrink_weight[0]
    qkv, probs, mixed, hidden, act, slope, member, pooled, count = forward(
        flat, segments, first_gain, first_bias, w3, query_bias, value_bias, wo, output_bias,
        second_gain, second_bias, we, expand_bias, ws, shrink_bias)
    tw, ow, ew, sw, inp, vec = backward(member, pooled, count, caption_image, logit_scale, first_gain, first_bias,
                                        second_gain, second_bias, qkv, probs, mixed, hidden, act, slope, flat,
                                        w3, wo, we, ws)
    captions = rows_here * CAPS * lax.axis_size("dp")
    outs = hand_out(vec, tw, ow, ew, sw, inp, captions)
    loss, factor = outs[0].reshape(1), outs[1].reshape(1)
    g1, b1, qb, vb, ob, g2, b2, sb, eb = (a.reshape(-1) for a in outs[2:11])
    tw, ow, ew, sw, inp = outs[11:]
    return (loss, factor, inp.reshape(1, rows_here, length, feat), g1, b1, tw, qb, vb, ow, ob, g2, b2, ew, eb, sw, sb)


HIGH = lax.Precision.HIGHEST


def shifted(shard, axis, by):
    peers = lax.axis_size(axis)
    pairs = [(i, i + by) for i in range(peers) if 0 <= i + by < peers]
    return lax.ppermute(shard, axis, pairs)


def layer_stats(values):
    center = values - jnp.mean(values, axis=-1, keepdims=True)
    spread = lax.rsqrt(jnp.mean(center * center, axis=-1, keepdims=True) + 1e-05)
    return (center * spread, spread)


def norm_back(grad_normed, normed, spread):
    return spread * (
        grad_normed
        - jnp.mean(grad_normed, axis=-1, keepdims=True)
        - normed * jnp.mean(grad_normed * normed, axis=-1, keepdims=True)
    )


def masked_scores(queries, key_heads, same_seg):
    raw = (
        jnp.einsum("rqhc,rkhc->rhqk", queries, key_heads, preferred_element_type=jnp.float32)
        * 0.125
    )
    return jnp.where(same_seg, raw, -1e30)


def sum_grads(grads):
    return (
        lax.psum_scatter(grads[0], ("tower", "dp"), scatter_dimension=0, tiled=True),
        lax.psum_scatter(grads[1], ("tower", "dp"), scatter_dimension=0, tiled=True),
        lax.psum_scatter(grads[2], ("tower", "dp"), scatter_dimension=0, tiled=True),
        lax.psum_scatter(grads[3], ("tower", "dp"), scatter_dimension=0, tiled=True),
        lax.psum_scatter(grads[4], ("tower", "dp"), scatter_dimension=0, tiled=True),
        lax.psum_scatter(grads[5], ("tower", "dp"), scatter_dimension=0, tiled=True),
        lax.psum_scatter(grads[6], ("tower", "dp"), scatter_dimension=0, tiled=True),
        lax.psum_scatter(grads[7], ("tower", "dp"), scatter_dimension=0, tiled=True),
        lax.psum_scatter(grads[8], ("tower", "dp"), scatter_dimension=0, tiled=True),
        lax.psum_scatter(grads[9], ("tower", "dp"), scatter_dimension=0, tiled=True),
        lax.psum_scatter(grads[10], ("tower", "dp"), scatter_dimension=0, tiled=True),
        lax.psum_scatter(grads[11], ("tower", "dp"), scatter_dimension=0, tiled=True),
        lax.psum_scatter(grads[12], ("tower", "dp"), scatter_dimension=0, tiled=True),
    )


def local(
    tokens,
    segments,
    caption_image,
    logit_scale,
    first_gain,
    first_bias,
    triple_weight,
    query_bias,
    value_bias,
    output_weight,
    output_bias,
    second_gain,
    second_bias,
    expand_weight,
    expand_bias,
    shrink_weight,
    shrink_bias,
):
    rows_here = tokens.shape[1]
    length = tokens.shape[2]
    features = tokens.shape[3]
    head_size = features // HEADS
    token_count = rows_here * length
    is_text = lax.axis_index("tower") == 1
    text_flag = is_text.astype(jnp.float32)
    position = jnp.arange(length, dtype=jnp.int32)
    image_segs = jnp.broadcast_to(
        (position >= IMG_TOK).astype(jnp.int32)[None, :], (rows_here, length)
    )
    seg_ids = jnp.where(is_text, segments, image_segs)
    same_seg = (seg_ids[:, :, None] == seg_ids[:, None, :])[:, None, :, :]
    head_shape = (rows_here, length, HEADS, head_size)
    gain_one = first_gain[0].astype(jnp.float32)
    shift_one = first_bias[0].astype(jnp.float32)
    triple_w = triple_weight[0]
    query_shift = query_bias[0].astype(jnp.float32)
    value_shift = value_bias[0].astype(jnp.float32)
    output_w = output_weight[0]
    output_shift = output_bias[0].astype(jnp.float32)
    gain_two = second_gain[0].astype(jnp.float32)
    shift_two = second_bias[0].astype(jnp.float32)
    expand_w = expand_weight[0]
    expand_shift = expand_bias[0].astype(jnp.float32)
    shrink_w = shrink_weight[0]
    shrink_shift = shrink_bias[0].astype(jnp.float32)
    inputs = tokens[0].reshape(token_count, features).astype(jnp.float32)
    normed_a, spread_a = layer_stats(inputs)
    normed_one = (normed_a * gain_one + shift_one).astype(jnp.bfloat16)
    triple = jnp.dot(normed_one, triple_w, preferred_element_type=jnp.float32)
    queries = (triple[:, :features] + query_shift).astype(jnp.bfloat16).reshape(head_shape)
    key_heads = triple[:, features : 2 * features].astype(jnp.bfloat16).reshape(head_shape)
    value_heads = (triple[:, 2 * features :] + value_shift).astype(jnp.bfloat16).reshape(head_shape)
    scores = masked_scores(queries, key_heads, same_seg)
    row_peak = jnp.max(scores, axis=-1, keepdims=True)
    log_total = row_peak + jnp.log(jnp.sum(jnp.exp(scores - row_peak), axis=-1, keepdims=True))
    attn_probs = jnp.exp(scores - log_total)
    mixed_low = (
        jnp.einsum(
            "rhqk,rkhc->rqhc",
            attn_probs.astype(jnp.bfloat16),
            value_heads,
            preferred_element_type=jnp.float32,
        )
        .reshape(token_count, features)
        .astype(jnp.bfloat16)
    )
    hidden = (
        inputs + jnp.dot(mixed_low, output_w, preferred_element_type=jnp.float32) + output_shift
    )
    normed_b, spread_b = layer_stats(hidden)
    normed_two = (normed_b * gain_two + shift_two).astype(jnp.bfloat16)
    expanded = jnp.dot(normed_two, expand_w, preferred_element_type=jnp.float32) + expand_shift
    activated, gelu_back = jax.vjp(jax.nn.gelu, expanded)
    active_low = activated.astype(jnp.bfloat16)
    block_out = (
        hidden + jnp.dot(active_low, shrink_w, preferred_element_type=jnp.float32) + shrink_shift
    )
    slot_ids = jnp.arange(CAPS, dtype=jnp.int32)
    member = (seg_ids[:, None, :] == slot_ids[None, :, None]).astype(jnp.float32)
    counts = jnp.maximum(jnp.sum(member, axis=2), 1.0)
    pooled = (
        jnp.einsum(
            "rst,rtd->rsd", member, block_out.reshape(rows_here, length, features), precision=HIGH
        )
        / counts[:, :, None]
    )
    inverse = lax.rsqrt(jnp.sum(pooled * pooled, axis=2, keepdims=True) + 1e-06)
    embedding = pooled * inverse
    first_slot = embedding[:, 0, :].astype(jnp.bfloat16)
    collected = lax.all_gather(first_slot, "dp", axis=0, tiled=True)
    image_table = shifted(collected, "tower", 1)
    text_low = embedding.reshape(rows_here * CAPS, features).astype(jnp.bfloat16)
    similar = jnp.einsum("cd,id->ci", text_low, image_table, preferred_element_type=jnp.float32)
    factor = logit_scale[0]
    logits = factor * similar
    logit_peak = jnp.max(logits, axis=1, keepdims=True)
    logit_total = logit_peak + jnp.log(jnp.sum(jnp.exp(logits - logit_peak), axis=1, keepdims=True))
    targets = caption_image.reshape(-1)
    image_ids = jnp.arange(image_table.shape[0], dtype=jnp.int32)
    target_hot = (image_ids[None, :] == targets[:, None]).astype(jnp.float32)
    picked = jnp.sum(logits * target_hot, axis=1)
    loss_here = jnp.sum(logit_total[:, 0] - picked) * text_flag
    grad_logits = (jnp.exp(logits - logit_total) - target_hot) * text_flag
    factor_here = jnp.sum(grad_logits * similar)
    loss_total, factor_total = lax.psum((loss_here, factor_here), ("tower", "dp"))
    caption_total = rows_here * CAPS * lax.axis_size("dp")
    grad_dots = (factor * grad_logits).astype(jnp.bfloat16)
    grad_emb = jnp.einsum(
        "ci,id->cd", grad_dots, image_table, preferred_element_type=jnp.float32
    ).reshape(rows_here, CAPS, features)
    grad_pooled = inverse * (
        grad_emb - embedding * jnp.sum(embedding * grad_emb, axis=2, keepdims=True)
    )
    grad_pooled = grad_pooled / counts[:, :, None]
    grad_out = jnp.einsum("rst,rsd->rtd", member, grad_pooled, precision=HIGH).reshape(
        token_count, features
    )
    shrink_bias_grad = jnp.sum(grad_out, axis=0)
    grad_out_low = grad_out.astype(jnp.bfloat16)
    shrink_weight_grad = jnp.einsum(
        "nf,nd->fd", active_low, grad_out_low, preferred_element_type=jnp.float32
    )
    grad_active = jnp.einsum(
        "nd,fd->nf", grad_out_low, shrink_w, preferred_element_type=jnp.float32
    )
    grad_expanded = gelu_back(grad_active)[0]
    expand_bias_grad = jnp.sum(grad_expanded, axis=0)
    grad_expanded_low = grad_expanded.astype(jnp.bfloat16)
    expand_weight_grad = jnp.einsum(
        "nd,nf->df", normed_two, grad_expanded_low, preferred_element_type=jnp.float32
    )
    grad_normed_two = jnp.einsum(
        "nf,df->nd", grad_expanded_low, expand_w, preferred_element_type=jnp.float32
    )
    second_gain_grad = jnp.sum(grad_normed_two * normed_b, axis=0)
    second_bias_grad = jnp.sum(grad_normed_two, axis=0)
    grad_hidden = grad_out + norm_back(grad_normed_two * gain_two, normed_b, spread_b)
    output_bias_grad = jnp.sum(grad_hidden, axis=0)
    grad_hidden_low = grad_hidden.astype(jnp.bfloat16)
    output_weight_grad = jnp.einsum(
        "nd,ne->de", mixed_low, grad_hidden_low, preferred_element_type=jnp.float32
    )
    grad_mixed = (
        jnp.einsum("ne,de->nd", grad_hidden_low, output_w, preferred_element_type=jnp.float32)
        .astype(jnp.bfloat16)
        .reshape(head_shape)
    )
    scores_again = masked_scores(queries, key_heads, same_seg)
    probs_again = jnp.exp(scores_again - log_total)
    probs_low = probs_again.astype(jnp.bfloat16)
    grad_values = jnp.einsum(
        "rhqk,rqhc->rkhc", probs_low, grad_mixed, preferred_element_type=jnp.float32
    )
    grad_probs = jnp.einsum(
        "rqhc,rkhc->rhqk", grad_mixed, value_heads, preferred_element_type=jnp.float32
    )
    grad_scores = (
        probs_again * (grad_probs - jnp.sum(probs_again * grad_probs, axis=-1, keepdims=True))
    ).astype(jnp.bfloat16)
    grad_queries = (
        jnp.einsum("rhqk,rkhc->rqhc", grad_scores, key_heads, preferred_element_type=jnp.float32)
        * 0.125
    )
    grad_keys = (
        jnp.einsum("rhqk,rqhc->rkhc", grad_scores, queries, preferred_element_type=jnp.float32)
        * 0.125
    )
    grad_queries = grad_queries.reshape(token_count, features)
    grad_keys = grad_keys.reshape(token_count, features)
    grad_values = grad_values.reshape(token_count, features)
    query_bias_grad = jnp.sum(grad_queries, axis=0)
    value_bias_grad = jnp.sum(grad_values, axis=0)
    grad_triple = jnp.concatenate([grad_queries, grad_keys, grad_values], axis=1).astype(
        jnp.bfloat16
    )
    triple_weight_grad = jnp.einsum(
        "nd,ne->de", normed_one, grad_triple, preferred_element_type=jnp.float32
    )
    grad_normed_one = jnp.einsum(
        "ne,de->nd", grad_triple, triple_w, preferred_element_type=jnp.float32
    )
    first_gain_grad = jnp.sum(grad_normed_one * normed_a, axis=0)
    first_bias_grad = jnp.sum(grad_normed_one, axis=0)
    input_grad = grad_hidden + norm_back(grad_normed_one * gain_one, normed_a, spread_a)
    shares = sum_grads(
        (
            first_gain_grad,
            first_bias_grad,
            triple_weight_grad,
            query_bias_grad,
            value_bias_grad,
            output_weight_grad,
            output_bias_grad,
            second_gain_grad,
            second_bias_grad,
            expand_weight_grad,
            expand_bias_grad,
            shrink_weight_grad,
            shrink_bias_grad,
        )
    )
    loss_out = (loss_total / caption_total).reshape(1)
    factor_out = factor_total.reshape(1)
    return (
        loss_out,
        factor_out,
        input_grad.reshape(1, rows_here, length, features),
        shares[0],
        shares[1],
        shares[2],
        shares[3],
        shares[4],
        shares[5],
        shares[6],
        shares[7],
        shares[8],
        shares[9],
        shares[10],
        shares[11],
        shares[12],
    )


def solution(mesh):
    placed = (
        P("tower", "dp", None, None),
        P("dp", None),
        P("dp", None),
        P(),
        P("tower", None),
        P("tower", None),
        P("tower", None, None),
        P("tower", None),
        P("tower", None),
        P("tower", None, None),
        P("tower", None),
        P("tower", None),
        P("tower", None),
        P("tower", None, None),
        P("tower", None),
        P("tower", None, None),
        P("tower", None),
    )
    fits = mesh.shape["tower"] == 2 and mesh.shape["dp"] == 2 * PLANE
    return jax.shard_map(
        local_fast if fits else local,
        mesh=mesh,
        in_specs=placed,
        out_specs=(
            P(),
            P(),
            P("tower", "dp", None, None),
            P(("tower", "dp")),
            P(("tower", "dp")),
            P(("tower", "dp"), None),
            P(("tower", "dp")),
            P(("tower", "dp")),
            P(("tower", "dp"), None),
            P(("tower", "dp")),
            P(("tower", "dp")),
            P(("tower", "dp")),
            P(("tower", "dp"), None),
            P(("tower", "dp")),
            P(("tower", "dp"), None),
            P(("tower", "dp")),
        ),
        check_vma=False,
    )
```

```python
import functools

import jax
import jax.numpy as jnp
from jax import lax
from jax.experimental import pallas as pl
from jax.experimental.pallas import tpu as pltpu
from jax.sharding import PartitionSpec as P

HEADS = 12
IMG_TOK = 50
CAPS = 4

f32, bf16 = jnp.float32, jnp.bfloat16
GELU_C = 0.7978845608028654
GELU_A = 0.044715
STEP_ROWS = 4


def mm(a, b):
    return jnp.dot(a, b, preferred_element_type=f32)


def mm_nt(a, b):
    return lax.dot_general(a, b, (((1,), (1,)), ((), ())), preferred_element_type=f32)


def mm_tn(a, b):
    return lax.dot_general(a, b, (((0,), (0,)), ((), ())), preferred_element_type=f32)


def stats(x):
    center = x - jnp.mean(x, axis=-1, keepdims=True)
    spread = lax.rsqrt(jnp.mean(center * center, axis=-1, keepdims=True) + 1e-05)
    return center * spread, spread


def low_pair(x):
    high = x.astype(bf16)
    return high, (x - high.astype(f32)).astype(bf16)


def fwd_kernel(tok, seg, g1, b1, qb, vb, ob, g2, b2, eb, sb, w3h, woh, weh, wsh,
               qkv, probs, mixed, hidden, act, slope, member_out, pooled_out, count_out,
               w3, wo, we, ws, pool_acc, count_acc, sems):
    i = pl.program_id(0)
    steps = pl.num_programs(0)
    rows_here, length = seg.shape
    slots = rows_here * CAPS
    feat = tok.shape[1]
    block = tok.shape[0]
    is_text = lax.axis_index("tower") == 1
    copies = [pltpu.make_async_copy(src, dst, sems.at[n])
              for n, (src, dst) in enumerate(((w3h, w3), (woh, wo), (weh, we), (wsh, ws)))]

    @pl.when(i == 0)
    def _():
        for c in copies:
            c.start()
        pool_acc[...] = jnp.zeros_like(pool_acc)
        count_acc[...] = jnp.zeros_like(count_acc)

    def arrive(n):
        @pl.when(i == 0)
        def _():
            copies[n].wait()

    x = tok[...].astype(f32)
    norm, _ = stats(x)
    n1 = (norm * g1[...].astype(f32) + b1[...].astype(f32)).astype(bf16)
    arrive(0)
    qkv[:, :feat] = (mm(n1, w3[:, :feat]) + qb[...].astype(f32)).astype(bf16)
    qkv[:, feat:2 * feat] = mm(n1, w3[:, feat:2 * feat]).astype(bf16)
    qkv[:, 2 * feat:] = (mm(n1, w3[:, 2 * feat:]) + vb[...].astype(f32)).astype(bf16)

    image_seg = (lax.broadcasted_iota(jnp.int32, (1, length), 1) >= IMG_TOK).astype(jnp.int32)
    row_segs = []
    for r in range(STEP_ROWS):
        s = seg[pl.ds(STEP_ROWS * i + r, 1), :]
        row_segs.append(jnp.where(is_text, s, image_seg))
    lane = lax.broadcasted_iota(jnp.int32, (128, 128), 1)
    first_half = lane < 64
    slot_lanes = []
    for pair in range(STEP_ROWS // 2):
        base = STEP_ROWS * i + 2 * pair
        keyed = jnp.concatenate(
            [row_segs[2 * pair] * rows_here + base, row_segs[2 * pair + 1] * rows_here + (base + 1)], axis=1)
        slot_lanes.append(keyed)
        across = jnp.broadcast_to(keyed.astype(f32), (128, 128))
        bias = jnp.where(across == across.T, 0.0, -1e30)
        bias = jnp.concatenate([bias, bias], axis=0)
        t0 = pair * 128
        for hp in range(HEADS // 2):
            c0 = hp * 128
            q = qkv[t0:t0 + 128, c0:c0 + 128] * jnp.asarray(0.125, bf16)
            k = qkv[t0:t0 + 128, feat + c0:feat + c0 + 128]
            v = qkv[t0:t0 + 128, 2 * feat + c0:2 * feat + c0 + 128]
            zero = jnp.zeros_like(q)
            q2 = jnp.concatenate([jnp.where(first_half, q, zero), jnp.where(first_half, zero, q)], axis=0)
            s = mm_nt(q2, k) + bias
            e = jnp.exp(s - jnp.max(s, axis=-1, keepdims=True))
            p = (e * (1.0 / jnp.sum(e, axis=-1, keepdims=True))).astype(bf16)
            probs[256 * pair:256 * (pair + 1), c0:c0 + 128] = p
            o = mm(p, v)
            mixed[t0:t0 + 128, c0:c0 + 128] = jnp.where(first_half, o[:128], o[128:]).astype(bf16)

    arrive(1)
    hid = x + mm(mixed[...], wo[...]) + ob[...].astype(f32)
    hidden[...] = hid
    norm2, _ = stats(hid)
    n2 = (norm2 * g2[...].astype(f32) + b2[...].astype(f32)).astype(bf16)
    arrive(2)
    arrive(3)
    out = hid + sb[...].astype(f32)
    tile = 768
    for f in range(0, we.shape[1], tile):
        v = mm(n2, we[:, f:f + tile]) + eb[:, f:f + tile].astype(f32)
        v2 = v * v
        cv = v * GELU_C
        t = jnp.tanh(cv * (1.0 + GELU_A * v2))
        h = 0.5 + 0.5 * t
        a = (v * h).astype(bf16)
        act[:, f:f + tile] = a
        slope[:, f:f + tile] = (h + h * (1.0 - h) * ((2.0 * cv) * (1.0 + (3.0 * GELU_A) * v2))).astype(bf16)
        out = out + mm(a, ws[f:f + tile, :])
    slot_row = jnp.concatenate(slot_lanes, axis=1)
    hot = (lax.broadcasted_iota(jnp.int32, (slots, block), 0) == slot_row)
    member = hot.astype(f32).astype(bf16)
    member_out[...] = member
    out_hi, out_lo = low_pair(out)
    pool_acc[...] += mm(member, out_hi) + mm(member, out_lo)
    count_acc[...] += jnp.broadcast_to(jnp.sum(hot.astype(f32), axis=1, keepdims=True), count_acc.shape)

    @pl.when(i == steps - 1)
    def _():
        counts = jnp.maximum(count_acc[...], 1.0)
        count_out[...] = counts
        pooled_out[...] = pool_acc[...] / counts[:, :1]


def forward(tokens, segments, g1, b1, w3, qb, vb, wo, ob, g2, b2, we, eb, ws, sb):
    count, feat = tokens.shape
    rows_here, length = segments.shape
    slots = rows_here * CAPS
    ff = we.shape[1]
    block = STEP_ROWS * length
    steps = count // block
    pairs = STEP_ROWS // 2
    whole = lambda a: pl.BlockSpec(a.shape, lambda i: (0,) * a.ndim)
    rows = lambda width: pl.BlockSpec((block, width), lambda i: (i, 0))
    anyw = pl.BlockSpec(memory_space=pl.ANY)
    smalls = (g1, b1, qb, vb, ob, g2, b2, eb, sb)
    return pl.pallas_call(
        fwd_kernel,
        grid=(steps,),
        in_specs=[rows(feat), whole(segments)] + [whole(a) for a in smalls] + [anyw] * 4,
        out_specs=[rows(3 * feat),
                   pl.BlockSpec((256 * pairs, feat), lambda i: (i, 0)),
                   rows(feat), rows(feat), rows(ff), rows(ff),
                   pl.BlockSpec((slots, block), lambda i: (0, i)),
                   pl.BlockSpec((slots, feat), lambda i: (0, 0)),
                   pl.BlockSpec((slots, 128), lambda i: (0, 0))],
        out_shape=[jax.ShapeDtypeStruct((count, 3 * feat), bf16),
                   jax.ShapeDtypeStruct((steps * pairs * 256, feat), bf16),
                   jax.ShapeDtypeStruct((count, feat), bf16),
                   jax.ShapeDtypeStruct((count, feat), f32),
                   jax.ShapeDtypeStruct((count, ff), bf16),
                   jax.ShapeDtypeStruct((count, ff), bf16),
                   jax.ShapeDtypeStruct((slots, count), bf16),
                   jax.ShapeDtypeStruct((slots, feat), f32),
                   jax.ShapeDtypeStruct((slots, 128), f32)],
        scratch_shapes=[pltpu.VMEM(w3.shape, bf16), pltpu.VMEM(wo.shape, bf16), pltpu.VMEM(we.shape, bf16),
                        pltpu.VMEM(ws.shape, bf16), pltpu.VMEM((slots, feat), f32), pltpu.VMEM((slots, 128), f32),
                        pltpu.SemaphoreType.DMA((4,))],
        compiler_params=pltpu.CompilerParams(vmem_limit_bytes=56 << 20, dimension_semantics=("arbitrary",)),
        name="fwd",
    )(tokens, segments, *smalls, w3, wo, we, ws)


MESH = pl.DeviceIdType.MESH
PLANE = 8
BLK = 256
CH = 768
HALF = CH // 2
ROWS = HALF // PLANE
N_CH = 12


def fold(x):
    return jnp.sum(x.reshape(x.shape[0] // 8, 8, x.shape[1]), axis=0)


def bwd_kernel(member, pooled, count, caption, scale, g1, b1, g2, b2,
               qkv_h, probs_h, mixed_h, hidden_h, act_h, slope_h, tok_h, w3_h, wo_h, we_h, ws_h,
               tw_out, ow_out, ew_out, sw_out, in_out, vec_out,
               cs, snd, prv, own, prcv, swrcv, fin, swfin,
               gol, gn2, hid, spread2, n2b, n1b, tok, act, slope, ws, we, ge, qkv, w3, wo, inbuf,
               imgs, elow, ebsum, attn_sum, vec, vecrcv, vecall,
               ld, psend, precv, xsend, xrecv, plsend, plrecv, swsend, swrecv, fsend, frecv, fout,
               gsend, grecv, esend, erecv, vsend, vrecv, outsem):
    t = lax.axis_index("tower")
    d = lax.axis_index("dp")
    p = d // 2
    c = lax.rem(d, 2)
    is_text = t == 1
    count_t = gol.shape[0]
    blocks = count_t // BLK
    feat = CH
    rows_here = caption.shape[0]
    other = 1 - c

    def peer(k):
        return lax.rem(p + k, PLANE)

    def at_core(tt, pp):
        return (tt, pp * 2 + c)

    partner = (t, p * 2 + other)

    def remote(src, dst, ssem, rsem, dev):
        return pltpu.make_async_remote_copy(src_ref=src, dst_ref=dst, send_sem=ssem, recv_sem=rsem,
                                            device_id=dev, device_id_type=MESH)

    barrier = pltpu.get_barrier_semaphore()
    pl.semaphore_signal(barrier, inc=1, device_id=partner, device_id_type=MESH)
    pl.semaphore_signal(barrier, inc=1, device_id=at_core(1 - t, p), device_id_type=MESH)
    for k in range(1, PLANE):
        pl.semaphore_signal(barrier, inc=1, device_id=at_core(t, peer(k)), device_id_type=MESH)
        pl.semaphore_signal(barrier, inc=1, device_id=at_core(1 - t, peer(k)), device_id_type=MESH)

    pooled_v = pooled[...]
    inverse = lax.rsqrt(jnp.sum(pooled_v * pooled_v, axis=1, keepdims=True) + 1e-06)
    emb = pooled_v * inverse
    emb_low = emb.astype(bf16)

    def lane(q):
        return jnp.where(q < 8, q // 2, q - 4)

    def pair_copy(q):
        return remote(snd.at[lax.rem(q, 2)], prv.at[q], psend.at[q], precv.at[q], partner)

    def x_copy(q):
        return remote(cs.at[q, 0:HALF], cs.at[q, 0:HALF], xsend.at[q], xrecv.at[q], at_core(1 - t, p))

    def plane_copy(q, k):
        row = pl.multiple_of(HALF * t + ROWS * peer(k), 16)
        return remote(cs.at[q, pl.ds(row, ROWS)], prcv.at[lane(q), k], plsend.at[q, k], plrecv.at[q, k],
                      at_core(t, peer(k)))

    def sw_copy(q, zz, y):
        to = 2 * zz + y
        k = lax.rem(to - p + PLANE, PLANE)
        row = pl.multiple_of(HALF * t + 4 * ROWS * y, 16)
        return remote(cs.at[q, pl.ds(row, 4 * ROWS)], swrcv.at[k], swsend.at[zz, y], swrecv.at[k], at_core(t, to))

    def plane_send(q):
        for k in range(1, PLANE):
            plane_copy(q, k).start()

    def sw_send(q, zz):
        for y in range(2):
            @pl.when(p != 2 * zz + y)
            def _():
                sw_copy(q, zz, y).start()

    def sw_sent(q, zz):
        for y in range(2):
            @pl.when(p != 2 * zz + y)
            def _():
                sw_copy(q, zz, y).wait_send()

    def chip_sum(q):
        pair_copy(q).wait_recv()
        slot = lax.rem(q, 2)
        for r in range(0, CH, 128):
            cs[q, r:r + 128, :] = (own[slot, r:r + 128, :] + prv[q, r:r + 128, :].astype(f32)).astype(bf16)
        x_copy(q).start()

    def chunk(q, left, right_of):
        slot = lax.rem(q, 2)

        @pl.when(q >= 2)
        def _():
            pair_copy(q - 2).wait_send()
        for mine in (False, True):
            right = right_of(c if mine else other)
            for r in range(0, CH, 256):
                part = mm_tn(left[:, r:r + 256], right)
                if mine:
                    own[slot, r:r + 256, :] = part
                else:
                    snd[slot, r:r + 256, :] = part.astype(bf16)
            if not mine:
                pair_copy(q).start()

    def gather_copy(k):
        return remote(elow, imgs.at[c, p], gsend.at[k], grecv.at[k], at_core(1 - t, peer(k)))

    def share_copy():
        return remote(imgs.at[c], imgs.at[c], esend, erecv, partner)

    def load(n, src, dst):
        return pltpu.make_async_copy(src, dst, ld.at[n])

    def tile_loads(i):
        s = lax.rem(i, 2)
        out = []
        ff = act_h.shape[1]
        for h in range(2):
            col = pl.multiple_of((ff // 2) * h + HALF * i, 128)
            here = pl.ds(HALF * h, HALF)
            out.append(load(8 * s + 4 * h, act_h.at[:, pl.ds(col, HALF)], act.at[s, :, here]))
            out.append(load(8 * s + 4 * h + 1, slope_h.at[:, pl.ds(col, HALF)], slope.at[s, :, here]))
            out.append(load(8 * s + 4 * h + 2, ws_h.at[pl.ds(col, HALF)], ws.at[s, here]))
            out.append(load(8 * s + 4 * h + 3, we_h.at[:, pl.ds(col, HALF)], we.at[s, :, here]))
        return out

    hid_load = load(16, hidden_h, hid)
    tok_load = load(17, tok_h, tok)
    qkv_load = load(18, qkv_h, qkv)
    w3_load = load(19, w3_h, w3)
    wo_load = load(20, wo_h, wo)
    mixed_load = load(21, mixed_h, slope.at[0])
    probs_loads = [load(22 + h, probs_h.at[pl.ds(count_t * h, count_t)], act.at[h]) for h in range(2)]

    @pl.when(t == 0)
    def _():
        elow[...] = emb_low[:rows_here]
        pl.semaphore_wait(barrier, 2 * PLANE)
        for k in range(PLANE):
            gather_copy(k).start()
        inbuf[0] = jnp.zeros_like(inbuf[0])
        for m in range(blocks):
            pltpu.make_async_copy(inbuf.at[0], in_out.at[pl.ds(BLK * m, BLK)], outsem.at[m]).start()

        @pl.loop(0, 4)
        def _(i):
            x_copy(2 * i).wait_recv()
            sw_send(2 * i, i)
            x_copy(2 * i + 1).wait_recv()
            plane_send(2 * i + 1)

        @pl.loop(8, N_CH)
        def _(q):
            x_copy(q).wait_recv()
            plane_send(q)
        for k in range(PLANE):
            gather_copy(k).wait_send()
        for m in range(blocks):
            pltpu.make_async_copy(inbuf.at[0], in_out.at[pl.ds(BLK * m, BLK)], outsem.at[m]).wait()

    @pl.when(is_text)
    def _():
        hid_load.start()
        tok_load.start()
        for cp in tile_loads(0):
            cp.start()
        for cp in tile_loads(1):
            cp.start()
        qkv_load.start()
        w3_load.start()
        wo_load.start()
        gain2, shift2 = g2[...].astype(f32), b2[...].astype(f32)
        gain1, shift1 = g1[...].astype(f32), b1[...].astype(f32)
        hid_load.wait()

        @pl.loop(0, blocks)
        def _(m):
            here = pl.ds(pl.multiple_of(m * BLK, BLK), BLK)
            norm, spread = stats(hid[here, :])
            n2b[here, :] = (norm * gain2 + shift2).astype(bf16)
            hid[here, :] = norm
            spread2[here, :] = spread
        tok_load.wait()

        @pl.loop(0, blocks)
        def _(m):
            here = pl.ds(pl.multiple_of(m * BLK, BLK), BLK)
            norm, _s = stats(tok[here, :].astype(f32))
            n1b[here, :] = (norm * gain1 + shift1).astype(bf16)
        gn2[...] = jnp.zeros_like(gn2)
        attn_sum[...] = jnp.zeros_like(attn_sum)
        vec[...] = jnp.zeros_like(vec)
        pl.semaphore_wait(barrier, 2 * PLANE)
        for k in range(PLANE):
            gather_copy(k).wait_recv()
        share_copy().start()
        share_copy().wait_send()
        remote(imgs.at[other], imgs.at[other], esend, erecv, partner).wait_recv()

        table = imgs[...].reshape(2 * PLANE * rows_here, feat)
        dots = mm_nt(emb_low, table)
        factor = scale[0]
        logits = factor * dots
        peak = jnp.max(logits, axis=1, keepdims=True)
        weight = jnp.exp(logits - peak)
        total = jnp.sum(weight, axis=1, keepdims=True)
        wanted = jnp.concatenate([caption[:, s:s + 1] for s in range(CAPS)], axis=0)
        span = 2 * rows_here
        inside = lax.rem(wanted, span)
        wanted = (inside // rows_here) * (PLANE * rows_here) + (wanted // span) * rows_here + lax.rem(inside, rows_here)
        hot = (lax.broadcasted_iota(jnp.int32, dots.shape, 1) == wanted).astype(f32)
        picked = jnp.sum(logits * hot, axis=1, keepdims=True)
        loss_here = jnp.sum(peak + jnp.log(total) - picked, axis=0, keepdims=True)
        grad_logits = weight / total - hot
        factor_here = jnp.sum(jnp.sum(grad_logits * dots, axis=1, keepdims=True), axis=0, keepdims=True)
        grad_emb = mm((factor * grad_logits).astype(bf16), table)
        counts = count[:, :1]
        grad_pool = inverse * (grad_emb - emb * jnp.sum(emb * grad_emb, axis=1, keepdims=True))
        vec[7:8, :] = jnp.sum(grad_pool, axis=0, keepdims=True)
        column = lax.broadcasted_iota(jnp.int32, (1, feat), 1)
        vec[12:13, :] = jnp.where(column == 0, loss_here, jnp.where(column == 1, factor_here, 0.0))
        gp_hi, gp_lo = low_pair(grad_pool / counts)
        for m in range(blocks):
            gol[BLK * m:BLK * (m + 1), :] = mm_tn(member[:, BLK * m:BLK * (m + 1)], gp_hi).astype(bf16)

        @pl.loop(0, 4)
        def _(i):
            s = lax.rem(i, 2)
            for cp in tile_loads(i):
                cp.wait()
            chunk(2 * i, act.at[s], lambda h: gol[:, pl.ds(pl.multiple_of(HALF * h, 128), HALF)])

            @pl.when(i > 0)
            def _():
                chip_sum(2 * i - 1)
                plane_send(2 * i - 1)
            sums = jnp.zeros((8, feat), f32)
            for m in range(blocks):
                here = slice(BLK * m, BLK * (m + 1))
                grad = mm_nt(gol[here, :], ws[s]) * slope[s, here, :].astype(f32)
                sums = sums + fold(grad)
                ge[here, :] = grad.astype(bf16)
            sums = jnp.sum(sums, axis=0, keepdims=True)
            for h in range(2):
                ebsum[:, pl.ds(pl.multiple_of(4 * HALF * h + HALF * i, 128), HALF)] = sums[:, HALF * h:HALF * (h + 1)]
            chunk(2 * i + 1, n2b, lambda h: ge[:, pl.ds(pl.multiple_of(HALF * h, 128), HALF)])
            chip_sum(2 * i)
            sw_send(2 * i, i)
            for m in range(blocks):
                here = slice(BLK * m, BLK * (m + 1))
                gn2[here, :] += mm_nt(ge[here, :], we[s])

            @pl.when(i < 2)
            def _():
                for cp in tile_loads(i + 2):
                    cp.start()

            @pl.when(i == 2)
            def _():
                mixed_load.start()
                probs_loads[0].start()
        probs_loads[1].start()
        chip_sum(7)
        plane_send(7)

        zeros8 = jnp.zeros((8, feat), f32)

        def norm2_back(m, sums):
            here = pl.ds(pl.multiple_of(m * BLK, BLK), BLK)
            norm, g_in = hid[here, :], gn2[here, :]
            hot_m = member[:, here]
            grad_out = mm_tn(hot_m, gp_hi) + mm_tn(hot_m, gp_lo)
            g = g_in * gain2
            back = spread2[here, :] * (g - jnp.mean(g, axis=1, keepdims=True)
                                       - norm * jnp.mean(g * norm, axis=1, keepdims=True))
            gh = grad_out + back
            gn2[here, :] = gh
            gol[here, :] = gh.astype(bf16)
            return (sums[0] + fold(g_in * norm), sums[1] + fold(g_in), sums[2] + fold(gh))
        sums = lax.fori_loop(0, blocks, norm2_back, (zeros8, zeros8, zeros8))
        for row, x in ((5, sums[0]), (6, sums[1]), (4, sums[2])):
            vec[row:row + 1, :] = jnp.sum(x, axis=0, keepdims=True)
        for n in range(4):
            vec[8 + n:9 + n, :] = ebsum[:, feat * n:feat * (n + 1)]

        mixed_load.wait()
        chunk(8, slope.at[0], lambda h: gol[:, pl.ds(pl.multiple_of(HALF * h, 128), HALF)])
        wo_load.wait()
        for m in range(blocks):
            here = slice(BLK * m, BLK * (m + 1))
            ge[here, :] = mm_nt(gol[here, :], wo[...]).astype(bf16)
        chip_sum(8)
        plane_send(8)

        qkv_load.wait()
        for cp in probs_loads:
            cp.wait()
        first_half = lax.broadcasted_iota(jnp.int32, (128, 128), 1) < 64

        def split(x):
            zero = jnp.zeros_like(x)
            return jnp.concatenate([jnp.where(first_half, x, zero), jnp.where(first_half, zero, x)], axis=0)

        @pl.loop(0, count_t // 128)
        def _(rp):
            here = pl.ds(pl.multiple_of(rp * 128, 128), 128)
            half = rp // (count_t // 256)
            prow = pl.ds(pl.multiple_of(lax.rem(rp, count_t // 256) * 256, 256), 256)
            for hp in range(HEADS // 2):
                c0 = hp * 128
                q, k, v = (qkv[here, feat * n + c0:feat * n + c0 + 128] for n in range(3))
                gm2 = split(ge[here, c0:c0 + 128])
                probs = act[half, prow, c0:c0 + 128]
                probs_f = probs.astype(f32)
                gp = mm_nt(gm2, v)
                weighted = probs_f * gp
                gs = (weighted - probs_f * jnp.sum(weighted, axis=1, keepdims=True)).astype(bf16)
                gv = mm_tn(probs, gm2)
                gk = mm_tn(gs, split(q)) * 0.125
                gq2 = mm(gs, k)
                gq = jnp.where(first_half, gq2[:128], gq2[128:]) * 0.125
                for n, x in ((0, gq), (1, gk), (2, gv)):
                    qkv[here, feat * n + c0:feat * n + c0 + 128] = x.astype(bf16)
                    if n != 1:
                        at = slice((feat if n else 0) + c0, (feat if n else 0) + c0 + 128)
                        attn_sum[:, at] += fold(x)
        vec[2:3, :] = jnp.sum(attn_sum[:, :feat], axis=0, keepdims=True)
        vec[3:4, :] = jnp.sum(attn_sum[:, feat:], axis=0, keepdims=True)

        @pl.loop(0, 3)
        def _(j):
            chunk(9 + j, n1b, lambda h: qkv[:, pl.ds(pl.multiple_of(CH * j + HALF * h, 128), HALF)])

            @pl.when(j > 0)
            def _():
                chip_sum(8 + j)
                plane_send(8 + j)
        w3_load.wait()

        def norm1_back(m, sums):
            here = pl.ds(pl.multiple_of(m * BLK, BLK), BLK)
            slot = lax.rem(m, 2)

            def out_copy(mm_):
                return pltpu.make_async_copy(inbuf.at[lax.rem(mm_, 2)],
                                             in_out.at[pl.ds(pl.multiple_of(mm_ * BLK, BLK), BLK)], outsem.at[mm_])

            g_in = mm_nt(qkv[here, :], w3[...])

            @pl.when(m == 0)
            def _():
                chip_sum(11)
                plane_send(11)

            @pl.when(m >= 2)
            def _():
                out_copy(m - 2).wait()
            norm, spread = stats(tok[here, :].astype(f32))
            g = g_in * gain1
            back = spread * (g - jnp.mean(g, axis=1, keepdims=True)
                             - norm * jnp.mean(g * norm, axis=1, keepdims=True))
            inbuf[slot] = gn2[here, :] + back
            out_copy(m).start()
            return (sums[0] + fold(g_in * norm), sums[1] + fold(g_in))
        sums = lax.fori_loop(0, blocks, norm1_back, (zeros8, zeros8))
        for row, x in ((0, sums[0]), (1, sums[1])):
            vec[row:row + 1, :] = jnp.sum(x, axis=0, keepdims=True)
        for m in (blocks - 2, blocks - 1):
            pltpu.make_async_copy(inbuf.at[m % 2], in_out.at[pl.ds(BLK * m, BLK)], outsem.at[m]).wait()

    mine8 = pl.ds(pl.multiple_of(8 * c, 8), 8)
    their8 = pl.ds(pl.multiple_of(8 * other, 8), 8)

    def v_pair():
        return remote(vec.at[their8], vecrcv.at[0], vsend.at[0], vrecv.at[0], partner)

    def v_plane(k):
        return remote(vec.at[mine8], vecrcv.at[k], vsend.at[k], vrecv.at[k], at_core(t, peer(k)))

    def v_share(half):
        return remote(vecall.at[half], vecall.at[half], vsend.at[8], vrecv.at[8], partner)

    def v_across():
        return remote(vecall, vecall, vsend.at[9], vrecv.at[9], at_core(1 - t, p))

    @pl.when(is_text)
    def _():
        v_pair().start()
        v_pair().wait_recv()
        vec[mine8, :] += vecrcv[0]
        for k in range(1, PLANE):
            v_plane(k).start()

    def total_of(block, get):
        out = block
        for k in range(1, PLANE):
            out = out + get(k).astype(f32)
        return out

    def finish(q, out, col, base):
        for k in range(1, PLANE):
            plane_copy(q, k).wait_recv()
        row = pl.multiple_of(HALF * t + ROWS * p, 16)
        fin[lane(q)] = total_of(cs[q, pl.ds(row, ROWS), :].astype(f32), lambda k: prcv[lane(q), k])
        keep_copy(q, out, col).start()
        give_copy(q, out, col).start()

    def keep_copy(q, out, col):
        n = ROWS // 2
        return pltpu.make_async_copy(fin.at[lane(q), pl.ds(pl.multiple_of(n * c, 8), n)], out.at[:, pl.ds(col, HALF)],
                                     fout.at[q])

    def give_copy(q, out, col):
        n = ROWS // 2
        return remote(fin.at[lane(q), pl.ds(pl.multiple_of(n * other, 8), n)], out.at[:, pl.ds(col, HALF)],
                      fsend.at[q], frecv.at[q], partner)

    def sw_keep():
        n = 2 * ROWS
        return pltpu.make_async_copy(swfin.at[pl.ds(pl.multiple_of(n * c, 8), n)],
                                     sw_out.at[:, pl.ds(pl.multiple_of(HALF * c, 128), HALF)], fout.at[0])

    def sw_give():
        n = 2 * ROWS
        return remote(swfin.at[pl.ds(pl.multiple_of(n * other, 8), n)],
                      sw_out.at[:, pl.ds(pl.multiple_of(HALF * c, 128), HALF)], fsend.at[0], frecv.at[0], partner)

    def wait_frecv(q, out, col_other):
        n = ROWS // 2
        remote(fin.at[lane(q), pl.ds(pl.multiple_of(n * other, 8), n)], out.at[:, pl.ds(col_other, HALF)],
               fsend.at[q], frecv.at[q], partner).wait_recv()

    for k in range(1, PLANE):
        remote(cs.at[0, 0:4 * ROWS], swrcv.at[k], swsend.at[0, 0], swrecv.at[k], partner).wait_recv()
    sw_q = 2 * (p // 2)
    sw_row = pl.multiple_of(HALF * t + 4 * ROWS * lax.rem(p, 2), 16)
    swfin[...] = total_of(cs[sw_q, pl.ds(sw_row, 4 * ROWS), :].astype(f32), lambda k: swrcv[k])
    sw_keep().start()
    sw_give().start()

    def ew_col(i, h):
        return pl.multiple_of(4 * HALF * h + HALF * i, 128)

    def tw_col(j, h):
        return pl.multiple_of(CH * j + HALF * h, 128)

    def ow_col(h):
        return pl.multiple_of(HALF * h, 128)

    @pl.loop(0, 4)
    def _(i):
        finish(2 * i + 1, ew_out, ew_col(i, c), None)
    finish(8, ow_out, ow_col(c), None)

    @pl.loop(0, 3)
    def _(j):
        finish(9 + j, tw_out, tw_col(j, c), None)

    @pl.when(is_text)
    def _():
        for k in range(1, PLANE):
            v_plane(k).wait_recv()
        vecall[c] = total_of(vec[mine8, :], lambda k: vecrcv[k])
        v_share(c).start()
        v_share(other).wait_recv()
        v_across().start()
        v_across().wait_send()
        v_share(c).wait_send()
        v_pair().wait_send()
        for k in range(1, PLANE):
            v_plane(k).wait_send()
        for q in (N_CH - 2, N_CH - 1):
            pair_copy(q).wait_send()

        @pl.loop(0, N_CH)
        def _(q):
            x_copy(q).wait_send()

    @pl.when(t == 0)
    def _():
        v_across().wait_recv()
    vec_out[...] = vecall[...]

    @pl.loop(0, 4)
    def _(i):
        sw_sent(2 * i, i)
        for k in range(1, PLANE):
            plane_copy(2 * i + 1, k).wait_send()
        keep_copy(2 * i + 1, ew_out, ew_col(i, c)).wait()
        give_copy(2 * i + 1, ew_out, ew_col(i, c)).wait_send()
        wait_frecv(2 * i + 1, ew_out, ew_col(i, other))

    @pl.loop(8, N_CH)
    def _(q):
        for k in range(1, PLANE):
            plane_copy(q, k).wait_send()
    keep_copy(8, ow_out, ow_col(c)).wait()
    give_copy(8, ow_out, ow_col(c)).wait_send()
    wait_frecv(8, ow_out, ow_col(other))

    @pl.loop(0, 3)
    def _(j):
        keep_copy(9 + j, tw_out, tw_col(j, c)).wait()
        give_copy(9 + j, tw_out, tw_col(j, c)).wait_send()
        wait_frecv(9 + j, tw_out, tw_col(j, other))
    sw_keep().wait()
    sw_give().wait_send()
    remote(swfin.at[pl.ds(0, 2 * ROWS)], sw_out.at[:, pl.ds(pl.multiple_of(HALF * other, 128), HALF)],
           fsend.at[0], frecv.at[0], partner).wait_recv()

    @pl.when(is_text)
    def _():
        pass


def backward(member, pooled, count, caption, scale, g1, b1, g2, b2,
             qkv, probs, mixed, hidden, act, slope, tokens, w3, wo, we, ws):
    n_tok, feat = tokens.shape
    rows_here = caption.shape[0]
    ff = we.shape[1]
    dma = pltpu.SemaphoreType.DMA
    vm = pltpu.VMEM
    vspec = pl.BlockSpec(memory_space=pltpu.VMEM)
    sspec = pl.BlockSpec(memory_space=pltpu.SMEM)
    anyw = pl.BlockSpec(memory_space=pl.ANY)
    shape = jax.ShapeDtypeStruct
    scratch = [
        vm((N_CH, CH, HALF), bf16), vm((2, CH, HALF), bf16), vm((N_CH, CH, HALF), bf16), vm((2, CH, HALF), f32),
        vm((N_CH - 4, PLANE, ROWS, HALF), bf16), vm((PLANE, 4 * ROWS, HALF), bf16),
        vm((N_CH - 4, ROWS, HALF), f32), vm((4 * ROWS, HALF), f32),
        vm((n_tok, feat), bf16), vm((n_tok, feat), f32), vm((n_tok, feat), f32), vm((n_tok, 1), f32),
        vm((n_tok, feat), bf16), vm((n_tok, feat), bf16), vm((n_tok, feat), bf16),
        vm((2, n_tok, CH), bf16), vm((2, n_tok, CH), bf16), vm((2, CH, feat), bf16), vm((2, feat, CH), bf16),
        vm((n_tok, feat), bf16), vm((n_tok, 3 * feat), bf16), vm(w3.shape, bf16), vm(wo.shape, bf16),
        vm((2, BLK, feat), f32),
        vm((2, PLANE, rows_here, feat), bf16), vm((rows_here, feat), bf16), vm((1, ff), f32), vm((8, 2 * feat), f32),
        vm((16, feat), f32), vm((PLANE, 8, feat), f32), vm((2, 8, feat), f32),
        dma((24,)), dma((N_CH,)), dma((N_CH,)), dma((N_CH,)), dma((N_CH,)), dma((N_CH, PLANE)), dma((N_CH, PLANE)),
        dma((4, 2)), dma((PLANE,)), dma((N_CH,)), dma((N_CH,)), dma((N_CH,)),
        dma((PLANE,)), dma((PLANE,)), dma, dma, dma((10,)), dma((10,)), dma((n_tok // BLK,)),
    ]
    return pl.pallas_call(
        bwd_kernel,
        in_specs=[vspec] * 4 + [sspec] + [vspec] * 4 + [anyw] * 11,
        out_specs=[anyw] * 5 + [vspec],
        out_shape=[shape((ROWS // 2, 3 * feat), f32), shape((ROWS // 2, feat), f32), shape((ROWS // 2, ff), f32),
                   shape((2 * ROWS, feat), f32), shape((n_tok, feat), f32), shape((2, 8, feat), f32)],
        scratch_shapes=scratch,
        compiler_params=pltpu.CompilerParams(vmem_limit_bytes=61 << 20, collective_id=0, has_side_effects=True),
        name="bwd",
    )(member, pooled, count, caption, scale, g1, b1, g2, b2,
      qkv, probs, mixed, hidden, act, slope, tokens, w3, wo, we, ws)


def hand_out_kernel(scale_by, vec, tw, ow, ew, sw, inp, loss, factor, *rest):
    smalls, bigs = rest[:9], rest[9:]
    bigs[4][...] = inp[...]

    @pl.when(pl.program_id(0) == 0)
    def _():
        for src, dst in zip((tw, ow, ew, sw), bigs):
            dst[...] = src[...]
        feat = vec.shape[2]
        width = smalls[0].shape[1]
        wide = smalls[8].shape[1]
        g = lax.axis_index("tower") * lax.axis_size("dp") + lax.axis_index("dp")
        turned = pltpu.roll(vec[0], lax.rem(feat - width * g, feat), axis=1)
        for n in range(8):
            smalls[n][...] = turned[n:n + 1, :width]
        per_row = feat // wide
        rows = jnp.broadcast_to(vec[1, pl.ds(g // per_row, 1), :], (8, feat))
        smalls[8][...] = pltpu.roll(rows, lax.rem(feat - wide * lax.rem(g, per_row), feat), axis=1)[:1, :wide]
        loss[...] = vec[1, 4:5, 0:1] * scale_by
        factor[...] = vec[1, 4:5, 1:2]


def hand_out(vec, tw, ow, ew, sw, inp, captions):
    devices = lax.axis_size("tower") * lax.axis_size("dp")
    feat = vec.shape[2]
    bigs = (tw, ow, ew, sw)
    outs = ([(1, 1)] * 2 + [(1, feat // devices)] * 8 + [(1, ew.shape[1] // devices)]
            + [a.shape for a in bigs])
    whole = lambda dims: pl.BlockSpec(dims, lambda i: (0,) * len(dims))
    moving = pl.BlockSpec((BLK, feat), lambda i: (i, 0))
    return pl.pallas_call(
        functools.partial(hand_out_kernel, 1.0 / captions),
        grid=(inp.shape[0] // BLK,),
        in_specs=[whole(vec.shape)] + [whole(a.shape) for a in bigs] + [moving],
        out_specs=[whole(dims) for dims in outs] + [moving],
        out_shape=[jax.ShapeDtypeStruct(dims, f32) for dims in outs + [inp.shape]],
        name="hand_out",
    )(vec, *bigs, inp)


def local_fast(tokens, segments, caption_image, logit_scale, first_gain, first_bias, triple_weight, query_bias,
               value_bias, output_weight, output_bias, second_gain, second_bias, expand_weight, expand_bias,
               shrink_weight, shrink_bias):
    rows_here, length, feat = tokens.shape[1:]
    flat = tokens[0].reshape(rows_here * length, feat)
    w3, wo, we, ws = triple_weight[0], output_weight[0], expand_weight[0], shrink_weight[0]
    qkv, probs, mixed, hidden, act, slope, member, pooled, count = forward(
        flat, segments, first_gain, first_bias, w3, query_bias, value_bias, wo, output_bias,
        second_gain, second_bias, we, expand_bias, ws, shrink_bias)
    tw, ow, ew, sw, inp, vec = backward(member, pooled, count, caption_image, logit_scale, first_gain, first_bias,
                                        second_gain, second_bias, qkv, probs, mixed, hidden, act, slope, flat,
                                        w3, wo, we, ws)
    captions = rows_here * CAPS * lax.axis_size("dp")
    outs = hand_out(vec, tw, ow, ew, sw, inp, captions)
    loss, factor = outs[0].reshape(1), outs[1].reshape(1)
    g1, b1, qb, vb, ob, g2, b2, sb, eb = (a.reshape(-1) for a in outs[2:11])
    tw, ow, ew, sw, inp = outs[11:]
    return (loss, factor, inp.reshape(1, rows_here, length, feat), g1, b1, tw, qb, vb, ow, ob, g2, b2, ew, eb, sw, sb)


HIGH = lax.Precision.HIGHEST


def shifted(shard, axis, by):
    peers = lax.axis_size(axis)
    pairs = [(i, i + by) for i in range(peers) if 0 <= i + by < peers]
    return lax.ppermute(shard, axis, pairs)


def layer_stats(values):
    center = values - jnp.mean(values, axis=-1, keepdims=True)
    spread = lax.rsqrt(jnp.mean(center * center, axis=-1, keepdims=True) + 1e-05)
    return (center * spread, spread)


def norm_back(grad_normed, normed, spread):
    return spread * (
        grad_normed
        - jnp.mean(grad_normed, axis=-1, keepdims=True)
        - normed * jnp.mean(grad_normed * normed, axis=-1, keepdims=True)
    )


def masked_scores(queries, key_heads, same_seg):
    raw = (
        jnp.einsum("rqhc,rkhc->rhqk", queries, key_heads, preferred_element_type=jnp.float32)
        * 0.125
    )
    return jnp.where(same_seg, raw, -1e30)


def sum_grads(grads):
    return (
        lax.psum_scatter(grads[0], ("tower", "dp"), scatter_dimension=0, tiled=True),
        lax.psum_scatter(grads[1], ("tower", "dp"), scatter_dimension=0, tiled=True),
        lax.psum_scatter(grads[2], ("tower", "dp"), scatter_dimension=0, tiled=True),
        lax.psum_scatter(grads[3], ("tower", "dp"), scatter_dimension=0, tiled=True),
        lax.psum_scatter(grads[4], ("tower", "dp"), scatter_dimension=0, tiled=True),
        lax.psum_scatter(grads[5], ("tower", "dp"), scatter_dimension=0, tiled=True),
        lax.psum_scatter(grads[6], ("tower", "dp"), scatter_dimension=0, tiled=True),
        lax.psum_scatter(grads[7], ("tower", "dp"), scatter_dimension=0, tiled=True),
        lax.psum_scatter(grads[8], ("tower", "dp"), scatter_dimension=0, tiled=True),
        lax.psum_scatter(grads[9], ("tower", "dp"), scatter_dimension=0, tiled=True),
        lax.psum_scatter(grads[10], ("tower", "dp"), scatter_dimension=0, tiled=True),
        lax.psum_scatter(grads[11], ("tower", "dp"), scatter_dimension=0, tiled=True),
        lax.psum_scatter(grads[12], ("tower", "dp"), scatter_dimension=0, tiled=True),
    )


def local(
    tokens,
    segments,
    caption_image,
    logit_scale,
    first_gain,
    first_bias,
    triple_weight,
    query_bias,
    value_bias,
    output_weight,
    output_bias,
    second_gain,
    second_bias,
    expand_weight,
    expand_bias,
    shrink_weight,
    shrink_bias,
):
    rows_here = tokens.shape[1]
    length = tokens.shape[2]
    features = tokens.shape[3]
    head_size = features // HEADS
    token_count = rows_here * length
    is_text = lax.axis_index("tower") == 1
    text_flag = is_text.astype(jnp.float32)
    position = jnp.arange(length, dtype=jnp.int32)
    image_segs = jnp.broadcast_to(
        (position >= IMG_TOK).astype(jnp.int32)[None, :], (rows_here, length)
    )
    seg_ids = jnp.where(is_text, segments, image_segs)
    same_seg = (seg_ids[:, :, None] == seg_ids[:, None, :])[:, None, :, :]
    head_shape = (rows_here, length, HEADS, head_size)
    gain_one = first_gain[0].astype(jnp.float32)
    shift_one = first_bias[0].astype(jnp.float32)
    triple_w = triple_weight[0]
    query_shift = query_bias[0].astype(jnp.float32)
    value_shift = value_bias[0].astype(jnp.float32)
    output_w = output_weight[0]
    output_shift = output_bias[0].astype(jnp.float32)
    gain_two = second_gain[0].astype(jnp.float32)
    shift_two = second_bias[0].astype(jnp.float32)
    expand_w = expand_weight[0]
    expand_shift = expand_bias[0].astype(jnp.float32)
    shrink_w = shrink_weight[0]
    shrink_shift = shrink_bias[0].astype(jnp.float32)
    inputs = tokens[0].reshape(token_count, features).astype(jnp.float32)
    normed_a, spread_a = layer_stats(inputs)
    normed_one = (normed_a * gain_one + shift_one).astype(jnp.bfloat16)
    triple = jnp.dot(normed_one, triple_w, preferred_element_type=jnp.float32)
    queries = (triple[:, :features] + query_shift).astype(jnp.bfloat16).reshape(head_shape)
    key_heads = triple[:, features : 2 * features].astype(jnp.bfloat16).reshape(head_shape)
    value_heads = (triple[:, 2 * features :] + value_shift).astype(jnp.bfloat16).reshape(head_shape)
    scores = masked_scores(queries, key_heads, same_seg)
    row_peak = jnp.max(scores, axis=-1, keepdims=True)
    log_total = row_peak + jnp.log(jnp.sum(jnp.exp(scores - row_peak), axis=-1, keepdims=True))
    attn_probs = jnp.exp(scores - log_total)
    mixed_low = (
        jnp.einsum(
            "rhqk,rkhc->rqhc",
            attn_probs.astype(jnp.bfloat16),
            value_heads,
            preferred_element_type=jnp.float32,
        )
        .reshape(token_count, features)
        .astype(jnp.bfloat16)
    )
    hidden = (
        inputs + jnp.dot(mixed_low, output_w, preferred_element_type=jnp.float32) + output_shift
    )
    normed_b, spread_b = layer_stats(hidden)
    normed_two = (normed_b * gain_two + shift_two).astype(jnp.bfloat16)
    expanded = jnp.dot(normed_two, expand_w, preferred_element_type=jnp.float32) + expand_shift
    activated, gelu_back = jax.vjp(jax.nn.gelu, expanded)
    active_low = activated.astype(jnp.bfloat16)
    block_out = (
        hidden + jnp.dot(active_low, shrink_w, preferred_element_type=jnp.float32) + shrink_shift
    )
    slot_ids = jnp.arange(CAPS, dtype=jnp.int32)
    member = (seg_ids[:, None, :] == slot_ids[None, :, None]).astype(jnp.float32)
    counts = jnp.maximum(jnp.sum(member, axis=2), 1.0)
    pooled = (
        jnp.einsum(
            "rst,rtd->rsd", member, block_out.reshape(rows_here, length, features), precision=HIGH
        )
        / counts[:, :, None]
    )
    inverse = lax.rsqrt(jnp.sum(pooled * pooled, axis=2, keepdims=True) + 1e-06)
    embedding = pooled * inverse
    first_slot = embedding[:, 0, :].astype(jnp.bfloat16)
    collected = lax.all_gather(first_slot, "dp", axis=0, tiled=True)
    image_table = shifted(collected, "tower", 1)
    text_low = embedding.reshape(rows_here * CAPS, features).astype(jnp.bfloat16)
    similar = jnp.einsum("cd,id->ci", text_low, image_table, preferred_element_type=jnp.float32)
    factor = logit_scale[0]
    logits = factor * similar
    logit_peak = jnp.max(logits, axis=1, keepdims=True)
    logit_total = logit_peak + jnp.log(jnp.sum(jnp.exp(logits - logit_peak), axis=1, keepdims=True))
    targets = caption_image.reshape(-1)
    image_ids = jnp.arange(image_table.shape[0], dtype=jnp.int32)
    target_hot = (image_ids[None, :] == targets[:, None]).astype(jnp.float32)
    picked = jnp.sum(logits * target_hot, axis=1)
    loss_here = jnp.sum(logit_total[:, 0] - picked) * text_flag
    grad_logits = (jnp.exp(logits - logit_total) - target_hot) * text_flag
    factor_here = jnp.sum(grad_logits * similar)
    loss_total, factor_total = lax.psum((loss_here, factor_here), ("tower", "dp"))
    caption_total = rows_here * CAPS * lax.axis_size("dp")
    grad_dots = (factor * grad_logits).astype(jnp.bfloat16)
    grad_emb = jnp.einsum(
        "ci,id->cd", grad_dots, image_table, preferred_element_type=jnp.float32
    ).reshape(rows_here, CAPS, features)
    grad_pooled = inverse * (
        grad_emb - embedding * jnp.sum(embedding * grad_emb, axis=2, keepdims=True)
    )
    grad_pooled = grad_pooled / counts[:, :, None]
    grad_out = jnp.einsum("rst,rsd->rtd", member, grad_pooled, precision=HIGH).reshape(
        token_count, features
    )
    shrink_bias_grad = jnp.sum(grad_out, axis=0)
    grad_out_low = grad_out.astype(jnp.bfloat16)
    shrink_weight_grad = jnp.einsum(
        "nf,nd->fd", active_low, grad_out_low, preferred_element_type=jnp.float32
    )
    grad_active = jnp.einsum(
        "nd,fd->nf", grad_out_low, shrink_w, preferred_element_type=jnp.float32
    )
    grad_expanded = gelu_back(grad_active)[0]
    expand_bias_grad = jnp.sum(grad_expanded, axis=0)
    grad_expanded_low = grad_expanded.astype(jnp.bfloat16)
    expand_weight_grad = jnp.einsum(
        "nd,nf->df", normed_two, grad_expanded_low, preferred_element_type=jnp.float32
    )
    grad_normed_two = jnp.einsum(
        "nf,df->nd", grad_expanded_low, expand_w, preferred_element_type=jnp.float32
    )
    second_gain_grad = jnp.sum(grad_normed_two * normed_b, axis=0)
    second_bias_grad = jnp.sum(grad_normed_two, axis=0)
    grad_hidden = grad_out + norm_back(grad_normed_two * gain_two, normed_b, spread_b)
    output_bias_grad = jnp.sum(grad_hidden, axis=0)
    grad_hidden_low = grad_hidden.astype(jnp.bfloat16)
    output_weight_grad = jnp.einsum(
        "nd,ne->de", mixed_low, grad_hidden_low, preferred_element_type=jnp.float32
    )
    grad_mixed = (
        jnp.einsum("ne,de->nd", grad_hidden_low, output_w, preferred_element_type=jnp.float32)
        .astype(jnp.bfloat16)
        .reshape(head_shape)
    )
    scores_again = masked_scores(queries, key_heads, same_seg)
    probs_again = jnp.exp(scores_again - log_total)
    probs_low = probs_again.astype(jnp.bfloat16)
    grad_values = jnp.einsum(
        "rhqk,rqhc->rkhc", probs_low, grad_mixed, preferred_element_type=jnp.float32
    )
    grad_probs = jnp.einsum(
        "rqhc,rkhc->rhqk", grad_mixed, value_heads, preferred_element_type=jnp.float32
    )
    grad_scores = (
        probs_again * (grad_probs - jnp.sum(probs_again * grad_probs, axis=-1, keepdims=True))
    ).astype(jnp.bfloat16)
    grad_queries = (
        jnp.einsum("rhqk,rkhc->rqhc", grad_scores, key_heads, preferred_element_type=jnp.float32)
        * 0.125
    )
    grad_keys = (
        jnp.einsum("rhqk,rqhc->rkhc", grad_scores, queries, preferred_element_type=jnp.float32)
        * 0.125
    )
    grad_queries = grad_queries.reshape(token_count, features)
    grad_keys = grad_keys.reshape(token_count, features)
    grad_values = grad_values.reshape(token_count, features)
    query_bias_grad = jnp.sum(grad_queries, axis=0)
    value_bias_grad = jnp.sum(grad_values, axis=0)
    grad_triple = jnp.concatenate([grad_queries, grad_keys, grad_values], axis=1).astype(
        jnp.bfloat16
    )
    triple_weight_grad = jnp.einsum(
        "nd,ne->de", normed_one, grad_triple, preferred_element_type=jnp.float32
    )
    grad_normed_one = jnp.einsum(
        "ne,de->nd", grad_triple, triple_w, preferred_element_type=jnp.float32
    )
    first_gain_grad = jnp.sum(grad_normed_one * normed_a, axis=0)
    first_bias_grad = jnp.sum(grad_normed_one, axis=0)
    input_grad = grad_hidden + norm_back(grad_normed_one * gain_one, normed_a, spread_a)
    shares = sum_grads(
        (
            first_gain_grad,
            first_bias_grad,
            triple_weight_grad,
            query_bias_grad,
            value_bias_grad,
            output_weight_grad,
            output_bias_grad,
            second_gain_grad,
            second_bias_grad,
            expand_weight_grad,
            expand_bias_grad,
            shrink_weight_grad,
            shrink_bias_grad,
        )
    )
    loss_out = (loss_total / caption_total).reshape(1)
    factor_out = factor_total.reshape(1)
    return (
        loss_out,
        factor_out,
        input_grad.reshape(1, rows_here, length, features),
        shares[0],
        shares[1],
        shares[2],
        shares[3],
        shares[4],
        shares[5],
        shares[6],
        shares[7],
        shares[8],
        shares[9],
        shares[10],
        shares[11],
        shares[12],
    )


def solution(mesh):
    placed = (
        P("tower", "dp", None, None),
        P("dp", None),
        P("dp", None),
        P(),
        P("tower", None),
        P("tower", None),
        P("tower", None, None),
        P("tower", None),
        P("tower", None),
        P("tower", None, None),
        P("tower", None),
        P("tower", None),
        P("tower", None),
        P("tower", None, None),
        P("tower", None),
        P("tower", None, None),
        P("tower", None),
    )
    fits = mesh.shape["tower"] == 2 and mesh.shape["dp"] == 2 * PLANE
    return jax.shard_map(
        local_fast if fits else local,
        mesh=mesh,
        in_specs=placed,
        out_specs=(
            P(),
            P(),
            P("tower", "dp", None, None),
            P(("tower", "dp")),
            P(("tower", "dp")),
            P(("tower", "dp"), None),
            P(("tower", "dp")),
            P(("tower", "dp")),
            P(("tower", "dp"), None),
            P(("tower", "dp")),
            P(("tower", "dp")),
            P(("tower", "dp")),
            P(("tower", "dp"), None),
            P(("tower", "dp")),
            P(("tower", "dp"), None),
            P(("tower", "dp")),
        ),
        check_vma=False,
    )
```

```python
import functools

import jax
import jax.numpy as jnp
from jax import lax
from jax.experimental import pallas as pl
from jax.experimental.pallas import tpu as pltpu
from jax.sharding import PartitionSpec as P

HEADS = 12
IMG_TOK = 50
CAPS = 4

f32, bf16 = jnp.float32, jnp.bfloat16
GELU_C = 0.7978845608028654
GELU_A = 0.044715
STEP_ROWS = 4


def mm(a, b):
    return jnp.dot(a, b, preferred_element_type=f32)


def mm_nt(a, b):
    return lax.dot_general(a, b, (((1,), (1,)), ((), ())), preferred_element_type=f32)


def mm_tn(a, b):
    return lax.dot_general(a, b, (((0,), (0,)), ((), ())), preferred_element_type=f32)


def stats(x):
    center = x - jnp.mean(x, axis=-1, keepdims=True)
    spread = lax.rsqrt(jnp.mean(center * center, axis=-1, keepdims=True) + 1e-05)
    return center * spread, spread


def split(x, first):
    zero = jnp.zeros_like(x)
    return jnp.concatenate([jnp.where(first, x, zero), jnp.where(first, zero, x)], axis=0)


def low_pair(x):
    high = x.astype(bf16)
    return high, (x - high.astype(f32)).astype(bf16)


def fwd_kernel(tok, seg, g1, b1, qb, vb, ob, g2, b2, eb, sb, w3h, woh, weh, wsh,
               qkv, probs, mixed, hidden, act, slope, member_out, pooled_out, count_out,
               w3, wo, we, ws, pool_acc, count_acc, sems):
    i = pl.program_id(0)
    steps = pl.num_programs(0)
    rows_here, length = seg.shape
    slots = rows_here * CAPS
    feat = tok.shape[1]
    block = tok.shape[0]
    is_text = lax.axis_index("tower") == 1
    copies = [pltpu.make_async_copy(src, dst, sems.at[n])
              for n, (src, dst) in enumerate(((w3h, w3), (woh, wo), (weh, we), (wsh, ws)))]

    @pl.when(i == 0)
    def _():
        for c in copies:
            c.start()
        pool_acc[...] = jnp.zeros_like(pool_acc)
        count_acc[...] = jnp.zeros_like(count_acc)

    def arrive(n):
        @pl.when(i == 0)
        def _():
            copies[n].wait()

    x = tok[...].astype(f32)
    norm, _ = stats(x)
    n1 = (norm * g1[...].astype(f32) + b1[...].astype(f32)).astype(bf16)
    arrive(0)
    qkv[:, :feat] = (mm(n1, w3[:, :feat]) + qb[...].astype(f32)).astype(bf16)
    qkv[:, feat:2 * feat] = mm(n1, w3[:, feat:2 * feat]).astype(bf16)
    qkv[:, 2 * feat:] = (mm(n1, w3[:, 2 * feat:]) + vb[...].astype(f32)).astype(bf16)

    image_seg = (lax.broadcasted_iota(jnp.int32, (1, length), 1) >= IMG_TOK).astype(jnp.int32)
    row_segs = []
    for r in range(STEP_ROWS):
        s = seg[pl.ds(STEP_ROWS * i + r, 1), :]
        row_segs.append(jnp.where(is_text, s, image_seg))
    lane = lax.broadcasted_iota(jnp.int32, (128, 128), 1)
    first_half = lane < 64
    slot_lanes = []
    for pair in range(STEP_ROWS // 2):
        base = STEP_ROWS * i + 2 * pair
        keyed = jnp.concatenate(
            [row_segs[2 * pair] * rows_here + base, row_segs[2 * pair + 1] * rows_here + (base + 1)], axis=1)
        slot_lanes.append(keyed)
        across = jnp.broadcast_to(keyed.astype(f32), (128, 128))
        bias = jnp.where(across == across.T, 0.0, -1e30)
        bias = jnp.concatenate([bias, bias], axis=1)
        here = slice(pair * 128, pair * 128 + 128)
        hps = range(HEADS // 2)
        scores = [mm_nt(qkv[here, feat + 128 * h:feat + 128 * h + 128],
                        split(qkv[here, 128 * h:128 * h + 128] * jnp.asarray(0.125, bf16), first_half)) + bias
                  for h in hps]
        lows = []
        for h in hps:
            e = jnp.exp(scores[h] - jnp.max(scores[h], axis=0, keepdims=True))
            p = (e * (1.0 / jnp.sum(e, axis=0, keepdims=True))).astype(bf16)
            probs[here, 256 * h:256 * h + 256] = p
            lows.append(p)
        for h in hps:
            o = mm_tn(lows[h], qkv[here, 2 * feat + 128 * h:2 * feat + 128 * h + 128])
            mixed[here, 128 * h:128 * h + 128] = jnp.where(first_half, o[:128], o[128:]).astype(bf16)

    arrive(1)
    hid = x + mm(mixed[...], wo[...]) + ob[...].astype(f32)
    hidden[...] = hid
    norm2, _ = stats(hid)
    n2 = (norm2 * g2[...].astype(f32) + b2[...].astype(f32)).astype(bf16)
    arrive(2)
    arrive(3)
    out = hid + sb[...].astype(f32)
    tile = 768
    starts = range(0, we.shape[1], tile)
    ahead = mm(n2, we[:, :tile])
    for f in starts:
        v = ahead + eb[:, f:f + tile].astype(f32)
        if f + tile < we.shape[1]:
            ahead = mm(n2, we[:, f + tile:f + 2 * tile])
        v2 = v * v
        cv = v * GELU_C
        t = jnp.tanh(cv * (1.0 + GELU_A * v2))
        h = 0.5 + 0.5 * t
        a = (v * h).astype(bf16)
        act[:, f:f + tile] = a
        slope[:, f:f + tile] = (h + h * (1.0 - h) * ((2.0 * cv) * (1.0 + (3.0 * GELU_A) * v2))).astype(bf16)
        out = out + mm(a, ws[f:f + tile, :])
    slot_row = jnp.concatenate(slot_lanes, axis=1)
    hot = (lax.broadcasted_iota(jnp.int32, (slots, block), 0) == slot_row)
    member = hot.astype(f32).astype(bf16)
    member_out[...] = member
    out_hi, out_lo = low_pair(out)
    pool_acc[...] += mm(member, out_hi) + mm(member, out_lo)
    count_acc[...] += jnp.broadcast_to(jnp.sum(hot.astype(f32), axis=1, keepdims=True), count_acc.shape)

    @pl.when(i == steps - 1)
    def _():
        counts = jnp.maximum(count_acc[...], 1.0)
        count_out[...] = counts
        pooled_out[...] = pool_acc[...] / counts[:, :1]


def forward(tokens, segments, g1, b1, w3, qb, vb, wo, ob, g2, b2, we, eb, ws, sb):
    count, feat = tokens.shape
    rows_here, length = segments.shape
    slots = rows_here * CAPS
    ff = we.shape[1]
    block = STEP_ROWS * length
    steps = count // block
    whole = lambda a: pl.BlockSpec(a.shape, lambda i: (0,) * a.ndim)
    rows = lambda width: pl.BlockSpec((block, width), lambda i: (i, 0))
    anyw = pl.BlockSpec(memory_space=pl.ANY)
    smalls = (g1, b1, qb, vb, ob, g2, b2, eb, sb)
    return pl.pallas_call(
        fwd_kernel,
        grid=(steps,),
        in_specs=[rows(feat), whole(segments)] + [whole(a) for a in smalls] + [anyw] * 4,
        out_specs=[rows(3 * feat),
                   rows(2 * feat),
                   rows(feat), rows(feat), rows(ff), rows(ff),
                   pl.BlockSpec((slots, block), lambda i: (0, i)),
                   pl.BlockSpec((slots, feat), lambda i: (0, 0)),
                   pl.BlockSpec((slots, 128), lambda i: (0, 0))],
        out_shape=[jax.ShapeDtypeStruct((count, 3 * feat), bf16),
                   jax.ShapeDtypeStruct((count, 2 * feat), bf16),
                   jax.ShapeDtypeStruct((count, feat), bf16),
                   jax.ShapeDtypeStruct((count, feat), f32),
                   jax.ShapeDtypeStruct((count, ff), bf16),
                   jax.ShapeDtypeStruct((count, ff), bf16),
                   jax.ShapeDtypeStruct((slots, count), bf16),
                   jax.ShapeDtypeStruct((slots, feat), f32),
                   jax.ShapeDtypeStruct((slots, 128), f32)],
        scratch_shapes=[pltpu.VMEM(w3.shape, bf16), pltpu.VMEM(wo.shape, bf16), pltpu.VMEM(we.shape, bf16),
                        pltpu.VMEM(ws.shape, bf16), pltpu.VMEM((slots, feat), f32), pltpu.VMEM((slots, 128), f32),
                        pltpu.SemaphoreType.DMA((4,))],
        compiler_params=pltpu.CompilerParams(vmem_limit_bytes=56 << 20, dimension_semantics=("arbitrary",)),
        name="fwd",
    )(tokens, segments, *smalls, w3, wo, we, ws)


MESH = pl.DeviceIdType.MESH
PLANE = 8
LINE = 4
BLK = 256
CH = 768
HALF = CH // 2
ROWS = HALF // PLANE
N_CH = 12
LONG = (1, 3, 5, 7, 8, 10)
SHORT = (9, 11)


def fold(x):
    return jnp.sum(x.reshape(x.shape[0] // 8, 8, x.shape[1]), axis=0)


def bwd_kernel(member, pooled, count, caption, scale, g1, b1, g2, b2,
               qkv_h, probs_h, mixed_h, hidden_h, act_h, slope_h, tok_h, w3_h, wo_h, we_h, ws_h,
               tw_out, ow_out, ew_out, sw_out, in_out, vec_out,
               cs, snd, prv, own, yrcv, ysw, zrcv, arcv, swrcv, fin, swfin,
               gol, gn2, hid, spread2, n2b, tok, act, slope, ws, we, ge, qkv, w3, wo,
               imgs, elow, ebsum, attn_sum, vec, vown, vpair, vrcv,
               ld, psend, precv, xsend, xrecv, ysend, yrecv, yswsend, yswrecv, zsend, zrecv, asend, arecv,
               swsend, swrecv, fsem, swfsem, gsem, esem, vpsem, vsem, outsem):
    t = lax.axis_index("tower")
    d = lax.axis_index("dp")
    p = d // 2
    c = lax.rem(d, 2)
    z = p // 2
    y = lax.rem(p, 2)
    is_text = t == 1
    count_t = gol.shape[0]
    blocks = count_t // BLK
    feat = CH
    rows_here = caption.shape[0]
    other = 1 - c

    def peer(k):
        return lax.rem(p + k, PLANE)

    def at_core(tt, pp):
        return (tt, pp * 2 + c)

    partner = (t, p * 2 + other)
    beside = at_core(t, 2 * z + (1 - y))
    across = at_core(1 - t, p)

    def remote(src, dst, ssem, rsem, dev):
        return pltpu.make_async_remote_copy(src_ref=src, dst_ref=dst, send_sem=ssem, recv_sem=rsem,
                                            device_id=dev, device_id_type=MESH)

    barrier = pltpu.get_barrier_semaphore()
    pl.semaphore_signal(barrier, inc=1, device_id=partner, device_id_type=MESH)
    pl.semaphore_signal(barrier, inc=1, device_id=across, device_id_type=MESH)
    for k in range(1, PLANE):
        pl.semaphore_signal(barrier, inc=1, device_id=at_core(t, peer(k)), device_id_type=MESH)
        pl.semaphore_signal(barrier, inc=1, device_id=at_core(1 - t, peer(k)), device_id_type=MESH)

    pooled_v = pooled[...]
    inverse = lax.rsqrt(jnp.sum(pooled_v * pooled_v, axis=1, keepdims=True) + 1e-06)
    emb = pooled_v * inverse
    emb_low = emb.astype(bf16)

    def pair_copy(q):
        slot = lax.rem(q, 2)
        return remote(snd.at[slot], prv.at[q], psend.at[slot], precv.at[q], partner)

    def x_all(q):
        return remote(cs.at[q, 0:LINE], cs.at[q, 0:LINE], xsend.at[q], xrecv.at[q], across)

    def x_line(q):
        return remote(cs.at[q, 0:LINE, y], cs.at[q, 0:LINE, y], xsend.at[q], xrecv.at[q], across)

    def y_copy(q):
        return remote(cs.at[q, :, 1 - y], yrcv.at[q // 2], ysend.at[q // 2], yrecv.at[q // 2], beside)

    def z_start(q):
        for k in range(1, LINE):
            to = lax.rem(z + k, LINE)
            remote(cs.at[q, LINE * t + to, y], zrcv.at[q // 2, k - 1], zsend.at[q // 2], zrecv.at[q // 2],
                   at_core(t, 2 * to + y)).start()

    def z_all(q):
        return remote(zrcv.at[q // 2], zrcv.at[q // 2], zsend.at[q // 2], zrecv.at[q // 2], partner)

    def a_start(q):
        for k in range(1, PLANE):
            to = peer(k)
            remote(cs.at[q, LINE * t + to // 2, lax.rem(to, 2)], arcv.at[(q - 9) // 2, k - 1],
                   asend.at[(q - 9) // 2], arecv.at[(q - 9) // 2], at_core(t, to)).start()

    def a_all(q):
        a = (q - 9) // 2
        return remote(arcv.at[a], arcv.at[a], asend.at[a], arecv.at[a], partner)

    def ysw_copy(i):
        return remote(cs.at[2 * i, pl.ds(LINE * t + 2 * (1 - y), 2)], ysw.at[i], yswsend.at[i], yswrecv.at[i], beside)

    def sw_z(i):
        k = lax.rem(i - z + LINE, LINE)
        return remote(cs.at[2 * i, pl.ds(LINE * t + 2 * y, 2)], swrcv.at[jnp.maximum(k, 1) - 1], swsend,
                      swrecv, at_core(t, 2 * i + y))

    def sw_mid(i):
        ysw_copy(i).wait_recv()
        for a in range(2):
            at = LINE * t + 2 * y + a
            cs[2 * i, at] = (cs[2 * i, at].astype(f32) + ysw[i, a].astype(f32)).astype(bf16)

        @pl.when(z != i)
        def _():
            sw_z(i).start()

    def long_mid(q):
        y_copy(q).wait_recv()
        for a in range(PLANE):
            cs[q, a, y] = (cs[q, a, y].astype(f32) + yrcv[q // 2, a].astype(f32)).astype(bf16)
        x_line(q).start()
        z_start(q)

    def chip_sum(q):
        pair_copy(q).wait_recv()
        slot = lax.rem(q, 2)
        n = 2 * ROWS
        for a in range(PLANE):
            total = own[slot, n * a:n * (a + 1), :] + prv[q, n * a:n * (a + 1), :].astype(f32)
            cs[q, a] = total.reshape(2, ROWS, HALF).astype(bf16)

    def chunk(q, left, right):
        slot = lax.rem(q, 2)

        @pl.when(q >= 2)
        def _():
            pair_copy(q - 2).wait_send()
        for r in range(0, CH, 256):
            part = mm_tn(left[:, r:r + 256], right)
            low, high = part[:, :HALF], part[:, HALF:]
            own[slot, r:r + 256, :] = jnp.where(c == 0, low, high)
            snd[slot, r:r + 256, :] = jnp.where(c == 0, high, low).astype(bf16)
        pair_copy(q).start()

    def gather_start():
        for k in range(PLANE):
            remote(elow, imgs.at[c, p], gsem.at[0], gsem.at[1], at_core(1 - t, peer(k))).start()

    def gather_all():
        return remote(imgs.at[c], imgs.at[c], gsem.at[0], gsem.at[1], partner)

    def share_copy(h):
        return remote(imgs.at[h], imgs.at[h], esem.at[0], esem.at[1], partner)

    def v_pair():
        return remote(vown.at[other], vpair, vpsem.at[0], vpsem.at[1], partner)

    def load(n, src, dst):
        return pltpu.make_async_copy(src, dst, ld.at[n])

    def tile_loads(i):
        s = lax.rem(i, 2)
        out = []
        ff = act_h.shape[1]
        for h in range(2):
            col = pl.multiple_of((ff // 2) * h + HALF * i, 128)
            here = pl.ds(HALF * h, HALF)
            out.append(load(8 * s + 4 * h, act_h.at[:, pl.ds(col, HALF)], act.at[s, :, here]))
            out.append(load(8 * s + 4 * h + 1, slope_h.at[:, pl.ds(col, HALF)], slope.at[s, :, here]))
            out.append(load(8 * s + 4 * h + 2, ws_h.at[pl.ds(col, HALF)], ws.at[s, here]))
            out.append(load(8 * s + 4 * h + 3, we_h.at[:, pl.ds(col, HALF)], we.at[s, :, here]))
        return out

    hid_load = load(16, hidden_h, hid)
    tok_load = load(17, tok_h, tok)
    qkv_load = load(18, qkv_h, qkv)
    w3_load = load(19, w3_h, w3)
    wo_load = load(20, wo_h, wo)
    mixed_load = load(21, mixed_h, slope.at[0])
    probs_loads = [load(22 + h, probs_h.at[:, pl.ds(feat * h, feat)], act.at[h]) for h in range(2)]

    @pl.when(t == 0)
    def _():
        elow[...] = emb_low[:rows_here]
        pl.semaphore_wait(barrier, 2 * PLANE)
        gather_start()
        gn2[:BLK, :] = jnp.zeros((BLK, feat), f32)
        for m in range(blocks):
            pltpu.make_async_copy(gn2.at[0:BLK], in_out.at[pl.ds(BLK * m, BLK)], outsem.at[m]).start()

        @pl.loop(0, 6)
        def _(i):
            @pl.when(i < 4)
            def _():
                x_all(2 * i).wait_recv()
                ysw_copy(i).start()

            @pl.when((i >= 1) & (i <= 4))
            def _():
                sw_mid(i - 1)

            @pl.when(i >= 2)
            def _():
                x_line(2 * i - 3).wait_recv()
                z_start(2 * i - 3)
        for q in (9, 8, 11, 10):
            if q in SHORT:
                x_all(q).wait_recv()
                a_start(q)
            else:
                x_line(q).wait_recv()
                z_start(q)
        gather_all().wait_send()
        for m in range(blocks):
            pltpu.make_async_copy(gn2.at[0:BLK], in_out.at[pl.ds(BLK * m, BLK)], outsem.at[m]).wait()

    @pl.when(is_text)
    def _():
        hid_load.start()
        tok_load.start()
        for cp in tile_loads(0):
            cp.start()
        for cp in tile_loads(1):
            cp.start()
        qkv_load.start()
        w3_load.start()
        wo_load.start()
        gain2, shift2 = g2[...].astype(f32), b2[...].astype(f32)
        gain1, shift1 = g1[...].astype(f32), b1[...].astype(f32)
        hid_load.wait()

        @pl.loop(0, blocks)
        def _(m):
            here = pl.ds(pl.multiple_of(m * BLK, BLK), BLK)
            norm, spread = stats(hid[here, :])
            n2b[here, :] = (norm * gain2 + shift2).astype(bf16)
            hid[here, :] = norm
            spread2[here, :] = spread
        gn2[...] = jnp.zeros_like(gn2)
        attn_sum[...] = jnp.zeros_like(attn_sum)
        vec[...] = jnp.zeros_like(vec)
        pl.semaphore_wait(barrier, 2 * PLANE)
        gather_all().wait_recv()
        share_copy(c).start()
        share_copy(c).wait_send()
        share_copy(other).wait_recv()

        table = imgs[...].reshape(2 * PLANE * rows_here, feat)
        dots = mm_nt(emb_low, table)
        factor = scale[0]
        logits = factor * dots
        peak = jnp.max(logits, axis=1, keepdims=True)
        weight = jnp.exp(logits - peak)
        total = jnp.sum(weight, axis=1, keepdims=True)
        wanted = jnp.concatenate([caption[:, s:s + 1] for s in range(CAPS)], axis=0)
        span = 2 * rows_here
        inside = lax.rem(wanted, span)
        wanted = (inside // rows_here) * (PLANE * rows_here) + (wanted // span) * rows_here + lax.rem(inside, rows_here)
        hot = (lax.broadcasted_iota(jnp.int32, dots.shape, 1) == wanted).astype(f32)
        picked = jnp.sum(logits * hot, axis=1, keepdims=True)
        loss_here = jnp.sum(peak + jnp.log(total) - picked, axis=0, keepdims=True)
        grad_logits = weight / total - hot
        factor_here = jnp.sum(jnp.sum(grad_logits * dots, axis=1, keepdims=True), axis=0, keepdims=True)
        grad_emb = mm((factor * grad_logits).astype(bf16), table)
        counts = count[:, :1]
        grad_pool = inverse * (grad_emb - emb * jnp.sum(emb * grad_emb, axis=1, keepdims=True))
        vec[7:8, :] = jnp.sum(grad_pool, axis=0, keepdims=True)
        column = lax.broadcasted_iota(jnp.int32, (1, feat), 1)
        vec[12:13, :] = jnp.where(column == 0, loss_here, jnp.where(column == 1, factor_here, 0.0))
        gp_hi, gp_lo = low_pair(grad_pool / counts)
        for m in range(blocks):
            gol[BLK * m:BLK * (m + 1), :] = mm_tn(member[:, BLK * m:BLK * (m + 1)], gp_hi).astype(bf16)

        @pl.loop(0, 4)
        def _(i):
            s = lax.rem(i, 2)
            for cp in tile_loads(i):
                cp.wait()
            chunk(2 * i, act.at[s], gol[...])

            @pl.when(i > 0)
            def _():
                chip_sum(2 * i - 1)
                y_copy(2 * i - 1).start()
            sums = jnp.zeros((8, feat), f32)
            for m in range(blocks):
                here = slice(BLK * m, BLK * (m + 1))
                grad = mm_nt(gol[here, :], ws[s]) * slope[s, here, :].astype(f32)
                sums = sums + fold(grad)
                ge[here, :] = grad.astype(bf16)
            sums = jnp.sum(sums, axis=0, keepdims=True)
            for h in range(2):
                ebsum[:, pl.ds(pl.multiple_of(4 * HALF * h + HALF * i, 128), HALF)] = sums[:, HALF * h:HALF * (h + 1)]
            chunk(2 * i + 1, n2b, ge[...])
            chip_sum(2 * i)
            x_all(2 * i).start()
            ysw_copy(i).start()

            @pl.when(i > 0)
            def _():
                sw_mid(i - 1)
            for m in range(blocks):
                here = slice(BLK * m, BLK * (m + 1))
                gn2[here, :] += mm_nt(ge[here, :], we[s])

            @pl.when(i >= 2)
            def _():
                long_mid(2 * i - 3)

            @pl.when(i < 2)
            def _():
                for cp in tile_loads(i + 2):
                    cp.start()

            @pl.when(i == 2)
            def _():
                mixed_load.start()
                probs_loads[0].start()
        probs_loads[1].start()
        chip_sum(7)
        y_copy(7).start()

        zeros8 = jnp.zeros((8, feat), f32)

        def norm2_back(m, sums):
            here = pl.ds(pl.multiple_of(m * BLK, BLK), BLK)
            norm, g_in = hid[here, :], gn2[here, :]
            hot_m = member[:, here]
            grad_out = mm_tn(hot_m, gp_hi) + mm_tn(hot_m, gp_lo)
            g = g_in * gain2
            back = spread2[here, :] * (g - jnp.mean(g, axis=1, keepdims=True)
                                       - norm * jnp.mean(g * norm, axis=1, keepdims=True))
            gh = grad_out + back
            gn2[here, :] = gh
            gol[here, :] = gh.astype(bf16)
            return (sums[0] + fold(g_in * norm), sums[1] + fold(g_in), sums[2] + fold(gh))
        sums = lax.fori_loop(0, blocks, norm2_back, (zeros8, zeros8, zeros8))
        for row, x in ((5, sums[0]), (6, sums[1]), (4, sums[2])):
            vec[row:row + 1, :] = jnp.sum(x, axis=0, keepdims=True)
        for n in range(4):
            vec[8 + n:9 + n, :] = ebsum[:, feat * n:feat * (n + 1)]
        sw_mid(3)

        mixed_load.wait()
        chunk(8, slope.at[0], gol[...])
        wo_load.wait()
        for m in range(blocks):
            here = slice(BLK * m, BLK * (m + 1))
            ge[here, :] = mm_nt(gol[here, :], wo[...]).astype(bf16)
        chip_sum(8)
        y_copy(8).start()
        long_mid(5)

        qkv_load.wait()
        for cp in probs_loads:
            cp.wait()
        first_half = lax.broadcasted_iota(jnp.int32, (128, 128), 1) < 64
        hps = range(HEADS // 2)

        @pl.loop(0, count_t // 128)
        def _(rp):
            here = pl.ds(pl.multiple_of(rp * 128, 128), 128)

            def probs_of(h):
                return act[h // 3, here, 256 * (h % 3):256 * (h % 3) + 256]

            def part(n, h):
                return qkv[here, feat * n + 128 * h:feat * n + 128 * h + 128]
            gm = [split(ge[here, 128 * h:128 * h + 128], first_half) for h in hps]
            gp = [mm_nt(part(2, h), gm[h]) for h in hps]
            gv = [mm(probs_of(h), gm[h]) for h in hps]
            gs = []
            for h in hps:
                probs_f = probs_of(h).astype(f32)
                weighted = probs_f * gp[h]
                gs.append((weighted - probs_f * jnp.sum(weighted, axis=0, keepdims=True)).astype(bf16))
            gk = [mm(gs[h], split(part(0, h), first_half)) * 0.125 for h in hps]
            gq = []
            for h in hps:
                both = mm_tn(gs[h], part(1, h))
                gq.append(jnp.where(first_half, both[:128], both[128:]) * 0.125)
            for h in hps:
                for n, x in ((0, gq[h]), (1, gk[h]), (2, gv[h])):
                    qkv[here, feat * n + 128 * h:feat * n + 128 * h + 128] = x.astype(bf16)
                for n, x in ((0, gq[h]), (1, gv[h])):
                    attn_sum[:, feat * n + 128 * h:feat * n + 128 * h + 128] += fold(x)
        vec[2:3, :] = jnp.sum(attn_sum[:, :feat], axis=0, keepdims=True)
        vec[3:4, :] = jnp.sum(attn_sum[:, feat:], axis=0, keepdims=True)

        tok_load.wait()

        @pl.loop(0, blocks)
        def _(m):
            here = pl.ds(pl.multiple_of(m * BLK, BLK), BLK)
            norm, _s = stats(tok[here, :].astype(f32))
            slope[1, here, :] = (norm * gain1 + shift1).astype(bf16)

        @pl.loop(0, 3)
        def _(j):
            chunk(9 + j, slope.at[1], qkv[:, pl.ds(pl.multiple_of(CH * j, 128), CH)])

            @pl.when(j == 1)
            def _():
                chip_sum(9)
                x_all(9).start()
                a_start(9)
                long_mid(7)
        chip_sum(10)
        y_copy(10).start()
        long_mid(8)
        w3_load.wait()

        def norm1_back(m, sums):
            here = pl.ds(pl.multiple_of(m * BLK, BLK), BLK)
            g_in = mm_nt(qkv[here, :], w3[...])

            @pl.when(m == 0)
            def _():
                chip_sum(11)
                x_all(11).start()
                a_start(11)

            norm, spread = stats(tok[here, :].astype(f32))
            g = g_in * gain1
            back = spread * (g - jnp.mean(g, axis=1, keepdims=True)
                             - norm * jnp.mean(g * norm, axis=1, keepdims=True))
            gn2[here, :] += back
            pltpu.make_async_copy(gn2.at[here], in_out.at[here], outsem.at[m]).start()
            return (sums[0] + fold(g_in * norm), sums[1] + fold(g_in))
        sums = lax.fori_loop(0, blocks, norm1_back, (zeros8, zeros8))
        for row, x in ((0, sums[0]), (1, sums[1])):
            vec[row:row + 1, :] = jnp.sum(x, axis=0, keepdims=True)

        width, wide = feat // (4 * PLANE), 4 * feat // (4 * PLANE)
        narrow = vec[0:8, :]
        broad = vec[8:16, :]
        scalars = vec[12:13, :128]
        turned = [broad] + [pltpu.roll(broad, feat - wide * j, axis=1) for j in range(1, feat // wide)]
        for g in range(4 * PLANE):
            one = narrow if g == 0 else pltpu.roll(narrow, feat - width * g, axis=1)
            row = g // (feat // wide)
            tail = turned[g % (feat // wide)][row:row + 1, :128]
            vown[g % 2, g // 2, 0:8, :] = one[:, :128]
            vown[g % 2, g // 2, 8:9, :] = tail
            vown[g % 2, g // 2, 9:10, :] = scalars
        v_pair().start()
        for m in range(blocks):
            here = pl.ds(BLK * m, BLK)
            pltpu.make_async_copy(gn2.at[here], in_out.at[here], outsem.at[m]).wait()
        v_pair().wait_recv()
        vown[c] += vpair[...]
        for k in range(PLANE):
            for tt in range(2):
                if tt == 0 or k:
                    remote(vown.at[c, PLANE * tt + peer(k)], vrcv.at[k], vsem.at[0], vsem.at[1],
                           at_core(tt, peer(k))).start()
        long_mid(10)

    half_rows = ROWS // 2

    def keep(n, out, col):
        return pltpu.make_async_copy(fin.at[n, pl.ds(pl.multiple_of(half_rows * c, 8), half_rows)],
                                     out.at[:, pl.ds(col, HALF)], fsem.at[0])

    def give(n, out, col):
        return remote(fin.at[n, pl.ds(pl.multiple_of(half_rows * other, 8), half_rows)],
                      out.at[:, pl.ds(col, HALF)], fsem.at[1], fsem.at[2], partner)

    def hand_over(n, total, out, col):
        fin[n] = total
        keep(n, out, col).start()
        give(n, out, col).start()

    def finish_long(q, out, col):
        z_all(q).wait_recv()
        total = cs[q, LINE * t + z, y].astype(f32)
        for k in range(LINE - 1):
            total = total + zrcv[q // 2, k].astype(f32)
        hand_over(q // 2, total, out, col)

    def finish_short(q, out, col):
        a_all(q).wait_recv()
        total = cs[q, LINE * t + z, y].astype(f32)
        for k in range(PLANE - 1):
            total = total + arcv[(q - 9) // 2, k].astype(f32)
        hand_over(len(LONG) + (q - 9) // 2, total, out, col)

    def sw_all():
        return remote(swrcv, swrcv, swsend, swrecv, partner)

    def sw_keep():
        n = 2 * ROWS
        return pltpu.make_async_copy(swfin.at[pl.ds(pl.multiple_of(n * c, 8), n)],
                                     sw_out.at[:, pl.ds(pl.multiple_of(HALF * c, 128), HALF)], swfsem.at[0])

    def sw_give():
        n = 2 * ROWS
        return remote(swfin.at[pl.ds(pl.multiple_of(n * other, 8), n)],
                      sw_out.at[:, pl.ds(pl.multiple_of(HALF * c, 128), HALF)], swfsem.at[1], swfsem.at[2], partner)

    sw_all().wait_recv()
    for a in range(2):
        total = cs[2 * z, LINE * t + 2 * y + a].astype(f32)
        for k in range(LINE - 1):
            total = total + swrcv[k, a].astype(f32)
        swfin[2 * ROWS * a:2 * ROWS * (a + 1), :] = total.reshape(2 * ROWS, HALF)
    sw_keep().start()
    sw_give().start()

    @pl.loop(0, 4)
    def _(i):
        finish_long(2 * i + 1, ew_out, pl.multiple_of(4 * HALF * c + HALF * i, 128))
    finish_short(9, tw_out, pl.multiple_of(HALF * c, 128))
    finish_long(8, ow_out, pl.multiple_of(HALF * c, 128))
    finish_short(11, tw_out, pl.multiple_of(2 * CH + HALF * c, 128))
    finish_long(10, tw_out, pl.multiple_of(CH + HALF * c, 128))

    @pl.when(is_text)
    def _():
        remote(vrcv.at[1:PLANE], vrcv.at[1:PLANE], vsem.at[0], vsem.at[1], partner).wait_recv()
        total = vown[c, PLANE + p]
        for k in range(1, PLANE):
            total = total + vrcv[k]
        vec_out[...] = total

    @pl.when(t == 0)
    def _():
        remote(vrcv, vrcv, vsem.at[0], vsem.at[1], partner).wait_recv()
        total = vrcv[0]
        for k in range(1, PLANE):
            total = total + vrcv[k]
        vec_out[...] = total

    @pl.when(is_text)
    def _():
        everything = vown.at[0, 0:2 * PLANE - 1]
        remote(everything, everything, vsem.at[0], vsem.at[1], partner).wait_send()
        v_pair().wait_send()
        for q in (N_CH - 2, N_CH - 1):
            pair_copy(q).wait_send()

        @pl.loop(0, 4)
        def _(i):
            x_all(2 * i).wait_send()
            x_line(2 * i + 1).wait_send()
            y_copy(2 * i + 1).wait_send()
        for q in (8, 10):
            x_line(q).wait_send()
            y_copy(q).wait_send()
        for q in SHORT:
            x_all(q).wait_send()

    @pl.loop(0, 4)
    def _(i):
        ysw_copy(i).wait_send()
        z_all(2 * i + 1).wait_send()
    for q in (8, 10):
        z_all(q).wait_send()
    for q in SHORT:
        a_all(q).wait_send()
    sw_all().wait_send()
    sw_keep().wait()
    sw_give().wait()
    lower = fin.at[:, 0:half_rows]
    pltpu.make_async_copy(lower, lower, fsem.at[0]).wait()
    remote(lower, lower, fsem.at[1], fsem.at[2], partner).wait()


def backward(member, pooled, count, caption, scale, g1, b1, g2, b2,
             qkv, probs, mixed, hidden, act, slope, tokens, w3, wo, we, ws):
    n_tok, feat = tokens.shape
    rows_here = caption.shape[0]
    ff = we.shape[1]
    dma = pltpu.SemaphoreType.DMA
    vm = pltpu.VMEM
    vspec = pl.BlockSpec(memory_space=pltpu.VMEM)
    sspec = pl.BlockSpec(memory_space=pltpu.SMEM)
    anyw = pl.BlockSpec(memory_space=pl.ANY)
    shape = jax.ShapeDtypeStruct
    longs, shorts = len(LONG), len(SHORT)
    scratch = [
        vm((N_CH, PLANE, 2, ROWS, HALF), bf16), vm((2, CH, HALF), bf16), vm((N_CH, CH, HALF), bf16),
        vm((2, CH, HALF), f32),
        vm((longs, PLANE, ROWS, HALF), bf16), vm((4, 2, 2, ROWS, HALF), bf16), vm((longs, LINE - 1, ROWS, HALF), bf16),
        vm((shorts, PLANE - 1, ROWS, HALF), bf16), vm((LINE - 1, 2, 2, ROWS, HALF), bf16),
        vm((longs + shorts, ROWS, HALF), f32), vm((4 * ROWS, HALF), f32),
        vm((n_tok, feat), bf16), vm((n_tok, feat), f32), vm((n_tok, feat), f32), vm((n_tok, 1), f32),
        vm((n_tok, feat), bf16), vm((n_tok, feat), bf16),
        vm((2, n_tok, CH), bf16), vm((2, n_tok, CH), bf16), vm((2, CH, feat), bf16), vm((2, feat, CH), bf16),
        vm((n_tok, feat), bf16), vm((n_tok, 3 * feat), bf16), vm(w3.shape, bf16), vm(wo.shape, bf16),
        vm((2, PLANE, rows_here, feat), bf16), vm((rows_here, feat), bf16), vm((1, ff), f32), vm((8, 2 * feat), f32),
        vm((16, feat), f32), vm((2, 2 * PLANE, 16, 128), f32), vm((2 * PLANE, 16, 128), f32), vm((PLANE, 16, 128), f32),
        dma((24,)), dma((2,)), dma((N_CH,)), dma((N_CH,)), dma((N_CH,)), dma((longs,)), dma((longs,)),
        dma((4,)), dma((4,)), dma((longs,)), dma((longs,)), dma((shorts,)), dma((shorts,)),
        dma, dma, dma((3,)), dma((3,)), dma((2,)), dma((2,)), dma((2,)), dma((2,)), dma((n_tok // BLK,)),
    ]
    return pl.pallas_call(
        bwd_kernel,
        in_specs=[vspec] * 4 + [sspec] + [vspec] * 4 + [anyw] * 11,
        out_specs=[anyw] * 5 + [vspec],
        out_shape=[shape((ROWS // 2, 3 * feat), f32), shape((ROWS // 2, feat), f32), shape((ROWS // 2, ff), f32),
                   shape((2 * ROWS, feat), f32), shape((n_tok, feat), f32), shape((16, 128), f32)],
        scratch_shapes=scratch,
        compiler_params=pltpu.CompilerParams(vmem_limit_bytes=61 << 20, collective_id=0, has_side_effects=True),
        name="bwd",
    )(member, pooled, count, caption, scale, g1, b1, g2, b2,
      qkv, probs, mixed, hidden, act, slope, tokens, w3, wo, we, ws)


def hand_out_kernel(scale_by, vec, tw, ow, ew, sw, inp, loss, factor, *rest):
    smalls, bigs = rest[:9], rest[9:]
    bigs[4][...] = inp[...]

    @pl.when(pl.program_id(0) == 0)
    def _():
        for src, dst in zip((tw, ow, ew, sw), bigs):
            dst[...] = src[...]
        width, wide = smalls[0].shape[1], smalls[8].shape[1]
        for n in range(8):
            smalls[n][...] = vec[n:n + 1, :width]
        smalls[8][...] = vec[8:9, :wide]
        loss[...] = vec[9:10, 0:1] * scale_by
        factor[...] = vec[9:10, 1:2]


def hand_out(vec, tw, ow, ew, sw, inp, captions):
    devices = lax.axis_size("tower") * lax.axis_size("dp")
    feat = tw.shape[1] // 3
    bigs = (tw, ow, ew, sw)
    outs = ([(1, 1)] * 2 + [(1, feat // devices)] * 8 + [(1, ew.shape[1] // devices)]
            + [a.shape for a in bigs])
    whole = lambda dims: pl.BlockSpec(dims, lambda i: (0,) * len(dims))
    moving = pl.BlockSpec((BLK, feat), lambda i: (i, 0))
    return pl.pallas_call(
        functools.partial(hand_out_kernel, 1.0 / captions),
        grid=(inp.shape[0] // BLK,),
        in_specs=[whole(vec.shape)] + [whole(a.shape) for a in bigs] + [moving],
        out_specs=[whole(dims) for dims in outs] + [moving],
        out_shape=[jax.ShapeDtypeStruct(dims, f32) for dims in outs + [inp.shape]],
        name="hand_out",
    )(vec, *bigs, inp)


def local_fast(tokens, segments, caption_image, logit_scale, first_gain, first_bias, triple_weight, query_bias,
               value_bias, output_weight, output_bias, second_gain, second_bias, expand_weight, expand_bias,
               shrink_weight, shrink_bias):
    rows_here, length, feat = tokens.shape[1:]
    flat = tokens[0].reshape(rows_here * length, feat)
    w3, wo, we, ws = triple_weight[0], output_weight[0], expand_weight[0], shrink_weight[0]
    qkv, probs, mixed, hidden, act, slope, member, pooled, count = forward(
        flat, segments, first_gain, first_bias, w3, query_bias, value_bias, wo, output_bias,
        second_gain, second_bias, we, expand_bias, ws, shrink_bias)
    tw, ow, ew, sw, inp, vec = backward(member, pooled, count, caption_image, logit_scale, first_gain, first_bias,
                                        second_gain, second_bias, qkv, probs, mixed, hidden, act, slope, flat,
                                        w3, wo, we, ws)
    captions = rows_here * CAPS * lax.axis_size("dp")
    outs = hand_out(vec, tw, ow, ew, sw, inp, captions)
    loss, factor = outs[0].reshape(1), outs[1].reshape(1)
    g1, b1, qb, vb, ob, g2, b2, sb, eb = (a.reshape(-1) for a in outs[2:11])
    tw, ow, ew, sw, inp = outs[11:]
    return (loss, factor, inp.reshape(1, rows_here, length, feat), g1, b1, tw, qb, vb, ow, ob, g2, b2, ew, eb, sw, sb)


HIGH = lax.Precision.HIGHEST


def shifted(shard, axis, by):
    peers = lax.axis_size(axis)
    pairs = [(i, i + by) for i in range(peers) if 0 <= i + by < peers]
    return lax.ppermute(shard, axis, pairs)


def layer_stats(values):
    center = values - jnp.mean(values, axis=-1, keepdims=True)
    spread = lax.rsqrt(jnp.mean(center * center, axis=-1, keepdims=True) + 1e-05)
    return (center * spread, spread)


def norm_back(grad_normed, normed, spread):
    return spread * (
        grad_normed
        - jnp.mean(grad_normed, axis=-1, keepdims=True)
        - normed * jnp.mean(grad_normed * normed, axis=-1, keepdims=True)
    )


def masked_scores(queries, key_heads, same_seg):
    raw = (
        jnp.einsum("rqhc,rkhc->rhqk", queries, key_heads, preferred_element_type=jnp.float32)
        * 0.125
    )
    return jnp.where(same_seg, raw, -1e30)


def sum_grads(grads):
    return (
        lax.psum_scatter(grads[0], ("tower", "dp"), scatter_dimension=0, tiled=True),
        lax.psum_scatter(grads[1], ("tower", "dp"), scatter_dimension=0, tiled=True),
        lax.psum_scatter(grads[2], ("tower", "dp"), scatter_dimension=0, tiled=True),
        lax.psum_scatter(grads[3], ("tower", "dp"), scatter_dimension=0, tiled=True),
        lax.psum_scatter(grads[4], ("tower", "dp"), scatter_dimension=0, tiled=True),
        lax.psum_scatter(grads[5], ("tower", "dp"), scatter_dimension=0, tiled=True),
        lax.psum_scatter(grads[6], ("tower", "dp"), scatter_dimension=0, tiled=True),
        lax.psum_scatter(grads[7], ("tower", "dp"), scatter_dimension=0, tiled=True),
        lax.psum_scatter(grads[8], ("tower", "dp"), scatter_dimension=0, tiled=True),
        lax.psum_scatter(grads[9], ("tower", "dp"), scatter_dimension=0, tiled=True),
        lax.psum_scatter(grads[10], ("tower", "dp"), scatter_dimension=0, tiled=True),
        lax.psum_scatter(grads[11], ("tower", "dp"), scatter_dimension=0, tiled=True),
        lax.psum_scatter(grads[12], ("tower", "dp"), scatter_dimension=0, tiled=True),
    )


def local(
    tokens,
    segments,
    caption_image,
    logit_scale,
    first_gain,
    first_bias,
    triple_weight,
    query_bias,
    value_bias,
    output_weight,
    output_bias,
    second_gain,
    second_bias,
    expand_weight,
    expand_bias,
    shrink_weight,
    shrink_bias,
):
    rows_here = tokens.shape[1]
    length = tokens.shape[2]
    features = tokens.shape[3]
    head_size = features // HEADS
    token_count = rows_here * length
    is_text = lax.axis_index("tower") == 1
    text_flag = is_text.astype(jnp.float32)
    position = jnp.arange(length, dtype=jnp.int32)
    image_segs = jnp.broadcast_to(
        (position >= IMG_TOK).astype(jnp.int32)[None, :], (rows_here, length)
    )
    seg_ids = jnp.where(is_text, segments, image_segs)
    same_seg = (seg_ids[:, :, None] == seg_ids[:, None, :])[:, None, :, :]
    head_shape = (rows_here, length, HEADS, head_size)
    gain_one = first_gain[0].astype(jnp.float32)
    shift_one = first_bias[0].astype(jnp.float32)
    triple_w = triple_weight[0]
    query_shift = query_bias[0].astype(jnp.float32)
    value_shift = value_bias[0].astype(jnp.float32)
    output_w = output_weight[0]
    output_shift = output_bias[0].astype(jnp.float32)
    gain_two = second_gain[0].astype(jnp.float32)
    shift_two = second_bias[0].astype(jnp.float32)
    expand_w = expand_weight[0]
    expand_shift = expand_bias[0].astype(jnp.float32)
    shrink_w = shrink_weight[0]
    shrink_shift = shrink_bias[0].astype(jnp.float32)
    inputs = tokens[0].reshape(token_count, features).astype(jnp.float32)
    normed_a, spread_a = layer_stats(inputs)
    normed_one = (normed_a * gain_one + shift_one).astype(jnp.bfloat16)
    triple = jnp.dot(normed_one, triple_w, preferred_element_type=jnp.float32)
    queries = (triple[:, :features] + query_shift).astype(jnp.bfloat16).reshape(head_shape)
    key_heads = triple[:, features : 2 * features].astype(jnp.bfloat16).reshape(head_shape)
    value_heads = (triple[:, 2 * features :] + value_shift).astype(jnp.bfloat16).reshape(head_shape)
    scores = masked_scores(queries, key_heads, same_seg)
    row_peak = jnp.max(scores, axis=-1, keepdims=True)
    log_total = row_peak + jnp.log(jnp.sum(jnp.exp(scores - row_peak), axis=-1, keepdims=True))
    attn_probs = jnp.exp(scores - log_total)
    mixed_low = (
        jnp.einsum(
            "rhqk,rkhc->rqhc",
            attn_probs.astype(jnp.bfloat16),
            value_heads,
            preferred_element_type=jnp.float32,
        )
        .reshape(token_count, features)
        .astype(jnp.bfloat16)
    )
    hidden = (
        inputs + jnp.dot(mixed_low, output_w, preferred_element_type=jnp.float32) + output_shift
    )
    normed_b, spread_b = layer_stats(hidden)
    normed_two = (normed_b * gain_two + shift_two).astype(jnp.bfloat16)
    expanded = jnp.dot(normed_two, expand_w, preferred_element_type=jnp.float32) + expand_shift
    activated, gelu_back = jax.vjp(jax.nn.gelu, expanded)
    active_low = activated.astype(jnp.bfloat16)
    block_out = (
        hidden + jnp.dot(active_low, shrink_w, preferred_element_type=jnp.float32) + shrink_shift
    )
    slot_ids = jnp.arange(CAPS, dtype=jnp.int32)
    member = (seg_ids[:, None, :] == slot_ids[None, :, None]).astype(jnp.float32)
    counts = jnp.maximum(jnp.sum(member, axis=2), 1.0)
    pooled = (
        jnp.einsum(
            "rst,rtd->rsd", member, block_out.reshape(rows_here, length, features), precision=HIGH
        )
        / counts[:, :, None]
    )
    inverse = lax.rsqrt(jnp.sum(pooled * pooled, axis=2, keepdims=True) + 1e-06)
    embedding = pooled * inverse
    first_slot = embedding[:, 0, :].astype(jnp.bfloat16)
    collected = lax.all_gather(first_slot, "dp", axis=0, tiled=True)
    image_table = shifted(collected, "tower", 1)
    text_low = embedding.reshape(rows_here * CAPS, features).astype(jnp.bfloat16)
    similar = jnp.einsum("cd,id->ci", text_low, image_table, preferred_element_type=jnp.float32)
    factor = logit_scale[0]
    logits = factor * similar
    logit_peak = jnp.max(logits, axis=1, keepdims=True)
    logit_total = logit_peak + jnp.log(jnp.sum(jnp.exp(logits - logit_peak), axis=1, keepdims=True))
    targets = caption_image.reshape(-1)
    image_ids = jnp.arange(image_table.shape[0], dtype=jnp.int32)
    target_hot = (image_ids[None, :] == targets[:, None]).astype(jnp.float32)
    picked = jnp.sum(logits * target_hot, axis=1)
    loss_here = jnp.sum(logit_total[:, 0] - picked) * text_flag
    grad_logits = (jnp.exp(logits - logit_total) - target_hot) * text_flag
    factor_here = jnp.sum(grad_logits * similar)
    loss_total, factor_total = lax.psum((loss_here, factor_here), ("tower", "dp"))
    caption_total = rows_here * CAPS * lax.axis_size("dp")
    grad_dots = (factor * grad_logits).astype(jnp.bfloat16)
    grad_emb = jnp.einsum(
        "ci,id->cd", grad_dots, image_table, preferred_element_type=jnp.float32
    ).reshape(rows_here, CAPS, features)
    grad_pooled = inverse * (
        grad_emb - embedding * jnp.sum(embedding * grad_emb, axis=2, keepdims=True)
    )
    grad_pooled = grad_pooled / counts[:, :, None]
    grad_out = jnp.einsum("rst,rsd->rtd", member, grad_pooled, precision=HIGH).reshape(
        token_count, features
    )
    shrink_bias_grad = jnp.sum(grad_out, axis=0)
    grad_out_low = grad_out.astype(jnp.bfloat16)
    shrink_weight_grad = jnp.einsum(
        "nf,nd->fd", active_low, grad_out_low, preferred_element_type=jnp.float32
    )
    grad_active = jnp.einsum(
        "nd,fd->nf", grad_out_low, shrink_w, preferred_element_type=jnp.float32
    )
    grad_expanded = gelu_back(grad_active)[0]
    expand_bias_grad = jnp.sum(grad_expanded, axis=0)
    grad_expanded_low = grad_expanded.astype(jnp.bfloat16)
    expand_weight_grad = jnp.einsum(
        "nd,nf->df", normed_two, grad_expanded_low, preferred_element_type=jnp.float32
    )
    grad_normed_two = jnp.einsum(
        "nf,df->nd", grad_expanded_low, expand_w, preferred_element_type=jnp.float32
    )
    second_gain_grad = jnp.sum(grad_normed_two * normed_b, axis=0)
    second_bias_grad = jnp.sum(grad_normed_two, axis=0)
    grad_hidden = grad_out + norm_back(grad_normed_two * gain_two, normed_b, spread_b)
    output_bias_grad = jnp.sum(grad_hidden, axis=0)
    grad_hidden_low = grad_hidden.astype(jnp.bfloat16)
    output_weight_grad = jnp.einsum(
        "nd,ne->de", mixed_low, grad_hidden_low, preferred_element_type=jnp.float32
    )
    grad_mixed = (
        jnp.einsum("ne,de->nd", grad_hidden_low, output_w, preferred_element_type=jnp.float32)
        .astype(jnp.bfloat16)
        .reshape(head_shape)
    )
    scores_again = masked_scores(queries, key_heads, same_seg)
    probs_again = jnp.exp(scores_again - log_total)
    probs_low = probs_again.astype(jnp.bfloat16)
    grad_values = jnp.einsum(
        "rhqk,rqhc->rkhc", probs_low, grad_mixed, preferred_element_type=jnp.float32
    )
    grad_probs = jnp.einsum(
        "rqhc,rkhc->rhqk", grad_mixed, value_heads, preferred_element_type=jnp.float32
    )
    grad_scores = (
        probs_again * (grad_probs - jnp.sum(probs_again * grad_probs, axis=-1, keepdims=True))
    ).astype(jnp.bfloat16)
    grad_queries = (
        jnp.einsum("rhqk,rkhc->rqhc", grad_scores, key_heads, preferred_element_type=jnp.float32)
        * 0.125
    )
    grad_keys = (
        jnp.einsum("rhqk,rqhc->rkhc", grad_scores, queries, preferred_element_type=jnp.float32)
        * 0.125
    )
    grad_queries = grad_queries.reshape(token_count, features)
    grad_keys = grad_keys.reshape(token_count, features)
    grad_values = grad_values.reshape(token_count, features)
    query_bias_grad = jnp.sum(grad_queries, axis=0)
    value_bias_grad = jnp.sum(grad_values, axis=0)
    grad_triple = jnp.concatenate([grad_queries, grad_keys, grad_values], axis=1).astype(
        jnp.bfloat16
    )
    triple_weight_grad = jnp.einsum(
        "nd,ne->de", normed_one, grad_triple, preferred_element_type=jnp.float32
    )
    grad_normed_one = jnp.einsum(
        "ne,de->nd", grad_triple, triple_w, preferred_element_type=jnp.float32
    )
    first_gain_grad = jnp.sum(grad_normed_one * normed_a, axis=0)
    first_bias_grad = jnp.sum(grad_normed_one, axis=0)
    input_grad = grad_hidden + norm_back(grad_normed_one * gain_one, normed_a, spread_a)
    shares = sum_grads(
        (
            first_gain_grad,
            first_bias_grad,
            triple_weight_grad,
            query_bias_grad,
            value_bias_grad,
            output_weight_grad,
            output_bias_grad,
            second_gain_grad,
            second_bias_grad,
            expand_weight_grad,
            expand_bias_grad,
            shrink_weight_grad,
            shrink_bias_grad,
        )
    )
    loss_out = (loss_total / caption_total).reshape(1)
    factor_out = factor_total.reshape(1)
    return (
        loss_out,
        factor_out,
        input_grad.reshape(1, rows_here, length, features),
        shares[0],
        shares[1],
        shares[2],
        shares[3],
        shares[4],
        shares[5],
        shares[6],
        shares[7],
        shares[8],
        shares[9],
        shares[10],
        shares[11],
        shares[12],
    )


def solution(mesh):
    placed = (
        P("tower", "dp", None, None),
        P("dp", None),
        P("dp", None),
        P(),
        P("tower", None),
        P("tower", None),
        P("tower", None, None),
        P("tower", None),
        P("tower", None),
        P("tower", None, None),
        P("tower", None),
        P("tower", None),
        P("tower", None),
        P("tower", None, None),
        P("tower", None),
        P("tower", None, None),
        P("tower", None),
    )
    fits = mesh.shape["tower"] == 2 and mesh.shape["dp"] == 2 * PLANE
    return jax.shard_map(
        local_fast if fits else local,
        mesh=mesh,
        in_specs=placed,
        out_specs=(
            P(),
            P(),
            P("tower", "dp", None, None),
            P(("tower", "dp")),
            P(("tower", "dp")),
            P(("tower", "dp"), None),
            P(("tower", "dp")),
            P(("tower", "dp")),
            P(("tower", "dp"), None),
            P(("tower", "dp")),
            P(("tower", "dp")),
            P(("tower", "dp")),
            P(("tower", "dp"), None),
            P(("tower", "dp")),
            P(("tower", "dp"), None),
            P(("tower", "dp")),
        ),
        check_vma=False,
    )
```

```python
import functools

import jax
import jax.numpy as jnp
from jax import lax
from jax.experimental import pallas as pl
from jax.experimental.pallas import tpu as pltpu
from jax.sharding import PartitionSpec as P

HEADS = 12
IMG_TOK = 50
CAPS = 4

f32, bf16 = jnp.float32, jnp.bfloat16
GELU_C = 0.7978845608028654
GELU_A = 0.044715
STEP_ROWS = 4
MESH = pl.DeviceIdType.MESH


def mm(a, b):
    return jnp.dot(a, b, preferred_element_type=f32)


def mm_nt(a, b):
    return lax.dot_general(a, b, (((1,), (1,)), ((), ())), preferred_element_type=f32)


def mm_tn(a, b):
    return lax.dot_general(a, b, (((0,), (0,)), ((), ())), preferred_element_type=f32)


def stats(x):
    center = x - jnp.mean(x, axis=-1, keepdims=True)
    spread = lax.rsqrt(jnp.mean(center * center, axis=-1, keepdims=True) + 1e-05)
    return center * spread, spread


def split(x, first):
    zero = jnp.zeros_like(x)
    return jnp.concatenate([jnp.where(first, x, zero), jnp.where(first, zero, x)], axis=0)


def low_pair(x):
    high = x.astype(bf16)
    return high, (x - high.astype(f32)).astype(bf16)


def fwd_kernel(tok, seg, g1, b1, qb, vb, ob, g2, b2, eb, sb, w3h, woh, weh, wsh,
               qkv, probs, mixed, normed_out, sums_out, slope, n1_out, n2_out, spread_out, member_out, pooled_out, count_out, table_out,
               w3, wo, we, ws, pool_acc, count_acc, act_sum, imgs, elow, sems, gsem, esem):
    i = pl.program_id(0)
    steps = pl.num_programs(0)
    rows_here, length = seg.shape
    slots = rows_here * CAPS
    feat = tok.shape[1]
    block = tok.shape[0]
    is_text = lax.axis_index("tower") == 1
    copies = [pltpu.make_async_copy(src, dst, sems.at[n])
              for n, (src, dst) in enumerate(((w3h, w3), (woh, wo), (weh, we), (wsh, ws)))]

    tower, d = lax.axis_index("tower"), lax.axis_index("dp")
    chip, core = d // 2, lax.rem(d, 2)
    other = 1 - core
    partner = (tower, chip * 2 + other)
    chips = imgs.shape[1]
    facing = [(1 - tower, lax.rem(chip + k, chips) * 2 + core) for k in range(chips)]

    def remote(src, dst, sem, dev):
        return pltpu.make_async_remote_copy(src_ref=src, dst_ref=dst, send_sem=sem.at[0], recv_sem=sem.at[1],
                                            device_id=dev, device_id_type=MESH)

    barrier = pltpu.get_barrier_semaphore()

    @pl.when(i == 0)
    def _():
        for c in copies:
            c.start()
        for dev in facing + [partner]:
            pl.semaphore_signal(barrier, inc=1, device_id=dev, device_id_type=MESH)
        pool_acc[...] = jnp.zeros_like(pool_acc)
        count_acc[...] = jnp.zeros_like(count_acc)
        act_sum[...] = jnp.zeros_like(act_sum)

    def arrive(n):
        @pl.when(i == 0)
        def _():
            copies[n].wait()

    x = tok[...].astype(f32)
    norm, _ = stats(x)
    n1 = (norm * g1[...].astype(f32) + b1[...].astype(f32)).astype(bf16)
    n1_out[...] = n1
    arrive(0)
    qkv[:, :feat] = (mm(n1, w3[:, :feat]) + qb[...].astype(f32)).astype(bf16)
    qkv[:, feat:2 * feat] = mm(n1, w3[:, feat:2 * feat]).astype(bf16)
    qkv[:, 2 * feat:] = (mm(n1, w3[:, 2 * feat:]) + vb[...].astype(f32)).astype(bf16)

    image_seg = (lax.broadcasted_iota(jnp.int32, (1, length), 1) >= IMG_TOK).astype(jnp.int32)
    row_segs = []
    for r in range(STEP_ROWS):
        s = seg[pl.ds(STEP_ROWS * i + r, 1), :]
        row_segs.append(jnp.where(is_text, s, image_seg))
    lane = lax.broadcasted_iota(jnp.int32, (128, 128), 1)
    first_half = lane < 64
    slot_lanes = []
    for pair in range(STEP_ROWS // 2):
        base = STEP_ROWS * i + 2 * pair
        keyed = jnp.concatenate(
            [row_segs[2 * pair] * rows_here + base, row_segs[2 * pair + 1] * rows_here + (base + 1)], axis=1)
        slot_lanes.append(keyed)
        across = jnp.broadcast_to(keyed.astype(f32), (128, 128))
        bias = jnp.where(across == across.T, 0.0, -1e30)
        bias = jnp.concatenate([bias, bias], axis=1)
        here = slice(pair * 128, pair * 128 + 128)
        hps = range(HEADS // 2)
        scores = [mm_nt(qkv[here, feat + 128 * h:feat + 128 * h + 128],
                        split(qkv[here, 128 * h:128 * h + 128] * jnp.asarray(0.125, bf16), first_half)) + bias
                  for h in hps]
        lows = []
        for h in hps:
            e = jnp.exp(scores[h] - jnp.max(scores[h], axis=0, keepdims=True))
            p = (e * (1.0 / jnp.sum(e, axis=0, keepdims=True))).astype(bf16)
            probs[here, 256 * h:256 * h + 256] = p
            lows.append(p)
        for h in hps:
            o = mm_tn(lows[h], qkv[here, 2 * feat + 128 * h:2 * feat + 128 * h + 128])
            mixed[here, 128 * h:128 * h + 128] = jnp.where(first_half, o[:128], o[128:]).astype(bf16)

    arrive(1)
    hid = x + mm(mixed[...], wo[...]) + ob[...].astype(f32)
    norm2, spread2 = stats(hid)
    normed_out[...] = norm2
    spread_out[...] = spread2
    n2 = (norm2 * g2[...].astype(f32) + b2[...].astype(f32)).astype(bf16)
    n2_out[...] = n2
    slot_row = jnp.concatenate(slot_lanes, axis=1)
    hot = (lax.broadcasted_iota(jnp.int32, (slots, block), 0) == slot_row)
    member = hot.astype(f32).astype(bf16)
    placed = (lax.broadcasted_iota(jnp.int32, (2 * slots, block), 0) == slot_row + slots * core)
    placed = placed.astype(f32).astype(bf16)
    arrive(2)
    arrive(3)
    out = hid + sb[...].astype(f32)
    tile = 768
    starts = range(0, we.shape[1], tile)
    ahead = mm(n2, we[:, :tile])
    for f in starts:
        v = ahead + eb[:, f:f + tile].astype(f32)
        if f + tile < we.shape[1]:
            ahead = mm(n2, we[:, f + tile:f + 2 * tile])
        v2 = v * v
        cv = v * GELU_C
        t = jnp.tanh(cv * (1.0 + GELU_A * v2))
        h = 0.5 + 0.5 * t
        a = (v * h).astype(bf16)
        act_sum[:, f:f + tile] += mm(placed, a)
        slope[:, f:f + tile] = (h + h * (1.0 - h) * ((2.0 * cv) * (1.0 + (3.0 * GELU_A) * v2))).astype(bf16)
        out = out + mm(a, ws[f:f + tile, :])
    member_out[...] = member
    out_hi, out_lo = low_pair(out)
    pool_acc[...] += mm(member, out_hi) + mm(member, out_lo)
    count_acc[...] += jnp.broadcast_to(jnp.sum(hot.astype(f32), axis=1, keepdims=True), count_acc.shape)

    @pl.when(i == steps - 1)
    def _():
        counts = jnp.maximum(count_acc[...], 1.0)
        pooled = pool_acc[...] / counts[:, :1]
        count_out[...] = counts
        for f in range(0, we.shape[1], tile):
            sums_out[f:f + tile, :] = act_sum[:, f:f + tile].astype(bf16).T
        pooled_out[...] = pooled
        pl.semaphore_wait(barrier, chips + 1)

        @pl.when(tower == 0)
        def _():
            first = pooled[:rows_here]
            elow[...] = (first * lax.rsqrt(jnp.sum(first * first, axis=1, keepdims=True) + 1e-06)).astype(bf16)
            for dev in facing:
                remote(elow, imgs.at[core, chip], gsem, dev).start()
            remote(imgs.at[0], imgs.at[0], gsem, partner).wait_send()

        @pl.when(tower == 1)
        def _():
            remote(imgs.at[core], imgs.at[core], gsem, partner).wait_recv()
            remote(imgs.at[core], imgs.at[core], esem, partner).start()
            remote(imgs.at[other], imgs.at[other], esem, partner).wait()
            table_out[...] = imgs[...]


def forward(tokens, segments, g1, b1, w3, qb, vb, wo, ob, g2, b2, we, eb, ws, sb):
    count, feat = tokens.shape
    rows_here, length = segments.shape
    slots = rows_here * CAPS
    ff = we.shape[1]
    block = STEP_ROWS * length
    steps = count // block
    table = (2, lax.axis_size("dp") // 2, rows_here, feat)
    whole = lambda a: pl.BlockSpec(a.shape, lambda i: (0,) * a.ndim)
    rows = lambda width: pl.BlockSpec((block, width), lambda i: (i, 0))
    anyw = pl.BlockSpec(memory_space=pl.ANY)
    smalls = (g1, b1, qb, vb, ob, g2, b2, eb, sb)
    return pl.pallas_call(
        fwd_kernel,
        grid=(steps,),
        in_specs=[rows(feat), whole(segments)] + [whole(a) for a in smalls] + [anyw] * 4,
        out_specs=[rows(3 * feat),
                   rows(2 * feat),
                   rows(feat), rows(feat), pl.BlockSpec((ff, 2 * slots), lambda i: (0, 0)), rows(ff), rows(feat), rows(feat), rows(1),
                   pl.BlockSpec((slots, block), lambda i: (0, i)),
                   pl.BlockSpec((slots, feat), lambda i: (0, 0)),
                   pl.BlockSpec((slots, 128), lambda i: (0, 0)),
                   pl.BlockSpec(table, lambda i: (0,) * 4)],
        out_shape=[jax.ShapeDtypeStruct((count, 3 * feat), bf16),
                   jax.ShapeDtypeStruct((count, 2 * feat), bf16),
                   jax.ShapeDtypeStruct((count, feat), bf16),
                   jax.ShapeDtypeStruct((count, feat), f32),
                   jax.ShapeDtypeStruct((ff, 2 * slots), bf16),
                   jax.ShapeDtypeStruct((count, ff), bf16),
                   jax.ShapeDtypeStruct((count, feat), bf16),
                   jax.ShapeDtypeStruct((count, feat), bf16),
                   jax.ShapeDtypeStruct((count, 1), f32),
                   jax.ShapeDtypeStruct((slots, count), bf16),
                   jax.ShapeDtypeStruct((slots, feat), f32),
                   jax.ShapeDtypeStruct((slots, 128), f32),
                   jax.ShapeDtypeStruct(table, bf16)],
        scratch_shapes=[pltpu.VMEM(w3.shape, bf16), pltpu.VMEM(wo.shape, bf16), pltpu.VMEM(we.shape, bf16),
                        pltpu.VMEM(ws.shape, bf16), pltpu.VMEM((slots, feat), f32), pltpu.VMEM((slots, 128), f32), pltpu.VMEM((2 * slots, ff), f32),
                        pltpu.VMEM(table, bf16), pltpu.VMEM((rows_here, feat), bf16),
                        pltpu.SemaphoreType.DMA((4,)), pltpu.SemaphoreType.DMA((2,)), pltpu.SemaphoreType.DMA((2,))],
        compiler_params=pltpu.CompilerParams(vmem_limit_bytes=56 << 20, dimension_semantics=("arbitrary",),
                                             collective_id=1, has_side_effects=True),
        name="fwd",
    )(tokens, segments, *smalls, w3, wo, we, ws)


PLANE = 8
LINE = 4
BLK = 256
CH = 768
HALF = CH // 2
ROWS = HALF // PLANE
N_CH = 8
WIDE = (0, 1, 3, 6)
LONG = (2, 4, 5, 7)
WIDE_AT = {q: n for n, q in enumerate(WIDE)}
LONG_AT = {q: n for n, q in enumerate(LONG)}


def fold(x):
    return jnp.sum(x.reshape(x.shape[0] // 8, 8, x.shape[1]), axis=0)


def bwd_kernel(member, pooled, count, imgs, act_sums, caption, scale, g1, b1, g2, b2,
               qkv_h, probs_h, mixed_h, normed_h, slope_h, n1_h, n2_h, spread_h, tok_h, w3_h, wo_h, we_h, ws_h,
               tw_out, ow_out, ew_out, sw_out, in_out, vec_out,
               cs, snd, prv, own, ylong, ywide, zrcv, fin, apair, asum, aall, gpall, swfin, xsw,
               gol, gn2, hid, spread2, n2b, tok, mixed, probs, slope, ws, we, ge, qkv, w3, wo,
               ebsum, attn_sum, vec, vown, vpair, vrcv,
               ld, psend, precv, xsend, xrecv, ysend, yrecv, zsend, zrecv,
               fsem, asem, gsem, swsem, vpsem, vsem, outsem):
    t = lax.axis_index("tower")
    d = lax.axis_index("dp")
    p = d // 2
    c = lax.rem(d, 2)
    z = p // 2
    y = lax.rem(p, 2)
    is_text = t == 1
    count_t = gol.shape[0]
    blocks = count_t // BLK
    feat = CH
    rows_here = caption.shape[1]
    other = 1 - c

    def peer(k):
        return lax.rem(p + k, PLANE)

    def at_core(tt, pp):
        return (tt, pp * 2 + c)

    partner = (t, p * 2 + other)
    beside = at_core(t, 2 * z + (1 - y))
    across = at_core(1 - t, p)

    def remote(src, dst, ssem, rsem, dev):
        return pltpu.make_async_remote_copy(src_ref=src, dst_ref=dst, send_sem=ssem, recv_sem=rsem,
                                            device_id=dev, device_id_type=MESH)

    barrier = pltpu.get_barrier_semaphore()
    pl.semaphore_signal(barrier, inc=1, device_id=partner, device_id_type=MESH)
    pl.semaphore_signal(barrier, inc=1, device_id=across, device_id_type=MESH)
    for k in range(1, PLANE):
        pl.semaphore_signal(barrier, inc=1, device_id=at_core(t, peer(k)), device_id_type=MESH)
        pl.semaphore_signal(barrier, inc=1, device_id=at_core(1 - t, peer(k)), device_id_type=MESH)

    pooled_v = pooled[...]
    inverse = lax.rsqrt(jnp.sum(pooled_v * pooled_v, axis=1, keepdims=True) + 1e-06)
    emb = pooled_v * inverse
    emb_low = emb.astype(bf16)

    def pair_copy(q):
        slot = lax.rem(q, 2)
        return remote(snd.at[slot], prv.at[q], psend.at[slot], precv.at[q], partner)

    def x_all(q):
        return remote(cs.at[q, 0:LINE], cs.at[q, 0:LINE], xsend.at[q], xrecv.at[q], across)

    def x_line(q):
        return remote(cs.at[q, 0:LINE, y], cs.at[q, 0:LINE, y], xsend.at[q], xrecv.at[q], across)

    def x_copy(q):
        return x_all(q) if q in WIDE else x_line(q)

    def y_copy(q):
        if q in LONG:
            src, dst = cs.at[q, :, 1 - y], ylong.at[LONG_AT[q]]
        else:
            src, dst = cs.at[q, pl.ds(LINE * t, LINE), 1 - y], ywide.at[WIDE_AT[q]]
        return remote(src, dst, ysend.at[q], yrecv.at[q], beside)

    def z_start(q):
        for k in range(1, LINE):
            to = lax.rem(z + k, LINE)
            remote(cs.at[q, LINE * t + to, y], zrcv.at[q, k - 1], zsend.at[q], zrecv.at[q],
                   at_core(t, 2 * to + y)).start()

    def z_all(q):
        return remote(zrcv.at[q], zrcv.at[q], zsend.at[q], zrecv.at[q], partner)

    def mid(q):
        y_copy(q).wait_recv()
        if q in LONG:
            for a in range(PLANE):
                cs[q, a, y] = (cs[q, a, y].astype(f32) + ylong[LONG_AT[q], a].astype(f32)).astype(bf16)
            x_line(q).start()
        else:
            for a in range(LINE):
                at = LINE * t + a
                cs[q, at, y] = (cs[q, at, y].astype(f32) + ywide[WIDE_AT[q], a].astype(f32)).astype(bf16)
        z_start(q)

    def a_pair():
        return remote(act_sums.at[:, :, other], apair, asem.at[0], asem.at[1], partner)

    def a_start():
        for k in range(1, PLANE):
            remote(asum.at[:, peer(k)], aall.at[:, :, pl.ds(pl.multiple_of(128 * p, 128), 128)],
                   asem.at[2], asem.at[3], at_core(t, peer(k))).start()

    def a_all():
        every = asum.at[:, 0:PLANE - 1]
        return remote(every, every, asem.at[2], asem.at[3], partner)

    def gp_beside():
        return remote(gpall.at[p, c], gpall.at[p, c], gsem.at[0], gsem.at[1], beside)

    def gp_line():
        gp_beside().wait_recv()
        for k in range(1, LINE):
            mine = gpall.at[pl.ds(2 * z, 2), c]
            remote(mine, mine, gsem.at[2], gsem.at[3], at_core(t, 2 * lax.rem(z + k, LINE) + y)).start()

    def gp_line_all():
        every = gpall.at[0:2 * (LINE - 1), 0]
        return remote(every, every, gsem.at[2], gsem.at[3], partner)

    def gp_share_copy():
        return remote(gpall.at[:, c], gpall.at[:, c], gsem.at[4], gsem.at[5], partner)

    def gp_share():
        gp_line_all().wait_recv()
        gp_share_copy().start()

    def sw_across():
        return remote(xsw, xsw, swsem.at[0], swsem.at[1], across)

    def sw_keep():
        return pltpu.make_async_copy(swfin, sw_out, swsem.at[2])

    def shrink():
        gp_share_copy().wait_recv()
        a_all().wait_recv()
        rows = gpall[...].reshape(-1, feat)
        xsw[...] = mm(aall[0], rows).astype(bf16)
        sw_across().start()
        swfin[...] = mm(aall[1], rows)
        sw_keep().start()

    half_rows = ROWS // 2

    def place(q):
        if q < 4:
            return ew_out, 4 * HALF * c + HALF * q
        if q == 4:
            return ow_out, HALF * c
        return tw_out, CH * (q - 5) + HALF * c

    def keep(q):
        out, col = place(q)
        return pltpu.make_async_copy(fin.at[q, pl.ds(pl.multiple_of(half_rows * c, 8), half_rows)],
                                     out.at[:, pl.ds(pl.multiple_of(col, 128), HALF)], fsem.at[0])

    def give(q):
        out, col = place(q)
        return remote(fin.at[q, pl.ds(pl.multiple_of(half_rows * other, 8), half_rows)],
                      out.at[:, pl.ds(pl.multiple_of(col, 128), HALF)], fsem.at[1], fsem.at[2], partner)

    def finish(q):
        z_all(q).wait_recv()
        total = cs[q, LINE * t + z, y].astype(f32)
        for k in range(LINE - 1):
            total = total + zrcv[q, k].astype(f32)
        fin[q] = total
        keep(q).start()
        give(q).start()

    def leave(q):
        chip_sum(q)
        if q in WIDE:
            x_all(q).start()
        y_copy(q).start()

    def chip_sum(q):
        pair_copy(q).wait_recv()
        slot = lax.rem(q, 2)
        n = 2 * ROWS
        for a in range(PLANE):
            total = own[slot, n * a:n * (a + 1), :] + prv[q, n * a:n * (a + 1), :].astype(f32)
            cs[q, a] = total.reshape(2, ROWS, HALF).astype(bf16)

    def chunk(q, left, right):
        slot = lax.rem(q, 2)

        @pl.when(q >= 2)
        def _():
            pair_copy(q - 2).wait_send()
        for r in range(0, CH, 256):
            part = mm_tn(left[:, r:r + 256], right)
            low, high = part[:, :HALF], part[:, HALF:]
            own[slot, r:r + 256, :] = jnp.where(c == 0, low, high)
            snd[slot, r:r + 256, :] = jnp.where(c == 0, high, low).astype(bf16)
        pair_copy(q).start()

    def v_pair():
        return remote(vown.at[other], vpair, vpsem.at[0], vpsem.at[1], partner)

    def load(n, src, dst):
        return pltpu.make_async_copy(src, dst, ld.at[n])

    def tile_loads(i):
        s = lax.rem(i, 2)
        out = []
        ff = slope_h.shape[1]
        for h in range(2):
            col = pl.multiple_of((ff // 2) * h + HALF * i, 128)
            here = pl.ds(HALF * h, HALF)
            out.append(load(6 * s + 3 * h, slope_h.at[:, pl.ds(col, HALF)], slope.at[s, :, here]))
            out.append(load(6 * s + 3 * h + 1, ws_h.at[pl.ds(col, HALF)], ws.at[s, here]))
            out.append(load(6 * s + 3 * h + 2, we_h.at[:, pl.ds(col, HALF)], we.at[s, :, here]))
        return out

    hid_load = load(16, normed_h, hid)
    tok_load = load(17, tok_h, tok)
    qkv_load = load(18, qkv_h, qkv)
    w3_load = load(19, w3_h, w3)
    wo_load = load(20, wo_h, wo)
    n2_load = load(24, n2_h, n2b)
    spread_load = load(25, spread_h, spread2)
    n1_load = load(26, n1_h, slope.at[1])
    mixed_load = load(21, mixed_h, mixed)
    probs_load = load(22, probs_h, probs)

    @pl.when(t == 0)
    def _():
        pl.semaphore_wait(barrier, 2 * PLANE)
        gn2[:BLK, :] = jnp.zeros((BLK, feat), f32)
        for m in range(blocks):
            pltpu.make_async_copy(gn2.at[0:BLK], in_out.at[pl.ds(BLK * m, BLK)], outsem.at[m]).start()

        def over(q):
            x_copy(q).wait_recv()
            if q in WIDE:
                y_copy(q).start()
            else:
                z_start(q)
        over(0)
        mid(0)
        over(1)
        finish(0)
        mid(1)
        over(3)
        finish(1)
        over(2)
        mid(3)
        sw_across().wait_recv()
        swfin[...] = xsw[...].astype(f32)
        sw_keep().start()
        finish(2)
        over(4)
        finish(3)
        finish(4)
        over(6)
        over(5)
        mid(6)
        finish(5)
        over(7)
        finish(6)
        finish(7)
        for m in range(blocks):
            pltpu.make_async_copy(gn2.at[0:BLK], in_out.at[pl.ds(BLK * m, BLK)], outsem.at[m]).wait()

    @pl.when(is_text)
    def _():
        for cp in tile_loads(0):
            cp.start()
        n2_load.start()
        for cp in tile_loads(1):
            cp.start()
        for cp in (hid_load, spread_load, mixed_load, wo_load, qkv_load, probs_load, w3_load, tok_load):
            cp.start()
        gain2, gain1 = g2[...].astype(f32), g1[...].astype(f32)
        gn2[...] = jnp.zeros_like(gn2)
        attn_sum[...] = jnp.zeros_like(attn_sum)
        vec[...] = jnp.zeros_like(vec)
        pl.semaphore_wait(barrier, 2 * PLANE)
        a_pair().start()

        table = imgs[...].reshape(2 * PLANE * rows_here, feat)
        dots = mm_nt(emb_low, table)
        factor = scale[0]
        logits = factor * dots
        peak = jnp.max(logits, axis=1, keepdims=True)
        weight = jnp.exp(logits - peak)
        total = jnp.sum(weight, axis=1, keepdims=True)
        eye = (lax.broadcasted_iota(jnp.int32, (rows_here, rows_here), 0)
               == lax.broadcasted_iota(jnp.int32, (rows_here, rows_here), 1))
        wanted = jnp.concatenate([jnp.sum(jnp.where(eye, caption[s:s + 1, :], 0), axis=1, keepdims=True)
                                  for s in range(CAPS)], axis=0)
        span = 2 * rows_here
        inside = lax.rem(wanted, span)
        wanted = (inside // rows_here) * (PLANE * rows_here) + (wanted // span) * rows_here + lax.rem(inside, rows_here)
        hot = (lax.broadcasted_iota(jnp.int32, dots.shape, 1) == wanted).astype(f32)
        picked = jnp.sum(logits * hot, axis=1, keepdims=True)
        loss_here = jnp.sum(peak + jnp.log(total) - picked, axis=0, keepdims=True)
        a_pair().wait_recv()
        asum[...] = act_sums[:, :, c] + apair[...]
        aall[:, :, pl.ds(pl.multiple_of(128 * p, 128), 128)] = asum[:, p]
        a_start()
        grad_logits = weight / total - hot
        factor_here = jnp.sum(jnp.sum(grad_logits * dots, axis=1, keepdims=True), axis=0, keepdims=True)
        grad_emb = mm((factor * grad_logits).astype(bf16), table)
        counts = count[:, :1]
        grad_pool = inverse * (grad_emb - emb * jnp.sum(emb * grad_emb, axis=1, keepdims=True))
        vec[7:8, :] = jnp.sum(grad_pool, axis=0, keepdims=True)
        column = lax.broadcasted_iota(jnp.int32, (1, feat), 1)
        vec[12:13, :] = jnp.where(column == 0, loss_here, jnp.where(column == 1, factor_here, 0.0))
        gp_hi, gp_lo = low_pair(grad_pool / counts)
        gpall[p, c] = gp_hi
        gp_beside().start()
        for m in range(blocks):
            gol[BLK * m:BLK * (m + 1), :] = mm_tn(member[:, BLK * m:BLK * (m + 1)], gp_hi).astype(bf16)

        @pl.loop(0, 4)
        def _(i):
            s = lax.rem(i, 2)
            for cp in tile_loads(i):
                cp.wait()

            def at(n, what, *of):
                @pl.when(i == n)
                def _():
                    what(*of)
            sums = jnp.zeros((8, feat), f32)
            for m in range(blocks):
                here = slice(BLK * m, BLK * (m + 1))
                grad = mm_nt(gol[here, :], ws[s]) * slope[s, here, :].astype(f32)
                sums = sums + fold(grad)
                ge[here, :] = grad.astype(bf16)
            sums = jnp.sum(sums, axis=0, keepdims=True)
            for h in range(2):
                ebsum[:, pl.ds(pl.multiple_of(4 * HALF * h + HALF * i, 128), HALF)] = sums[:, HALF * h:HALF * (h + 1)]
            at(1, gp_line)
            at(1, leave, 0)
            at(2, leave, 1)
            at(3, leave, 2)

            @pl.when(i == 0)
            def _():
                n2_load.wait()
            chunk(i, n2b, ge[...])
            at(2, mid, 0)
            at(3, mid, 1)
            for m in range(blocks):
                here = slice(BLK * m, BLK * (m + 1))
                gn2[here, :] += mm_nt(ge[here, :], we[s])

            @pl.when(i < 2)
            def _():
                for cp in tile_loads(i + 2):
                    cp.start()
        n1_load.start()
        hid_load.wait()
        spread_load.wait()

        zeros8 = jnp.zeros((8, feat), f32)

        def norm2_back(m, sums):
            here = pl.ds(pl.multiple_of(m * BLK, BLK), BLK)
            norm, g_in = hid[here, :], gn2[here, :]
            hot_m = member[:, here]
            grad_out = mm_tn(hot_m, gp_hi) + mm_tn(hot_m, gp_lo)
            g = g_in * gain2
            back = spread2[here, :] * (g - jnp.mean(g, axis=1, keepdims=True)
                                       - norm * jnp.mean(g * norm, axis=1, keepdims=True))
            gh = grad_out + back
            gn2[here, :] = gh
            gol[here, :] = gh.astype(bf16)
            return (sums[0] + fold(g_in * norm), sums[1] + fold(g_in), sums[2] + fold(gh))
        sums = lax.fori_loop(0, blocks, norm2_back, (zeros8, zeros8, zeros8))
        for row, x in ((5, sums[0]), (6, sums[1]), (4, sums[2])):
            vec[row:row + 1, :] = jnp.sum(x, axis=0, keepdims=True)
        for n in range(4):
            vec[8 + n:9 + n, :] = ebsum[:, feat * n:feat * (n + 1)]
        leave(3)

        mixed_load.wait()
        chunk(4, mixed, gol[...])
        wo_load.wait()
        for m in range(blocks):
            here = slice(BLK * m, BLK * (m + 1))
            ge[here, :] = mm_nt(gol[here, :], wo[...]).astype(bf16)

        qkv_load.wait()
        probs_load.wait()
        first_half = lax.broadcasted_iota(jnp.int32, (128, 128), 1) < 64
        hps = range(HEADS // 2)

        @pl.loop(0, count_t // 128)
        def _(rp):
            here = pl.ds(pl.multiple_of(rp * 128, 128), 128)

            def probs_of(h):
                return probs[here, 256 * h:256 * h + 256]

            def part(n, h):
                return qkv[here, feat * n + 128 * h:feat * n + 128 * h + 128]
            gm = [split(ge[here, 128 * h:128 * h + 128], first_half) for h in hps]
            gp = [mm_nt(part(2, h), gm[h]) for h in hps]
            gv = [mm(probs_of(h), gm[h]) for h in hps]
            gs = []
            for h in hps:
                probs_f = probs_of(h).astype(f32)
                weighted = probs_f * gp[h]
                gs.append((weighted - probs_f * jnp.sum(weighted, axis=0, keepdims=True)).astype(bf16))
            gk = [mm(gs[h], split(part(0, h), first_half)) * 0.125 for h in hps]
            gq = []
            for h in hps:
                both = mm_tn(gs[h], part(1, h))
                gq.append(jnp.where(first_half, both[:128], both[128:]) * 0.125)
            for h in hps:
                for n, x in ((0, gq[h]), (1, gk[h]), (2, gv[h])):
                    qkv[here, feat * n + 128 * h:feat * n + 128 * h + 128] = x.astype(bf16)
                for n, x in ((0, gq[h]), (1, gv[h])):
                    attn_sum[:, feat * n + 128 * h:feat * n + 128 * h + 128] += fold(x)

            @pl.when(rp == 1)
            def _():
                leave(4)
                mid(2)

            @pl.when(rp == 4)
            def _():
                gp_share()

            @pl.when(rp == 5)
            def _():
                mid(3)
        vec[2:3, :] = jnp.sum(attn_sum[:, :feat], axis=0, keepdims=True)
        vec[3:4, :] = jnp.sum(attn_sum[:, feat:], axis=0, keepdims=True)

        n1_load.wait()

        @pl.loop(0, 3)
        def _(j):
            chunk(5 + j, slope.at[1], qkv[:, pl.ds(pl.multiple_of(CH * j, 128), CH)])

            @pl.when(j == 0)
            def _():
                shrink()
                finish(0)

            @pl.when(j == 1)
            def _():
                leave(5)
        finish(1)
        mid(4)
        tok_load.wait()
        w3_load.wait()

        def norm1_back(m, sums):
            here = pl.ds(pl.multiple_of(m * BLK, BLK), BLK)
            g_in = mm_nt(qkv[here, :], w3[...])

            @pl.when(m == 0)
            def _():
                leave(6)
                finish(2)

            @pl.when(m == 1)
            def _():
                leave(7)

            @pl.when(m == 2)
            def _():
                finish(3)

            @pl.when(m == 3)
            def _():
                mid(5)
            norm, spread = stats(tok[here, :].astype(f32))
            g = g_in * gain1
            back = spread * (g - jnp.mean(g, axis=1, keepdims=True)
                             - norm * jnp.mean(g * norm, axis=1, keepdims=True))
            gn2[here, :] += back
            pltpu.make_async_copy(gn2.at[here], in_out.at[here], outsem.at[m]).start()
            return (sums[0] + fold(g_in * norm), sums[1] + fold(g_in))
        sums = lax.fori_loop(0, blocks, norm1_back, (zeros8, zeros8))
        for row, x in ((0, sums[0]), (1, sums[1])):
            vec[row:row + 1, :] = jnp.sum(x, axis=0, keepdims=True)

        width, wide = feat // (4 * PLANE), 4 * feat // (4 * PLANE)
        narrow = vec[0:8, :]
        broad = vec[8:16, :]
        scalars = vec[12:13, :128]
        turned = [broad] + [pltpu.roll(broad, feat - wide * j, axis=1) for j in range(1, feat // wide)]
        for g in range(4 * PLANE):
            one = narrow if g == 0 else pltpu.roll(narrow, feat - width * g, axis=1)
            row = g // (feat // wide)
            tail = turned[g % (feat // wide)][row:row + 1, :128]
            vown[g % 2, g // 2, 0:8, :] = one[:, :128]
            vown[g % 2, g // 2, 8:9, :] = tail
            vown[g % 2, g // 2, 9:10, :] = scalars
        v_pair().start()
        finish(4)
        mid(6)
        for m in range(blocks):
            here = pl.ds(BLK * m, BLK)
            pltpu.make_async_copy(gn2.at[here], in_out.at[here], outsem.at[m]).wait()
        v_pair().wait_recv()
        vown[c] += vpair[...]
        for k in range(PLANE):
            for tt in range(2):
                if tt == 0 or k:
                    remote(vown.at[c, PLANE * tt + peer(k)], vrcv.at[k], vsem.at[0], vsem.at[1],
                           at_core(tt, peer(k))).start()
        finish(5)
        mid(7)
        finish(6)
        finish(7)

    @pl.when(is_text)
    def _():
        remote(vrcv.at[1:PLANE], vrcv.at[1:PLANE], vsem.at[0], vsem.at[1], partner).wait_recv()
        total = vown[c, PLANE + p]
        for k in range(1, PLANE):
            total = total + vrcv[k]
        vec_out[...] = total

    @pl.when(t == 0)
    def _():
        remote(vrcv, vrcv, vsem.at[0], vsem.at[1], partner).wait_recv()
        total = vrcv[0]
        for k in range(1, PLANE):
            total = total + vrcv[k]
        vec_out[...] = total

    @pl.when(is_text)
    def _():
        everything = vown.at[0, 0:2 * PLANE - 1]
        remote(everything, everything, vsem.at[0], vsem.at[1], partner).wait_send()
        v_pair().wait_send()
        for q in (N_CH - 2, N_CH - 1):
            pair_copy(q).wait_send()

        for q in range(N_CH):
            x_copy(q).wait_send()
        for q in LONG:
            y_copy(q).wait_send()
        a_pair().wait_send()
        a_all().wait_send()
        gp_beside().wait_send()
        gp_line_all().wait_send()
        gp_share_copy().wait_send()
        sw_across().wait_send()
    for q in WIDE:
        y_copy(q).wait_send()
    for q in range(N_CH):
        z_all(q).wait_send()
    sw_keep().wait()
    lower = fin.at[:, 0:half_rows]
    pltpu.make_async_copy(lower, lower, fsem.at[0]).wait()
    remote(lower, lower, fsem.at[1], fsem.at[2], partner).wait()


def backward(member, pooled, count, imgs, sums, caption, scale, g1, b1, g2, b2,
             qkv, probs, mixed, normed, slope, n1, n2, spread, tokens, w3, wo, we, ws):
    n_tok, feat = tokens.shape
    ff = we.shape[1]
    dma = pltpu.SemaphoreType.DMA
    vm = pltpu.VMEM
    vspec = pl.BlockSpec(memory_space=pltpu.VMEM)
    sspec = pl.BlockSpec(memory_space=pltpu.SMEM)
    anyw = pl.BlockSpec(memory_space=pl.ANY)
    shape = jax.ShapeDtypeStruct
    long, wide = len(LONG), len(WIDE)
    apart = sums.shape[:2] + sums.shape[3:]
    slots = member.shape[0]
    scratch = [
        vm((N_CH, PLANE, 2, ROWS, HALF), bf16), vm((2, CH, HALF), bf16), vm((N_CH, CH, HALF), bf16),
        vm((2, CH, HALF), f32),
        vm((long, PLANE, ROWS, HALF), bf16), vm((wide, LINE, ROWS, HALF), bf16), vm((N_CH, LINE - 1, ROWS, HALF), bf16),
        vm((N_CH, ROWS, HALF), f32), vm(apart, bf16), vm(apart, bf16), vm((2, apart[2], PLANE * 128), bf16),
        vm((PLANE, 2, slots, feat), bf16), vm((2 * ROWS, feat), f32), vm((2 * ROWS, feat), bf16),
        vm((n_tok, feat), bf16), vm((n_tok, feat), f32), vm((n_tok, feat), f32), vm((n_tok, 1), f32),
        vm((n_tok, feat), bf16), vm((n_tok, feat), bf16),
        vm((n_tok, feat), bf16), vm((n_tok, 2 * feat), bf16), vm((2, n_tok, CH), bf16), vm((2, CH, feat), bf16), vm((2, feat, CH), bf16),
        vm((n_tok, feat), bf16), vm((n_tok, 3 * feat), bf16), vm(w3.shape, bf16), vm(wo.shape, bf16),
        vm((1, ff), f32), vm((8, 2 * feat), f32),
        vm((16, feat), f32), vm((2, 2 * PLANE, 16, 128), f32), vm((2 * PLANE, 16, 128), f32), vm((PLANE, 16, 128), f32),
        dma((27,)), dma((2,)), dma((N_CH,)), dma((N_CH,)), dma((N_CH,)), dma((N_CH,)), dma((N_CH,)),
        dma((N_CH,)), dma((N_CH,)), dma((3,)), dma((4,)), dma((6,)), dma((3,)), dma((2,)), dma((2,)),
        dma((n_tok // BLK,)),
    ]
    return pl.pallas_call(
        bwd_kernel,
        in_specs=[vspec] * 6 + [sspec] + [vspec] * 4 + [anyw] * 13,
        out_specs=[anyw] * 5 + [vspec],
        out_shape=[shape((ROWS // 2, 3 * feat), f32), shape((ROWS // 2, feat), f32), shape((ROWS // 2, ff), f32),
                   shape((2 * ROWS, feat), f32), shape((n_tok, feat), f32), shape((16, 128), f32)],
        scratch_shapes=scratch,
        compiler_params=pltpu.CompilerParams(vmem_limit_bytes=61 << 20, collective_id=0, has_side_effects=True),
        name="bwd",
    )(member, pooled, count, imgs, sums, caption, scale, g1, b1, g2, b2,
      qkv, probs, mixed, normed, slope, n1, n2, spread, tokens, w3, wo, we, ws)


def hand_out_kernel(scale_by, vec, *rest):
    bigs, loss, factor, smalls = rest[:5], rest[5], rest[6], rest[7:16]
    outs, held, sem_in, sem_out = rest[16:21], rest[21:26], rest[26], rest[27]
    parts = []
    for src, dst, buf in zip(bigs, outs, held):
        count = max(src.shape[0] // BLK, 1)
        rows = src.shape[0] // count
        for n in range(count):
            parts.append((src.at[rows * n:rows * (n + 1)], buf.at[rows * n:rows * (n + 1)],
                          dst.at[rows * n:rows * (n + 1)]))
    ins = [pltpu.make_async_copy(a, b, sem_in.at[n]) for n, (a, b, _) in enumerate(parts)]
    outs = [pltpu.make_async_copy(b, c, sem_out.at[n]) for n, (_, b, c) in enumerate(parts)]
    for move in ins:
        move.start()
    width, wide = smalls[0].shape[1], smalls[8].shape[1]
    for n in range(8):
        smalls[n][...] = vec[n:n + 1, :width]
    smalls[8][...] = vec[8:9, :wide]
    loss[...] = vec[9:10, 0:1] * scale_by
    factor[...] = vec[9:10, 1:2]
    for first, second in zip(ins, outs):
        first.wait()
        second.start()
    for move in outs:
        move.wait()


def hand_out(vec, tw, ow, ew, sw, inp, captions):
    devices = lax.axis_size("tower") * lax.axis_size("dp")
    bigs = (inp, sw, ew, tw, ow)
    feat = inp.shape[1]
    outs = ([(1, 1)] * 2 + [(1, feat // devices)] * 8 + [(1, ew.shape[1] // devices)]
            + [a.shape for a in bigs])
    moves = 4 + inp.shape[0] // BLK
    vspec = pl.BlockSpec(memory_space=pltpu.VMEM)
    anyw = pl.BlockSpec(memory_space=pl.ANY)
    return pl.pallas_call(
        functools.partial(hand_out_kernel, 1.0 / captions),
        in_specs=[vspec] + [anyw] * 5,
        out_specs=[vspec] * 11 + [anyw] * 5,
        out_shape=[jax.ShapeDtypeStruct(dims, f32) for dims in outs],
        scratch_shapes=[pltpu.VMEM(a.shape, f32) for a in bigs]
        + [pltpu.SemaphoreType.DMA((moves,)), pltpu.SemaphoreType.DMA((moves,))],
        name="hand_out",
    )(vec, *bigs)


def local_fast(tokens, segments, caption_image, logit_scale, first_gain, first_bias, triple_weight, query_bias,
               value_bias, output_weight, output_bias, second_gain, second_bias, expand_weight, expand_bias,
               shrink_weight, shrink_bias):
    rows_here, length, feat = tokens.shape[1:]
    flat = tokens[0].reshape(rows_here * length, feat)
    w3, wo, we, ws = triple_weight[0], output_weight[0], expand_weight[0], shrink_weight[0]
    qkv, probs, mixed, normed, sums, slope, n1, n2, spread, member, pooled, count, table = forward(
        flat, segments, first_gain, first_bias, w3, query_bias, value_bias, wo, output_bias,
        second_gain, second_bias, we, expand_bias, ws, shrink_bias)
    sums = sums.reshape(2, PLANE, 2, sums.shape[0] // (4 * PLANE), sums.shape[1])
    tw, ow, ew, sw, inp, vec = backward(member, pooled, count, table, sums, caption_image.T, logit_scale, first_gain, first_bias,
                                        second_gain, second_bias, qkv, probs, mixed, normed, slope, n1, n2, spread, flat,
                                        w3, wo, we, ws)
    captions = rows_here * CAPS * lax.axis_size("dp")
    outs = hand_out(vec, tw, ow, ew, sw, inp, captions)
    loss, factor = outs[0].reshape(1), outs[1].reshape(1)
    g1, b1, qb, vb, ob, g2, b2, sb, eb = (a.reshape(-1) for a in outs[2:11])
    inp, sw, ew, tw, ow = outs[11:]
    return (loss, factor, inp.reshape(1, rows_here, length, feat), g1, b1, tw, qb, vb, ow, ob, g2, b2, ew, eb, sw, sb)


HIGH = lax.Precision.HIGHEST


def shifted(shard, axis, by):
    peers = lax.axis_size(axis)
    pairs = [(i, i + by) for i in range(peers) if 0 <= i + by < peers]
    return lax.ppermute(shard, axis, pairs)


def layer_stats(values):
    center = values - jnp.mean(values, axis=-1, keepdims=True)
    spread = lax.rsqrt(jnp.mean(center * center, axis=-1, keepdims=True) + 1e-05)
    return (center * spread, spread)


def norm_back(grad_normed, normed, spread):
    return spread * (
        grad_normed
        - jnp.mean(grad_normed, axis=-1, keepdims=True)
        - normed * jnp.mean(grad_normed * normed, axis=-1, keepdims=True)
    )


def masked_scores(queries, key_heads, same_seg):
    raw = (
        jnp.einsum("rqhc,rkhc->rhqk", queries, key_heads, preferred_element_type=jnp.float32)
        * 0.125
    )
    return jnp.where(same_seg, raw, -1e30)


def sum_grads(grads):
    return (
        lax.psum_scatter(grads[0], ("tower", "dp"), scatter_dimension=0, tiled=True),
        lax.psum_scatter(grads[1], ("tower", "dp"), scatter_dimension=0, tiled=True),
        lax.psum_scatter(grads[2], ("tower", "dp"), scatter_dimension=0, tiled=True),
        lax.psum_scatter(grads[3], ("tower", "dp"), scatter_dimension=0, tiled=True),
        lax.psum_scatter(grads[4], ("tower", "dp"), scatter_dimension=0, tiled=True),
        lax.psum_scatter(grads[5], ("tower", "dp"), scatter_dimension=0, tiled=True),
        lax.psum_scatter(grads[6], ("tower", "dp"), scatter_dimension=0, tiled=True),
        lax.psum_scatter(grads[7], ("tower", "dp"), scatter_dimension=0, tiled=True),
        lax.psum_scatter(grads[8], ("tower", "dp"), scatter_dimension=0, tiled=True),
        lax.psum_scatter(grads[9], ("tower", "dp"), scatter_dimension=0, tiled=True),
        lax.psum_scatter(grads[10], ("tower", "dp"), scatter_dimension=0, tiled=True),
        lax.psum_scatter(grads[11], ("tower", "dp"), scatter_dimension=0, tiled=True),
        lax.psum_scatter(grads[12], ("tower", "dp"), scatter_dimension=0, tiled=True),
    )


def local(
    tokens,
    segments,
    caption_image,
    logit_scale,
    first_gain,
    first_bias,
    triple_weight,
    query_bias,
    value_bias,
    output_weight,
    output_bias,
    second_gain,
    second_bias,
    expand_weight,
    expand_bias,
    shrink_weight,
    shrink_bias,
):
    rows_here = tokens.shape[1]
    length = tokens.shape[2]
    features = tokens.shape[3]
    head_size = features // HEADS
    token_count = rows_here * length
    is_text = lax.axis_index("tower") == 1
    text_flag = is_text.astype(jnp.float32)
    position = jnp.arange(length, dtype=jnp.int32)
    image_segs = jnp.broadcast_to(
        (position >= IMG_TOK).astype(jnp.int32)[None, :], (rows_here, length)
    )
    seg_ids = jnp.where(is_text, segments, image_segs)
    same_seg = (seg_ids[:, :, None] == seg_ids[:, None, :])[:, None, :, :]
    head_shape = (rows_here, length, HEADS, head_size)
    gain_one = first_gain[0].astype(jnp.float32)
    shift_one = first_bias[0].astype(jnp.float32)
    triple_w = triple_weight[0]
    query_shift = query_bias[0].astype(jnp.float32)
    value_shift = value_bias[0].astype(jnp.float32)
    output_w = output_weight[0]
    output_shift = output_bias[0].astype(jnp.float32)
    gain_two = second_gain[0].astype(jnp.float32)
    shift_two = second_bias[0].astype(jnp.float32)
    expand_w = expand_weight[0]
    expand_shift = expand_bias[0].astype(jnp.float32)
    shrink_w = shrink_weight[0]
    shrink_shift = shrink_bias[0].astype(jnp.float32)
    inputs = tokens[0].reshape(token_count, features).astype(jnp.float32)
    normed_a, spread_a = layer_stats(inputs)
    normed_one = (normed_a * gain_one + shift_one).astype(jnp.bfloat16)
    triple = jnp.dot(normed_one, triple_w, preferred_element_type=jnp.float32)
    queries = (triple[:, :features] + query_shift).astype(jnp.bfloat16).reshape(head_shape)
    key_heads = triple[:, features : 2 * features].astype(jnp.bfloat16).reshape(head_shape)
    value_heads = (triple[:, 2 * features :] + value_shift).astype(jnp.bfloat16).reshape(head_shape)
    scores = masked_scores(queries, key_heads, same_seg)
    row_peak = jnp.max(scores, axis=-1, keepdims=True)
    log_total = row_peak + jnp.log(jnp.sum(jnp.exp(scores - row_peak), axis=-1, keepdims=True))
    attn_probs = jnp.exp(scores - log_total)
    mixed_low = (
        jnp.einsum(
            "rhqk,rkhc->rqhc",
            attn_probs.astype(jnp.bfloat16),
            value_heads,
            preferred_element_type=jnp.float32,
        )
        .reshape(token_count, features)
        .astype(jnp.bfloat16)
    )
    hidden = (
        inputs + jnp.dot(mixed_low, output_w, preferred_element_type=jnp.float32) + output_shift
    )
    normed_b, spread_b = layer_stats(hidden)
    normed_two = (normed_b * gain_two + shift_two).astype(jnp.bfloat16)
    expanded = jnp.dot(normed_two, expand_w, preferred_element_type=jnp.float32) + expand_shift
    activated, gelu_back = jax.vjp(jax.nn.gelu, expanded)
    active_low = activated.astype(jnp.bfloat16)
    block_out = (
        hidden + jnp.dot(active_low, shrink_w, preferred_element_type=jnp.float32) + shrink_shift
    )
    slot_ids = jnp.arange(CAPS, dtype=jnp.int32)
    member = (seg_ids[:, None, :] == slot_ids[None, :, None]).astype(jnp.float32)
    counts = jnp.maximum(jnp.sum(member, axis=2), 1.0)
    pooled = (
        jnp.einsum(
            "rst,rtd->rsd", member, block_out.reshape(rows_here, length, features), precision=HIGH
        )
        / counts[:, :, None]
    )
    inverse = lax.rsqrt(jnp.sum(pooled * pooled, axis=2, keepdims=True) + 1e-06)
    embedding = pooled * inverse
    first_slot = embedding[:, 0, :].astype(jnp.bfloat16)
    collected = lax.all_gather(first_slot, "dp", axis=0, tiled=True)
    image_table = shifted(collected, "tower", 1)
    text_low = embedding.reshape(rows_here * CAPS, features).astype(jnp.bfloat16)
    similar = jnp.einsum("cd,id->ci", text_low, image_table, preferred_element_type=jnp.float32)
    factor = logit_scale[0]
    logits = factor * similar
    logit_peak = jnp.max(logits, axis=1, keepdims=True)
    logit_total = logit_peak + jnp.log(jnp.sum(jnp.exp(logits - logit_peak), axis=1, keepdims=True))
    targets = caption_image.reshape(-1)
    image_ids = jnp.arange(image_table.shape[0], dtype=jnp.int32)
    target_hot = (image_ids[None, :] == targets[:, None]).astype(jnp.float32)
    picked = jnp.sum(logits * target_hot, axis=1)
    loss_here = jnp.sum(logit_total[:, 0] - picked) * text_flag
    grad_logits = (jnp.exp(logits - logit_total) - target_hot) * text_flag
    factor_here = jnp.sum(grad_logits * similar)
    loss_total, factor_total = lax.psum((loss_here, factor_here), ("tower", "dp"))
    caption_total = rows_here * CAPS * lax.axis_size("dp")
    grad_dots = (factor * grad_logits).astype(jnp.bfloat16)
    grad_emb = jnp.einsum(
        "ci,id->cd", grad_dots, image_table, preferred_element_type=jnp.float32
    ).reshape(rows_here, CAPS, features)
    grad_pooled = inverse * (
        grad_emb - embedding * jnp.sum(embedding * grad_emb, axis=2, keepdims=True)
    )
    grad_pooled = grad_pooled / counts[:, :, None]
    grad_out = jnp.einsum("rst,rsd->rtd", member, grad_pooled, precision=HIGH).reshape(
        token_count, features
    )
    shrink_bias_grad = jnp.sum(grad_out, axis=0)
    grad_out_low = grad_out.astype(jnp.bfloat16)
    shrink_weight_grad = jnp.einsum(
        "nf,nd->fd", active_low, grad_out_low, preferred_element_type=jnp.float32
    )
    grad_active = jnp.einsum(
        "nd,fd->nf", grad_out_low, shrink_w, preferred_element_type=jnp.float32
    )
    grad_expanded = gelu_back(grad_active)[0]
    expand_bias_grad = jnp.sum(grad_expanded, axis=0)
    grad_expanded_low = grad_expanded.astype(jnp.bfloat16)
    expand_weight_grad = jnp.einsum(
        "nd,nf->df", normed_two, grad_expanded_low, preferred_element_type=jnp.float32
    )
    grad_normed_two = jnp.einsum(
        "nf,df->nd", grad_expanded_low, expand_w, preferred_element_type=jnp.float32
    )
    second_gain_grad = jnp.sum(grad_normed_two * normed_b, axis=0)
    second_bias_grad = jnp.sum(grad_normed_two, axis=0)
    grad_hidden = grad_out + norm_back(grad_normed_two * gain_two, normed_b, spread_b)
    output_bias_grad = jnp.sum(grad_hidden, axis=0)
    grad_hidden_low = grad_hidden.astype(jnp.bfloat16)
    output_weight_grad = jnp.einsum(
        "nd,ne->de", mixed_low, grad_hidden_low, preferred_element_type=jnp.float32
    )
    grad_mixed = (
        jnp.einsum("ne,de->nd", grad_hidden_low, output_w, preferred_element_type=jnp.float32)
        .astype(jnp.bfloat16)
        .reshape(head_shape)
    )
    scores_again = masked_scores(queries, key_heads, same_seg)
    probs_again = jnp.exp(scores_again - log_total)
    probs_low = probs_again.astype(jnp.bfloat16)
    grad_values = jnp.einsum(
        "rhqk,rqhc->rkhc", probs_low, grad_mixed, preferred_element_type=jnp.float32
    )
    grad_probs = jnp.einsum(
        "rqhc,rkhc->rhqk", grad_mixed, value_heads, preferred_element_type=jnp.float32
    )
    grad_scores = (
        probs_again * (grad_probs - jnp.sum(probs_again * grad_probs, axis=-1, keepdims=True))
    ).astype(jnp.bfloat16)
    grad_queries = (
        jnp.einsum("rhqk,rkhc->rqhc", grad_scores, key_heads, preferred_element_type=jnp.float32)
        * 0.125
    )
    grad_keys = (
        jnp.einsum("rhqk,rqhc->rkhc", grad_scores, queries, preferred_element_type=jnp.float32)
        * 0.125
    )
    grad_queries = grad_queries.reshape(token_count, features)
    grad_keys = grad_keys.reshape(token_count, features)
    grad_values = grad_values.reshape(token_count, features)
    query_bias_grad = jnp.sum(grad_queries, axis=0)
    value_bias_grad = jnp.sum(grad_values, axis=0)
    grad_triple = jnp.concatenate([grad_queries, grad_keys, grad_values], axis=1).astype(
        jnp.bfloat16
    )
    triple_weight_grad = jnp.einsum(
        "nd,ne->de", normed_one, grad_triple, preferred_element_type=jnp.float32
    )
    grad_normed_one = jnp.einsum(
        "ne,de->nd", grad_triple, triple_w, preferred_element_type=jnp.float32
    )
    first_gain_grad = jnp.sum(grad_normed_one * normed_a, axis=0)
    first_bias_grad = jnp.sum(grad_normed_one, axis=0)
    input_grad = grad_hidden + norm_back(grad_normed_one * gain_one, normed_a, spread_a)
    shares = sum_grads(
        (
            first_gain_grad,
            first_bias_grad,
            triple_weight_grad,
            query_bias_grad,
            value_bias_grad,
            output_weight_grad,
            output_bias_grad,
            second_gain_grad,
            second_bias_grad,
            expand_weight_grad,
            expand_bias_grad,
            shrink_weight_grad,
            shrink_bias_grad,
        )
    )
    loss_out = (loss_total / caption_total).reshape(1)
    factor_out = factor_total.reshape(1)
    return (
        loss_out,
        factor_out,
        input_grad.reshape(1, rows_here, length, features),
        shares[0],
        shares[1],
        shares[2],
        shares[3],
        shares[4],
        shares[5],
        shares[6],
        shares[7],
        shares[8],
        shares[9],
        shares[10],
        shares[11],
        shares[12],
    )


def solution(mesh):
    placed = (
        P("tower", "dp", None, None),
        P("dp", None),
        P("dp", None),
        P(),
        P("tower", None),
        P("tower", None),
        P("tower", None, None),
        P("tower", None),
        P("tower", None),
        P("tower", None, None),
        P("tower", None),
        P("tower", None),
        P("tower", None),
        P("tower", None, None),
        P("tower", None),
        P("tower", None, None),
        P("tower", None),
    )
    fits = mesh.shape["tower"] == 2 and mesh.shape["dp"] == 2 * PLANE
    return jax.shard_map(
        local_fast if fits else local,
        mesh=mesh,
        in_specs=placed,
        out_specs=(
            P(),
            P(),
            P("tower", "dp", None, None),
            P(("tower", "dp")),
            P(("tower", "dp")),
            P(("tower", "dp"), None),
            P(("tower", "dp")),
            P(("tower", "dp")),
            P(("tower", "dp"), None),
            P(("tower", "dp")),
            P(("tower", "dp")),
            P(("tower", "dp")),
            P(("tower", "dp"), None),
            P(("tower", "dp")),
            P(("tower", "dp"), None),
            P(("tower", "dp")),
        ),
        check_vma=False,
    )
```

```python
import functools

import jax
import jax.numpy as jnp
from jax import lax
from jax.experimental import pallas as pl
from jax.experimental.pallas import tpu as pltpu
from jax.sharding import PartitionSpec as P

HEADS = 12
IMG_TOK = 50
CAPS = 4

f32, bf16 = jnp.float32, jnp.bfloat16
GELU_C = 0.7978845608028654
GELU_A = 0.044715
STEP_ROWS = 4
MESH = pl.DeviceIdType.MESH


def mm(a, b):
    return jnp.dot(a, b, preferred_element_type=f32)


def mm_nt(a, b):
    return lax.dot_general(a, b, (((1,), (1,)), ((), ())), preferred_element_type=f32)


def mm_tn(a, b):
    return lax.dot_general(a, b, (((0,), (0,)), ((), ())), preferred_element_type=f32)


def stats(x):
    center = x - jnp.mean(x, axis=-1, keepdims=True)
    spread = lax.rsqrt(jnp.mean(center * center, axis=-1, keepdims=True) + 1e-05)
    return center * spread, spread


def split(x, first):
    zero = jnp.zeros_like(x)
    return jnp.concatenate([jnp.where(first, x, zero), jnp.where(first, zero, x)], axis=0)


def low_pair(x):
    high = x.astype(bf16)
    return high, (x - high.astype(f32)).astype(bf16)


def fwd_kernel(tok, seg, g1, b1, qb, vb, ob, g2, b2, eb, sb, w3h, woh, weh, wsh,
               qkv_h, probs_h, mixed_h, normed_h, sums_out, slope_h, n1_h, n2_h, spread_out, member_out, pooled_out, count_out, table_out,
               w3, wo, we, ws, pool_acc, count_acc, act_sum, imgs, elow, out_acc,
               qkv_b, probs_b, mixed_b, normed_b, slope_b, n1_b, n2_b, sems, gsem, esem, osem):
    i = pl.program_id(0)
    steps = pl.num_programs(0)
    rows_here, length = seg.shape
    slots = rows_here * CAPS
    feat = tok.shape[1]
    block = tok.shape[0]
    is_text = lax.axis_index("tower") == 1
    copies = [pltpu.make_async_copy(src, dst, sems.at[n])
              for n, (src, dst) in enumerate(((w3h, w3), (woh, wo), (weh, we), (wsh, ws)))]

    tower, d = lax.axis_index("tower"), lax.axis_index("dp")
    chip, core = d // 2, lax.rem(d, 2)
    other = 1 - core
    partner = (tower, chip * 2 + other)
    chips = imgs.shape[1]
    facing = [(1 - tower, lax.rem(chip + k, chips) * 2 + core) for k in range(chips)]

    def remote(src, dst, sem, dev):
        return pltpu.make_async_remote_copy(src_ref=src, dst_ref=dst, send_sem=sem.at[0], recv_sem=sem.at[1],
                                            device_id=dev, device_id_type=MESH)

    slot = lax.rem(i, 2)
    saved = ((qkv_b, qkv_h), (probs_b, probs_h), (mixed_b, mixed_h), (normed_b, normed_h), (slope_b, slope_h),
             (n1_b, n1_h), (n2_b, n2_h))
    qkv, probs, mixed, normed_out, slope, n1_out, n2_out = (buf.at[slot] for buf, _ in saved)

    def save(n, step):
        buf, out = saved[n]
        at = lax.rem(step, 2)
        return pltpu.make_async_copy(buf.at[at], out.at[pl.ds(pl.multiple_of(step * block, block), block)],
                                     osem.at[at, n])

    def leave(*which):
        @pl.when(is_text)
        def _():
            for n in which:
                save(n, i).start()

    @pl.when(is_text & (i >= 2))
    def _():
        for n in range(len(saved)):
            save(n, i - 2).wait()

    barrier = pltpu.get_barrier_semaphore()

    @pl.when(i == 0)
    def _():
        copies[0].start()
        copies[1].start()
        for dev in facing + [partner]:
            pl.semaphore_signal(barrier, inc=1, device_id=dev, device_id_type=MESH)
        pool_acc[...] = jnp.zeros_like(pool_acc)
        count_acc[...] = jnp.zeros_like(count_acc)
        act_sum[...] = jnp.zeros_like(act_sum)

    def arrive(n):
        @pl.when(i == 0)
        def _():
            copies[n].wait()

    x = tok[...].astype(f32)
    norm, _ = stats(x)
    n1 = (norm * g1[...].astype(f32) + b1[...].astype(f32)).astype(bf16)
    n1_out[...] = n1
    leave(5)
    arrive(0)

    @pl.when(i == 0)
    def _():
        copies[2].start()
        copies[3].start()
    qkv[:, :feat] = (mm(n1, w3[:, :feat]) + qb[...].astype(f32)).astype(bf16)
    qkv[:, feat:2 * feat] = mm(n1, w3[:, feat:2 * feat]).astype(bf16)
    qkv[:, 2 * feat:] = (mm(n1, w3[:, 2 * feat:]) + vb[...].astype(f32)).astype(bf16)

    leave(0)

    image_seg = (lax.broadcasted_iota(jnp.int32, (1, length), 1) >= IMG_TOK).astype(jnp.int32)
    row_segs = []
    for r in range(STEP_ROWS):
        s = seg[pl.ds(STEP_ROWS * i + r, 1), :]
        row_segs.append(jnp.where(is_text, s, image_seg))
    lane = lax.broadcasted_iota(jnp.int32, (128, 128), 1)
    first_half = lane < 64
    slot_lanes = []
    for pair in range(STEP_ROWS // 2):
        base = STEP_ROWS * i + 2 * pair
        keyed = jnp.concatenate(
            [row_segs[2 * pair] * rows_here + base, row_segs[2 * pair + 1] * rows_here + (base + 1)], axis=1)
        slot_lanes.append(keyed)
        across = jnp.broadcast_to(keyed.astype(f32), (128, 128))
        bias = jnp.where(across == across.T, 0.0, -1e30)
        bias = jnp.concatenate([bias, bias], axis=1)
        here = slice(pair * 128, pair * 128 + 128)
        hps = range(HEADS // 2)
        scores = [mm_nt(qkv[here, feat + 128 * h:feat + 128 * h + 128],
                        split(qkv[here, 128 * h:128 * h + 128] * jnp.asarray(0.125, bf16), first_half)) + bias
                  for h in hps]
        lows = []
        for h in hps:
            e = jnp.exp(scores[h] - jnp.max(scores[h], axis=0, keepdims=True))
            p = (e * (1.0 / jnp.sum(e, axis=0, keepdims=True))).astype(bf16)
            probs[here, 256 * h:256 * h + 256] = p
            lows.append(p)
        for h in hps:
            o = mm_tn(lows[h], qkv[here, 2 * feat + 128 * h:2 * feat + 128 * h + 128])
            mixed[here, 128 * h:128 * h + 128] = jnp.where(first_half, o[:128], o[128:]).astype(bf16)

    leave(1, 2)
    arrive(1)
    hid = x + mm(mixed[...], wo[...]) + ob[...].astype(f32)
    norm2, spread2 = stats(hid)
    normed_out[...] = norm2
    spread_out[...] = spread2
    n2 = (norm2 * g2[...].astype(f32) + b2[...].astype(f32)).astype(bf16)
    n2_out[...] = n2
    leave(3, 6)
    slot_row = jnp.concatenate(slot_lanes, axis=1)
    hot = (lax.broadcasted_iota(jnp.int32, (slots, block), 0) == slot_row)
    member = hot.astype(f32).astype(bf16)
    placed = (lax.broadcasted_iota(jnp.int32, (2 * slots, block), 0) == slot_row + slots * core)
    placed = placed.astype(f32).astype(bf16)
    arrive(2)
    arrive(3)
    base = hid + sb[...].astype(f32)
    tile = 768
    width = we.shape[1]

    def feed_forward(keep):
        out = base
        ahead = mm(n2, we[:, :tile])
        for f in range(0, width, tile):
            v = ahead + eb[:, f:f + tile].astype(f32)
            if f + tile < width:
                ahead = mm(n2, we[:, f + tile:f + 2 * tile])
            v2 = v * v
            cv = v * GELU_C
            h = 0.5 + 0.5 * jnp.tanh(cv * (1.0 + GELU_A * v2))
            a = (v * h).astype(bf16)
            if keep:
                act_sum[:, f:f + tile] += mm(placed, a)
                slope[:, f:f + tile] = (h + h * (1.0 - h) * ((2.0 * cv) * (1.0 + (3.0 * GELU_A) * v2))).astype(bf16)
            out = out + mm(a, ws[f:f + tile, :])
        out_acc[...] = out

    @pl.when(is_text)
    def _():
        feed_forward(True)
    leave(4)

    @pl.when(tower == 0)
    def _():
        feed_forward(False)
    out = out_acc[...]
    member_out[...] = member
    out_hi, out_lo = low_pair(out)
    pool_acc[...] += mm(member, out_hi) + mm(member, out_lo)
    count_acc[...] += jnp.broadcast_to(jnp.sum(hot.astype(f32), axis=1, keepdims=True), count_acc.shape)

    @pl.when(i == steps - 1)
    def _():
        counts = jnp.maximum(count_acc[...], 1.0)
        pooled = pool_acc[...] / counts[:, :1]
        count_out[...] = counts
        pooled_out[...] = pooled
        pl.semaphore_wait(barrier, chips + 1)

        @pl.when(tower == 0)
        def _():
            first = pooled[:rows_here]
            elow[...] = (first * lax.rsqrt(jnp.sum(first * first, axis=1, keepdims=True) + 1e-06)).astype(bf16)
            for dev in facing:
                remote(elow, imgs.at[core, chip], gsem, dev).start()
            remote(imgs.at[0], imgs.at[0], gsem, partner).wait_send()

        @pl.when(tower == 1)
        def _():
            for f in range(0, width, tile):
                sums_out[f:f + tile, :] = act_sum[:, f:f + tile].astype(bf16).T
            remote(imgs.at[core], imgs.at[core], gsem, partner).wait_recv()
            remote(imgs.at[core], imgs.at[core], esem, partner).start()
            remote(imgs.at[other], imgs.at[other], esem, partner).wait()
            table_out[...] = imgs[...]
            for n in range(len(saved)):
                save(n, i - 1).wait()
                save(n, i).wait()


def forward(tokens, segments, g1, b1, w3, qb, vb, wo, ob, g2, b2, we, eb, ws, sb):
    count, feat = tokens.shape
    rows_here, length = segments.shape
    slots = rows_here * CAPS
    ff = we.shape[1]
    block = STEP_ROWS * length
    steps = count // block
    table = (2, lax.axis_size("dp") // 2, rows_here, feat)
    whole = lambda a: pl.BlockSpec(a.shape, lambda i: (0,) * a.ndim)
    rows = lambda width: pl.BlockSpec((block, width), lambda i: (i, 0))
    anyw = pl.BlockSpec(memory_space=pl.ANY)
    smalls = (g1, b1, qb, vb, ob, g2, b2, eb, sb)
    return pl.pallas_call(
        fwd_kernel,
        grid=(steps,),
        in_specs=[rows(feat), whole(segments)] + [whole(a) for a in smalls] + [anyw] * 4,
        out_specs=[anyw] * 4 + [pl.BlockSpec((ff, 2 * slots), lambda i: (0, 0))] + [anyw] * 3 + [
                   rows(1),
                   pl.BlockSpec((slots, block), lambda i: (0, i)),
                   pl.BlockSpec((slots, feat), lambda i: (0, 0)),
                   pl.BlockSpec((slots, 128), lambda i: (0, 0)),
                   pl.BlockSpec(table, lambda i: (0,) * 4)],
        out_shape=[jax.ShapeDtypeStruct((count, 3 * feat), bf16),
                   jax.ShapeDtypeStruct((count, 2 * feat), bf16),
                   jax.ShapeDtypeStruct((count, feat), bf16),
                   jax.ShapeDtypeStruct((count, feat), f32),
                   jax.ShapeDtypeStruct((ff, 2 * slots), bf16),
                   jax.ShapeDtypeStruct((count, ff), bf16),
                   jax.ShapeDtypeStruct((count, feat), bf16),
                   jax.ShapeDtypeStruct((count, feat), bf16),
                   jax.ShapeDtypeStruct((count, 1), f32),
                   jax.ShapeDtypeStruct((slots, count), bf16),
                   jax.ShapeDtypeStruct((slots, feat), f32),
                   jax.ShapeDtypeStruct((slots, 128), f32),
                   jax.ShapeDtypeStruct(table, bf16)],
        scratch_shapes=[pltpu.VMEM(w3.shape, bf16), pltpu.VMEM(wo.shape, bf16), pltpu.VMEM(we.shape, bf16),
                        pltpu.VMEM(ws.shape, bf16), pltpu.VMEM((slots, feat), f32), pltpu.VMEM((slots, 128), f32), pltpu.VMEM((2 * slots, ff), f32),
                        pltpu.VMEM(table, bf16), pltpu.VMEM((rows_here, feat), bf16), pltpu.VMEM((block, feat), f32),
                        pltpu.VMEM((2, block, 3 * feat), bf16), pltpu.VMEM((2, block, 2 * feat), bf16),
                        pltpu.VMEM((2, block, feat), bf16), pltpu.VMEM((2, block, feat), f32),
                        pltpu.VMEM((2, block, ff), bf16), pltpu.VMEM((2, block, feat), bf16),
                        pltpu.VMEM((2, block, feat), bf16),
                        pltpu.SemaphoreType.DMA((4,)), pltpu.SemaphoreType.DMA((2,)), pltpu.SemaphoreType.DMA((2,)),
                        pltpu.SemaphoreType.DMA((2, 7))],
        compiler_params=pltpu.CompilerParams(vmem_limit_bytes=56 << 20, dimension_semantics=("arbitrary",),
                                             collective_id=1, has_side_effects=True),
        name="fwd",
    )(tokens, segments, *smalls, w3, wo, we, ws)


PLANE = 8
LINE = 4
BLK = 256
CH = 768
HALF = CH // 2
ROWS = HALF // PLANE
N_CH = 8
WIDE = (0, 2, 4, 7)
LONG = (1, 3, 5)
DEEP = (6,)
TEXT_PLAN = {
    ("ga", 1): (("cross",), ("leave", 0),),
    ("ga", 2): (("leave", 1),),
    ("ew", 2): (("mid", 0),),
    ("ga", 3): (("leave", 2),),
    "ow": (("mid", 1), ("leave", 3),),
    ("attn", 0): (("mid", 2), ("leave", 4),),
    ("attn", 5): (("share",),),
    ("tw", 0): (("mid", 3), ("rows",), ("finish", 0),),
    ("tw", 1): (("leave", 5),),
    ("tw", 2): (("mid", 4), ("finish", 1),),
    ("gn1", 0): (("leave", 6),),
    ("gn1", 1): (("finish", 2), ("leave", 7),),
    ("gn1", 3): (("finish", 3), ("mid", 5),),
    "end": (("mid", 6), ("mid", 7), ("finish", 6), ("finish", 4), ("finish", 5), ("finish", 7),),
}
IMAGE_PLAN = (
    ("over", 0), ("mid", 0), ("over", 2), ("over", 1), ("mid", 2), ("finish", 0), ("over", 4), ("over", 3), ("finish", 1), ("mid", 4), ("finish", 2), ("over", 7), ("over", 5), ("rows",), ("finish", 3), ("finish", 4), ("mid", 7), ("finish", 5), ("take", 6), ("finish", 7),
)
WIDE_AT = {q: n for n, q in enumerate(WIDE)}
LONG_AT = {q: n for n, q in enumerate(LONG + DEEP)}
DEEP_AT = {q: n for n, q in enumerate(DEEP)}


def fold(x):
    return jnp.sum(x.reshape(x.shape[0] // 8, 8, x.shape[1]), axis=0)


def bwd_kernel(member, pooled, count, imgs, act_sums, caption, scale, g1, b1, g2, b2,
               qkv_h, probs_h, mixed_h, normed_h, slope_h, n1_h, n2_h, spread_h, tok_h, w3_h, wo_h, we_h, ws_h,
               tw_out, ow_out, ew_out, sw_out, in_out, vec_out,
               cs, snd, prv, own, ylong, ywide, zrcv, zdeep, xfin, fin, apair, asum, aall, gpall, swfin, xsw,
               gol, gn2, hid, spread2, n2b, tok, mixed, probs, slope, ws, we, ge, qkv, w3, wo,
               ebsum, attn_sum, vec, vown, vpair, vrcv,
               ld, psend, precv, xsend, xrecv, ysend, yrecv, zsend, zrecv,
               fsem, asem, gsem, swsem, vpsem, vsem, outsem):
    t = lax.axis_index("tower")
    d = lax.axis_index("dp")
    p = d // 2
    c = lax.rem(d, 2)
    z = p // 2
    y = lax.rem(p, 2)
    is_text = t == 1
    count_t = gol.shape[0]
    blocks = count_t // BLK
    feat = CH
    rows_here = caption.shape[1]
    other = 1 - c

    def peer(k):
        return lax.rem(p + k, PLANE)

    def at_core(tt, pp):
        return (tt, pp * 2 + c)

    partner = (t, p * 2 + other)
    beside = at_core(t, 2 * z + (1 - y))
    across = at_core(1 - t, p)

    def remote(src, dst, ssem, rsem, dev):
        return pltpu.make_async_remote_copy(src_ref=src, dst_ref=dst, send_sem=ssem, recv_sem=rsem,
                                            device_id=dev, device_id_type=MESH)

    barrier = pltpu.get_barrier_semaphore()
    pl.semaphore_signal(barrier, inc=1, device_id=partner, device_id_type=MESH)
    pl.semaphore_signal(barrier, inc=1, device_id=across, device_id_type=MESH)
    for k in range(1, PLANE):
        pl.semaphore_signal(barrier, inc=1, device_id=at_core(t, peer(k)), device_id_type=MESH)
        pl.semaphore_signal(barrier, inc=1, device_id=at_core(1 - t, peer(k)), device_id_type=MESH)

    pooled_v = pooled[...]
    inverse = lax.rsqrt(jnp.sum(pooled_v * pooled_v, axis=1, keepdims=True) + 1e-06)
    emb = pooled_v * inverse
    emb_low = emb.astype(bf16)

    def pair_copy(q):
        slot = lax.rem(q, 2)
        return remote(snd.at[slot], prv.at[q], psend.at[slot], precv.at[q], partner)

    def x_all(q):
        return remote(cs.at[q, 0:LINE], cs.at[q, 0:LINE], xsend.at[q], xrecv.at[q], across)

    def x_line(q):
        return remote(cs.at[q, 0:LINE, y], cs.at[q, 0:LINE, y], xsend.at[q], xrecv.at[q], across)

    def x_sum(q):
        n = DEEP_AT[q]
        return remote(xfin.at[n], xfin.at[n], xsend.at[q], xrecv.at[q], across)

    def x_copy(q):
        return x_all(q) if q in WIDE else x_line(q) if q in LONG else x_sum(q)

    def y_copy(q):
        if q not in WIDE:
            src, dst = cs.at[q, :, 1 - y], ylong.at[LONG_AT[q]]
        else:
            src, dst = cs.at[q, pl.ds(LINE * t, LINE), 1 - y], ywide.at[WIDE_AT[q]]
        return remote(src, dst, ysend.at[q], yrecv.at[q], beside)

    def z_start(q):
        for k in range(1, LINE):
            to = lax.rem(z + k, LINE)
            remote(cs.at[q, LINE * t + to, y], zrcv.at[q, k - 1], zsend.at[q], zrecv.at[q],
                   at_core(t, 2 * to + y)).start()
            if q in DEEP:
                remote(cs.at[q, to, y], zdeep.at[DEEP_AT[q], k - 1], zsend.at[N_CH + DEEP_AT[q]],
                       zrecv.at[N_CH + DEEP_AT[q]], at_core(t, 2 * to + y)).start()

    def z_all(q):
        return remote(zrcv.at[q], zrcv.at[q], zsend.at[q], zrecv.at[q], partner)

    def z_deep(q):
        n = DEEP_AT[q]
        return remote(zdeep.at[n], zdeep.at[n], zsend.at[N_CH + n], zrecv.at[N_CH + n], partner)

    def mid(q):
        y_copy(q).wait_recv()
        if q not in WIDE:
            for a in range(PLANE):
                cs[q, a, y] = (cs[q, a, y].astype(f32) + ylong[LONG_AT[q], a].astype(f32)).astype(bf16)
            if q in LONG:
                x_line(q).start()
        else:
            for a in range(LINE):
                at = LINE * t + a
                cs[q, at, y] = (cs[q, at, y].astype(f32) + ywide[WIDE_AT[q], a].astype(f32)).astype(bf16)
        z_start(q)

    def a_pair():
        return remote(act_sums.at[:, :, other], apair, asem.at[0], asem.at[1], partner)

    def a_start():
        a_pair().wait_recv()
        asum[...] = act_sums[:, :, c] + apair[...]
        aall[:, :, pl.ds(pl.multiple_of(128 * p, 128), 128)] = asum[:, p]
        for k in range(1, PLANE):
            remote(asum.at[:, peer(k)], aall.at[:, :, pl.ds(pl.multiple_of(128 * p, 128), 128)],
                   asem.at[2], asem.at[3], at_core(t, peer(k))).start()

    def a_all():
        every = asum.at[:, 0:PLANE - 1]
        return remote(every, every, asem.at[2], asem.at[3], partner)

    def gp_beside():
        return remote(gpall.at[p, c], gpall.at[p, c], gsem.at[0], gsem.at[1], beside)

    def gp_line():
        gp_beside().wait_recv()
        for k in range(1, LINE):
            mine = gpall.at[pl.ds(2 * z, 2), c]
            remote(mine, mine, gsem.at[2], gsem.at[3], at_core(t, 2 * lax.rem(z + k, LINE) + y)).start()

    def gp_line_all():
        every = gpall.at[0:2 * (LINE - 1), 0]
        return remote(every, every, gsem.at[2], gsem.at[3], partner)

    def gp_share_copy():
        return remote(gpall.at[:, c], gpall.at[:, c], gsem.at[4], gsem.at[5], partner)

    def gp_share():
        gp_line_all().wait_recv()
        gp_share_copy().start()

    def sw_across():
        return remote(xsw, xsw, swsem.at[0], swsem.at[1], across)

    def sw_keep():
        return pltpu.make_async_copy(swfin, sw_out, swsem.at[2])

    def shrink():
        gp_share_copy().wait_recv()
        a_all().wait_recv()
        rows = gpall[...].reshape(-1, feat)
        xsw[...] = mm(aall[0], rows).astype(bf16)
        sw_across().start()
        swfin[...] = mm(aall[1], rows)
        sw_keep().start()

    half_rows = ROWS // 2

    def place(q):
        if q < 4:
            return ew_out, 4 * HALF * c + HALF * q
        if q == 4:
            return ow_out, HALF * c
        return tw_out, CH * (q - 5) + HALF * c

    def keep(q):
        out, col = place(q)
        return pltpu.make_async_copy(fin.at[q, pl.ds(pl.multiple_of(half_rows * c, 8), half_rows)],
                                     out.at[:, pl.ds(pl.multiple_of(col, 128), HALF)], fsem.at[0])

    def give(q):
        out, col = place(q)
        return remote(fin.at[q, pl.ds(pl.multiple_of(half_rows * other, 8), half_rows)],
                      out.at[:, pl.ds(pl.multiple_of(col, 128), HALF)], fsem.at[1], fsem.at[2], partner)

    def finish(q):
        z_all(q).wait_recv()
        total = cs[q, LINE * t + z, y].astype(f32)
        for k in range(LINE - 1):
            total = total + zrcv[q, k].astype(f32)
        if q in DEEP:
            z_deep(q).wait_recv()
            theirs = cs[q, z, y].astype(f32)
            for k in range(LINE - 1):
                theirs = theirs + zdeep[DEEP_AT[q], k].astype(f32)
            xfin[DEEP_AT[q]] = theirs.astype(bf16)
            x_sum(q).start()
        fin[q] = total
        keep(q).start()
        give(q).start()

    def take(q):
        x_sum(q).wait_recv()
        fin[q] = xfin[DEEP_AT[q]].astype(f32)
        keep(q).start()
        give(q).start()

    def leave(q):
        chip_sum(q)
        if q in WIDE:
            x_all(q).start()
        y_copy(q).start()

    def chip_sum(q):
        pair_copy(q).wait_recv()
        slot = lax.rem(q, 2)
        n = 2 * ROWS
        for a in range(PLANE):
            total = own[slot, n * a:n * (a + 1), :] + prv[q, n * a:n * (a + 1), :].astype(f32)
            cs[q, a] = total.reshape(2, ROWS, HALF).astype(bf16)

    def chunk(q, left, right):
        slot = lax.rem(q, 2)

        @pl.when(q >= 2)
        def _():
            pair_copy(q - 2).wait_send()
        for r in range(0, CH, 256):
            part = mm_tn(left[:, r:r + 256], right)
            low, high = part[:, :HALF], part[:, HALF:]
            own[slot, r:r + 256, :] = jnp.where(c == 0, low, high)
            snd[slot, r:r + 256, :] = jnp.where(c == 0, high, low).astype(bf16)
        pair_copy(q).start()

    def v_pair():
        return remote(vown.at[other], vpair, vpsem.at[0], vpsem.at[1], partner)

    def load(n, src, dst):
        return pltpu.make_async_copy(src, dst, ld.at[n])

    def tile_loads(i):
        s = lax.rem(i, 2)
        out = []
        ff = slope_h.shape[1]
        for h in range(2):
            col = pl.multiple_of((ff // 2) * h + HALF * i, 128)
            here = pl.ds(HALF * h, HALF)
            out.append(load(6 * s + 3 * h, slope_h.at[:, pl.ds(col, HALF)], slope.at[s, :, here]))
            out.append(load(6 * s + 3 * h + 1, ws_h.at[pl.ds(col, HALF)], ws.at[s, here]))
            out.append(load(6 * s + 3 * h + 2, we_h.at[:, pl.ds(col, HALF)], we.at[s, :, here]))
        return out

    hid_load = load(16, normed_h, hid)
    tok_load = load(17, tok_h, tok)
    qkv_load = load(18, qkv_h, qkv)
    w3_load = load(19, w3_h, w3)
    wo_load = load(20, wo_h, wo)
    n2_load = load(24, n2_h, n2b)
    spread_load = load(25, spread_h, spread2)
    n1_load = load(26, n1_h, slope.at[1])
    mixed_load = load(21, mixed_h, mixed)
    probs_load = load(22, probs_h, probs)

    @pl.when(t == 0)
    def _():
        pl.semaphore_wait(barrier, 2 * PLANE)
        gn2[:BLK, :] = jnp.zeros((BLK, feat), f32)
        for m in range(blocks):
            pltpu.make_async_copy(gn2.at[0:BLK], in_out.at[pl.ds(BLK * m, BLK)], outsem.at[m]).start()

        def over(q):
            x_copy(q).wait_recv()
            if q in WIDE:
                y_copy(q).start()
            else:
                z_start(q)

        def rows_over():
            sw_across().wait_recv()
            swfin[...] = xsw[...].astype(f32)
            sw_keep().start()
        acts = {"over": over, "mid": mid, "finish": finish, "take": take, "rows": rows_over}
        for what, *of in IMAGE_PLAN:
            acts[what](*of)
        for m in range(blocks):
            pltpu.make_async_copy(gn2.at[0:BLK], in_out.at[pl.ds(BLK * m, BLK)], outsem.at[m]).wait()

    @pl.when(is_text)
    def _():
        for cp in tile_loads(0):
            cp.start()
        n2_load.start()
        for cp in tile_loads(1):
            cp.start()
        for cp in (hid_load, spread_load, mixed_load, wo_load, qkv_load, probs_load, w3_load, tok_load):
            cp.start()
        gain2, gain1 = g2[...].astype(f32), g1[...].astype(f32)
        gn2[...] = jnp.zeros_like(gn2)
        attn_sum[...] = jnp.zeros_like(attn_sum)
        vec[...] = jnp.zeros_like(vec)
        pl.semaphore_wait(barrier, 2 * PLANE)
        a_pair().start()

        table = imgs[...].reshape(2 * PLANE * rows_here, feat)
        dots = mm_nt(emb_low, table)
        factor = scale[0]
        logits = factor * dots
        peak = jnp.max(logits, axis=1, keepdims=True)
        weight = jnp.exp(logits - peak)
        total = jnp.sum(weight, axis=1, keepdims=True)
        eye = (lax.broadcasted_iota(jnp.int32, (rows_here, rows_here), 0)
               == lax.broadcasted_iota(jnp.int32, (rows_here, rows_here), 1))
        wanted = jnp.concatenate([jnp.sum(jnp.where(eye, caption[s:s + 1, :], 0), axis=1, keepdims=True)
                                  for s in range(CAPS)], axis=0)
        span = 2 * rows_here
        inside = lax.rem(wanted, span)
        wanted = (inside // rows_here) * (PLANE * rows_here) + (wanted // span) * rows_here + lax.rem(inside, rows_here)
        hot = (lax.broadcasted_iota(jnp.int32, dots.shape, 1) == wanted).astype(f32)
        picked = jnp.sum(logits * hot, axis=1, keepdims=True)
        loss_here = jnp.sum(peak + jnp.log(total) - picked, axis=0, keepdims=True)
        a_start()
        grad_logits = weight / total - hot
        factor_here = jnp.sum(jnp.sum(grad_logits * dots, axis=1, keepdims=True), axis=0, keepdims=True)
        grad_emb = mm((factor * grad_logits).astype(bf16), table)
        counts = count[:, :1]
        grad_pool = inverse * (grad_emb - emb * jnp.sum(emb * grad_emb, axis=1, keepdims=True))
        vec[7:8, :] = jnp.sum(grad_pool, axis=0, keepdims=True)
        column = lax.broadcasted_iota(jnp.int32, (1, feat), 1)
        vec[12:13, :] = jnp.where(column == 0, loss_here, jnp.where(column == 1, factor_here, 0.0))
        gp_hi, gp_lo = low_pair(grad_pool / counts)
        gpall[p, c] = gp_hi
        gp_beside().start()
        for m in range(blocks):
            gol[BLK * m:BLK * (m + 1), :] = mm_tn(member[:, BLK * m:BLK * (m + 1)], gp_hi).astype(bf16)

        acts = {"leave": leave, "mid": mid, "finish": finish, "cross": gp_line, "share": gp_share, "rows": shrink}

        def now(place):
            for what, *of in TEXT_PLAN.get(place, ()):
                acts[what](*of)

        def now_in(loop, index, count):
            for n in range(count):
                if (loop, n) in TEXT_PLAN:
                    pl.when(index == n)(functools.partial(now, (loop, n)))

        @pl.loop(0, 4)
        def _(i):
            s = lax.rem(i, 2)
            for cp in tile_loads(i):
                cp.wait()

            sums = jnp.zeros((8, feat), f32)
            for m in range(blocks):
                here = slice(BLK * m, BLK * (m + 1))
                grad = mm_nt(gol[here, :], ws[s]) * slope[s, here, :].astype(f32)
                sums = sums + fold(grad)
                ge[here, :] = grad.astype(bf16)
            sums = jnp.sum(sums, axis=0, keepdims=True)
            for h in range(2):
                ebsum[:, pl.ds(pl.multiple_of(4 * HALF * h + HALF * i, 128), HALF)] = sums[:, HALF * h:HALF * (h + 1)]
            now_in("ga", i, 4)

            @pl.when(i == 0)
            def _():
                n2_load.wait()
            chunk(i, n2b, ge[...])
            now_in("ew", i, 4)
            for m in range(blocks):
                here = slice(BLK * m, BLK * (m + 1))
                gn2[here, :] += mm_nt(ge[here, :], we[s])
            now_in("gn", i, 4)

            @pl.when(i < 2)
            def _():
                for cp in tile_loads(i + 2):
                    cp.start()
        n1_load.start()
        hid_load.wait()
        spread_load.wait()

        zeros8 = jnp.zeros((8, feat), f32)

        def norm2_back(m, sums):
            here = pl.ds(pl.multiple_of(m * BLK, BLK), BLK)
            norm, g_in = hid[here, :], gn2[here, :]
            hot_m = member[:, here]
            grad_out = mm_tn(hot_m, gp_hi) + mm_tn(hot_m, gp_lo)
            g = g_in * gain2
            back = spread2[here, :] * (g - jnp.mean(g, axis=1, keepdims=True)
                                       - norm * jnp.mean(g * norm, axis=1, keepdims=True))
            gh = grad_out + back
            gn2[here, :] = gh
            gol[here, :] = gh.astype(bf16)
            return (sums[0] + fold(g_in * norm), sums[1] + fold(g_in), sums[2] + fold(gh))
        sums = lax.fori_loop(0, blocks, norm2_back, (zeros8, zeros8, zeros8))
        for row, x in ((5, sums[0]), (6, sums[1]), (4, sums[2])):
            vec[row:row + 1, :] = jnp.sum(x, axis=0, keepdims=True)
        for n in range(4):
            vec[8 + n:9 + n, :] = ebsum[:, feat * n:feat * (n + 1)]
        now("norm")

        mixed_load.wait()
        chunk(4, mixed, gol[...])
        now("ow")
        wo_load.wait()
        for m in range(blocks):
            here = slice(BLK * m, BLK * (m + 1))
            ge[here, :] = mm_nt(gol[here, :], wo[...]).astype(bf16)
        now("gm")

        qkv_load.wait()
        probs_load.wait()
        first_half = lax.broadcasted_iota(jnp.int32, (128, 128), 1) < 64
        hps = range(HEADS // 2)

        @pl.loop(0, count_t // 128)
        def _(rp):
            here = pl.ds(pl.multiple_of(rp * 128, 128), 128)

            def probs_of(h):
                return probs[here, 256 * h:256 * h + 256]

            def part(n, h):
                return qkv[here, feat * n + 128 * h:feat * n + 128 * h + 128]
            gm = [split(ge[here, 128 * h:128 * h + 128], first_half) for h in hps]
            gp = [mm_nt(part(2, h), gm[h]) for h in hps]
            gv = [mm(probs_of(h), gm[h]) for h in hps]
            gs = []
            for h in hps:
                probs_f = probs_of(h).astype(f32)
                weighted = probs_f * gp[h]
                gs.append((weighted - probs_f * jnp.sum(weighted, axis=0, keepdims=True)).astype(bf16))
            gk = [mm(gs[h], split(part(0, h), first_half)) * 0.125 for h in hps]
            gq = []
            for h in hps:
                both = mm_tn(gs[h], part(1, h))
                gq.append(jnp.where(first_half, both[:128], both[128:]) * 0.125)
            for h in hps:
                for n, x in ((0, gq[h]), (1, gk[h]), (2, gv[h])):
                    qkv[here, feat * n + 128 * h:feat * n + 128 * h + 128] = x.astype(bf16)
                for n, x in ((0, gq[h]), (1, gv[h])):
                    attn_sum[:, feat * n + 128 * h:feat * n + 128 * h + 128] += fold(x)

            now_in("attn", rp, count_t // 128)
        vec[2:3, :] = jnp.sum(attn_sum[:, :feat], axis=0, keepdims=True)
        vec[3:4, :] = jnp.sum(attn_sum[:, feat:], axis=0, keepdims=True)

        n1_load.wait()

        @pl.loop(0, 3)
        def _(j):
            chunk(5 + j, slope.at[1], qkv[:, pl.ds(pl.multiple_of(CH * j, 128), CH)])

            now_in("tw", j, 3)
        tok_load.wait()
        w3_load.wait()

        def norm1_back(m, sums):
            here = pl.ds(pl.multiple_of(m * BLK, BLK), BLK)
            g_in = mm_nt(qkv[here, :], w3[...])

            now_in("gn1", m, blocks)
            norm, spread = stats(tok[here, :].astype(f32))
            g = g_in * gain1
            back = spread * (g - jnp.mean(g, axis=1, keepdims=True)
                             - norm * jnp.mean(g * norm, axis=1, keepdims=True))
            gn2[here, :] += back
            pltpu.make_async_copy(gn2.at[here], in_out.at[here], outsem.at[m]).start()
            return (sums[0] + fold(g_in * norm), sums[1] + fold(g_in))
        sums = lax.fori_loop(0, blocks, norm1_back, (zeros8, zeros8))
        for row, x in ((0, sums[0]), (1, sums[1])):
            vec[row:row + 1, :] = jnp.sum(x, axis=0, keepdims=True)

        width, wide = feat // (4 * PLANE), 4 * feat // (4 * PLANE)
        narrow = vec[0:8, :]
        broad = vec[8:16, :]
        scalars = vec[12:13, :128]
        turned = [broad] + [pltpu.roll(broad, feat - wide * j, axis=1) for j in range(1, feat // wide)]
        for g in range(4 * PLANE):
            one = narrow if g == 0 else pltpu.roll(narrow, feat - width * g, axis=1)
            row = g // (feat // wide)
            tail = turned[g % (feat // wide)][row:row + 1, :128]
            vown[g % 2, g // 2, 0:8, :] = one[:, :128]
            vown[g % 2, g // 2, 8:9, :] = tail
            vown[g % 2, g // 2, 9:10, :] = scalars
        v_pair().start()
        now("small")
        for m in range(blocks):
            here = pl.ds(BLK * m, BLK)
            pltpu.make_async_copy(gn2.at[here], in_out.at[here], outsem.at[m]).wait()
        v_pair().wait_recv()
        vown[c] += vpair[...]
        for k in range(PLANE):
            for tt in range(2):
                if tt == 0 or k:
                    remote(vown.at[c, PLANE * tt + peer(k)], vrcv.at[k], vsem.at[0], vsem.at[1],
                           at_core(tt, peer(k))).start()
        now("end")

    @pl.when(is_text)
    def _():
        remote(vrcv.at[1:PLANE], vrcv.at[1:PLANE], vsem.at[0], vsem.at[1], partner).wait_recv()
        total = vown[c, PLANE + p]
        for k in range(1, PLANE):
            total = total + vrcv[k]
        vec_out[...] = total

    @pl.when(t == 0)
    def _():
        remote(vrcv, vrcv, vsem.at[0], vsem.at[1], partner).wait_recv()
        total = vrcv[0]
        for k in range(1, PLANE):
            total = total + vrcv[k]
        vec_out[...] = total

    @pl.when(is_text)
    def _():
        everything = vown.at[0, 0:2 * PLANE - 1]
        remote(everything, everything, vsem.at[0], vsem.at[1], partner).wait_send()
        v_pair().wait_send()
        for q in (N_CH - 2, N_CH - 1):
            pair_copy(q).wait_send()

        for q in range(N_CH):
            x_copy(q).wait_send()
        for q in LONG + DEEP:
            y_copy(q).wait_send()
        for q in DEEP:
            z_deep(q).wait_send()
            z_all(q).wait_send()
        a_pair().wait_send()
        a_all().wait_send()
        gp_beside().wait_send()
        gp_line_all().wait_send()
        gp_share_copy().wait_send()
        sw_across().wait_send()
    for q in WIDE:
        y_copy(q).wait_send()
    for q in WIDE + LONG:
        z_all(q).wait_send()
    sw_keep().wait()
    lower = fin.at[:, 0:half_rows]
    pltpu.make_async_copy(lower, lower, fsem.at[0]).wait()
    remote(lower, lower, fsem.at[1], fsem.at[2], partner).wait()


def backward(member, pooled, count, imgs, sums, caption, scale, g1, b1, g2, b2,
             qkv, probs, mixed, normed, slope, n1, n2, spread, tokens, w3, wo, we, ws):
    n_tok, feat = tokens.shape
    ff = we.shape[1]
    dma = pltpu.SemaphoreType.DMA
    vm = pltpu.VMEM
    vspec = pl.BlockSpec(memory_space=pltpu.VMEM)
    sspec = pl.BlockSpec(memory_space=pltpu.SMEM)
    anyw = pl.BlockSpec(memory_space=pl.ANY)
    shape = jax.ShapeDtypeStruct
    long, wide, deep = len(LONG + DEEP), len(WIDE), len(DEEP)
    apart = sums.shape[:2] + sums.shape[3:]
    slots = member.shape[0]
    scratch = [
        vm((N_CH, PLANE, 2, ROWS, HALF), bf16), vm((2, CH, HALF), bf16), vm((N_CH, CH, HALF), bf16),
        vm((2, CH, HALF), f32),
        vm((max(long, 1), PLANE, ROWS, HALF), bf16), vm((max(wide, 1), LINE, ROWS, HALF), bf16), vm((N_CH, LINE - 1, ROWS, HALF), bf16),
        vm((max(deep, 1), LINE - 1, ROWS, HALF), bf16), vm((max(deep, 1), ROWS, HALF), bf16),
        vm((N_CH, ROWS, HALF), f32), vm(apart, bf16), vm(apart, bf16), vm((2, apart[2], PLANE * 128), bf16),
        vm((PLANE, 2, slots, feat), bf16), vm((2 * ROWS, feat), f32), vm((2 * ROWS, feat), bf16),
        vm((n_tok, feat), bf16), vm((n_tok, feat), f32), vm((n_tok, feat), f32), vm((n_tok, 1), f32),
        vm((n_tok, feat), bf16), vm((n_tok, feat), bf16),
        vm((n_tok, feat), bf16), vm((n_tok, 2 * feat), bf16), vm((2, n_tok, CH), bf16), vm((2, CH, feat), bf16), vm((2, feat, CH), bf16),
        vm((n_tok, feat), bf16), vm((n_tok, 3 * feat), bf16), vm(w3.shape, bf16), vm(wo.shape, bf16),
        vm((1, ff), f32), vm((8, 2 * feat), f32),
        vm((16, feat), f32), vm((2, 2 * PLANE, 16, 128), f32), vm((2 * PLANE, 16, 128), f32), vm((PLANE, 16, 128), f32),
        dma((27,)), dma((2,)), dma((N_CH,)), dma((N_CH,)), dma((N_CH,)), dma((N_CH,)), dma((N_CH,)),
        dma((N_CH + deep,)), dma((N_CH + deep,)), dma((3,)), dma((4,)), dma((6,)), dma((3,)), dma((2,)), dma((2,)),
        dma((n_tok // BLK,)),
    ]
    return pl.pallas_call(
        bwd_kernel,
        in_specs=[vspec] * 6 + [sspec] + [vspec] * 4 + [anyw] * 13,
        out_specs=[anyw] * 5 + [vspec],
        out_shape=[shape((ROWS // 2, 3 * feat), f32), shape((ROWS // 2, feat), f32), shape((ROWS // 2, ff), f32),
                   shape((2 * ROWS, feat), f32), shape((n_tok, feat), f32), shape((16, 128), f32)],
        scratch_shapes=scratch,
        compiler_params=pltpu.CompilerParams(vmem_limit_bytes=61 << 20, collective_id=0, has_side_effects=True),
        name="bwd",
    )(member, pooled, count, imgs, sums, caption, scale, g1, b1, g2, b2,
      qkv, probs, mixed, normed, slope, n1, n2, spread, tokens, w3, wo, we, ws)


def hand_out_kernel(scale_by, vec, *rest):
    bigs, loss, factor, smalls = rest[:5], rest[5], rest[6], rest[7:16]
    outs, held, sem_in, sem_out = rest[16:21], rest[21:26], rest[26], rest[27]
    parts = []
    for src, dst, buf in zip(bigs, outs, held):
        count = max(src.shape[0] // BLK, 1)
        rows = src.shape[0] // count
        for n in range(count):
            parts.append((src.at[rows * n:rows * (n + 1)], buf.at[rows * n:rows * (n + 1)],
                          dst.at[rows * n:rows * (n + 1)]))
    ins = [pltpu.make_async_copy(a, b, sem_in.at[n]) for n, (a, b, _) in enumerate(parts)]
    outs = [pltpu.make_async_copy(b, c, sem_out.at[n]) for n, (_, b, c) in enumerate(parts)]
    for move in ins:
        move.start()
    width, wide = smalls[0].shape[1], smalls[8].shape[1]
    for n in range(8):
        smalls[n][...] = vec[n:n + 1, :width]
    smalls[8][...] = vec[8:9, :wide]
    loss[...] = vec[9:10, 0:1] * scale_by
    factor[...] = vec[9:10, 1:2]
    for first, second in zip(ins, outs):
        first.wait()
        second.start()
    for move in outs:
        move.wait()


def hand_out(vec, tw, ow, ew, sw, inp, captions):
    devices = lax.axis_size("tower") * lax.axis_size("dp")
    bigs = (inp, sw, ew, tw, ow)
    feat = inp.shape[1]
    outs = ([(1, 1)] * 2 + [(1, feat // devices)] * 8 + [(1, ew.shape[1] // devices)]
            + [a.shape for a in bigs])
    moves = 4 + inp.shape[0] // BLK
    vspec = pl.BlockSpec(memory_space=pltpu.VMEM)
    anyw = pl.BlockSpec(memory_space=pl.ANY)
    return pl.pallas_call(
        functools.partial(hand_out_kernel, 1.0 / captions),
        in_specs=[vspec] + [anyw] * 5,
        out_specs=[vspec] * 11 + [anyw] * 5,
        out_shape=[jax.ShapeDtypeStruct(dims, f32) for dims in outs],
        scratch_shapes=[pltpu.VMEM(a.shape, f32) for a in bigs]
        + [pltpu.SemaphoreType.DMA((moves,)), pltpu.SemaphoreType.DMA((moves,))],
        name="hand_out",
    )(vec, *bigs)


def local_fast(tokens, segments, caption_image, logit_scale, first_gain, first_bias, triple_weight, query_bias,
               value_bias, output_weight, output_bias, second_gain, second_bias, expand_weight, expand_bias,
               shrink_weight, shrink_bias):
    rows_here, length, feat = tokens.shape[1:]
    flat = tokens[0].reshape(rows_here * length, feat)
    w3, wo, we, ws = triple_weight[0], output_weight[0], expand_weight[0], shrink_weight[0]
    qkv, probs, mixed, normed, sums, slope, n1, n2, spread, member, pooled, count, table = forward(
        flat, segments, first_gain, first_bias, w3, query_bias, value_bias, wo, output_bias,
        second_gain, second_bias, we, expand_bias, ws, shrink_bias)
    sums = sums.reshape(2, PLANE, 2, sums.shape[0] // (4 * PLANE), sums.shape[1])
    tw, ow, ew, sw, inp, vec = backward(member, pooled, count, table, sums, caption_image.T, logit_scale, first_gain, first_bias,
                                        second_gain, second_bias, qkv, probs, mixed, normed, slope, n1, n2, spread, flat,
                                        w3, wo, we, ws)
    captions = rows_here * CAPS * lax.axis_size("dp")
    outs = hand_out(vec, tw, ow, ew, sw, inp, captions)
    loss, factor = outs[0].reshape(1), outs[1].reshape(1)
    g1, b1, qb, vb, ob, g2, b2, sb, eb = (a.reshape(-1) for a in outs[2:11])
    inp, sw, ew, tw, ow = outs[11:]
    return (loss, factor, inp.reshape(1, rows_here, length, feat), g1, b1, tw, qb, vb, ow, ob, g2, b2, ew, eb, sw, sb)


HIGH = lax.Precision.HIGHEST


def shifted(shard, axis, by):
    peers = lax.axis_size(axis)
    pairs = [(i, i + by) for i in range(peers) if 0 <= i + by < peers]
    return lax.ppermute(shard, axis, pairs)


def layer_stats(values):
    center = values - jnp.mean(values, axis=-1, keepdims=True)
    spread = lax.rsqrt(jnp.mean(center * center, axis=-1, keepdims=True) + 1e-05)
    return (center * spread, spread)


def norm_back(grad_normed, normed, spread):
    return spread * (
        grad_normed
        - jnp.mean(grad_normed, axis=-1, keepdims=True)
        - normed * jnp.mean(grad_normed * normed, axis=-1, keepdims=True)
    )


def masked_scores(queries, key_heads, same_seg):
    raw = (
        jnp.einsum("rqhc,rkhc->rhqk", queries, key_heads, preferred_element_type=jnp.float32)
        * 0.125
    )
    return jnp.where(same_seg, raw, -1e30)


def sum_grads(grads):
    return (
        lax.psum_scatter(grads[0], ("tower", "dp"), scatter_dimension=0, tiled=True),
        lax.psum_scatter(grads[1], ("tower", "dp"), scatter_dimension=0, tiled=True),
        lax.psum_scatter(grads[2], ("tower", "dp"), scatter_dimension=0, tiled=True),
        lax.psum_scatter(grads[3], ("tower", "dp"), scatter_dimension=0, tiled=True),
        lax.psum_scatter(grads[4], ("tower", "dp"), scatter_dimension=0, tiled=True),
        lax.psum_scatter(grads[5], ("tower", "dp"), scatter_dimension=0, tiled=True),
        lax.psum_scatter(grads[6], ("tower", "dp"), scatter_dimension=0, tiled=True),
        lax.psum_scatter(grads[7], ("tower", "dp"), scatter_dimension=0, tiled=True),
        lax.psum_scatter(grads[8], ("tower", "dp"), scatter_dimension=0, tiled=True),
        lax.psum_scatter(grads[9], ("tower", "dp"), scatter_dimension=0, tiled=True),
        lax.psum_scatter(grads[10], ("tower", "dp"), scatter_dimension=0, tiled=True),
        lax.psum_scatter(grads[11], ("tower", "dp"), scatter_dimension=0, tiled=True),
        lax.psum_scatter(grads[12], ("tower", "dp"), scatter_dimension=0, tiled=True),
    )


def local(
    tokens,
    segments,
    caption_image,
    logit_scale,
    first_gain,
    first_bias,
    triple_weight,
    query_bias,
    value_bias,
    output_weight,
    output_bias,
    second_gain,
    second_bias,
    expand_weight,
    expand_bias,
    shrink_weight,
    shrink_bias,
):
    rows_here = tokens.shape[1]
    length = tokens.shape[2]
    features = tokens.shape[3]
    head_size = features // HEADS
    token_count = rows_here * length
    is_text = lax.axis_index("tower") == 1
    text_flag = is_text.astype(jnp.float32)
    position = jnp.arange(length, dtype=jnp.int32)
    image_segs = jnp.broadcast_to(
        (position >= IMG_TOK).astype(jnp.int32)[None, :], (rows_here, length)
    )
    seg_ids = jnp.where(is_text, segments, image_segs)
    same_seg = (seg_ids[:, :, None] == seg_ids[:, None, :])[:, None, :, :]
    head_shape = (rows_here, length, HEADS, head_size)
    gain_one = first_gain[0].astype(jnp.float32)
    shift_one = first_bias[0].astype(jnp.float32)
    triple_w = triple_weight[0]
    query_shift = query_bias[0].astype(jnp.float32)
    value_shift = value_bias[0].astype(jnp.float32)
    output_w = output_weight[0]
    output_shift = output_bias[0].astype(jnp.float32)
    gain_two = second_gain[0].astype(jnp.float32)
    shift_two = second_bias[0].astype(jnp.float32)
    expand_w = expand_weight[0]
    expand_shift = expand_bias[0].astype(jnp.float32)
    shrink_w = shrink_weight[0]
    shrink_shift = shrink_bias[0].astype(jnp.float32)
    inputs = tokens[0].reshape(token_count, features).astype(jnp.float32)
    normed_a, spread_a = layer_stats(inputs)
    normed_one = (normed_a * gain_one + shift_one).astype(jnp.bfloat16)
    triple = jnp.dot(normed_one, triple_w, preferred_element_type=jnp.float32)
    queries = (triple[:, :features] + query_shift).astype(jnp.bfloat16).reshape(head_shape)
    key_heads = triple[:, features : 2 * features].astype(jnp.bfloat16).reshape(head_shape)
    value_heads = (triple[:, 2 * features :] + value_shift).astype(jnp.bfloat16).reshape(head_shape)
    scores = masked_scores(queries, key_heads, same_seg)
    row_peak = jnp.max(scores, axis=-1, keepdims=True)
    log_total = row_peak + jnp.log(jnp.sum(jnp.exp(scores - row_peak), axis=-1, keepdims=True))
    attn_probs = jnp.exp(scores - log_total)
    mixed_low = (
        jnp.einsum(
            "rhqk,rkhc->rqhc",
            attn_probs.astype(jnp.bfloat16),
            value_heads,
            preferred_element_type=jnp.float32,
        )
        .reshape(token_count, features)
        .astype(jnp.bfloat16)
    )
    hidden = (
        inputs + jnp.dot(mixed_low, output_w, preferred_element_type=jnp.float32) + output_shift
    )
    normed_b, spread_b = layer_stats(hidden)
    normed_two = (normed_b * gain_two + shift_two).astype(jnp.bfloat16)
    expanded = jnp.dot(normed_two, expand_w, preferred_element_type=jnp.float32) + expand_shift
    activated, gelu_back = jax.vjp(jax.nn.gelu, expanded)
    active_low = activated.astype(jnp.bfloat16)
    block_out = (
        hidden + jnp.dot(active_low, shrink_w, preferred_element_type=jnp.float32) + shrink_shift
    )
    slot_ids = jnp.arange(CAPS, dtype=jnp.int32)
    member = (seg_ids[:, None, :] == slot_ids[None, :, None]).astype(jnp.float32)
    counts = jnp.maximum(jnp.sum(member, axis=2), 1.0)
    pooled = (
        jnp.einsum(
            "rst,rtd->rsd", member, block_out.reshape(rows_here, length, features), precision=HIGH
        )
        / counts[:, :, None]
    )
    inverse = lax.rsqrt(jnp.sum(pooled * pooled, axis=2, keepdims=True) + 1e-06)
    embedding = pooled * inverse
    first_slot = embedding[:, 0, :].astype(jnp.bfloat16)
    collected = lax.all_gather(first_slot, "dp", axis=0, tiled=True)
    image_table = shifted(collected, "tower", 1)
    text_low = embedding.reshape(rows_here * CAPS, features).astype(jnp.bfloat16)
    similar = jnp.einsum("cd,id->ci", text_low, image_table, preferred_element_type=jnp.float32)
    factor = logit_scale[0]
    logits = factor * similar
    logit_peak = jnp.max(logits, axis=1, keepdims=True)
    logit_total = logit_peak + jnp.log(jnp.sum(jnp.exp(logits - logit_peak), axis=1, keepdims=True))
    targets = caption_image.reshape(-1)
    image_ids = jnp.arange(image_table.shape[0], dtype=jnp.int32)
    target_hot = (image_ids[None, :] == targets[:, None]).astype(jnp.float32)
    picked = jnp.sum(logits * target_hot, axis=1)
    loss_here = jnp.sum(logit_total[:, 0] - picked) * text_flag
    grad_logits = (jnp.exp(logits - logit_total) - target_hot) * text_flag
    factor_here = jnp.sum(grad_logits * similar)
    loss_total, factor_total = lax.psum((loss_here, factor_here), ("tower", "dp"))
    caption_total = rows_here * CAPS * lax.axis_size("dp")
    grad_dots = (factor * grad_logits).astype(jnp.bfloat16)
    grad_emb = jnp.einsum(
        "ci,id->cd", grad_dots, image_table, preferred_element_type=jnp.float32
    ).reshape(rows_here, CAPS, features)
    grad_pooled = inverse * (
        grad_emb - embedding * jnp.sum(embedding * grad_emb, axis=2, keepdims=True)
    )
    grad_pooled = grad_pooled / counts[:, :, None]
    grad_out = jnp.einsum("rst,rsd->rtd", member, grad_pooled, precision=HIGH).reshape(
        token_count, features
    )
    shrink_bias_grad = jnp.sum(grad_out, axis=0)
    grad_out_low = grad_out.astype(jnp.bfloat16)
    shrink_weight_grad = jnp.einsum(
        "nf,nd->fd", active_low, grad_out_low, preferred_element_type=jnp.float32
    )
    grad_active = jnp.einsum(
        "nd,fd->nf", grad_out_low, shrink_w, preferred_element_type=jnp.float32
    )
    grad_expanded = gelu_back(grad_active)[0]
    expand_bias_grad = jnp.sum(grad_expanded, axis=0)
    grad_expanded_low = grad_expanded.astype(jnp.bfloat16)
    expand_weight_grad = jnp.einsum(
        "nd,nf->df", normed_two, grad_expanded_low, preferred_element_type=jnp.float32
    )
    grad_normed_two = jnp.einsum(
        "nf,df->nd", grad_expanded_low, expand_w, preferred_element_type=jnp.float32
    )
    second_gain_grad = jnp.sum(grad_normed_two * normed_b, axis=0)
    second_bias_grad = jnp.sum(grad_normed_two, axis=0)
    grad_hidden = grad_out + norm_back(grad_normed_two * gain_two, normed_b, spread_b)
    output_bias_grad = jnp.sum(grad_hidden, axis=0)
    grad_hidden_low = grad_hidden.astype(jnp.bfloat16)
    output_weight_grad = jnp.einsum(
        "nd,ne->de", mixed_low, grad_hidden_low, preferred_element_type=jnp.float32
    )
    grad_mixed = (
        jnp.einsum("ne,de->nd", grad_hidden_low, output_w, preferred_element_type=jnp.float32)
        .astype(jnp.bfloat16)
        .reshape(head_shape)
    )
    scores_again = masked_scores(queries, key_heads, same_seg)
    probs_again = jnp.exp(scores_again - log_total)
    probs_low = probs_again.astype(jnp.bfloat16)
    grad_values = jnp.einsum(
        "rhqk,rqhc->rkhc", probs_low, grad_mixed, preferred_element_type=jnp.float32
    )
    grad_probs = jnp.einsum(
        "rqhc,rkhc->rhqk", grad_mixed, value_heads, preferred_element_type=jnp.float32
    )
    grad_scores = (
        probs_again * (grad_probs - jnp.sum(probs_again * grad_probs, axis=-1, keepdims=True))
    ).astype(jnp.bfloat16)
    grad_queries = (
        jnp.einsum("rhqk,rkhc->rqhc", grad_scores, key_heads, preferred_element_type=jnp.float32)
        * 0.125
    )
    grad_keys = (
        jnp.einsum("rhqk,rqhc->rkhc", grad_scores, queries, preferred_element_type=jnp.float32)
        * 0.125
    )
    grad_queries = grad_queries.reshape(token_count, features)
    grad_keys = grad_keys.reshape(token_count, features)
    grad_values = grad_values.reshape(token_count, features)
    query_bias_grad = jnp.sum(grad_queries, axis=0)
    value_bias_grad = jnp.sum(grad_values, axis=0)
    grad_triple = jnp.concatenate([grad_queries, grad_keys, grad_values], axis=1).astype(
        jnp.bfloat16
    )
    triple_weight_grad = jnp.einsum(
        "nd,ne->de", normed_one, grad_triple, preferred_element_type=jnp.float32
    )
    grad_normed_one = jnp.einsum(
        "ne,de->nd", grad_triple, triple_w, preferred_element_type=jnp.float32
    )
    first_gain_grad = jnp.sum(grad_normed_one * normed_a, axis=0)
    first_bias_grad = jnp.sum(grad_normed_one, axis=0)
    input_grad = grad_hidden + norm_back(grad_normed_one * gain_one, normed_a, spread_a)
    shares = sum_grads(
        (
            first_gain_grad,
            first_bias_grad,
            triple_weight_grad,
            query_bias_grad,
            value_bias_grad,
            output_weight_grad,
            output_bias_grad,
            second_gain_grad,
            second_bias_grad,
            expand_weight_grad,
            expand_bias_grad,
            shrink_weight_grad,
            shrink_bias_grad,
        )
    )
    loss_out = (loss_total / caption_total).reshape(1)
    factor_out = factor_total.reshape(1)
    return (
        loss_out,
        factor_out,
        input_grad.reshape(1, rows_here, length, features),
        shares[0],
        shares[1],
        shares[2],
        shares[3],
        shares[4],
        shares[5],
        shares[6],
        shares[7],
        shares[8],
        shares[9],
        shares[10],
        shares[11],
        shares[12],
    )


def solution(mesh):
    placed = (
        P("tower", "dp", None, None),
        P("dp", None),
        P("dp", None),
        P(),
        P("tower", None),
        P("tower", None),
        P("tower", None, None),
        P("tower", None),
        P("tower", None),
        P("tower", None, None),
        P("tower", None),
        P("tower", None),
        P("tower", None),
        P("tower", None, None),
        P("tower", None),
        P("tower", None, None),
        P("tower", None),
    )
    fits = mesh.shape["tower"] == 2 and mesh.shape["dp"] == 2 * PLANE
    return jax.shard_map(
        local_fast if fits else local,
        mesh=mesh,
        in_specs=placed,
        out_specs=(
            P(),
            P(),
            P("tower", "dp", None, None),
            P(("tower", "dp")),
            P(("tower", "dp")),
            P(("tower", "dp"), None),
            P(("tower", "dp")),
            P(("tower", "dp")),
            P(("tower", "dp"), None),
            P(("tower", "dp")),
            P(("tower", "dp")),
            P(("tower", "dp")),
            P(("tower", "dp"), None),
            P(("tower", "dp")),
            P(("tower", "dp"), None),
            P(("tower", "dp")),
        ),
        check_vma=False,
    )
```

```python
import functools

import jax
import jax.numpy as jnp
from jax import lax
from jax.experimental import pallas as pl
from jax.experimental.pallas import tpu as pltpu
from jax.sharding import PartitionSpec as P

HEADS = 12
IMG_TOK = 50
CAPS = 4

f32, bf16 = jnp.float32, jnp.bfloat16
GELU_C = 0.7978845608028654
GELU_A = 0.044715
STEP_ROWS = 4
MESH = pl.DeviceIdType.MESH


def mm(a, b):
    return jnp.dot(a, b, preferred_element_type=f32)


def mm_nt(a, b):
    return lax.dot_general(a, b, (((1,), (1,)), ((), ())), preferred_element_type=f32)


def mm_tn(a, b):
    return lax.dot_general(a, b, (((0,), (0,)), ((), ())), preferred_element_type=f32)


def stats(x):
    center = x - jnp.mean(x, axis=-1, keepdims=True)
    spread = lax.rsqrt(jnp.mean(center * center, axis=-1, keepdims=True) + 1e-05)
    return center * spread, spread


def split(x, first):
    zero = jnp.zeros_like(x)
    return jnp.concatenate([jnp.where(first, x, zero), jnp.where(first, zero, x)], axis=0)


def low_pair(x):
    high = x.astype(bf16)
    return high, (x - high.astype(f32)).astype(bf16)


def fwd_kernel(tok, seg, g1, b1, qb, vb, ob, g2, b2, eb, sb, w3h, woh, weh, wsh,
               qkv_h, probs_h, mixed_h, normed_h, sums_out, slope_h, n1_h, n2_h, spread_out, member_out, pooled_out, count_out, table_out,
               w3, wo, we, ws, pool_acc, count_acc, act_sum, imgs, elow,
               qkv_b, probs_b, mixed_b, normed_b, slope_b, n1_b, n2_b, sems, gsem, esem, osem):
    i = pl.program_id(0)
    steps = pl.num_programs(0)
    rows_here, length = seg.shape
    slots = rows_here * CAPS
    feat = tok.shape[1]
    block = tok.shape[0]
    is_text = lax.axis_index("tower") == 1
    copies = [pltpu.make_async_copy(src, dst, sems.at[n])
              for n, (src, dst) in enumerate(((w3h, w3), (woh, wo), (weh, we), (wsh, ws)))]

    tower, d = lax.axis_index("tower"), lax.axis_index("dp")
    chip, core = d // 2, lax.rem(d, 2)
    other = 1 - core
    partner = (tower, chip * 2 + other)
    chips = imgs.shape[1]
    facing = [(1 - tower, lax.rem(chip + k, chips) * 2 + core) for k in range(chips)]

    def remote(src, dst, sem, dev):
        return pltpu.make_async_remote_copy(src_ref=src, dst_ref=dst, send_sem=sem.at[0], recv_sem=sem.at[1],
                                            device_id=dev, device_id_type=MESH)

    slot = lax.rem(i, 2)
    saved = ((qkv_b, qkv_h), (probs_b, probs_h), (mixed_b, mixed_h), (normed_b, normed_h), (slope_b, slope_h),
             (n1_b, n1_h), (n2_b, n2_h))
    qkv, probs, mixed, normed_out, slope, n1_out, n2_out = (buf.at[slot] for buf, _ in saved)

    def save(n, step):
        buf, out = saved[n]
        at = lax.rem(step, 2)
        return pltpu.make_async_copy(buf.at[at], out.at[pl.ds(pl.multiple_of(step * block, block), block)],
                                     osem.at[at, n])

    def leave(*which):
        for n in which:
            save(n, i).start()

    @pl.when(is_text & (i >= 2))
    def _():
        for n in range(len(saved)):
            save(n, i - 2).wait()

    barrier = pltpu.get_barrier_semaphore()

    @pl.when(i == 0)
    def _():
        copies[0].start()
        copies[1].start()
        for dev in facing + [partner]:
            pl.semaphore_signal(barrier, inc=1, device_id=dev, device_id_type=MESH)
        pool_acc[...] = jnp.zeros_like(pool_acc)
        count_acc[...] = jnp.zeros_like(count_acc)
        act_sum[...] = jnp.zeros_like(act_sum)

    def arrive(n):
        @pl.when(i == 0)
        def _():
            copies[n].wait()

    tile = 768
    width = we.shape[1]
    hps = range(HEADS // 2)

    def text_segments(pair):
        base = STEP_ROWS * i + 2 * pair
        keyed = jnp.concatenate([seg[pl.ds(base + r, 1), :] * rows_here + (base + r) for r in range(2)], axis=1)
        across = jnp.broadcast_to(keyed.astype(f32), (128, 128))
        return keyed, jnp.where(across == across.T, 0.0, -1e30)

    def image_place(index, per_row, first_row):
        row = jnp.zeros_like(index)
        for r in range(1, STEP_ROWS):
            row = row + (index >= r * per_row).astype(jnp.int32)
        behind = (index - row * per_row >= IMG_TOK).astype(jnp.int32)
        return behind * rows_here + row + first_row

    def run(keep):
        per_row = length if keep else -(-IMG_TOK // 8) * 8
        both = 2 * per_row
        count = STEP_ROWS * per_row
        if keep:
            x = tok[...].astype(f32)
        else:
            x = jnp.concatenate([tok[length * r:length * r + per_row, :].astype(f32) for r in range(STEP_ROWS)], axis=0)
        norm, _ = stats(x)
        n1 = (norm * g1[...].astype(f32) + b1[...].astype(f32)).astype(bf16)
        if keep:
            n1_out[...] = n1
            leave(5)
        arrive(0)

        @pl.when(i == 0)
        def _():
            copies[2].start()
            copies[3].start()
        qkv[:count, :feat] = (mm(n1, w3[:, :feat]) + qb[...].astype(f32)).astype(bf16)
        qkv[:count, feat:2 * feat] = mm(n1, w3[:, feat:2 * feat]).astype(bf16)
        qkv[:count, 2 * feat:] = (mm(n1, w3[:, 2 * feat:]) + vb[...].astype(f32)).astype(bf16)
        if keep:
            leave(0)
        first_half = lax.broadcasted_iota(jnp.int32, (both, 128), 1) < 64
        slot_lanes = []
        for pair in range(STEP_ROWS // 2):
            if keep:
                keyed, bias = text_segments(pair)
                slot_lanes.append(keyed)
                bias = jnp.concatenate([bias, bias], axis=1)
            else:
                down = lax.broadcasted_iota(jnp.int32, (both, 2 * both), 0)
                over = lax.broadcasted_iota(jnp.int32, (both, 2 * both), 1)
                over = jnp.where(over >= both, over - both, over)
                bias = jnp.where(image_place(down, per_row, 0) == image_place(over, per_row, 0), 0.0, -1e30)
            here = slice(pair * both, (pair + 1) * both)
            scores = [mm_nt(qkv[here, feat + 128 * h:feat + 128 * h + 128],
                            split(qkv[here, 128 * h:128 * h + 128] * jnp.asarray(0.125, bf16), first_half)) + bias
                      for h in hps]
            lows = []
            for h in hps:
                e = jnp.exp(scores[h] - jnp.max(scores[h], axis=0, keepdims=True))
                p = (e * (1.0 / jnp.sum(e, axis=0, keepdims=True))).astype(bf16)
                if keep:
                    probs[here, 256 * h:256 * h + 256] = p
                lows.append(p)
            for h in hps:
                o = mm_tn(lows[h], qkv[here, 2 * feat + 128 * h:2 * feat + 128 * h + 128])
                mixed[here, 128 * h:128 * h + 128] = jnp.where(first_half, o[:both], o[both:]).astype(bf16)
        arrive(1)
        hid = x + mm(mixed[:count, :], wo[...]) + ob[...].astype(f32)
        norm2, spread2 = stats(hid)
        n2 = (norm2 * g2[...].astype(f32) + b2[...].astype(f32)).astype(bf16)
        if keep:
            normed_out[...] = norm2
            spread_out[...] = spread2
            n2_out[...] = n2
            leave(1, 2, 3, 6)
            slot_row = jnp.concatenate(slot_lanes, axis=1)
        else:
            slot_row = image_place(lax.broadcasted_iota(jnp.int32, (1, count), 1), per_row, STEP_ROWS * i)
        hot = (lax.broadcasted_iota(jnp.int32, (slots, count), 0) == slot_row)
        member = hot.astype(f32).astype(bf16)
        if keep:
            member_out[...] = member
            placed = (lax.broadcasted_iota(jnp.int32, (2 * slots, count), 0) == slot_row + slots * core)
            placed = placed.astype(f32).astype(bf16)
        arrive(2)
        arrive(3)
        out = hid + sb[...].astype(f32)
        ahead = mm(n2, we[:, :tile])
        for f in range(0, width, tile):
            v = ahead + eb[:, f:f + tile].astype(f32)
            if f + tile < width:
                ahead = mm(n2, we[:, f + tile:f + 2 * tile])
            v2 = v * v
            cv = v * GELU_C
            h = 0.5 + 0.5 * jnp.tanh(cv * (1.0 + GELU_A * v2))
            a = (v * h).astype(bf16)
            if keep:
                act_sum[:, f:f + tile] += mm(placed, a)
                slope[:, f:f + tile] = (h + h * (1.0 - h) * ((2.0 * cv) * (1.0 + (3.0 * GELU_A) * v2))).astype(bf16)
            out = out + mm(a, ws[f:f + tile, :])
        if keep:
            leave(4)
        out_hi, out_lo = low_pair(out)
        pool_acc[...] += mm(member, out_hi) + mm(member, out_lo)
        count_acc[...] += jnp.broadcast_to(jnp.sum(hot.astype(f32), axis=1, keepdims=True), count_acc.shape)

    pl.when(is_text)(functools.partial(run, True))
    pl.when(tower == 0)(functools.partial(run, False))

    @pl.when(i == steps - 1)
    def _():
        counts = jnp.maximum(count_acc[...], 1.0)
        pooled = pool_acc[...] / counts[:, :1]
        count_out[...] = counts
        pooled_out[...] = pooled
        pl.semaphore_wait(barrier, chips + 1)

        @pl.when(tower == 0)
        def _():
            first = pooled[:rows_here]
            elow[...] = (first * lax.rsqrt(jnp.sum(first * first, axis=1, keepdims=True) + 1e-06)).astype(bf16)
            for dev in facing:
                remote(elow, imgs.at[core, chip], gsem, dev).start()
            remote(imgs.at[0], imgs.at[0], gsem, partner).wait_send()

        @pl.when(tower == 1)
        def _():
            for f in range(0, width, tile):
                sums_out[f:f + tile, :] = act_sum[:, f:f + tile].astype(bf16).T
            remote(imgs.at[core], imgs.at[core], gsem, partner).wait_recv()
            remote(imgs.at[core], imgs.at[core], esem, partner).start()
            remote(imgs.at[other], imgs.at[other], esem, partner).wait()
            table_out[...] = imgs[...]
            for n in range(len(saved)):
                save(n, i - 1).wait()
                save(n, i).wait()


def forward(tokens, segments, g1, b1, w3, qb, vb, wo, ob, g2, b2, we, eb, ws, sb):
    count, feat = tokens.shape
    rows_here, length = segments.shape
    slots = rows_here * CAPS
    ff = we.shape[1]
    block = STEP_ROWS * length
    steps = count // block
    table = (2, lax.axis_size("dp") // 2, rows_here, feat)
    whole = lambda a: pl.BlockSpec(a.shape, lambda i: (0,) * a.ndim)
    rows = lambda width: pl.BlockSpec((block, width), lambda i: (i, 0))
    anyw = pl.BlockSpec(memory_space=pl.ANY)
    smalls = (g1, b1, qb, vb, ob, g2, b2, eb, sb)
    return pl.pallas_call(
        fwd_kernel,
        grid=(steps,),
        in_specs=[rows(feat), whole(segments)] + [whole(a) for a in smalls] + [anyw] * 4,
        out_specs=[anyw] * 4 + [pl.BlockSpec((ff, 2 * slots), lambda i: (0, 0))] + [anyw] * 3 + [
                   rows(1),
                   pl.BlockSpec((slots, block), lambda i: (0, i)),
                   pl.BlockSpec((slots, feat), lambda i: (0, 0)),
                   pl.BlockSpec((slots, 128), lambda i: (0, 0)),
                   pl.BlockSpec(table, lambda i: (0,) * 4)],
        out_shape=[jax.ShapeDtypeStruct((count, 3 * feat), bf16),
                   jax.ShapeDtypeStruct((count, 2 * feat), bf16),
                   jax.ShapeDtypeStruct((count, feat), bf16),
                   jax.ShapeDtypeStruct((count, feat), f32),
                   jax.ShapeDtypeStruct((ff, 2 * slots), bf16),
                   jax.ShapeDtypeStruct((count, ff), bf16),
                   jax.ShapeDtypeStruct((count, feat), bf16),
                   jax.ShapeDtypeStruct((count, feat), bf16),
                   jax.ShapeDtypeStruct((count, 1), f32),
                   jax.ShapeDtypeStruct((slots, count), bf16),
                   jax.ShapeDtypeStruct((slots, feat), f32),
                   jax.ShapeDtypeStruct((slots, 128), f32),
                   jax.ShapeDtypeStruct(table, bf16)],
        scratch_shapes=[pltpu.VMEM(w3.shape, bf16), pltpu.VMEM(wo.shape, bf16), pltpu.VMEM(we.shape, bf16),
                        pltpu.VMEM(ws.shape, bf16), pltpu.VMEM((slots, feat), f32), pltpu.VMEM((slots, 128), f32), pltpu.VMEM((2 * slots, ff), f32),
                        pltpu.VMEM(table, bf16), pltpu.VMEM((rows_here, feat), bf16),
                        pltpu.VMEM((2, block, 3 * feat), bf16), pltpu.VMEM((2, block, 2 * feat), bf16),
                        pltpu.VMEM((2, block, feat), bf16), pltpu.VMEM((2, block, feat), f32),
                        pltpu.VMEM((2, block, ff), bf16), pltpu.VMEM((2, block, feat), bf16),
                        pltpu.VMEM((2, block, feat), bf16),
                        pltpu.SemaphoreType.DMA((4,)), pltpu.SemaphoreType.DMA((2,)), pltpu.SemaphoreType.DMA((2,)),
                        pltpu.SemaphoreType.DMA((2, 7))],
        compiler_params=pltpu.CompilerParams(vmem_limit_bytes=56 << 20, dimension_semantics=("arbitrary",),
                                             collective_id=1, has_side_effects=True),
        name="fwd",
    )(tokens, segments, *smalls, w3, wo, we, ws)


PLANE = 8
LINE = 4
BLK = 256
CH = 768
HALF = CH // 2
ROWS = HALF // PLANE
N_CH = 8
WIDE = (0, 2, 4, 7)
LONG = (1, 3, 5)
DEEP = (6,)
TEXT_PLAN = {
    ("ga", 1): (("cross",), ("leave", 0),),
    ("ga", 2): (("leave", 1),),
    ("ew", 2): (("mid", 0),),
    ("ga", 3): (("leave", 2),),
    "ow": (("mid", 1), ("leave", 3),),
    ("attn", 0): (("mid", 2), ("leave", 4),),
    ("attn", 5): (("share",),),
    ("tw", 0): (("mid", 3), ("rows",), ("finish", 0),),
    ("tw", 1): (("leave", 5),),
    ("tw", 2): (("mid", 4), ("finish", 1),),
    ("gn1", 0): (("leave", 6),),
    ("gn1", 1): (("finish", 2), ("leave", 7),),
    ("gn1", 3): (("finish", 3), ("mid", 5),),
    "end": (("mid", 6), ("mid", 7), ("finish", 6), ("finish", 4), ("finish", 5), ("finish", 7),),
}
IMAGE_PLAN = (
    ("over", 0), ("mid", 0), ("over", 2), ("over", 1), ("mid", 2), ("finish", 0), ("over", 4), ("over", 3), ("finish", 1), ("mid", 4), ("finish", 2), ("over", 7), ("over", 5), ("rows",), ("finish", 3), ("finish", 4), ("mid", 7), ("finish", 5), ("take", 6), ("finish", 7),
)
WIDE_AT = {q: n for n, q in enumerate(WIDE)}
LONG_AT = {q: n for n, q in enumerate(LONG + DEEP)}
DEEP_AT = {q: n for n, q in enumerate(DEEP)}


def fold(x):
    return jnp.sum(x.reshape(x.shape[0] // 8, 8, x.shape[1]), axis=0)


def bwd_kernel(member, pooled, count, imgs, act_sums, caption, scale, g1, b1, g2, b2,
               qkv_h, probs_h, mixed_h, normed_h, slope_h, n1_h, n2_h, spread_h, tok_h, w3_h, wo_h, we_h, ws_h,
               tw_out, ow_out, ew_out, sw_out, in_out, vec_out,
               cs, snd, prv, own, ylong, ywide, zrcv, zdeep, xfin, fin, apair, asum, aall, gpall, swfin, xsw,
               gol, gn2, hid, spread2, n2b, tok, mixed, probs, slope, ws, we, ge, qkv, w3, wo,
               ebsum, attn_sum, vec, vown, vpair, vrcv,
               ld, psend, precv, xsend, xrecv, ysend, yrecv, zsend, zrecv,
               fsem, asem, gsem, swsem, vpsem, vsem, outsem):
    t = lax.axis_index("tower")
    d = lax.axis_index("dp")
    p = d // 2
    c = lax.rem(d, 2)
    z = p // 2
    y = lax.rem(p, 2)
    is_text = t == 1
    count_t = gol.shape[0]
    blocks = count_t // BLK
    feat = CH
    rows_here = caption.shape[1]
    other = 1 - c

    def peer(k):
        return lax.rem(p + k, PLANE)

    def at_core(tt, pp):
        return (tt, pp * 2 + c)

    partner = (t, p * 2 + other)
    beside = at_core(t, 2 * z + (1 - y))
    across = at_core(1 - t, p)

    def remote(src, dst, ssem, rsem, dev):
        return pltpu.make_async_remote_copy(src_ref=src, dst_ref=dst, send_sem=ssem, recv_sem=rsem,
                                            device_id=dev, device_id_type=MESH)

    barrier = pltpu.get_barrier_semaphore()
    pl.semaphore_signal(barrier, inc=1, device_id=partner, device_id_type=MESH)
    pl.semaphore_signal(barrier, inc=1, device_id=across, device_id_type=MESH)
    for k in range(1, PLANE):
        pl.semaphore_signal(barrier, inc=1, device_id=at_core(t, peer(k)), device_id_type=MESH)
        pl.semaphore_signal(barrier, inc=1, device_id=at_core(1 - t, peer(k)), device_id_type=MESH)

    pooled_v = pooled[...]
    inverse = lax.rsqrt(jnp.sum(pooled_v * pooled_v, axis=1, keepdims=True) + 1e-06)
    emb = pooled_v * inverse
    emb_low = emb.astype(bf16)

    def pair_copy(q):
        slot = lax.rem(q, 2)
        return remote(snd.at[slot], prv.at[q], psend.at[slot], precv.at[q], partner)

    def x_all(q):
        return remote(cs.at[q, 0:LINE], cs.at[q, 0:LINE], xsend.at[q], xrecv.at[q], across)

    def x_line(q):
        return remote(cs.at[q, 0:LINE, y], cs.at[q, 0:LINE, y], xsend.at[q], xrecv.at[q], across)

    def x_sum(q):
        n = DEEP_AT[q]
        return remote(xfin.at[n], xfin.at[n], xsend.at[q], xrecv.at[q], across)

    def x_copy(q):
        return x_all(q) if q in WIDE else x_line(q) if q in LONG else x_sum(q)

    def y_copy(q):
        if q not in WIDE:
            src, dst = cs.at[q, :, 1 - y], ylong.at[LONG_AT[q]]
        else:
            src, dst = cs.at[q, pl.ds(LINE * t, LINE), 1 - y], ywide.at[WIDE_AT[q]]
        return remote(src, dst, ysend.at[q], yrecv.at[q], beside)

    def z_start(q):
        for k in range(1, LINE):
            to = lax.rem(z + k, LINE)
            remote(cs.at[q, LINE * t + to, y], zrcv.at[q, k - 1], zsend.at[q], zrecv.at[q],
                   at_core(t, 2 * to + y)).start()
            if q in DEEP:
                remote(cs.at[q, to, y], zdeep.at[DEEP_AT[q], k - 1], zsend.at[N_CH + DEEP_AT[q]],
                       zrecv.at[N_CH + DEEP_AT[q]], at_core(t, 2 * to + y)).start()

    def z_all(q):
        return remote(zrcv.at[q], zrcv.at[q], zsend.at[q], zrecv.at[q], partner)

    def z_deep(q):
        n = DEEP_AT[q]
        return remote(zdeep.at[n], zdeep.at[n], zsend.at[N_CH + n], zrecv.at[N_CH + n], partner)

    def mid(q):
        y_copy(q).wait_recv()
        if q not in WIDE:
            for a in range(PLANE):
                cs[q, a, y] = (cs[q, a, y].astype(f32) + ylong[LONG_AT[q], a].astype(f32)).astype(bf16)
            if q in LONG:
                x_line(q).start()
        else:
            for a in range(LINE):
                at = LINE * t + a
                cs[q, at, y] = (cs[q, at, y].astype(f32) + ywide[WIDE_AT[q], a].astype(f32)).astype(bf16)
        z_start(q)

    def a_pair():
        return remote(act_sums.at[:, :, other], apair, asem.at[0], asem.at[1], partner)

    def a_start():
        a_pair().wait_recv()
        asum[...] = act_sums[:, :, c] + apair[...]
        aall[:, :, pl.ds(pl.multiple_of(128 * p, 128), 128)] = asum[:, p]
        for k in range(1, PLANE):
            remote(asum.at[:, peer(k)], aall.at[:, :, pl.ds(pl.multiple_of(128 * p, 128), 128)],
                   asem.at[2], asem.at[3], at_core(t, peer(k))).start()

    def a_all():
        every = asum.at[:, 0:PLANE - 1]
        return remote(every, every, asem.at[2], asem.at[3], partner)

    def gp_beside():
        return remote(gpall.at[p, c], gpall.at[p, c], gsem.at[0], gsem.at[1], beside)

    def gp_line():
        gp_beside().wait_recv()
        for k in range(1, LINE):
            mine = gpall.at[pl.ds(2 * z, 2), c]
            remote(mine, mine, gsem.at[2], gsem.at[3], at_core(t, 2 * lax.rem(z + k, LINE) + y)).start()

    def gp_line_all():
        every = gpall.at[0:2 * (LINE - 1), 0]
        return remote(every, every, gsem.at[2], gsem.at[3], partner)

    def gp_share_copy():
        return remote(gpall.at[:, c], gpall.at[:, c], gsem.at[4], gsem.at[5], partner)

    def gp_share():
        gp_line_all().wait_recv()
        gp_share_copy().start()

    def sw_across():
        return remote(xsw, xsw, swsem.at[0], swsem.at[1], across)

    def sw_keep():
        return pltpu.make_async_copy(swfin, sw_out, swsem.at[2])

    def shrink():
        gp_share_copy().wait_recv()
        a_all().wait_recv()
        rows = gpall[...].reshape(-1, feat)
        xsw[...] = mm(aall[0], rows).astype(bf16)
        sw_across().start()
        swfin[...] = mm(aall[1], rows)
        sw_keep().start()

    half_rows = ROWS // 2

    def place(q):
        if q < 4:
            return ew_out, 4 * HALF * c + HALF * q
        if q == 4:
            return ow_out, HALF * c
        return tw_out, CH * (q - 5) + HALF * c

    def keep(q):
        out, col = place(q)
        return pltpu.make_async_copy(fin.at[q, pl.ds(pl.multiple_of(half_rows * c, 8), half_rows)],
                                     out.at[:, pl.ds(pl.multiple_of(col, 128), HALF)], fsem.at[0])

    def give(q):
        out, col = place(q)
        return remote(fin.at[q, pl.ds(pl.multiple_of(half_rows * other, 8), half_rows)],
                      out.at[:, pl.ds(pl.multiple_of(col, 128), HALF)], fsem.at[1], fsem.at[2], partner)

    def finish(q):
        z_all(q).wait_recv()
        total = cs[q, LINE * t + z, y].astype(f32)
        for k in range(LINE - 1):
            total = total + zrcv[q, k].astype(f32)
        if q in DEEP:
            z_deep(q).wait_recv()
            theirs = cs[q, z, y].astype(f32)
            for k in range(LINE - 1):
                theirs = theirs + zdeep[DEEP_AT[q], k].astype(f32)
            xfin[DEEP_AT[q]] = theirs.astype(bf16)
            x_sum(q).start()
        fin[q] = total
        keep(q).start()
        give(q).start()

    def take(q):
        x_sum(q).wait_recv()
        fin[q] = xfin[DEEP_AT[q]].astype(f32)
        keep(q).start()
        give(q).start()

    def leave(q):
        chip_sum(q)
        if q in WIDE:
            x_all(q).start()
        y_copy(q).start()

    def chip_sum(q):
        pair_copy(q).wait_recv()
        slot = lax.rem(q, 2)
        n = 2 * ROWS
        for a in range(PLANE):
            total = own[slot, n * a:n * (a + 1), :] + prv[q, n * a:n * (a + 1), :].astype(f32)
            cs[q, a] = total.reshape(2, ROWS, HALF).astype(bf16)

    def chunk(q, left, right):
        slot = lax.rem(q, 2)

        @pl.when(q >= 2)
        def _():
            pair_copy(q - 2).wait_send()
        for r in range(0, CH, 256):
            part = mm_tn(left[:, r:r + 256], right)
            low, high = part[:, :HALF], part[:, HALF:]
            own[slot, r:r + 256, :] = jnp.where(c == 0, low, high)
            snd[slot, r:r + 256, :] = jnp.where(c == 0, high, low).astype(bf16)
        pair_copy(q).start()

    def v_pair():
        return remote(vown.at[other], vpair, vpsem.at[0], vpsem.at[1], partner)

    def load(n, src, dst):
        return pltpu.make_async_copy(src, dst, ld.at[n])

    def tile_loads(i):
        s = lax.rem(i, 2)
        out = []
        ff = slope_h.shape[1]
        for h in range(2):
            col = pl.multiple_of((ff // 2) * h + HALF * i, 128)
            here = pl.ds(HALF * h, HALF)
            out.append(load(6 * s + 3 * h, slope_h.at[:, pl.ds(col, HALF)], slope.at[s, :, here]))
            out.append(load(6 * s + 3 * h + 1, ws_h.at[pl.ds(col, HALF)], ws.at[s, here]))
            out.append(load(6 * s + 3 * h + 2, we_h.at[:, pl.ds(col, HALF)], we.at[s, :, here]))
        return out

    hid_load = load(16, normed_h, hid)
    tok_load = load(17, tok_h, tok)
    qkv_load = load(18, qkv_h, qkv)
    w3_load = load(19, w3_h, w3)
    wo_load = load(20, wo_h, wo)
    n2_load = load(24, n2_h, n2b)
    spread_load = load(25, spread_h, spread2)
    n1_load = load(26, n1_h, slope.at[1])
    mixed_load = load(21, mixed_h, mixed)
    probs_load = load(22, probs_h, probs)

    @pl.when(t == 0)
    def _():
        pl.semaphore_wait(barrier, 2 * PLANE)
        gn2[:BLK, :] = jnp.zeros((BLK, feat), f32)
        for m in range(blocks):
            pltpu.make_async_copy(gn2.at[0:BLK], in_out.at[pl.ds(BLK * m, BLK)], outsem.at[m]).start()

        def over(q):
            x_copy(q).wait_recv()
            if q in WIDE:
                y_copy(q).start()
            else:
                z_start(q)

        def rows_over():
            sw_across().wait_recv()
            swfin[...] = xsw[...].astype(f32)
            sw_keep().start()
        acts = {"over": over, "mid": mid, "finish": finish, "take": take, "rows": rows_over}
        for what, *of in IMAGE_PLAN:
            acts[what](*of)
        for m in range(blocks):
            pltpu.make_async_copy(gn2.at[0:BLK], in_out.at[pl.ds(BLK * m, BLK)], outsem.at[m]).wait()

    @pl.when(is_text)
    def _():
        for cp in tile_loads(0):
            cp.start()
        n2_load.start()
        for cp in tile_loads(1):
            cp.start()
        for cp in (hid_load, spread_load, mixed_load, wo_load, qkv_load, probs_load, w3_load, tok_load):
            cp.start()
        gain2, gain1 = g2[...].astype(f32), g1[...].astype(f32)
        gn2[...] = jnp.zeros_like(gn2)
        attn_sum[...] = jnp.zeros_like(attn_sum)
        vec[...] = jnp.zeros_like(vec)
        pl.semaphore_wait(barrier, 2 * PLANE)
        a_pair().start()

        table = imgs[...].reshape(2 * PLANE * rows_here, feat)
        dots = mm_nt(emb_low, table)
        factor = scale[0]
        logits = factor * dots
        peak = jnp.max(logits, axis=1, keepdims=True)
        weight = jnp.exp(logits - peak)
        total = jnp.sum(weight, axis=1, keepdims=True)
        eye = (lax.broadcasted_iota(jnp.int32, (rows_here, rows_here), 0)
               == lax.broadcasted_iota(jnp.int32, (rows_here, rows_here), 1))
        wanted = jnp.concatenate([jnp.sum(jnp.where(eye, caption[s:s + 1, :], 0), axis=1, keepdims=True)
                                  for s in range(CAPS)], axis=0)
        span = 2 * rows_here
        inside = lax.rem(wanted, span)
        wanted = (inside // rows_here) * (PLANE * rows_here) + (wanted // span) * rows_here + lax.rem(inside, rows_here)
        hot = (lax.broadcasted_iota(jnp.int32, dots.shape, 1) == wanted).astype(f32)
        picked = jnp.sum(logits * hot, axis=1, keepdims=True)
        loss_here = jnp.sum(peak + jnp.log(total) - picked, axis=0, keepdims=True)
        a_start()
        grad_logits = weight / total - hot
        factor_here = jnp.sum(jnp.sum(grad_logits * dots, axis=1, keepdims=True), axis=0, keepdims=True)
        grad_emb = mm((factor * grad_logits).astype(bf16), table)
        counts = count[:, :1]
        grad_pool = inverse * (grad_emb - emb * jnp.sum(emb * grad_emb, axis=1, keepdims=True))
        vec[7:8, :] = jnp.sum(grad_pool, axis=0, keepdims=True)
        column = lax.broadcasted_iota(jnp.int32, (1, feat), 1)
        vec[12:13, :] = jnp.where(column == 0, loss_here, jnp.where(column == 1, factor_here, 0.0))
        gp_hi, gp_lo = low_pair(grad_pool / counts)
        gpall[p, c] = gp_hi
        gp_beside().start()
        for m in range(blocks):
            gol[BLK * m:BLK * (m + 1), :] = mm_tn(member[:, BLK * m:BLK * (m + 1)], gp_hi).astype(bf16)

        acts = {"leave": leave, "mid": mid, "finish": finish, "cross": gp_line, "share": gp_share, "rows": shrink}

        def now(place):
            for what, *of in TEXT_PLAN.get(place, ()):
                acts[what](*of)

        def now_in(loop, index, count):
            for n in range(count):
                if (loop, n) in TEXT_PLAN:
                    pl.when(index == n)(functools.partial(now, (loop, n)))

        @pl.loop(0, 4)
        def _(i):
            s = lax.rem(i, 2)
            for cp in tile_loads(i):
                cp.wait()

            sums = jnp.zeros((8, feat), f32)
            for m in range(blocks):
                here = slice(BLK * m, BLK * (m + 1))
                grad = mm_nt(gol[here, :], ws[s]) * slope[s, here, :].astype(f32)
                sums = sums + fold(grad)
                ge[here, :] = grad.astype(bf16)
            sums = jnp.sum(sums, axis=0, keepdims=True)
            for h in range(2):
                ebsum[:, pl.ds(pl.multiple_of(4 * HALF * h + HALF * i, 128), HALF)] = sums[:, HALF * h:HALF * (h + 1)]
            now_in("ga", i, 4)

            @pl.when(i == 0)
            def _():
                n2_load.wait()
            chunk(i, n2b, ge[...])
            now_in("ew", i, 4)
            for m in range(blocks):
                here = slice(BLK * m, BLK * (m + 1))
                gn2[here, :] += mm_nt(ge[here, :], we[s])
            now_in("gn", i, 4)

            @pl.when(i < 2)
            def _():
                for cp in tile_loads(i + 2):
                    cp.start()
        n1_load.start()
        hid_load.wait()
        spread_load.wait()

        zeros8 = jnp.zeros((8, feat), f32)

        def norm2_back(m, sums):
            here = pl.ds(pl.multiple_of(m * BLK, BLK), BLK)
            norm, g_in = hid[here, :], gn2[here, :]
            hot_m = member[:, here]
            grad_out = mm_tn(hot_m, gp_hi) + mm_tn(hot_m, gp_lo)
            g = g_in * gain2
            back = spread2[here, :] * (g - jnp.mean(g, axis=1, keepdims=True)
                                       - norm * jnp.mean(g * norm, axis=1, keepdims=True))
            gh = grad_out + back
            gn2[here, :] = gh
            gol[here, :] = gh.astype(bf16)
            return (sums[0] + fold(g_in * norm), sums[1] + fold(g_in), sums[2] + fold(gh))
        sums = lax.fori_loop(0, blocks, norm2_back, (zeros8, zeros8, zeros8))
        for row, x in ((5, sums[0]), (6, sums[1]), (4, sums[2])):
            vec[row:row + 1, :] = jnp.sum(x, axis=0, keepdims=True)
        for n in range(4):
            vec[8 + n:9 + n, :] = ebsum[:, feat * n:feat * (n + 1)]
        now("norm")

        mixed_load.wait()
        chunk(4, mixed, gol[...])
        now("ow")
        wo_load.wait()
        for m in range(blocks):
            here = slice(BLK * m, BLK * (m + 1))
            ge[here, :] = mm_nt(gol[here, :], wo[...]).astype(bf16)
        now("gm")

        qkv_load.wait()
        probs_load.wait()
        first_half = lax.broadcasted_iota(jnp.int32, (128, 128), 1) < 64
        hps = range(HEADS // 2)

        @pl.loop(0, count_t // 128)
        def _(rp):
            here = pl.ds(pl.multiple_of(rp * 128, 128), 128)

            def probs_of(h):
                return probs[here, 256 * h:256 * h + 256]

            def part(n, h):
                return qkv[here, feat * n + 128 * h:feat * n + 128 * h + 128]
            gm = [split(ge[here, 128 * h:128 * h + 128], first_half) for h in hps]
            gp = [mm_nt(part(2, h), gm[h]) for h in hps]
            gv = [mm(probs_of(h), gm[h]) for h in hps]
            gs = []
            for h in hps:
                probs_f = probs_of(h).astype(f32)
                weighted = probs_f * gp[h]
                gs.append((weighted - probs_f * jnp.sum(weighted, axis=0, keepdims=True)).astype(bf16))
            gk = [mm(gs[h], split(part(0, h), first_half)) * 0.125 for h in hps]
            gq = []
            for h in hps:
                both = mm_tn(gs[h], part(1, h))
                gq.append(jnp.where(first_half, both[:128], both[128:]) * 0.125)
            for h in hps:
                for n, x in ((0, gq[h]), (1, gk[h]), (2, gv[h])):
                    qkv[here, feat * n + 128 * h:feat * n + 128 * h + 128] = x.astype(bf16)
                for n, x in ((0, gq[h]), (1, gv[h])):
                    attn_sum[:, feat * n + 128 * h:feat * n + 128 * h + 128] += fold(x)

            now_in("attn", rp, count_t // 128)
        vec[2:3, :] = jnp.sum(attn_sum[:, :feat], axis=0, keepdims=True)
        vec[3:4, :] = jnp.sum(attn_sum[:, feat:], axis=0, keepdims=True)

        n1_load.wait()

        @pl.loop(0, 3)
        def _(j):
            chunk(5 + j, slope.at[1], qkv[:, pl.ds(pl.multiple_of(CH * j, 128), CH)])

            now_in("tw", j, 3)
        tok_load.wait()
        w3_load.wait()

        def norm1_back(m, sums):
            here = pl.ds(pl.multiple_of(m * BLK, BLK), BLK)
            g_in = mm_nt(qkv[here, :], w3[...])

            now_in("gn1", m, blocks)
            norm, spread = stats(tok[here, :].astype(f32))
            g = g_in * gain1
            back = spread * (g - jnp.mean(g, axis=1, keepdims=True)
                             - norm * jnp.mean(g * norm, axis=1, keepdims=True))
            gn2[here, :] += back
            pltpu.make_async_copy(gn2.at[here], in_out.at[here], outsem.at[m]).start()
            return (sums[0] + fold(g_in * norm), sums[1] + fold(g_in))
        sums = lax.fori_loop(0, blocks, norm1_back, (zeros8, zeros8))
        for row, x in ((0, sums[0]), (1, sums[1])):
            vec[row:row + 1, :] = jnp.sum(x, axis=0, keepdims=True)

        width, wide = feat // (4 * PLANE), 4 * feat // (4 * PLANE)
        narrow = vec[0:8, :]
        broad = vec[8:16, :]
        scalars = vec[12:13, :128]
        turned = [broad] + [pltpu.roll(broad, feat - wide * j, axis=1) for j in range(1, feat // wide)]
        for g in range(4 * PLANE):
            one = narrow if g == 0 else pltpu.roll(narrow, feat - width * g, axis=1)
            row = g // (feat // wide)
            tail = turned[g % (feat // wide)][row:row + 1, :128]
            vown[g % 2, g // 2, 0:8, :] = one[:, :128]
            vown[g % 2, g // 2, 8:9, :] = tail
            vown[g % 2, g // 2, 9:10, :] = scalars
        v_pair().start()
        now("small")
        for m in range(blocks):
            here = pl.ds(BLK * m, BLK)
            pltpu.make_async_copy(gn2.at[here], in_out.at[here], outsem.at[m]).wait()
        v_pair().wait_recv()
        vown[c] += vpair[...]
        for k in range(PLANE):
            for tt in range(2):
                if tt == 0 or k:
                    remote(vown.at[c, PLANE * tt + peer(k)], vrcv.at[k], vsem.at[0], vsem.at[1],
                           at_core(tt, peer(k))).start()
        now("end")

    @pl.when(is_text)
    def _():
        remote(vrcv.at[1:PLANE], vrcv.at[1:PLANE], vsem.at[0], vsem.at[1], partner).wait_recv()
        total = vown[c, PLANE + p]
        for k in range(1, PLANE):
            total = total + vrcv[k]
        vec_out[...] = total

    @pl.when(t == 0)
    def _():
        remote(vrcv, vrcv, vsem.at[0], vsem.at[1], partner).wait_recv()
        total = vrcv[0]
        for k in range(1, PLANE):
            total = total + vrcv[k]
        vec_out[...] = total

    @pl.when(is_text)
    def _():
        everything = vown.at[0, 0:2 * PLANE - 1]
        remote(everything, everything, vsem.at[0], vsem.at[1], partner).wait_send()
        v_pair().wait_send()
        for q in (N_CH - 2, N_CH - 1):
            pair_copy(q).wait_send()

        for q in range(N_CH):
            x_copy(q).wait_send()
        for q in LONG + DEEP:
            y_copy(q).wait_send()
        for q in DEEP:
            z_deep(q).wait_send()
            z_all(q).wait_send()
        a_pair().wait_send()
        a_all().wait_send()
        gp_beside().wait_send()
        gp_line_all().wait_send()
        gp_share_copy().wait_send()
        sw_across().wait_send()
    for q in WIDE:
        y_copy(q).wait_send()
    for q in WIDE + LONG:
        z_all(q).wait_send()
    sw_keep().wait()
    lower = fin.at[:, 0:half_rows]
    pltpu.make_async_copy(lower, lower, fsem.at[0]).wait()
    remote(lower, lower, fsem.at[1], fsem.at[2], partner).wait()


def backward(member, pooled, count, imgs, sums, caption, scale, g1, b1, g2, b2,
             qkv, probs, mixed, normed, slope, n1, n2, spread, tokens, w3, wo, we, ws):
    n_tok, feat = tokens.shape
    ff = we.shape[1]
    dma = pltpu.SemaphoreType.DMA
    vm = pltpu.VMEM
    vspec = pl.BlockSpec(memory_space=pltpu.VMEM)
    sspec = pl.BlockSpec(memory_space=pltpu.SMEM)
    anyw = pl.BlockSpec(memory_space=pl.ANY)
    shape = jax.ShapeDtypeStruct
    long, wide, deep = len(LONG + DEEP), len(WIDE), len(DEEP)
    apart = sums.shape[:2] + sums.shape[3:]
    slots = member.shape[0]
    scratch = [
        vm((N_CH, PLANE, 2, ROWS, HALF), bf16), vm((2, CH, HALF), bf16), vm((N_CH, CH, HALF), bf16),
        vm((2, CH, HALF), f32),
        vm((max(long, 1), PLANE, ROWS, HALF), bf16), vm((max(wide, 1), LINE, ROWS, HALF), bf16), vm((N_CH, LINE - 1, ROWS, HALF), bf16),
        vm((max(deep, 1), LINE - 1, ROWS, HALF), bf16), vm((max(deep, 1), ROWS, HALF), bf16),
        vm((N_CH, ROWS, HALF), f32), vm(apart, bf16), vm(apart, bf16), vm((2, apart[2], PLANE * 128), bf16),
        vm((PLANE, 2, slots, feat), bf16), vm((2 * ROWS, feat), f32), vm((2 * ROWS, feat), bf16),
        vm((n_tok, feat), bf16), vm((n_tok, feat), f32), vm((n_tok, feat), f32), vm((n_tok, 1), f32),
        vm((n_tok, feat), bf16), vm((n_tok, feat), bf16),
        vm((n_tok, feat), bf16), vm((n_tok, 2 * feat), bf16), vm((2, n_tok, CH), bf16), vm((2, CH, feat), bf16), vm((2, feat, CH), bf16),
        vm((n_tok, feat), bf16), vm((n_tok, 3 * feat), bf16), vm(w3.shape, bf16), vm(wo.shape, bf16),
        vm((1, ff), f32), vm((8, 2 * feat), f32),
        vm((16, feat), f32), vm((2, 2 * PLANE, 16, 128), f32), vm((2 * PLANE, 16, 128), f32), vm((PLANE, 16, 128), f32),
        dma((27,)), dma((2,)), dma((N_CH,)), dma((N_CH,)), dma((N_CH,)), dma((N_CH,)), dma((N_CH,)),
        dma((N_CH + deep,)), dma((N_CH + deep,)), dma((3,)), dma((4,)), dma((6,)), dma((3,)), dma((2,)), dma((2,)),
        dma((n_tok // BLK,)),
    ]
    return pl.pallas_call(
        bwd_kernel,
        in_specs=[vspec] * 6 + [sspec] + [vspec] * 4 + [anyw] * 13,
        out_specs=[anyw] * 5 + [vspec],
        out_shape=[shape((ROWS // 2, 3 * feat), f32), shape((ROWS // 2, feat), f32), shape((ROWS // 2, ff), f32),
                   shape((2 * ROWS, feat), f32), shape((n_tok, feat), f32), shape((16, 128), f32)],
        scratch_shapes=scratch,
        compiler_params=pltpu.CompilerParams(vmem_limit_bytes=61 << 20, collective_id=0, has_side_effects=True),
        name="bwd",
    )(member, pooled, count, imgs, sums, caption, scale, g1, b1, g2, b2,
      qkv, probs, mixed, normed, slope, n1, n2, spread, tokens, w3, wo, we, ws)


def hand_out_kernel(scale_by, vec, *rest):
    bigs, loss, factor, smalls = rest[:5], rest[5], rest[6], rest[7:16]
    outs, held, sem_in, sem_out = rest[16:21], rest[21:26], rest[26], rest[27]
    parts = []
    for src, dst, buf in zip(bigs, outs, held):
        count = max(src.shape[0] // BLK, 1)
        rows = src.shape[0] // count
        for n in range(count):
            parts.append((src.at[rows * n:rows * (n + 1)], buf.at[rows * n:rows * (n + 1)],
                          dst.at[rows * n:rows * (n + 1)]))
    ins = [pltpu.make_async_copy(a, b, sem_in.at[n]) for n, (a, b, _) in enumerate(parts)]
    outs = [pltpu.make_async_copy(b, c, sem_out.at[n]) for n, (_, b, c) in enumerate(parts)]
    for move in ins:
        move.start()
    width, wide = smalls[0].shape[1], smalls[8].shape[1]
    for n in range(8):
        smalls[n][...] = vec[n:n + 1, :width]
    smalls[8][...] = vec[8:9, :wide]
    loss[...] = vec[9:10, 0:1] * scale_by
    factor[...] = vec[9:10, 1:2]
    for first, second in zip(ins, outs):
        first.wait()
        second.start()
    for move in outs:
        move.wait()


def hand_out(vec, tw, ow, ew, sw, inp, captions):
    devices = lax.axis_size("tower") * lax.axis_size("dp")
    bigs = (inp, sw, ew, tw, ow)
    feat = inp.shape[1]
    outs = ([(1, 1)] * 2 + [(1, feat // devices)] * 8 + [(1, ew.shape[1] // devices)]
            + [a.shape for a in bigs])
    moves = 4 + inp.shape[0] // BLK
    vspec = pl.BlockSpec(memory_space=pltpu.VMEM)
    anyw = pl.BlockSpec(memory_space=pl.ANY)
    return pl.pallas_call(
        functools.partial(hand_out_kernel, 1.0 / captions),
        in_specs=[vspec] + [anyw] * 5,
        out_specs=[vspec] * 11 + [anyw] * 5,
        out_shape=[jax.ShapeDtypeStruct(dims, f32) for dims in outs],
        scratch_shapes=[pltpu.VMEM(a.shape, f32) for a in bigs]
        + [pltpu.SemaphoreType.DMA((moves,)), pltpu.SemaphoreType.DMA((moves,))],
        name="hand_out",
    )(vec, *bigs)


def local_fast(tokens, segments, caption_image, logit_scale, first_gain, first_bias, triple_weight, query_bias,
               value_bias, output_weight, output_bias, second_gain, second_bias, expand_weight, expand_bias,
               shrink_weight, shrink_bias):
    rows_here, length, feat = tokens.shape[1:]
    flat = tokens[0].reshape(rows_here * length, feat)
    w3, wo, we, ws = triple_weight[0], output_weight[0], expand_weight[0], shrink_weight[0]
    qkv, probs, mixed, normed, sums, slope, n1, n2, spread, member, pooled, count, table = forward(
        flat, segments, first_gain, first_bias, w3, query_bias, value_bias, wo, output_bias,
        second_gain, second_bias, we, expand_bias, ws, shrink_bias)
    sums = sums.reshape(2, PLANE, 2, sums.shape[0] // (4 * PLANE), sums.shape[1])
    tw, ow, ew, sw, inp, vec = backward(member, pooled, count, table, sums, caption_image.T, logit_scale, first_gain, first_bias,
                                        second_gain, second_bias, qkv, probs, mixed, normed, slope, n1, n2, spread, flat,
                                        w3, wo, we, ws)
    captions = rows_here * CAPS * lax.axis_size("dp")
    outs = hand_out(vec, tw, ow, ew, sw, inp, captions)
    loss, factor = outs[0].reshape(1), outs[1].reshape(1)
    g1, b1, qb, vb, ob, g2, b2, sb, eb = (a.reshape(-1) for a in outs[2:11])
    inp, sw, ew, tw, ow = outs[11:]
    return (loss, factor, inp.reshape(1, rows_here, length, feat), g1, b1, tw, qb, vb, ow, ob, g2, b2, ew, eb, sw, sb)


HIGH = lax.Precision.HIGHEST


def shifted(shard, axis, by):
    peers = lax.axis_size(axis)
    pairs = [(i, i + by) for i in range(peers) if 0 <= i + by < peers]
    return lax.ppermute(shard, axis, pairs)


def layer_stats(values):
    center = values - jnp.mean(values, axis=-1, keepdims=True)
    spread = lax.rsqrt(jnp.mean(center * center, axis=-1, keepdims=True) + 1e-05)
    return (center * spread, spread)


def norm_back(grad_normed, normed, spread):
    return spread * (
        grad_normed
        - jnp.mean(grad_normed, axis=-1, keepdims=True)
        - normed * jnp.mean(grad_normed * normed, axis=-1, keepdims=True)
    )


def masked_scores(queries, key_heads, same_seg):
    raw = (
        jnp.einsum("rqhc,rkhc->rhqk", queries, key_heads, preferred_element_type=jnp.float32)
        * 0.125
    )
    return jnp.where(same_seg, raw, -1e30)


def sum_grads(grads):
    return (
        lax.psum_scatter(grads[0], ("tower", "dp"), scatter_dimension=0, tiled=True),
        lax.psum_scatter(grads[1], ("tower", "dp"), scatter_dimension=0, tiled=True),
        lax.psum_scatter(grads[2], ("tower", "dp"), scatter_dimension=0, tiled=True),
        lax.psum_scatter(grads[3], ("tower", "dp"), scatter_dimension=0, tiled=True),
        lax.psum_scatter(grads[4], ("tower", "dp"), scatter_dimension=0, tiled=True),
        lax.psum_scatter(grads[5], ("tower", "dp"), scatter_dimension=0, tiled=True),
        lax.psum_scatter(grads[6], ("tower", "dp"), scatter_dimension=0, tiled=True),
        lax.psum_scatter(grads[7], ("tower", "dp"), scatter_dimension=0, tiled=True),
        lax.psum_scatter(grads[8], ("tower", "dp"), scatter_dimension=0, tiled=True),
        lax.psum_scatter(grads[9], ("tower", "dp"), scatter_dimension=0, tiled=True),
        lax.psum_scatter(grads[10], ("tower", "dp"), scatter_dimension=0, tiled=True),
        lax.psum_scatter(grads[11], ("tower", "dp"), scatter_dimension=0, tiled=True),
        lax.psum_scatter(grads[12], ("tower", "dp"), scatter_dimension=0, tiled=True),
    )


def local(
    tokens,
    segments,
    caption_image,
    logit_scale,
    first_gain,
    first_bias,
    triple_weight,
    query_bias,
    value_bias,
    output_weight,
    output_bias,
    second_gain,
    second_bias,
    expand_weight,
    expand_bias,
    shrink_weight,
    shrink_bias,
):
    rows_here = tokens.shape[1]
    length = tokens.shape[2]
    features = tokens.shape[3]
    head_size = features // HEADS
    token_count = rows_here * length
    is_text = lax.axis_index("tower") == 1
    text_flag = is_text.astype(jnp.float32)
    position = jnp.arange(length, dtype=jnp.int32)
    image_segs = jnp.broadcast_to(
        (position >= IMG_TOK).astype(jnp.int32)[None, :], (rows_here, length)
    )
    seg_ids = jnp.where(is_text, segments, image_segs)
    same_seg = (seg_ids[:, :, None] == seg_ids[:, None, :])[:, None, :, :]
    head_shape = (rows_here, length, HEADS, head_size)
    gain_one = first_gain[0].astype(jnp.float32)
    shift_one = first_bias[0].astype(jnp.float32)
    triple_w = triple_weight[0]
    query_shift = query_bias[0].astype(jnp.float32)
    value_shift = value_bias[0].astype(jnp.float32)
    output_w = output_weight[0]
    output_shift = output_bias[0].astype(jnp.float32)
    gain_two = second_gain[0].astype(jnp.float32)
    shift_two = second_bias[0].astype(jnp.float32)
    expand_w = expand_weight[0]
    expand_shift = expand_bias[0].astype(jnp.float32)
    shrink_w = shrink_weight[0]
    shrink_shift = shrink_bias[0].astype(jnp.float32)
    inputs = tokens[0].reshape(token_count, features).astype(jnp.float32)
    normed_a, spread_a = layer_stats(inputs)
    normed_one = (normed_a * gain_one + shift_one).astype(jnp.bfloat16)
    triple = jnp.dot(normed_one, triple_w, preferred_element_type=jnp.float32)
    queries = (triple[:, :features] + query_shift).astype(jnp.bfloat16).reshape(head_shape)
    key_heads = triple[:, features : 2 * features].astype(jnp.bfloat16).reshape(head_shape)
    value_heads = (triple[:, 2 * features :] + value_shift).astype(jnp.bfloat16).reshape(head_shape)
    scores = masked_scores(queries, key_heads, same_seg)
    row_peak = jnp.max(scores, axis=-1, keepdims=True)
    log_total = row_peak + jnp.log(jnp.sum(jnp.exp(scores - row_peak), axis=-1, keepdims=True))
    attn_probs = jnp.exp(scores - log_total)
    mixed_low = (
        jnp.einsum(
            "rhqk,rkhc->rqhc",
            attn_probs.astype(jnp.bfloat16),
            value_heads,
            preferred_element_type=jnp.float32,
        )
        .reshape(token_count, features)
        .astype(jnp.bfloat16)
    )
    hidden = (
        inputs + jnp.dot(mixed_low, output_w, preferred_element_type=jnp.float32) + output_shift
    )
    normed_b, spread_b = layer_stats(hidden)
    normed_two = (normed_b * gain_two + shift_two).astype(jnp.bfloat16)
    expanded = jnp.dot(normed_two, expand_w, preferred_element_type=jnp.float32) + expand_shift
    activated, gelu_back = jax.vjp(jax.nn.gelu, expanded)
    active_low = activated.astype(jnp.bfloat16)
    block_out = (
        hidden + jnp.dot(active_low, shrink_w, preferred_element_type=jnp.float32) + shrink_shift
    )
    slot_ids = jnp.arange(CAPS, dtype=jnp.int32)
    member = (seg_ids[:, None, :] == slot_ids[None, :, None]).astype(jnp.float32)
    counts = jnp.maximum(jnp.sum(member, axis=2), 1.0)
    pooled = (
        jnp.einsum(
            "rst,rtd->rsd", member, block_out.reshape(rows_here, length, features), precision=HIGH
        )
        / counts[:, :, None]
    )
    inverse = lax.rsqrt(jnp.sum(pooled * pooled, axis=2, keepdims=True) + 1e-06)
    embedding = pooled * inverse
    first_slot = embedding[:, 0, :].astype(jnp.bfloat16)
    collected = lax.all_gather(first_slot, "dp", axis=0, tiled=True)
    image_table = shifted(collected, "tower", 1)
    text_low = embedding.reshape(rows_here * CAPS, features).astype(jnp.bfloat16)
    similar = jnp.einsum("cd,id->ci", text_low, image_table, preferred_element_type=jnp.float32)
    factor = logit_scale[0]
    logits = factor * similar
    logit_peak = jnp.max(logits, axis=1, keepdims=True)
    logit_total = logit_peak + jnp.log(jnp.sum(jnp.exp(logits - logit_peak), axis=1, keepdims=True))
    targets = caption_image.reshape(-1)
    image_ids = jnp.arange(image_table.shape[0], dtype=jnp.int32)
    target_hot = (image_ids[None, :] == targets[:, None]).astype(jnp.float32)
    picked = jnp.sum(logits * target_hot, axis=1)
    loss_here = jnp.sum(logit_total[:, 0] - picked) * text_flag
    grad_logits = (jnp.exp(logits - logit_total) - target_hot) * text_flag
    factor_here = jnp.sum(grad_logits * similar)
    loss_total, factor_total = lax.psum((loss_here, factor_here), ("tower", "dp"))
    caption_total = rows_here * CAPS * lax.axis_size("dp")
    grad_dots = (factor * grad_logits).astype(jnp.bfloat16)
    grad_emb = jnp.einsum(
        "ci,id->cd", grad_dots, image_table, preferred_element_type=jnp.float32
    ).reshape(rows_here, CAPS, features)
    grad_pooled = inverse * (
        grad_emb - embedding * jnp.sum(embedding * grad_emb, axis=2, keepdims=True)
    )
    grad_pooled = grad_pooled / counts[:, :, None]
    grad_out = jnp.einsum("rst,rsd->rtd", member, grad_pooled, precision=HIGH).reshape(
        token_count, features
    )
    shrink_bias_grad = jnp.sum(grad_out, axis=0)
    grad_out_low = grad_out.astype(jnp.bfloat16)
    shrink_weight_grad = jnp.einsum(
        "nf,nd->fd", active_low, grad_out_low, preferred_element_type=jnp.float32
    )
    grad_active = jnp.einsum(
        "nd,fd->nf", grad_out_low, shrink_w, preferred_element_type=jnp.float32
    )
    grad_expanded = gelu_back(grad_active)[0]
    expand_bias_grad = jnp.sum(grad_expanded, axis=0)
    grad_expanded_low = grad_expanded.astype(jnp.bfloat16)
    expand_weight_grad = jnp.einsum(
        "nd,nf->df", normed_two, grad_expanded_low, preferred_element_type=jnp.float32
    )
    grad_normed_two = jnp.einsum(
        "nf,df->nd", grad_expanded_low, expand_w, preferred_element_type=jnp.float32
    )
    second_gain_grad = jnp.sum(grad_normed_two * normed_b, axis=0)
    second_bias_grad = jnp.sum(grad_normed_two, axis=0)
    grad_hidden = grad_out + norm_back(grad_normed_two * gain_two, normed_b, spread_b)
    output_bias_grad = jnp.sum(grad_hidden, axis=0)
    grad_hidden_low = grad_hidden.astype(jnp.bfloat16)
    output_weight_grad = jnp.einsum(
        "nd,ne->de", mixed_low, grad_hidden_low, preferred_element_type=jnp.float32
    )
    grad_mixed = (
        jnp.einsum("ne,de->nd", grad_hidden_low, output_w, preferred_element_type=jnp.float32)
        .astype(jnp.bfloat16)
        .reshape(head_shape)
    )
    scores_again = masked_scores(queries, key_heads, same_seg)
    probs_again = jnp.exp(scores_again - log_total)
    probs_low = probs_again.astype(jnp.bfloat16)
    grad_values = jnp.einsum(
        "rhqk,rqhc->rkhc", probs_low, grad_mixed, preferred_element_type=jnp.float32
    )
    grad_probs = jnp.einsum(
        "rqhc,rkhc->rhqk", grad_mixed, value_heads, preferred_element_type=jnp.float32
    )
    grad_scores = (
        probs_again * (grad_probs - jnp.sum(probs_again * grad_probs, axis=-1, keepdims=True))
    ).astype(jnp.bfloat16)
    grad_queries = (
        jnp.einsum("rhqk,rkhc->rqhc", grad_scores, key_heads, preferred_element_type=jnp.float32)
        * 0.125
    )
    grad_keys = (
        jnp.einsum("rhqk,rqhc->rkhc", grad_scores, queries, preferred_element_type=jnp.float32)
        * 0.125
    )
    grad_queries = grad_queries.reshape(token_count, features)
    grad_keys = grad_keys.reshape(token_count, features)
    grad_values = grad_values.reshape(token_count, features)
    query_bias_grad = jnp.sum(grad_queries, axis=0)
    value_bias_grad = jnp.sum(grad_values, axis=0)
    grad_triple = jnp.concatenate([grad_queries, grad_keys, grad_values], axis=1).astype(
        jnp.bfloat16
    )
    triple_weight_grad = jnp.einsum(
        "nd,ne->de", normed_one, grad_triple, preferred_element_type=jnp.float32
    )
    grad_normed_one = jnp.einsum(
        "ne,de->nd", grad_triple, triple_w, preferred_element_type=jnp.float32
    )
    first_gain_grad = jnp.sum(grad_normed_one * normed_a, axis=0)
    first_bias_grad = jnp.sum(grad_normed_one, axis=0)
    input_grad = grad_hidden + norm_back(grad_normed_one * gain_one, normed_a, spread_a)
    shares = sum_grads(
        (
            first_gain_grad,
            first_bias_grad,
            triple_weight_grad,
            query_bias_grad,
            value_bias_grad,
            output_weight_grad,
            output_bias_grad,
            second_gain_grad,
            second_bias_grad,
            expand_weight_grad,
            expand_bias_grad,
            shrink_weight_grad,
            shrink_bias_grad,
        )
    )
    loss_out = (loss_total / caption_total).reshape(1)
    factor_out = factor_total.reshape(1)
    return (
        loss_out,
        factor_out,
        input_grad.reshape(1, rows_here, length, features),
        shares[0],
        shares[1],
        shares[2],
        shares[3],
        shares[4],
        shares[5],
        shares[6],
        shares[7],
        shares[8],
        shares[9],
        shares[10],
        shares[11],
        shares[12],
    )


def solution(mesh):
    placed = (
        P("tower", "dp", None, None),
        P("dp", None),
        P("dp", None),
        P(),
        P("tower", None),
        P("tower", None),
        P("tower", None, None),
        P("tower", None),
        P("tower", None),
        P("tower", None, None),
        P("tower", None),
        P("tower", None),
        P("tower", None),
        P("tower", None, None),
        P("tower", None),
        P("tower", None, None),
        P("tower", None),
    )
    fits = mesh.shape["tower"] == 2 and mesh.shape["dp"] == 2 * PLANE
    return jax.shard_map(
        local_fast if fits else local,
        mesh=mesh,
        in_specs=placed,
        out_specs=(
            P(),
            P(),
            P("tower", "dp", None, None),
            P(("tower", "dp")),
            P(("tower", "dp")),
            P(("tower", "dp"), None),
            P(("tower", "dp")),
            P(("tower", "dp")),
            P(("tower", "dp"), None),
            P(("tower", "dp")),
            P(("tower", "dp")),
            P(("tower", "dp")),
            P(("tower", "dp"), None),
            P(("tower", "dp")),
            P(("tower", "dp"), None),
            P(("tower", "dp")),
        ),
        check_vma=False,
    )
```

```python
import functools

import jax
import jax.numpy as jnp
from jax import lax
from jax.experimental import pallas as pl
from jax.experimental.pallas import tpu as pltpu
from jax.sharding import PartitionSpec as P

HEADS = 12
IMG_TOK = 50
CAPS = 4

f32, bf16 = jnp.float32, jnp.bfloat16
GELU_C = 0.7978845608028654
GELU_A = 0.044715
STEP_ROWS = 4
MESH = pl.DeviceIdType.MESH


def mm(a, b):
    return jnp.dot(a, b, preferred_element_type=f32)


def mm_nt(a, b):
    return lax.dot_general(a, b, (((1,), (1,)), ((), ())), preferred_element_type=f32)


def mm_tn(a, b):
    return lax.dot_general(a, b, (((0,), (0,)), ((), ())), preferred_element_type=f32)


def stats(x):
    center = x - jnp.mean(x, axis=-1, keepdims=True)
    spread = lax.rsqrt(jnp.mean(center * center, axis=-1, keepdims=True) + 1e-05)
    return center * spread, spread


def split(x, first):
    zero = jnp.zeros_like(x)
    return jnp.concatenate([jnp.where(first, x, zero), jnp.where(first, zero, x)], axis=0)


def low_pair(x):
    high = x.astype(bf16)
    return high, (x - high.astype(f32)).astype(bf16)


def fwd_kernel(tok, seg, g1, b1, qb, vb, ob, g2, b2, eb, sb, w3h, woh, weh, wsh,
               qkv_h, probs_h, mixed_h, normed_h, sums_out, slope_h, n1_h, n2_h, spread_out, member_out, pooled_out, count_out, table_out,
               w3, wo, we, ws, pool_acc, count_acc, act_sum, imgs, elow,
               qkv_b, probs_b, mixed_b, normed_b, slope_b, n1_b, n2_b, sems, gsem, esem, osem):
    i = pl.program_id(0)
    steps = pl.num_programs(0)
    rows_here, length = seg.shape
    slots = rows_here * CAPS
    feat = tok.shape[1]
    block = tok.shape[0]
    is_text = lax.axis_index("tower") == 1
    copies = [pltpu.make_async_copy(src, dst, sems.at[n])
              for n, (src, dst) in enumerate(((w3h, w3), (woh, wo), (weh, we), (wsh, ws)))]

    tower, d = lax.axis_index("tower"), lax.axis_index("dp")
    chip, core = d // 2, lax.rem(d, 2)
    other = 1 - core
    partner = (tower, chip * 2 + other)
    chips = imgs.shape[1]
    facing = [(1 - tower, lax.rem(chip + k, chips) * 2 + core) for k in range(chips)]

    def remote(src, dst, sem, dev):
        return pltpu.make_async_remote_copy(src_ref=src, dst_ref=dst, send_sem=sem.at[0], recv_sem=sem.at[1],
                                            device_id=dev, device_id_type=MESH)

    slot = lax.rem(i, 2)
    saved = ((qkv_b, qkv_h), (probs_b, probs_h), (mixed_b, mixed_h), (normed_b, normed_h), (slope_b, slope_h),
             (n1_b, n1_h), (n2_b, n2_h))
    qkv, probs, mixed, normed_out, slope, n1_out, n2_out = (buf.at[slot] for buf, _ in saved)

    def save(n, step):
        buf, out = saved[n]
        at = lax.rem(step, 2)
        return pltpu.make_async_copy(buf.at[at], out.at[pl.ds(pl.multiple_of(step * block, block), block)],
                                     osem.at[at, n])

    def leave(*which):
        for n in which:
            save(n, i).start()

    @pl.when(is_text & (i >= 2))
    def _():
        for n in range(len(saved)):
            save(n, i - 2).wait()

    barrier = pltpu.get_barrier_semaphore()

    @pl.when(i == 0)
    def _():
        copies[0].start()
        copies[1].start()
        for dev in facing + [partner]:
            pl.semaphore_signal(barrier, inc=1, device_id=dev, device_id_type=MESH)
        pool_acc[...] = jnp.zeros_like(pool_acc)
        count_acc[...] = jnp.zeros_like(count_acc)
        act_sum[...] = jnp.zeros_like(act_sum)

    def arrive(n):
        @pl.when(i == 0)
        def _():
            copies[n].wait()

    tile = 768
    width = we.shape[1]
    hps = range(HEADS // 2)

    def text_segments(pair):
        base = STEP_ROWS * i + 2 * pair
        keyed = jnp.concatenate([seg[pl.ds(base + r, 1), :] * rows_here + (base + r) for r in range(2)], axis=1)
        across = jnp.broadcast_to(keyed.astype(f32), (128, 128))
        return keyed, jnp.where(across == across.T, 0.0, -1e30)

    def image_place(index, per_row, first_row):
        row = jnp.zeros_like(index)
        for r in range(1, STEP_ROWS):
            row = row + (index >= r * per_row).astype(jnp.int32)
        behind = (index - row * per_row >= IMG_TOK).astype(jnp.int32)
        return behind * rows_here + row + first_row

    def run(keep):
        per_row = length if keep else -(-IMG_TOK // 8) * 8
        both = 2 * per_row
        count = STEP_ROWS * per_row
        if keep:
            x = tok[...].astype(f32)
        else:
            x = jnp.concatenate([tok[length * r:length * r + per_row, :].astype(f32) for r in range(STEP_ROWS)], axis=0)
        norm, _ = stats(x)
        n1 = (norm * g1[...].astype(f32) + b1[...].astype(f32)).astype(bf16)
        if keep:
            n1_out[...] = n1
            leave(5)
        arrive(0)

        @pl.when(i == 0)
        def _():
            copies[2].start()
            copies[3].start()
        qkv[:count, :feat] = (mm(n1, w3[:, :feat]) + qb[...].astype(f32)).astype(bf16)
        qkv[:count, feat:2 * feat] = mm(n1, w3[:, feat:2 * feat]).astype(bf16)
        qkv[:count, 2 * feat:] = (mm(n1, w3[:, 2 * feat:]) + vb[...].astype(f32)).astype(bf16)
        if keep:
            leave(0)
        first_half = lax.broadcasted_iota(jnp.int32, (both, 128), 1) < 64
        slot_lanes = []
        for pair in range(STEP_ROWS // 2):
            if keep:
                keyed, bias = text_segments(pair)
                slot_lanes.append(keyed)
                bias = jnp.concatenate([bias, bias], axis=1)
            else:
                down = lax.broadcasted_iota(jnp.int32, (both, 2 * both), 0)
                over = lax.broadcasted_iota(jnp.int32, (both, 2 * both), 1)
                over = jnp.where(over >= both, over - both, over)
                bias = jnp.where(image_place(down, per_row, 0) == image_place(over, per_row, 0), 0.0, -1e30)
            here = slice(pair * both, (pair + 1) * both)
            scores = [mm_nt(qkv[here, feat + 128 * h:feat + 128 * h + 128],
                            split(qkv[here, 128 * h:128 * h + 128] * jnp.asarray(0.125, bf16), first_half)) + bias
                      for h in hps]
            lows = []
            for h in hps:
                e = jnp.exp(scores[h] - jnp.max(scores[h], axis=0, keepdims=True))
                p = (e * (1.0 / jnp.sum(e, axis=0, keepdims=True))).astype(bf16)
                if keep:
                    probs[here, 256 * h:256 * h + 256] = p
                lows.append(p)
            for h in hps:
                o = mm_tn(lows[h], qkv[here, 2 * feat + 128 * h:2 * feat + 128 * h + 128])
                mixed[here, 128 * h:128 * h + 128] = jnp.where(first_half, o[:both], o[both:]).astype(bf16)
        arrive(1)
        hid = x + mm(mixed[:count, :], wo[...]) + ob[...].astype(f32)
        norm2, spread2 = stats(hid)
        n2 = (norm2 * g2[...].astype(f32) + b2[...].astype(f32)).astype(bf16)
        if keep:
            normed_out[...] = norm2
            spread_out[...] = spread2
            n2_out[...] = n2
            leave(1, 2, 3, 6)
            slot_row = jnp.concatenate(slot_lanes, axis=1)
        else:
            slot_row = image_place(lax.broadcasted_iota(jnp.int32, (1, count), 1), per_row, STEP_ROWS * i)
        hot = (lax.broadcasted_iota(jnp.int32, (slots, count), 0) == slot_row)
        member = hot.astype(f32).astype(bf16)
        if keep:
            member_out[...] = member
            placed = (lax.broadcasted_iota(jnp.int32, (2 * slots, count), 0) == slot_row + slots * core)
            placed = placed.astype(f32).astype(bf16)
        arrive(2)
        arrive(3)
        out = hid + sb[...].astype(f32)
        ahead = mm(n2, we[:, :tile])
        for f in range(0, width, tile):
            v = ahead + eb[:, f:f + tile].astype(f32)
            if f + tile < width:
                ahead = mm(n2, we[:, f + tile:f + 2 * tile])
            v2 = v * v
            cv = v * GELU_C
            h = 0.5 + 0.5 * jnp.tanh(cv * (1.0 + GELU_A * v2))
            a = (v * h).astype(bf16)
            if keep:
                act_sum[:, f:f + tile] += mm(placed, a)
                slope[:, f:f + tile] = (h + h * (1.0 - h) * ((2.0 * cv) * (1.0 + (3.0 * GELU_A) * v2))).astype(bf16)
            out = out + mm(a, ws[f:f + tile, :])
        if keep:
            leave(4)
        out_hi, out_lo = low_pair(out)
        pool_acc[...] += mm(member, out_hi) + mm(member, out_lo)
        count_acc[...] += jnp.broadcast_to(jnp.sum(hot.astype(f32), axis=1, keepdims=True), count_acc.shape)

    pl.when(is_text)(functools.partial(run, True))
    pl.when(tower == 0)(functools.partial(run, False))

    @pl.when(i == steps - 1)
    def _():
        counts = jnp.maximum(count_acc[...], 1.0)
        pooled = pool_acc[...] / counts[:, :1]
        count_out[...] = counts
        pooled_out[...] = pooled
        pl.semaphore_wait(barrier, chips + 1)

        @pl.when(tower == 0)
        def _():
            first = pooled[:rows_here]
            elow[...] = (first * lax.rsqrt(jnp.sum(first * first, axis=1, keepdims=True) + 1e-06)).astype(bf16)
            for dev in facing:
                remote(elow, imgs.at[core, chip], gsem, dev).start()
            remote(imgs.at[0], imgs.at[0], gsem, partner).wait_send()

        @pl.when(tower == 1)
        def _():
            for f in range(0, width, tile):
                sums_out[f:f + tile, :] = act_sum[:, f:f + tile].astype(bf16).T
            remote(imgs.at[core], imgs.at[core], gsem, partner).wait_recv()
            remote(imgs.at[core], imgs.at[core], esem, partner).start()
            remote(imgs.at[other], imgs.at[other], esem, partner).wait()
            table_out[...] = imgs[...]
            for n in range(len(saved)):
                save(n, i - 1).wait()
                save(n, i).wait()


def forward(tokens, segments, g1, b1, w3, qb, vb, wo, ob, g2, b2, we, eb, ws, sb):
    count, feat = tokens.shape
    rows_here, length = segments.shape
    slots = rows_here * CAPS
    ff = we.shape[1]
    block = STEP_ROWS * length
    steps = count // block
    table = (2, lax.axis_size("dp") // 2, rows_here, feat)
    whole = lambda a: pl.BlockSpec(a.shape, lambda i: (0,) * a.ndim)
    rows = lambda width: pl.BlockSpec((block, width), lambda i: (i, 0))
    anyw = pl.BlockSpec(memory_space=pl.ANY)
    smalls = (g1, b1, qb, vb, ob, g2, b2, eb, sb)
    return pl.pallas_call(
        fwd_kernel,
        grid=(steps,),
        in_specs=[rows(feat), whole(segments)] + [whole(a) for a in smalls] + [anyw] * 4,
        out_specs=[anyw] * 4 + [pl.BlockSpec((ff, 2 * slots), lambda i: (0, 0))] + [anyw] * 3 + [
                   rows(1),
                   pl.BlockSpec((slots, block), lambda i: (0, i)),
                   pl.BlockSpec((slots, feat), lambda i: (0, 0)),
                   pl.BlockSpec((slots, 128), lambda i: (0, 0)),
                   pl.BlockSpec(table, lambda i: (0,) * 4)],
        out_shape=[jax.ShapeDtypeStruct((count, 3 * feat), bf16),
                   jax.ShapeDtypeStruct((count, 2 * feat), bf16),
                   jax.ShapeDtypeStruct((count, feat), bf16),
                   jax.ShapeDtypeStruct((count, feat), f32),
                   jax.ShapeDtypeStruct((ff, 2 * slots), bf16),
                   jax.ShapeDtypeStruct((count, ff), bf16),
                   jax.ShapeDtypeStruct((count, feat), bf16),
                   jax.ShapeDtypeStruct((count, feat), bf16),
                   jax.ShapeDtypeStruct((count, 1), f32),
                   jax.ShapeDtypeStruct((slots, count), bf16),
                   jax.ShapeDtypeStruct((slots, feat), f32),
                   jax.ShapeDtypeStruct((slots, 128), f32),
                   jax.ShapeDtypeStruct(table, bf16)],
        scratch_shapes=[pltpu.VMEM(w3.shape, bf16), pltpu.VMEM(wo.shape, bf16), pltpu.VMEM(we.shape, bf16),
                        pltpu.VMEM(ws.shape, bf16), pltpu.VMEM((slots, feat), f32), pltpu.VMEM((slots, 128), f32), pltpu.VMEM((2 * slots, ff), f32),
                        pltpu.VMEM(table, bf16), pltpu.VMEM((rows_here, feat), bf16),
                        pltpu.VMEM((2, block, 3 * feat), bf16), pltpu.VMEM((2, block, 2 * feat), bf16),
                        pltpu.VMEM((2, block, feat), bf16), pltpu.VMEM((2, block, feat), f32),
                        pltpu.VMEM((2, block, ff), bf16), pltpu.VMEM((2, block, feat), bf16),
                        pltpu.VMEM((2, block, feat), bf16),
                        pltpu.SemaphoreType.DMA((4,)), pltpu.SemaphoreType.DMA((2,)), pltpu.SemaphoreType.DMA((2,)),
                        pltpu.SemaphoreType.DMA((2, 7))],
        compiler_params=pltpu.CompilerParams(vmem_limit_bytes=56 << 20, dimension_semantics=("arbitrary",),
                                             collective_id=1, has_side_effects=True),
        name="fwd",
    )(tokens, segments, *smalls, w3, wo, we, ws)


PLANE = 8
LINE = 4
BLK = 256
CH = 768
HALF = CH // 2
ROWS = HALF // PLANE
N_CH = 8
WIDE = (0, 2, 4, 7)
LONG = (1, 3, 6)
DEEP = (5,)
TEXT_PLAN = {
    ("ga", 1): (("leave", 0),),
    ("gn", 1): (("cross",),),
    ("ga", 2): (("leave", 1),),
    ("ew", 2): (("mid", 0),),
    ("ga", 3): (("leave", 2),),
    "ow": (("mid", 1), ("leave", 3),),
    ("attn", 0): (("mid", 2), ("leave", 4),),
    ("tw", 0): (("share",), ("mid", 3),),
    ("tw", 1): (("leave", 5),),
    ("tw", 2): (("finish", 0), ("mid", 4), ("rows",), ("leave", 6),),
    ("gn1", 0): (("finish", 1), ("leave", 7),),
    ("gn1", 2): (("finish", 2),),
    ("gn1", 3): (("mid", 5),),
    "small": (("finish", 3),),
    "end": (("mid", 6), ("mid", 7), ("finish", 5), ("finish", 4), ("finish", 6), ("finish", 7),),
}
IMAGE_PLAN = (
    ("over", 0), ("mid", 0), ("over", 2), ("over", 1), ("mid", 2), ("finish", 0), ("over", 4), ("over", 3), ("finish", 1), ("mid", 4), ("finish", 2), ("over", 7), ("mid", 7), ("rows",), ("finish", 3), ("finish", 4), ("over", 6), ("take", 5), ("finish", 7), ("finish", 6),
)
WIDE_AT = {q: n for n, q in enumerate(WIDE)}
LONG_AT = {q: n for n, q in enumerate(LONG + DEEP)}
DEEP_AT = {q: n for n, q in enumerate(DEEP)}


def fold(x):
    return jnp.sum(x.reshape(x.shape[0] // 8, 8, x.shape[1]), axis=0)


def bwd_kernel(member, pooled, count, imgs, act_sums, caption, scale, g1, b1, g2, b2,
               qkv_h, probs_h, mixed_h, normed_h, slope_h, n1_h, n2_h, spread_h, tok_h, w3_h, wo_h, we_h, ws_h,
               tw_out, ow_out, ew_out, sw_out, in_out, vec_out,
               cs, snd, prv, own, ylong, ywide, zrcv, zdeep, xfin, fin, apair, asum, aall, gpall, swfin, xsw,
               gol, gn2, hid, spread2, n2b, tok, mixed, probs, slope, ws, we, ge, qkv, w3, wo,
               ebsum, attn_sum, vec, vown, vpair, vrcv,
               ld, psend, precv, xsend, xrecv, ysend, yrecv, zsend, zrecv,
               fsem, asem, gsem, swsem, vpsem, vsem, outsem):
    t = lax.axis_index("tower")
    d = lax.axis_index("dp")
    p = d // 2
    c = lax.rem(d, 2)
    z = p // 2
    y = lax.rem(p, 2)
    is_text = t == 1
    count_t = gol.shape[0]
    blocks = count_t // BLK
    feat = CH
    rows_here = caption.shape[1]
    other = 1 - c

    def peer(k):
        return lax.rem(p + k, PLANE)

    def at_core(tt, pp):
        return (tt, pp * 2 + c)

    partner = (t, p * 2 + other)
    beside = at_core(t, 2 * z + (1 - y))
    across = at_core(1 - t, p)

    def remote(src, dst, ssem, rsem, dev):
        return pltpu.make_async_remote_copy(src_ref=src, dst_ref=dst, send_sem=ssem, recv_sem=rsem,
                                            device_id=dev, device_id_type=MESH)

    barrier = pltpu.get_barrier_semaphore()
    pl.semaphore_signal(barrier, inc=1, device_id=partner, device_id_type=MESH)
    pl.semaphore_signal(barrier, inc=1, device_id=across, device_id_type=MESH)
    for k in range(1, PLANE):
        pl.semaphore_signal(barrier, inc=1, device_id=at_core(t, peer(k)), device_id_type=MESH)
        pl.semaphore_signal(barrier, inc=1, device_id=at_core(1 - t, peer(k)), device_id_type=MESH)

    pooled_v = pooled[...]
    inverse = lax.rsqrt(jnp.sum(pooled_v * pooled_v, axis=1, keepdims=True) + 1e-06)
    emb = pooled_v * inverse
    emb_low = emb.astype(bf16)

    def pair_copy(q):
        slot = lax.rem(q, 2)
        return remote(snd.at[slot], prv.at[q], psend.at[slot], precv.at[q], partner)

    def x_all(q):
        return remote(cs.at[q, 0:LINE], cs.at[q, 0:LINE], xsend.at[q], xrecv.at[q], across)

    def x_line(q):
        return remote(cs.at[q, 0:LINE, y], cs.at[q, 0:LINE, y], xsend.at[q], xrecv.at[q], across)

    def x_sum(q):
        n = DEEP_AT[q]
        return remote(xfin.at[n], xfin.at[n], xsend.at[q], xrecv.at[q], across)

    def x_copy(q):
        return x_all(q) if q in WIDE else x_line(q) if q in LONG else x_sum(q)

    def y_copy(q):
        if q not in WIDE:
            src, dst = cs.at[q, :, 1 - y], ylong.at[LONG_AT[q]]
        else:
            src, dst = cs.at[q, pl.ds(LINE * t, LINE), 1 - y], ywide.at[WIDE_AT[q]]
        return remote(src, dst, ysend.at[q], yrecv.at[q], beside)

    def z_start(q):
        for k in range(1, LINE):
            to = lax.rem(z + k, LINE)
            remote(cs.at[q, LINE * t + to, y], zrcv.at[q, k - 1], zsend.at[q], zrecv.at[q],
                   at_core(t, 2 * to + y)).start()
            if q in DEEP:
                remote(cs.at[q, to, y], zdeep.at[DEEP_AT[q], k - 1], zsend.at[N_CH + DEEP_AT[q]],
                       zrecv.at[N_CH + DEEP_AT[q]], at_core(t, 2 * to + y)).start()

    def z_all(q):
        return remote(zrcv.at[q], zrcv.at[q], zsend.at[q], zrecv.at[q], partner)

    def z_deep(q):
        n = DEEP_AT[q]
        return remote(zdeep.at[n], zdeep.at[n], zsend.at[N_CH + n], zrecv.at[N_CH + n], partner)

    def mid(q):
        y_copy(q).wait_recv()
        if q not in WIDE:
            for a in range(PLANE):
                cs[q, a, y] = (cs[q, a, y].astype(f32) + ylong[LONG_AT[q], a].astype(f32)).astype(bf16)
            if q in LONG:
                x_line(q).start()
        else:
            for a in range(LINE):
                at = LINE * t + a
                cs[q, at, y] = (cs[q, at, y].astype(f32) + ywide[WIDE_AT[q], a].astype(f32)).astype(bf16)
        z_start(q)

    def a_pair():
        return remote(act_sums.at[:, :, other], apair, asem.at[0], asem.at[1], partner)

    def a_start():
        a_pair().wait_recv()
        asum[...] = act_sums[:, :, c] + apair[...]
        aall[:, :, pl.ds(pl.multiple_of(128 * p, 128), 128)] = asum[:, p]
        for k in range(1, PLANE):
            remote(asum.at[:, peer(k)], aall.at[:, :, pl.ds(pl.multiple_of(128 * p, 128), 128)],
                   asem.at[2], asem.at[3], at_core(t, peer(k))).start()

    def a_all():
        every = asum.at[:, 0:PLANE - 1]
        return remote(every, every, asem.at[2], asem.at[3], partner)

    def gp_beside():
        return remote(gpall.at[p, c], gpall.at[p, c], gsem.at[0], gsem.at[1], beside)

    def gp_line():
        gp_beside().wait_recv()
        for k in range(1, LINE):
            mine = gpall.at[pl.ds(2 * z, 2), c]
            remote(mine, mine, gsem.at[2], gsem.at[3], at_core(t, 2 * lax.rem(z + k, LINE) + y)).start()

    def gp_line_all():
        every = gpall.at[0:2 * (LINE - 1), 0]
        return remote(every, every, gsem.at[2], gsem.at[3], partner)

    def gp_share_copy():
        return remote(gpall.at[:, c], gpall.at[:, c], gsem.at[4], gsem.at[5], partner)

    def gp_share():
        gp_line_all().wait_recv()
        gp_share_copy().start()

    def sw_across():
        return remote(xsw, xsw, swsem.at[0], swsem.at[1], across)

    def sw_keep():
        return pltpu.make_async_copy(swfin, sw_out, swsem.at[2])

    def shrink():
        gp_share_copy().wait_recv()
        a_all().wait_recv()
        rows = gpall[...].reshape(-1, feat)
        xsw[...] = mm(aall[0], rows).astype(bf16)
        sw_across().start()
        swfin[...] = mm(aall[1], rows)
        sw_keep().start()

    half_rows = ROWS // 2

    def place(q):
        if q < 4:
            return ew_out, 4 * HALF * c + HALF * q
        if q == 4:
            return ow_out, HALF * c
        return tw_out, CH * (q - 5) + HALF * c

    def keep(q):
        out, col = place(q)
        return pltpu.make_async_copy(fin.at[q, pl.ds(pl.multiple_of(half_rows * c, 8), half_rows)],
                                     out.at[:, pl.ds(pl.multiple_of(col, 128), HALF)], fsem.at[0])

    def give(q):
        out, col = place(q)
        return remote(fin.at[q, pl.ds(pl.multiple_of(half_rows * other, 8), half_rows)],
                      out.at[:, pl.ds(pl.multiple_of(col, 128), HALF)], fsem.at[1], fsem.at[2], partner)

    def finish(q):
        z_all(q).wait_recv()
        total = cs[q, LINE * t + z, y].astype(f32)
        for k in range(LINE - 1):
            total = total + zrcv[q, k].astype(f32)
        if q in DEEP:
            z_deep(q).wait_recv()
            theirs = cs[q, z, y].astype(f32)
            for k in range(LINE - 1):
                theirs = theirs + zdeep[DEEP_AT[q], k].astype(f32)
            xfin[DEEP_AT[q]] = theirs.astype(bf16)
            x_sum(q).start()
        fin[q] = total
        keep(q).start()
        give(q).start()

    def take(q):
        x_sum(q).wait_recv()
        fin[q] = xfin[DEEP_AT[q]].astype(f32)
        keep(q).start()
        give(q).start()

    def leave(q):
        chip_sum(q)
        if q in WIDE:
            x_all(q).start()
        y_copy(q).start()

    def chip_sum(q):
        pair_copy(q).wait_recv()
        slot = lax.rem(q, 2)
        n = 2 * ROWS
        for a in range(PLANE):
            total = own[slot, n * a:n * (a + 1), :] + prv[q, n * a:n * (a + 1), :].astype(f32)
            cs[q, a] = total.reshape(2, ROWS, HALF).astype(bf16)

    def chunk(q, left, right):
        slot = lax.rem(q, 2)

        @pl.when(q >= 2)
        def _():
            pair_copy(q - 2).wait_send()
        for r in range(0, CH, 256):
            part = mm_tn(left[:, r:r + 256], right)
            low, high = part[:, :HALF], part[:, HALF:]
            own[slot, r:r + 256, :] = jnp.where(c == 0, low, high)
            snd[slot, r:r + 256, :] = jnp.where(c == 0, high, low).astype(bf16)
        pair_copy(q).start()

    def v_pair():
        return remote(vown.at[other], vpair, vpsem.at[0], vpsem.at[1], partner)

    def load(n, src, dst):
        return pltpu.make_async_copy(src, dst, ld.at[n])

    def tile_loads(i):
        s = lax.rem(i, 2)
        out = []
        ff = slope_h.shape[1]
        for h in range(2):
            col = pl.multiple_of((ff // 2) * h + HALF * i, 128)
            here = pl.ds(HALF * h, HALF)
            out.append(load(6 * s + 3 * h, slope_h.at[:, pl.ds(col, HALF)], slope.at[s, :, here]))
            out.append(load(6 * s + 3 * h + 1, ws_h.at[pl.ds(col, HALF)], ws.at[s, here]))
            out.append(load(6 * s + 3 * h + 2, we_h.at[:, pl.ds(col, HALF)], we.at[s, :, here]))
        return out

    hid_load = load(16, normed_h, hid)
    tok_load = load(17, tok_h, tok)
    qkv_load = load(18, qkv_h, qkv)
    w3_load = load(19, w3_h, w3)
    wo_load = load(20, wo_h, wo)
    n2_load = load(24, n2_h, n2b)
    spread_load = load(25, spread_h, spread2)
    n1_load = load(26, n1_h, slope.at[1])
    mixed_load = load(21, mixed_h, mixed)
    probs_load = load(22, probs_h, probs)

    @pl.when(t == 0)
    def _():
        pl.semaphore_wait(barrier, 2 * PLANE)
        gn2[:BLK, :] = jnp.zeros((BLK, feat), f32)
        for m in range(blocks):
            pltpu.make_async_copy(gn2.at[0:BLK], in_out.at[pl.ds(BLK * m, BLK)], outsem.at[m]).start()

        def over(q):
            x_copy(q).wait_recv()
            if q in WIDE:
                y_copy(q).start()
            else:
                z_start(q)

        def rows_over():
            sw_across().wait_recv()
            swfin[...] = xsw[...].astype(f32)
            sw_keep().start()
        acts = {"over": over, "mid": mid, "finish": finish, "take": take, "rows": rows_over}
        for what, *of in IMAGE_PLAN:
            acts[what](*of)
        for m in range(blocks):
            pltpu.make_async_copy(gn2.at[0:BLK], in_out.at[pl.ds(BLK * m, BLK)], outsem.at[m]).wait()

    @pl.when(is_text)
    def _():
        for cp in tile_loads(0):
            cp.start()
        n2_load.start()
        for cp in tile_loads(1):
            cp.start()
        for cp in (hid_load, spread_load, mixed_load, wo_load, qkv_load, probs_load, w3_load, tok_load):
            cp.start()
        gain2, gain1 = g2[...].astype(f32), g1[...].astype(f32)
        gn2[...] = jnp.zeros_like(gn2)
        attn_sum[...] = jnp.zeros_like(attn_sum)
        vec[...] = jnp.zeros_like(vec)
        pl.semaphore_wait(barrier, 2 * PLANE)
        a_pair().start()

        table = imgs[...].reshape(2 * PLANE * rows_here, feat)
        dots = mm_nt(emb_low, table)
        factor = scale[0]
        logits = factor * dots
        peak = jnp.max(logits, axis=1, keepdims=True)
        weight = jnp.exp(logits - peak)
        total = jnp.sum(weight, axis=1, keepdims=True)
        eye = (lax.broadcasted_iota(jnp.int32, (rows_here, rows_here), 0)
               == lax.broadcasted_iota(jnp.int32, (rows_here, rows_here), 1))
        wanted = jnp.concatenate([jnp.sum(jnp.where(eye, caption[s:s + 1, :], 0), axis=1, keepdims=True)
                                  for s in range(CAPS)], axis=0)
        span = 2 * rows_here
        inside = lax.rem(wanted, span)
        wanted = (inside // rows_here) * (PLANE * rows_here) + (wanted // span) * rows_here + lax.rem(inside, rows_here)
        hot = (lax.broadcasted_iota(jnp.int32, dots.shape, 1) == wanted).astype(f32)
        picked = jnp.sum(logits * hot, axis=1, keepdims=True)
        loss_here = jnp.sum(peak + jnp.log(total) - picked, axis=0, keepdims=True)
        a_start()
        grad_logits = weight / total - hot
        factor_here = jnp.sum(jnp.sum(grad_logits * dots, axis=1, keepdims=True), axis=0, keepdims=True)
        grad_emb = mm((factor * grad_logits).astype(bf16), table)
        counts = count[:, :1]
        grad_pool = inverse * (grad_emb - emb * jnp.sum(emb * grad_emb, axis=1, keepdims=True))
        vec[7:8, :] = jnp.sum(grad_pool, axis=0, keepdims=True)
        column = lax.broadcasted_iota(jnp.int32, (1, feat), 1)
        vec[12:13, :] = jnp.where(column == 0, loss_here, jnp.where(column == 1, factor_here, 0.0))
        gp_hi, gp_lo = low_pair(grad_pool / counts)
        gpall[p, c] = gp_hi
        gp_beside().start()
        for m in range(blocks):
            gol[BLK * m:BLK * (m + 1), :] = mm_tn(member[:, BLK * m:BLK * (m + 1)], gp_hi).astype(bf16)

        acts = {"leave": leave, "mid": mid, "finish": finish, "cross": gp_line, "share": gp_share, "rows": shrink}

        def now(place):
            for what, *of in TEXT_PLAN.get(place, ()):
                acts[what](*of)

        def now_in(loop, index, count):
            for n in range(count):
                if (loop, n) in TEXT_PLAN:
                    pl.when(index == n)(functools.partial(now, (loop, n)))

        @pl.loop(0, 4)
        def _(i):
            s = lax.rem(i, 2)
            for cp in tile_loads(i):
                cp.wait()

            sums = jnp.zeros((8, feat), f32)
            for m in range(blocks):
                here = slice(BLK * m, BLK * (m + 1))
                grad = mm_nt(gol[here, :], ws[s]) * slope[s, here, :].astype(f32)
                sums = sums + fold(grad)
                ge[here, :] = grad.astype(bf16)
            sums = jnp.sum(sums, axis=0, keepdims=True)
            for h in range(2):
                ebsum[:, pl.ds(pl.multiple_of(4 * HALF * h + HALF * i, 128), HALF)] = sums[:, HALF * h:HALF * (h + 1)]
            now_in("ga", i, 4)

            @pl.when(i == 0)
            def _():
                n2_load.wait()
            chunk(i, n2b, ge[...])
            now_in("ew", i, 4)
            for m in range(blocks):
                here = slice(BLK * m, BLK * (m + 1))
                gn2[here, :] += mm_nt(ge[here, :], we[s])
            now_in("gn", i, 4)

            @pl.when(i < 2)
            def _():
                for cp in tile_loads(i + 2):
                    cp.start()
        n1_load.start()
        hid_load.wait()
        spread_load.wait()

        zeros8 = jnp.zeros((8, feat), f32)

        def norm2_back(m, sums):
            here = pl.ds(pl.multiple_of(m * BLK, BLK), BLK)
            norm, g_in = hid[here, :], gn2[here, :]
            hot_m = member[:, here]
            grad_out = mm_tn(hot_m, gp_hi) + mm_tn(hot_m, gp_lo)
            g = g_in * gain2
            back = spread2[here, :] * (g - jnp.mean(g, axis=1, keepdims=True)
                                       - norm * jnp.mean(g * norm, axis=1, keepdims=True))
            gh = grad_out + back
            gn2[here, :] = gh
            gol[here, :] = gh.astype(bf16)
            return (sums[0] + fold(g_in * norm), sums[1] + fold(g_in), sums[2] + fold(gh))
        sums = lax.fori_loop(0, blocks, norm2_back, (zeros8, zeros8, zeros8))
        for row, x in ((5, sums[0]), (6, sums[1]), (4, sums[2])):
            vec[row:row + 1, :] = jnp.sum(x, axis=0, keepdims=True)
        for n in range(4):
            vec[8 + n:9 + n, :] = ebsum[:, feat * n:feat * (n + 1)]
        now("norm")

        mixed_load.wait()
        chunk(4, mixed, gol[...])
        now("ow")
        wo_load.wait()
        for m in range(blocks):
            here = slice(BLK * m, BLK * (m + 1))
            ge[here, :] = mm_nt(gol[here, :], wo[...]).astype(bf16)
        now("gm")

        qkv_load.wait()
        probs_load.wait()
        first_half = lax.broadcasted_iota(jnp.int32, (128, 128), 1) < 64
        hps = range(HEADS // 2)

        @pl.loop(0, count_t // 128)
        def _(rp):
            here = pl.ds(pl.multiple_of(rp * 128, 128), 128)

            def probs_of(h):
                return probs[here, 256 * h:256 * h + 256]

            def part(n, h):
                return qkv[here, feat * n + 128 * h:feat * n + 128 * h + 128]
            gm = [split(ge[here, 128 * h:128 * h + 128], first_half) for h in hps]
            gp = [mm_nt(part(2, h), gm[h]) for h in hps]
            gv = [mm(probs_of(h), gm[h]) for h in hps]
            gs = []
            for h in hps:
                probs_f = probs_of(h).astype(f32)
                weighted = probs_f * gp[h]
                gs.append((weighted - probs_f * jnp.sum(weighted, axis=0, keepdims=True)).astype(bf16))
            gk = [mm(gs[h], split(part(0, h), first_half)) * 0.125 for h in hps]
            gq = []
            for h in hps:
                both = mm_tn(gs[h], part(1, h))
                gq.append(jnp.where(first_half, both[:128], both[128:]) * 0.125)
            for h in hps:
                for n, x in ((0, gq[h]), (1, gk[h]), (2, gv[h])):
                    qkv[here, feat * n + 128 * h:feat * n + 128 * h + 128] = x.astype(bf16)
                for n, x in ((0, gq[h]), (1, gv[h])):
                    attn_sum[:, feat * n + 128 * h:feat * n + 128 * h + 128] += fold(x)

            now_in("attn", rp, count_t // 128)
        vec[2:3, :] = jnp.sum(attn_sum[:, :feat], axis=0, keepdims=True)
        vec[3:4, :] = jnp.sum(attn_sum[:, feat:], axis=0, keepdims=True)

        n1_load.wait()

        @pl.loop(0, 3)
        def _(j):
            chunk(5 + j, slope.at[1], qkv[:, pl.ds(pl.multiple_of(CH * j, 128), CH)])

            now_in("tw", j, 3)
        tok_load.wait()
        w3_load.wait()

        def norm1_back(m, sums):
            here = pl.ds(pl.multiple_of(m * BLK, BLK), BLK)
            g_in = mm_nt(qkv[here, :], w3[...])

            now_in("gn1", m, blocks)
            norm, spread = stats(tok[here, :].astype(f32))
            g = g_in * gain1
            back = spread * (g - jnp.mean(g, axis=1, keepdims=True)
                             - norm * jnp.mean(g * norm, axis=1, keepdims=True))
            gn2[here, :] += back
            pltpu.make_async_copy(gn2.at[here], in_out.at[here], outsem.at[m]).start()
            return (sums[0] + fold(g_in * norm), sums[1] + fold(g_in))
        sums = lax.fori_loop(0, blocks, norm1_back, (zeros8, zeros8))
        for row, x in ((0, sums[0]), (1, sums[1])):
            vec[row:row + 1, :] = jnp.sum(x, axis=0, keepdims=True)

        width, wide = feat // (4 * PLANE), 4 * feat // (4 * PLANE)
        narrow = vec[0:8, :]
        broad = vec[8:16, :]
        scalars = vec[12:13, :128]
        turned = [broad] + [pltpu.roll(broad, feat - wide * j, axis=1) for j in range(1, feat // wide)]
        for g in range(4 * PLANE):
            one = narrow if g == 0 else pltpu.roll(narrow, feat - width * g, axis=1)
            row = g // (feat // wide)
            tail = turned[g % (feat // wide)][row:row + 1, :128]
            vown[g % 2, g // 2, 0:8, :] = one[:, :128]
            vown[g % 2, g // 2, 8:9, :] = tail
            vown[g % 2, g // 2, 9:10, :] = scalars
        v_pair().start()
        now("small")
        for m in range(blocks):
            here = pl.ds(BLK * m, BLK)
            pltpu.make_async_copy(gn2.at[here], in_out.at[here], outsem.at[m]).wait()
        v_pair().wait_recv()
        vown[c] += vpair[...]
        for k in range(PLANE):
            for tt in range(2):
                if tt == 0 or k:
                    remote(vown.at[c, PLANE * tt + peer(k)], vrcv.at[k], vsem.at[0], vsem.at[1],
                           at_core(tt, peer(k))).start()
        now("end")

    @pl.when(is_text)
    def _():
        remote(vrcv.at[1:PLANE], vrcv.at[1:PLANE], vsem.at[0], vsem.at[1], partner).wait_recv()
        total = vown[c, PLANE + p]
        for k in range(1, PLANE):
            total = total + vrcv[k]
        vec_out[...] = total

    @pl.when(t == 0)
    def _():
        remote(vrcv, vrcv, vsem.at[0], vsem.at[1], partner).wait_recv()
        total = vrcv[0]
        for k in range(1, PLANE):
            total = total + vrcv[k]
        vec_out[...] = total

    @pl.when(is_text)
    def _():
        everything = vown.at[0, 0:2 * PLANE - 1]
        remote(everything, everything, vsem.at[0], vsem.at[1], partner).wait_send()
        v_pair().wait_send()
        for q in (N_CH - 2, N_CH - 1):
            pair_copy(q).wait_send()

        for q in range(N_CH):
            x_copy(q).wait_send()
        for q in LONG + DEEP:
            y_copy(q).wait_send()
        for q in DEEP:
            z_deep(q).wait_send()
            z_all(q).wait_send()
        a_pair().wait_send()
        a_all().wait_send()
        gp_beside().wait_send()
        gp_line_all().wait_send()
        gp_share_copy().wait_send()
        sw_across().wait_send()
    for q in WIDE:
        y_copy(q).wait_send()
    for q in WIDE + LONG:
        z_all(q).wait_send()
    sw_keep().wait()
    lower = fin.at[:, 0:half_rows]
    pltpu.make_async_copy(lower, lower, fsem.at[0]).wait()
    remote(lower, lower, fsem.at[1], fsem.at[2], partner).wait()


def backward(member, pooled, count, imgs, sums, caption, scale, g1, b1, g2, b2,
             qkv, probs, mixed, normed, slope, n1, n2, spread, tokens, w3, wo, we, ws):
    n_tok, feat = tokens.shape
    ff = we.shape[1]
    dma = pltpu.SemaphoreType.DMA
    vm = pltpu.VMEM
    vspec = pl.BlockSpec(memory_space=pltpu.VMEM)
    sspec = pl.BlockSpec(memory_space=pltpu.SMEM)
    anyw = pl.BlockSpec(memory_space=pl.ANY)
    shape = jax.ShapeDtypeStruct
    long, wide, deep = len(LONG + DEEP), len(WIDE), len(DEEP)
    apart = sums.shape[:2] + sums.shape[3:]
    slots = member.shape[0]
    scratch = [
        vm((N_CH, PLANE, 2, ROWS, HALF), bf16), vm((2, CH, HALF), bf16), vm((N_CH, CH, HALF), bf16),
        vm((2, CH, HALF), f32),
        vm((max(long, 1), PLANE, ROWS, HALF), bf16), vm((max(wide, 1), LINE, ROWS, HALF), bf16), vm((N_CH, LINE - 1, ROWS, HALF), bf16),
        vm((max(deep, 1), LINE - 1, ROWS, HALF), bf16), vm((max(deep, 1), ROWS, HALF), bf16),
        vm((N_CH, ROWS, HALF), f32), vm(apart, bf16), vm(apart, bf16), vm((2, apart[2], PLANE * 128), bf16),
        vm((PLANE, 2, slots, feat), bf16), vm((2 * ROWS, feat), f32), vm((2 * ROWS, feat), bf16),
        vm((n_tok, feat), bf16), vm((n_tok, feat), f32), vm((n_tok, feat), f32), vm((n_tok, 1), f32),
        vm((n_tok, feat), bf16), vm((n_tok, feat), bf16),
        vm((n_tok, feat), bf16), vm((n_tok, 2 * feat), bf16), vm((2, n_tok, CH), bf16), vm((2, CH, feat), bf16), vm((2, feat, CH), bf16),
        vm((n_tok, feat), bf16), vm((n_tok, 3 * feat), bf16), vm(w3.shape, bf16), vm(wo.shape, bf16),
        vm((1, ff), f32), vm((8, 2 * feat), f32),
        vm((16, feat), f32), vm((2, 2 * PLANE, 16, 128), f32), vm((2 * PLANE, 16, 128), f32), vm((PLANE, 16, 128), f32),
        dma((27,)), dma((2,)), dma((N_CH,)), dma((N_CH,)), dma((N_CH,)), dma((N_CH,)), dma((N_CH,)),
        dma((N_CH + deep,)), dma((N_CH + deep,)), dma((3,)), dma((4,)), dma((6,)), dma((3,)), dma((2,)), dma((2,)),
        dma((n_tok // BLK,)),
    ]
    return pl.pallas_call(
        bwd_kernel,
        in_specs=[vspec] * 6 + [sspec] + [vspec] * 4 + [anyw] * 13,
        out_specs=[anyw] * 5 + [vspec],
        out_shape=[shape((ROWS // 2, 3 * feat), f32), shape((ROWS // 2, feat), f32), shape((ROWS // 2, ff), f32),
                   shape((2 * ROWS, feat), f32), shape((n_tok, feat), f32), shape((16, 128), f32)],
        scratch_shapes=scratch,
        compiler_params=pltpu.CompilerParams(vmem_limit_bytes=61 << 20, collective_id=0, has_side_effects=True),
        name="bwd",
    )(member, pooled, count, imgs, sums, caption, scale, g1, b1, g2, b2,
      qkv, probs, mixed, normed, slope, n1, n2, spread, tokens, w3, wo, we, ws)


def hand_out_kernel(scale_by, vec, *rest):
    bigs, loss, factor, smalls = rest[:5], rest[5], rest[6], rest[7:16]
    outs, held, sem_in, sem_out = rest[16:21], rest[21:26], rest[26], rest[27]
    parts = []
    for src, dst, buf in zip(bigs, outs, held):
        count = max(src.shape[0] // BLK, 1)
        rows = src.shape[0] // count
        for n in range(count):
            parts.append((src.at[rows * n:rows * (n + 1)], buf.at[rows * n:rows * (n + 1)],
                          dst.at[rows * n:rows * (n + 1)]))
    ins = [pltpu.make_async_copy(a, b, sem_in.at[n]) for n, (a, b, _) in enumerate(parts)]
    outs = [pltpu.make_async_copy(b, c, sem_out.at[n]) for n, (_, b, c) in enumerate(parts)]
    for move in ins:
        move.start()
    width, wide = smalls[0].shape[1], smalls[8].shape[1]
    for n in range(8):
        smalls[n][...] = vec[n:n + 1, :width]
    smalls[8][...] = vec[8:9, :wide]
    loss[...] = vec[9:10, 0:1] * scale_by
    factor[...] = vec[9:10, 1:2]
    for first, second in zip(ins, outs):
        first.wait()
        second.start()
    for move in outs:
        move.wait()


def hand_out(vec, tw, ow, ew, sw, inp, captions):
    devices = lax.axis_size("tower") * lax.axis_size("dp")
    bigs = (inp, sw, ew, tw, ow)
    feat = inp.shape[1]
    outs = ([(1, 1)] * 2 + [(1, feat // devices)] * 8 + [(1, ew.shape[1] // devices)]
            + [a.shape for a in bigs])
    moves = 4 + inp.shape[0] // BLK
    vspec = pl.BlockSpec(memory_space=pltpu.VMEM)
    anyw = pl.BlockSpec(memory_space=pl.ANY)
    return pl.pallas_call(
        functools.partial(hand_out_kernel, 1.0 / captions),
        in_specs=[vspec] + [anyw] * 5,
        out_specs=[vspec] * 11 + [anyw] * 5,
        out_shape=[jax.ShapeDtypeStruct(dims, f32) for dims in outs],
        scratch_shapes=[pltpu.VMEM(a.shape, f32) for a in bigs]
        + [pltpu.SemaphoreType.DMA((moves,)), pltpu.SemaphoreType.DMA((moves,))],
        name="hand_out",
    )(vec, *bigs)


def local_fast(tokens, segments, caption_image, logit_scale, first_gain, first_bias, triple_weight, query_bias,
               value_bias, output_weight, output_bias, second_gain, second_bias, expand_weight, expand_bias,
               shrink_weight, shrink_bias):
    rows_here, length, feat = tokens.shape[1:]
    flat = tokens[0].reshape(rows_here * length, feat)
    w3, wo, we, ws = triple_weight[0], output_weight[0], expand_weight[0], shrink_weight[0]
    qkv, probs, mixed, normed, sums, slope, n1, n2, spread, member, pooled, count, table = forward(
        flat, segments, first_gain, first_bias, w3, query_bias, value_bias, wo, output_bias,
        second_gain, second_bias, we, expand_bias, ws, shrink_bias)
    sums = sums.reshape(2, PLANE, 2, sums.shape[0] // (4 * PLANE), sums.shape[1])
    tw, ow, ew, sw, inp, vec = backward(member, pooled, count, table, sums, caption_image.T, logit_scale, first_gain, first_bias,
                                        second_gain, second_bias, qkv, probs, mixed, normed, slope, n1, n2, spread, flat,
                                        w3, wo, we, ws)
    captions = rows_here * CAPS * lax.axis_size("dp")
    outs = hand_out(vec, tw, ow, ew, sw, inp, captions)
    loss, factor = outs[0].reshape(1), outs[1].reshape(1)
    g1, b1, qb, vb, ob, g2, b2, sb, eb = (a.reshape(-1) for a in outs[2:11])
    inp, sw, ew, tw, ow = outs[11:]
    return (loss, factor, inp.reshape(1, rows_here, length, feat), g1, b1, tw, qb, vb, ow, ob, g2, b2, ew, eb, sw, sb)


HIGH = lax.Precision.HIGHEST


def shifted(shard, axis, by):
    peers = lax.axis_size(axis)
    pairs = [(i, i + by) for i in range(peers) if 0 <= i + by < peers]
    return lax.ppermute(shard, axis, pairs)


def layer_stats(values):
    center = values - jnp.mean(values, axis=-1, keepdims=True)
    spread = lax.rsqrt(jnp.mean(center * center, axis=-1, keepdims=True) + 1e-05)
    return (center * spread, spread)


def norm_back(grad_normed, normed, spread):
    return spread * (
        grad_normed
        - jnp.mean(grad_normed, axis=-1, keepdims=True)
        - normed * jnp.mean(grad_normed * normed, axis=-1, keepdims=True)
    )


def masked_scores(queries, key_heads, same_seg):
    raw = (
        jnp.einsum("rqhc,rkhc->rhqk", queries, key_heads, preferred_element_type=jnp.float32)
        * 0.125
    )
    return jnp.where(same_seg, raw, -1e30)


def sum_grads(grads):
    return (
        lax.psum_scatter(grads[0], ("tower", "dp"), scatter_dimension=0, tiled=True),
        lax.psum_scatter(grads[1], ("tower", "dp"), scatter_dimension=0, tiled=True),
        lax.psum_scatter(grads[2], ("tower", "dp"), scatter_dimension=0, tiled=True),
        lax.psum_scatter(grads[3], ("tower", "dp"), scatter_dimension=0, tiled=True),
        lax.psum_scatter(grads[4], ("tower", "dp"), scatter_dimension=0, tiled=True),
        lax.psum_scatter(grads[5], ("tower", "dp"), scatter_dimension=0, tiled=True),
        lax.psum_scatter(grads[6], ("tower", "dp"), scatter_dimension=0, tiled=True),
        lax.psum_scatter(grads[7], ("tower", "dp"), scatter_dimension=0, tiled=True),
        lax.psum_scatter(grads[8], ("tower", "dp"), scatter_dimension=0, tiled=True),
        lax.psum_scatter(grads[9], ("tower", "dp"), scatter_dimension=0, tiled=True),
        lax.psum_scatter(grads[10], ("tower", "dp"), scatter_dimension=0, tiled=True),
        lax.psum_scatter(grads[11], ("tower", "dp"), scatter_dimension=0, tiled=True),
        lax.psum_scatter(grads[12], ("tower", "dp"), scatter_dimension=0, tiled=True),
    )


def local(
    tokens,
    segments,
    caption_image,
    logit_scale,
    first_gain,
    first_bias,
    triple_weight,
    query_bias,
    value_bias,
    output_weight,
    output_bias,
    second_gain,
    second_bias,
    expand_weight,
    expand_bias,
    shrink_weight,
    shrink_bias,
):
    rows_here = tokens.shape[1]
    length = tokens.shape[2]
    features = tokens.shape[3]
    head_size = features // HEADS
    token_count = rows_here * length
    is_text = lax.axis_index("tower") == 1
    text_flag = is_text.astype(jnp.float32)
    position = jnp.arange(length, dtype=jnp.int32)
    image_segs = jnp.broadcast_to(
        (position >= IMG_TOK).astype(jnp.int32)[None, :], (rows_here, length)
    )
    seg_ids = jnp.where(is_text, segments, image_segs)
    same_seg = (seg_ids[:, :, None] == seg_ids[:, None, :])[:, None, :, :]
    head_shape = (rows_here, length, HEADS, head_size)
    gain_one = first_gain[0].astype(jnp.float32)
    shift_one = first_bias[0].astype(jnp.float32)
    triple_w = triple_weight[0]
    query_shift = query_bias[0].astype(jnp.float32)
    value_shift = value_bias[0].astype(jnp.float32)
    output_w = output_weight[0]
    output_shift = output_bias[0].astype(jnp.float32)
    gain_two = second_gain[0].astype(jnp.float32)
    shift_two = second_bias[0].astype(jnp.float32)
    expand_w = expand_weight[0]
    expand_shift = expand_bias[0].astype(jnp.float32)
    shrink_w = shrink_weight[0]
    shrink_shift = shrink_bias[0].astype(jnp.float32)
    inputs = tokens[0].reshape(token_count, features).astype(jnp.float32)
    normed_a, spread_a = layer_stats(inputs)
    normed_one = (normed_a * gain_one + shift_one).astype(jnp.bfloat16)
    triple = jnp.dot(normed_one, triple_w, preferred_element_type=jnp.float32)
    queries = (triple[:, :features] + query_shift).astype(jnp.bfloat16).reshape(head_shape)
    key_heads = triple[:, features : 2 * features].astype(jnp.bfloat16).reshape(head_shape)
    value_heads = (triple[:, 2 * features :] + value_shift).astype(jnp.bfloat16).reshape(head_shape)
    scores = masked_scores(queries, key_heads, same_seg)
    row_peak = jnp.max(scores, axis=-1, keepdims=True)
    log_total = row_peak + jnp.log(jnp.sum(jnp.exp(scores - row_peak), axis=-1, keepdims=True))
    attn_probs = jnp.exp(scores - log_total)
    mixed_low = (
        jnp.einsum(
            "rhqk,rkhc->rqhc",
            attn_probs.astype(jnp.bfloat16),
            value_heads,
            preferred_element_type=jnp.float32,
        )
        .reshape(token_count, features)
        .astype(jnp.bfloat16)
    )
    hidden = (
        inputs + jnp.dot(mixed_low, output_w, preferred_element_type=jnp.float32) + output_shift
    )
    normed_b, spread_b = layer_stats(hidden)
    normed_two = (normed_b * gain_two + shift_two).astype(jnp.bfloat16)
    expanded = jnp.dot(normed_two, expand_w, preferred_element_type=jnp.float32) + expand_shift
    activated, gelu_back = jax.vjp(jax.nn.gelu, expanded)
    active_low = activated.astype(jnp.bfloat16)
    block_out = (
        hidden + jnp.dot(active_low, shrink_w, preferred_element_type=jnp.float32) + shrink_shift
    )
    slot_ids = jnp.arange(CAPS, dtype=jnp.int32)
    member = (seg_ids[:, None, :] == slot_ids[None, :, None]).astype(jnp.float32)
    counts = jnp.maximum(jnp.sum(member, axis=2), 1.0)
    pooled = (
        jnp.einsum(
            "rst,rtd->rsd", member, block_out.reshape(rows_here, length, features), precision=HIGH
        )
        / counts[:, :, None]
    )
    inverse = lax.rsqrt(jnp.sum(pooled * pooled, axis=2, keepdims=True) + 1e-06)
    embedding = pooled * inverse
    first_slot = embedding[:, 0, :].astype(jnp.bfloat16)
    collected = lax.all_gather(first_slot, "dp", axis=0, tiled=True)
    image_table = shifted(collected, "tower", 1)
    text_low = embedding.reshape(rows_here * CAPS, features).astype(jnp.bfloat16)
    similar = jnp.einsum("cd,id->ci", text_low, image_table, preferred_element_type=jnp.float32)
    factor = logit_scale[0]
    logits = factor * similar
    logit_peak = jnp.max(logits, axis=1, keepdims=True)
    logit_total = logit_peak + jnp.log(jnp.sum(jnp.exp(logits - logit_peak), axis=1, keepdims=True))
    targets = caption_image.reshape(-1)
    image_ids = jnp.arange(image_table.shape[0], dtype=jnp.int32)
    target_hot = (image_ids[None, :] == targets[:, None]).astype(jnp.float32)
    picked = jnp.sum(logits * target_hot, axis=1)
    loss_here = jnp.sum(logit_total[:, 0] - picked) * text_flag
    grad_logits = (jnp.exp(logits - logit_total) - target_hot) * text_flag
    factor_here = jnp.sum(grad_logits * similar)
    loss_total, factor_total = lax.psum((loss_here, factor_here), ("tower", "dp"))
    caption_total = rows_here * CAPS * lax.axis_size("dp")
    grad_dots = (factor * grad_logits).astype(jnp.bfloat16)
    grad_emb = jnp.einsum(
        "ci,id->cd", grad_dots, image_table, preferred_element_type=jnp.float32
    ).reshape(rows_here, CAPS, features)
    grad_pooled = inverse * (
        grad_emb - embedding * jnp.sum(embedding * grad_emb, axis=2, keepdims=True)
    )
    grad_pooled = grad_pooled / counts[:, :, None]
    grad_out = jnp.einsum("rst,rsd->rtd", member, grad_pooled, precision=HIGH).reshape(
        token_count, features
    )
    shrink_bias_grad = jnp.sum(grad_out, axis=0)
    grad_out_low = grad_out.astype(jnp.bfloat16)
    shrink_weight_grad = jnp.einsum(
        "nf,nd->fd", active_low, grad_out_low, preferred_element_type=jnp.float32
    )
    grad_active = jnp.einsum(
        "nd,fd->nf", grad_out_low, shrink_w, preferred_element_type=jnp.float32
    )
    grad_expanded = gelu_back(grad_active)[0]
    expand_bias_grad = jnp.sum(grad_expanded, axis=0)
    grad_expanded_low = grad_expanded.astype(jnp.bfloat16)
    expand_weight_grad = jnp.einsum(
        "nd,nf->df", normed_two, grad_expanded_low, preferred_element_type=jnp.float32
    )
    grad_normed_two = jnp.einsum(
        "nf,df->nd", grad_expanded_low, expand_w, preferred_element_type=jnp.float32
    )
    second_gain_grad = jnp.sum(grad_normed_two * normed_b, axis=0)
    second_bias_grad = jnp.sum(grad_normed_two, axis=0)
    grad_hidden = grad_out + norm_back(grad_normed_two * gain_two, normed_b, spread_b)
    output_bias_grad = jnp.sum(grad_hidden, axis=0)
    grad_hidden_low = grad_hidden.astype(jnp.bfloat16)
    output_weight_grad = jnp.einsum(
        "nd,ne->de", mixed_low, grad_hidden_low, preferred_element_type=jnp.float32
    )
    grad_mixed = (
        jnp.einsum("ne,de->nd", grad_hidden_low, output_w, preferred_element_type=jnp.float32)
        .astype(jnp.bfloat16)
        .reshape(head_shape)
    )
    scores_again = masked_scores(queries, key_heads, same_seg)
    probs_again = jnp.exp(scores_again - log_total)
    probs_low = probs_again.astype(jnp.bfloat16)
    grad_values = jnp.einsum(
        "rhqk,rqhc->rkhc", probs_low, grad_mixed, preferred_element_type=jnp.float32
    )
    grad_probs = jnp.einsum(
        "rqhc,rkhc->rhqk", grad_mixed, value_heads, preferred_element_type=jnp.float32
    )
    grad_scores = (
        probs_again * (grad_probs - jnp.sum(probs_again * grad_probs, axis=-1, keepdims=True))
    ).astype(jnp.bfloat16)
    grad_queries = (
        jnp.einsum("rhqk,rkhc->rqhc", grad_scores, key_heads, preferred_element_type=jnp.float32)
        * 0.125
    )
    grad_keys = (
        jnp.einsum("rhqk,rqhc->rkhc", grad_scores, queries, preferred_element_type=jnp.float32)
        * 0.125
    )
    grad_queries = grad_queries.reshape(token_count, features)
    grad_keys = grad_keys.reshape(token_count, features)
    grad_values = grad_values.reshape(token_count, features)
    query_bias_grad = jnp.sum(grad_queries, axis=0)
    value_bias_grad = jnp.sum(grad_values, axis=0)
    grad_triple = jnp.concatenate([grad_queries, grad_keys, grad_values], axis=1).astype(
        jnp.bfloat16
    )
    triple_weight_grad = jnp.einsum(
        "nd,ne->de", normed_one, grad_triple, preferred_element_type=jnp.float32
    )
    grad_normed_one = jnp.einsum(
        "ne,de->nd", grad_triple, triple_w, preferred_element_type=jnp.float32
    )
    first_gain_grad = jnp.sum(grad_normed_one * normed_a, axis=0)
    first_bias_grad = jnp.sum(grad_normed_one, axis=0)
    input_grad = grad_hidden + norm_back(grad_normed_one * gain_one, normed_a, spread_a)
    shares = sum_grads(
        (
            first_gain_grad,
            first_bias_grad,
            triple_weight_grad,
            query_bias_grad,
            value_bias_grad,
            output_weight_grad,
            output_bias_grad,
            second_gain_grad,
            second_bias_grad,
            expand_weight_grad,
            expand_bias_grad,
            shrink_weight_grad,
            shrink_bias_grad,
        )
    )
    loss_out = (loss_total / caption_total).reshape(1)
    factor_out = factor_total.reshape(1)
    return (
        loss_out,
        factor_out,
        input_grad.reshape(1, rows_here, length, features),
        shares[0],
        shares[1],
        shares[2],
        shares[3],
        shares[4],
        shares[5],
        shares[6],
        shares[7],
        shares[8],
        shares[9],
        shares[10],
        shares[11],
        shares[12],
    )


def solution(mesh):
    placed = (
        P("tower", "dp", None, None),
        P("dp", None),
        P("dp", None),
        P(),
        P("tower", None),
        P("tower", None),
        P("tower", None, None),
        P("tower", None),
        P("tower", None),
        P("tower", None, None),
        P("tower", None),
        P("tower", None),
        P("tower", None),
        P("tower", None, None),
        P("tower", None),
        P("tower", None, None),
        P("tower", None),
    )
    fits = mesh.shape["tower"] == 2 and mesh.shape["dp"] == 2 * PLANE
    return jax.shard_map(
        local_fast if fits else local,
        mesh=mesh,
        in_specs=placed,
        out_specs=(
            P(),
            P(),
            P("tower", "dp", None, None),
            P(("tower", "dp")),
            P(("tower", "dp")),
            P(("tower", "dp"), None),
            P(("tower", "dp")),
            P(("tower", "dp")),
            P(("tower", "dp"), None),
            P(("tower", "dp")),
            P(("tower", "dp")),
            P(("tower", "dp")),
            P(("tower", "dp"), None),
            P(("tower", "dp")),
            P(("tower", "dp"), None),
            P(("tower", "dp")),
        ),
        check_vma=False,
    )
```
